32 devices in a mesh: rep: 2 (over core), ex: 16 (over z, y, x).
Axes of the slice: x: 2, y: 2, z: 4, core: 2. Of those that a mesh axis runs over, the one named last changes fastest.
Arguments:
- tokens: bfloat16 [4096, 2048], P(('rep', 'ex')), may hold values from -6 to 6
- out_cot: bfloat16 [4096, 2048], P(('rep', 'ex')), may hold values from -6 to 6
- destination: int32 [4096], P(('rep', 'ex')), may hold values from 0 to 4095, as said below
- doc_lengths: int32 [32, 4], P(('rep', 'ex')), may hold values from 1 to 112, 128 in all within a row
- routes: int32 [4096, 8], P(('rep', 'ex')), may hold values from 0 to 15, all different within a row
- fill_order: int32 [32, 1024], P(('rep', 'ex')), may hold values from 0 to 1023, each once within a row
- query_weight: bfloat16 [2048, 2048], P(('rep', 'ex')), may hold values from -0.125 to 0.125
- key_weight: bfloat16 [2048, 2048], P(('rep', 'ex')), may hold values from -0.125 to 0.125
- value_weight: bfloat16 [2048, 2048], P(('rep', 'ex')), may hold values from -0.125 to 0.125
- output_weight: bfloat16 [2048, 2048], P(('rep', 'ex')), may hold values from -0.5 to 0.5
- query_gain: bfloat16 [2048], P(('rep', 'ex')), may hold values from 0.5 to 1.5
- key_gain: bfloat16 [2048], P(('rep', 'ex')), may hold values from 0.5 to 1.5
- attn_gain: bfloat16 [2048], P(('rep', 'ex')), may hold values from 0.5 to 1.5
- moe_gain: bfloat16 [2048], P(('rep', 'ex')), may hold values from 0.5 to 1.5
- router_weight: bfloat16 [2048, 16], P(('rep', 'ex')), may hold values from -0.0625 to 0.0625
- expert_gate: bfloat16 [16, 2048, 1024], P('ex', 'rep'), may hold values from -0.125 to 0.125
- expert_up: bfloat16 [16, 2048, 1024], P('ex', 'rep'), may hold values from -0.125 to 0.125
- expert_down: bfloat16 [16, 1024, 2048], P('ex', 'rep'), may hold values from -6 to 6
Outputs:
- block_output: bfloat16 [4096, 2048], P(('rep', 'ex'))
- grad_tokens: bfloat16 [4096, 2048], P(('rep', 'ex'))
- grad_query_weight: float32 [2048, 2048], P(('rep', 'ex'))
- grad_key_weight: float32 [2048, 2048], P(('rep', 'ex'))
- grad_value_weight: float32 [2048, 2048], P(('rep', 'ex'))
- grad_output_weight: float32 [2048, 2048], P(('rep', 'ex'))
- grad_query_gain: float32 [2048], P(('rep', 'ex'))
- grad_key_gain: float32 [2048], P(('rep', 'ex'))
- grad_attn_gain: float32 [2048], P(('rep', 'ex'))
- grad_moe_gain: float32 [2048], P(('rep', 'ex'))
- grad_router_weight: float32 [2048, 16], P(('rep', 'ex'))
- grad_expert_gate: float32 [16, 2048, 1024], P('ex', 'rep')
- grad_expert_up: float32 [16, 2048, 1024], P('ex', 'rep')
- grad_expert_down: float32 [16, 1024, 2048], P('ex', 'rep')
The draws below stay inside these ranges and needn't reach their ends.
Inputs may be any that keep to these rules, and one draw needn't show every extreme that they name: `destination`: A permutation of all token rows that keeps every token within its group of 2048 consecutive rows (one index of rep). Each device of a group sends exactly 8 of its rows to each device of the group, and the rows that device s of the group sends to a device land, in their given order, at its packed rows s * (8) to (s + 1) * 8 - 1. `doc_lengths`: each row gives 4 segment lengths that add up to 128. `routes`: each row names 8 different experts. `fill_order`: each row lists every pair number t * 8 + j of its block once.
All inputs are finite; a program needn't handle non-finite values.
Results may differ from the reference program's by a relative error of at most 0.019.
Values may be sent and summed in bfloat16 or wider, within the bound.
A program may use at most 320 MiB of HBM per device.

```python
import math
import jax
import jax.numpy as jnp
import numpy as np
from jax import lax

D = 2048
HEADS = 16
HEAD_DIM = 128
FF = 1024
TOP = 8
EXPERTS = 16
TOK_DEV = 128
DOCS = 4
SEQ_MAX = 112
CAP = 64
PAIRS = 1024
TOKENS = 4096
N_EX = 16
DEVICES = 32


def draw_destination(key, part):
    per_block = TOK_DEV // N_EX
    keys = jax.random.split(jax.random.fold_in(key, 11), DEVICES)
    shuffled = jax.vmap(lambda one_key: jax.random.permutation(one_key, TOK_DEV))(keys).astype(jnp.int32)
    target_device = shuffled // per_block
    member = (target_device[:, :, None] == jnp.arange(N_EX, dtype=jnp.int32)[None, None, :]).astype(jnp.int32)
    earlier = jnp.cumsum(member, axis=1) - member
    arrival = jnp.sum(earlier * member, axis=2)
    device_index = jnp.arange(DEVICES, dtype=jnp.int32)
    group_index = device_index // N_EX
    member_index = device_index % N_EX
    packed = group_index[:, None] * (N_EX * TOK_DEV) + target_device * TOK_DEV + member_index[:, None] * per_block + arrival
    return packed.reshape(-1).astype(jnp.int32)


def steps_of(own_key, extent, cuts, smallest, high):
    factor_of, own = 1.0, jax.random.fold_in(own_key, 6)
    for axis_at, parts in cuts:
        steps = jnp.exp(jax.random.uniform(jax.random.fold_in(own, axis_at), (parts,), jnp.float32, smallest / len(cuts), high / len(cuts)))
        factor_of = factor_of * jnp.repeat(steps, extent[axis_at] // parts).reshape([-1 if axis == axis_at else 1 for axis in range(len(extent))])
    return factor_of


def choose_distinct(key, rows, amount, top, lift):
    sequence = jax.random.permutation(jax.random.fold_in(key, 1), amount)
    favour = sequence
    for power in range(3):
        favour = favour * favour // amount
    favour = favour * lift // amount
    chance = jax.random.randint(jax.random.fold_in(key, 2), (rows, amount), 0, 4096) + favour
    sure = jax.random.permutation(jax.random.fold_in(key, 3), rows)[jnp.arange(amount) % rows]
    chance = jnp.where(jnp.arange(rows)[:, None] == sure[None, :], 1 << 14, chance)
    priority = chance * amount + jnp.arange(amount)
    return lax.top_k(priority.astype(jnp.int32), top)[1].astype(jnp.int32)


def split_up(amount, total, reach, slope):
    weights = [(1 << 20) // math.isqrt(rank ** slope) + 1 for rank in range(2, amount + 1)]
    spare, counts = total - reach - (amount - 1), [1] * (amount - 1)
    while spare > 0:
        candidates = [i for i in range(amount - 1) if counts[i] < reach]
        whole, remaining = sum([weights[i] for i in candidates]), spare
        for i in candidates:
            extra = min(reach - counts[i], max(1, remaining * weights[i] // whole), spare)
            counts[i] = counts[i] + extra
            spare = spare - extra
    return np.array([reach] + counts)


def uneven_parts(own_key, number_of, total, reach, lean):
    if number_of == 2:
        one = jax.random.randint(own_key, (), max(1, total - reach), min(reach, total - 1) + 1)
        return jnp.stack([one, total - one])
    sizes = jnp.asarray(split_up(number_of, total, reach, lean), jnp.int32)
    pairs = (number_of - 1) // 2
    donor, receiver = sizes[1:1 + 2 * pairs:2], sizes[2:2 + 2 * pairs:2]
    margin = jnp.minimum(donor - 1, reach - receiver)
    moved = jax.random.randint(jax.random.fold_in(own_key, 1), (pairs,), 0, 1 << 20) % (margin + 1)
    sizes = sizes.at[1:1 + 2 * pairs:2].set(donor - moved).at[2:2 + 2 * pairs:2].set(receiver + moved)
    return sizes[jax.random.permutation(jax.random.fold_in(own_key, 2), number_of)]


def centred(key, dims, spread, most, cuts=(), kind=jnp.bfloat16):
    loudness = steps_of(key, dims, cuts, -0.22, 0.18) if cuts else 1.0
    array = jax.random.normal(key, dims, jnp.float32) * spread * loudness
    return jnp.minimum(jnp.maximum(array, -most), most).astype(kind)


def setup_inputs(seed: int = 0) -> dict:
    seeds = jax.random.split(jax.random.key(seed), 19)
    return {
        "tokens": centred(seeds[0], (TOKENS, D), 1.0, 6.0, ((0, 32),)),
        "out_cot": centred(seeds[1], (TOKENS, D), 1.0, 6.0, ((0, 32),)),
        "destination": draw_destination(jax.random.fold_in(seeds[18], 71), 0),
        "doc_lengths": jax.vmap(lambda own: uneven_parts(own, DOCS, TOK_DEV, SEQ_MAX, 1))(jax.random.split(seeds[3], DEVICES)).reshape((DEVICES, DOCS)).astype(jnp.int32),
        "routes": choose_distinct(seeds[4], TOKENS, EXPERTS, TOP, 4096),
        "fill_order": jax.vmap(lambda own: jax.random.permutation(own, PAIRS))(jax.random.split(seeds[5], DEVICES)).reshape((DEVICES, PAIRS)).astype(jnp.int32),
        "query_weight": centred(seeds[6], (D, D), D ** -0.5, 0.125, ((0, 32),)),
        "key_weight": centred(seeds[7], (D, D), D ** -0.5, 0.125, ((0, 32),)),
        "value_weight": centred(seeds[8], (D, D), D ** -0.5, 0.125, ((0, 32),)),
        "output_weight": centred(seeds[9], (D, D), (D // 16) ** -0.5, 0.5, ((0, 32),)),
        "query_gain": jnp.clip(1.0 + 0.1 * jax.random.normal(seeds[10], (D,), jnp.float32), 0.5, 1.5).astype(jnp.bfloat16),
        "key_gain": jnp.clip(1.0 + 0.1 * jax.random.normal(seeds[11], (D,), jnp.float32), 0.5, 1.5).astype(jnp.bfloat16),
        "attn_gain": jnp.clip(1.0 + 0.1 * jax.random.normal(seeds[12], (D,), jnp.float32), 0.5, 1.5).astype(jnp.bfloat16),
        "moe_gain": jnp.clip(1.0 + 0.1 * jax.random.normal(seeds[13], (D,), jnp.float32), 0.5, 1.5).astype(jnp.bfloat16),
        "router_weight": centred(seeds[14], (D, EXPERTS), (4 * D) ** -0.5, 0.0625, ((0, 32),)),
        "expert_gate": centred(seeds[15], (EXPERTS, D, FF), D ** -0.5, 0.125, ((0, 16), (1, 2))),
        "expert_up": centred(seeds[16], (EXPERTS, D, FF), D ** -0.5, 0.125, ((0, 16), (1, 2))),
        "expert_down": centred(seeds[17], (EXPERTS, FF, D), (max(FF // 1024, 1)) ** -0.5, 6.0, ((0, 16), (1, 2))),
    }


epsilon = 1e-05
rope_base = 10000.0
masked_score = -1e+30

@jax.custom_vjp
def low(v):
    return lax.optimization_barrier(v.astype(jnp.bfloat16)).astype(jnp.float32)

@jax.custom_vjp
def low_back(v):
    return v

def low_keep(v):
    return (low(v), None)

def low_pass(kept, grad):
    return (grad,)

def back_keep(v):
    return (v, None)

def back_low(kept, grad):
    return (low(grad),)
low.defvjp(low_keep, low_pass)
low_back.defvjp(back_keep, back_low)

def highest(left, right):
    return jnp.dot(left, right, precision=lax.Precision.HIGHEST, preferred_element_type=jnp.float32)

def normalize(values):
    return values * lax.rsqrt(lax.optimization_barrier(jnp.mean(values * values, axis=-1, keepdims=True)) + epsilon)

def rotate_half(values):
    middle = values.shape[-1] // 2
    return jnp.concatenate([-values[..., middle:], values[..., :middle]], axis=-1)

def rope_tables(position):
    steps = jnp.arange(HEAD_DIM // 2, dtype=jnp.float32) * (2.0 / HEAD_DIM)
    inverse = rope_base ** (-steps)
    angle = position.astype(jnp.float32)[:, None] * inverse[None, :]
    cosine = jnp.concatenate([jnp.cos(angle), jnp.cos(angle)], axis=-1)[:, None, :]
    sine = jnp.concatenate([jnp.sin(angle), jnp.sin(angle)], axis=-1)[:, None, :]
    return (cosine, sine)

def segment_tables(lengths, row_count):
    ends = jnp.cumsum(lengths).astype(jnp.int32)
    starts = ends - lengths
    row_index = jnp.arange(row_count, dtype=jnp.int32)
    segment = lax.optimization_barrier(jnp.sum((row_index[:, None] >= ends[None, :]).astype(jnp.int32), axis=1))
    numbers = jnp.arange(lengths.shape[0], dtype=jnp.int32)
    begin = lax.optimization_barrier(jnp.sum(jnp.where(segment[:, None] == numbers[None, :], starts[None, :], 0), axis=1))
    return (segment, row_index - begin, segment < lengths.shape[0] - 1)

def slot_tables(route_rows, filling, live_rows, experts, capacity):
    top_count = route_rows.shape[1]
    pair_expert = route_rows.reshape(-1)
    pair_live = jnp.repeat(live_rows, top_count)
    ordered_expert = pair_expert[filling]
    ordered_live = pair_live[filling]
    member = ((ordered_expert[:, None] == jnp.arange(experts, dtype=jnp.int32)[None, :]) & ordered_live[:, None]).astype(jnp.int32)
    earlier = jnp.cumsum(member, axis=0) - member
    ordered_slot = lax.optimization_barrier(jnp.sum(earlier * member, axis=1)).astype(jnp.int32)
    slot_index = jnp.zeros_like(ordered_slot).at[filling].set(ordered_slot)
    return (slot_index, pair_live & (slot_index < capacity))

def reference(tokens, out_cot, destination, doc_lengths, routes, fill_order, query_weight, key_weight, value_weight, output_weight, query_gain, key_gain, attn_gain, moe_gain, router_weight, expert_gate, expert_up, expert_down):
    all_index = jnp.arange(TOKENS, dtype=jnp.int32)
    source = jnp.zeros((TOKENS,), jnp.int32).at[destination].set(all_index)
    hidden_in = tokens.astype(jnp.float32)[source]
    cot_in = out_cot.astype(jnp.float32)[source]
    segment, position, live_rows = jax.vmap(lambda lengths_row: segment_tables(lengths_row, TOK_DEV))(doc_lengths)
    routes_dev = routes.reshape(DEVICES, TOK_DEV, TOP)
    slot_index, keep_pair = jax.vmap(lambda route_rows, filling, live_row: slot_tables(route_rows, filling, live_row, EXPERTS, CAP))(routes_dev, fill_order, live_rows)
    span = DEVICES * CAP
    device_index = jnp.arange(DEVICES, dtype=jnp.int32)[:, None]
    flat_slot = routes_dev.reshape(DEVICES, PAIRS) * span + device_index * CAP + slot_index
    target = jnp.where(keep_pair, flat_slot, EXPERTS * span).reshape(-1)
    pair_index = jnp.arange(TOKENS * TOP, dtype=jnp.int32)
    slot_pair = jnp.full((EXPERTS * span,), TOKENS * TOP, jnp.int32).at[target].set(pair_index, mode='drop')
    slot_row = (slot_pair // TOP).reshape(EXPERTS, span)
    safe_target = jnp.minimum(target, EXPERTS * span - 1).reshape(TOKENS, TOP)
    keep_float = keep_pair.reshape(TOKENS, TOP).astype(jnp.float32)
    live_column = live_rows.reshape(TOKENS, 1).astype(jnp.float32)
    cosine, sine = rope_tables(position.reshape(-1))
    score_scale = HEAD_DIM ** (-0.5)

    def attend(block_data):
        query_block, key_block, value_block, segment_block = block_data
        local_index = jnp.arange(TOK_DEV, dtype=jnp.int32)
        visible = (segment_block[:, None] == segment_block[None, :]) & (local_index[None, :] <= local_index[:, None])
        scores = jnp.einsum('qhd,khd->hqk', query_block, key_block, precision=lax.Precision.HIGHEST) * score_scale
        scores = low_back(jnp.where(visible[None], scores, masked_score))
        probs = jax.nn.softmax(scores, axis=-1)
        return jnp.einsum('hqk,khd->qhd', low(probs), value_block, precision=lax.Precision.HIGHEST)

    def forward(hidden, query_full, key_full, value_full, output_full, query_scale, key_scale, attn_scale, moe_scale, router_full, gate_all, up_all, down_all):
        attn_in = low(normalize(hidden) * attn_scale)
        query_pre = low_back(highest(attn_in, query_full))
        key_pre = low_back(highest(attn_in, key_full))
        value_pre = low(low_back(highest(attn_in, value_full)))
        query_norm = (normalize(query_pre) * query_scale).reshape(TOKENS, HEADS, HEAD_DIM)
        key_norm = (normalize(key_pre) * key_scale).reshape(TOKENS, HEADS, HEAD_DIM)
        query_rot = low(query_norm * cosine + rotate_half(query_norm) * sine)
        key_rot = low(key_norm * cosine + rotate_half(key_norm) * sine)
        shape_dev = (DEVICES, TOK_DEV, HEADS, HEAD_DIM)
        mixed = lax.map(jax.checkpoint(attend), (query_rot.reshape(shape_dev), key_rot.reshape(shape_dev), value_pre.reshape(shape_dev), segment))
        mixed = low_back(low(mixed.reshape(TOKENS, D)))
        branch = low_back(highest(mixed, output_full))
        after_attn = hidden + live_column * branch
        moe_in = low(normalize(after_attn) * moe_scale)
        router_probs = jax.nn.softmax(highest(moe_in, router_full), axis=-1)
        gates = jnp.take_along_axis(router_probs, routes, axis=1) * keep_float
        padded = jnp.concatenate([moe_in, jnp.zeros((1, D), jnp.float32)], axis=0)

        def expert(block_data):
            slot_rows, gate_matrix, up_matrix, down_matrix = block_data
            rows_in = low_back(padded[slot_rows])
            gate_pre = low_back(highest(rows_in, gate_matrix))
            up_pre = low_back(highest(rows_in, up_matrix))
            middle = low(jax.nn.silu(gate_pre) * up_pre)
            return low_back(low(highest(middle, down_matrix)))
        results = lax.map(jax.checkpoint(expert), (slot_row, gate_all, up_all, down_all)).reshape(EXPERTS * span, D)
        mixture = jnp.zeros((TOKENS, D), jnp.float32)
        for choice_index in range(TOP):
            mixture = mixture + gates[:, choice_index:choice_index + 1] * results[safe_target[:, choice_index]]
        return after_attn + mixture
    primals = (hidden_in, query_weight.astype(jnp.float32), key_weight.astype(jnp.float32), value_weight.astype(jnp.float32), output_weight.astype(jnp.float32), query_gain.astype(jnp.float32), key_gain.astype(jnp.float32), attn_gain.astype(jnp.float32), moe_gain.astype(jnp.float32), router_weight.astype(jnp.float32), expert_gate.astype(jnp.float32), expert_up.astype(jnp.float32), expert_down.astype(jnp.float32))
    output, pullback = jax.vjp(forward, *primals)
    grads = pullback(cot_in)
    return (output[destination].astype(jnp.bfloat16), grads[0][destination].astype(jnp.bfloat16), grads[1], grads[2], grads[3], grads[4], grads[5], grads[6], grads[7], grads[8], grads[9], grads[10], grads[11], grads[12])
```

```python
import jax
import jax.numpy as jnp
from jax import lax
from jax.sharding import PartitionSpec as P

HEADS = 16
HEAD_DIM = 128

epsilon = 1e-05
rope_base = 10000.0
masked_score = -1e30
bf16 = jnp.bfloat16
f32 = jnp.float32


def normalize(values):
    scale = lax.rsqrt(jnp.mean(values * values, axis=-1, keepdims=True) + epsilon)
    return (values * scale, scale)


def norm_back(grad_normed, normed, scale):
    return scale * (grad_normed - normed * jnp.mean(grad_normed * normed, axis=-1, keepdims=True))


def rotate_half(values):
    middle = values.shape[-1] // 2
    return jnp.concatenate([-values[..., middle:], values[..., :middle]], axis=-1)


def rotate_back(values):
    middle = values.shape[-1] // 2
    return jnp.concatenate([values[..., middle:], -values[..., :middle]], axis=-1)


def rope_tables(position):
    steps = jnp.arange(HEAD_DIM // 2, dtype=f32) * (2.0 / HEAD_DIM)
    inverse = rope_base ** (-steps)
    angle = position.astype(f32)[:, None] * inverse[None, :]
    cosine = jnp.concatenate([jnp.cos(angle), jnp.cos(angle)], axis=-1)[:, None, :]
    sine = jnp.concatenate([jnp.sin(angle), jnp.sin(angle)], axis=-1)[:, None, :]
    return (cosine, sine)


def segment_tables(lengths, row_count):
    count = lengths.shape[0]
    numbers = jnp.arange(count, dtype=jnp.int32)
    before = (numbers[None, :] < numbers[:, None]).astype(jnp.int32)
    starts = jnp.sum(before * lengths[None, :], axis=1)
    ends = starts + lengths
    row_index = jnp.arange(row_count, dtype=jnp.int32)
    segment = jnp.sum((row_index[:, None] >= ends[None, :]).astype(jnp.int32), axis=1)
    begin = jnp.sum(jnp.where(segment[:, None] == numbers[None, :], starts[None, :], 0), axis=1)
    return (segment, row_index - begin, segment < count - 1)


def slot_tables(routes, filling, live_rows, experts, capacity):
    row_count, top_count = routes.shape
    order = jnp.arange(row_count * top_count, dtype=jnp.int32)
    rows = jnp.arange(row_count, dtype=jnp.int32)
    hot_row = (filling[None, :] // top_count == rows[:, None]).astype(bf16)
    hot_choice = (filling % top_count)[:, None] == jnp.arange(top_count, dtype=jnp.int32)[None, :]
    high = jnp.where(hot_choice, (order // 64)[:, None], 0).astype(bf16)
    lower = jnp.where(hot_choice, (order % 64)[:, None], 0).astype(bf16)
    ranks = jnp.dot(
        hot_row, jnp.concatenate([high, lower], axis=1), preferred_element_type=f32
    ).astype(jnp.int32)
    rank = ranks[:, :top_count] * 64 + ranks[:, top_count:]
    chosen = routes[:, :, None] == jnp.arange(experts, dtype=jnp.int32)[None, None, :]
    rank_table = jnp.sum(jnp.where(chosen, rank[:, :, None], 0), axis=1)
    counted = jnp.any(chosen, axis=1) & live_rows[:, None]
    earlier = counted[:, None, :] & (rank_table[:, None, :] < rank_table[None, :, :])
    slot = jnp.sum(earlier.astype(jnp.int32), axis=0)
    kept = counted & (slot < capacity)
    return (jnp.where(kept, slot, -1), kept)


def attention_scores(query_low, key_low, visible):
    scores = jnp.einsum(
        "qhd,khd->hqk", query_low, key_low, preferred_element_type=f32
    ) * HEAD_DIM ** (-0.5)
    return jnp.where(visible[None], scores, masked_score)


def body(
    tokens,
    out_cot,
    destination,
    doc_lengths,
    routes,
    fill_order,
    query_weight,
    key_weight,
    value_weight,
    output_weight,
    query_gain,
    key_gain,
    attn_gain,
    moe_gain,
    router_weight,
    expert_gate,
    expert_up,
    expert_down,
):
    both = ("rep", "ex")
    group_size = lax.axis_size("ex")
    row_count, model_width = tokens.shape
    block_rows = row_count // group_size
    row_index = jnp.arange(row_count, dtype=jnp.int32)
    placed = destination // row_count % group_size * block_rows + destination % block_rows
    to_send = (placed[None, :] == row_index[:, None]).astype(bf16)
    inbound = jnp.dot(
        to_send, jnp.concatenate([tokens, out_cot], axis=1), preferred_element_type=f32
    ).astype(bf16)
    packed = lax.all_to_all(inbound, "ex", split_axis=0, concat_axis=0, tiled=True)
    hidden_in, cot_in = packed[:, :model_width], packed[:, model_width:]
    query_full = lax.all_gather(query_weight, both, axis=0, tiled=True)
    key_full = lax.all_gather(key_weight, both, axis=0, tiled=True)
    value_full = lax.all_gather(value_weight, both, axis=0, tiled=True)
    gains = jnp.concatenate(
        [jnp.stack([query_gain, key_gain, attn_gain, moe_gain], axis=1), router_weight], axis=1
    )
    gains = lax.all_gather(gains, both, axis=0, tiled=True)
    query_scale, key_scale, attn_scale, moe_scale = (gains[:, i].astype(f32) for i in range(4))
    router_full = gains[:, 4:]
    output_full = lax.all_gather(output_weight, both, axis=0, tiled=True)
    gate_full = lax.all_gather(expert_gate[0], "rep", axis=0, tiled=True)
    up_full = lax.all_gather(expert_up[0], "rep", axis=0, tiled=True)
    down_full = lax.all_gather(expert_down[0], "rep", axis=0, tiled=True)
    cot_all = lax.all_gather(cot_in, "ex", axis=0)

    segment, position, live_rows = segment_tables(doc_lengths[0], row_count)
    live_column = live_rows.astype(f32)[:, None]
    hidden = hidden_in.astype(f32)
    normed_attn, scale_attn = normalize(hidden)
    attn_in = (normed_attn * attn_scale).astype(bf16)
    query_pre = jnp.dot(attn_in, query_full, preferred_element_type=f32)
    key_pre = jnp.dot(attn_in, key_full, preferred_element_type=f32)
    value_pre = jnp.dot(attn_in, value_full, preferred_element_type=f32)
    normed_query, scale_query = normalize(query_pre)
    normed_key, scale_key = normalize(key_pre)
    cosine, sine = rope_tables(position)
    query_norm = (normed_query * query_scale).reshape(row_count, HEADS, HEAD_DIM)
    key_norm = (normed_key * key_scale).reshape(row_count, HEADS, HEAD_DIM)
    query_low = (query_norm * cosine + rotate_half(query_norm) * sine).astype(bf16)
    key_low = (key_norm * cosine + rotate_half(key_norm) * sine).astype(bf16)
    value_low = value_pre.astype(bf16).reshape(row_count, HEADS, HEAD_DIM)
    visible = (segment[:, None] == segment[None, :]) & (row_index[None, :] <= row_index[:, None])
    scores = attention_scores(query_low, key_low, visible)
    peak = jnp.max(scores, axis=-1, keepdims=True)
    weights_exp = jnp.exp(scores - peak)
    probs = weights_exp / jnp.sum(weights_exp, axis=-1, keepdims=True)
    probs_low = probs.astype(bf16)
    mixed = jnp.einsum("hqk,khd->qhd", probs_low, value_low, preferred_element_type=f32)
    mixed = mixed.reshape(row_count, model_width).astype(bf16)
    branch = jnp.dot(mixed, output_full, preferred_element_type=f32)
    after_attn = hidden + live_column * branch
    normed_moe, scale_moe = normalize(after_attn)
    moe_in = (normed_moe * moe_scale).astype(bf16)
    logits = jnp.dot(moe_in, router_full, preferred_element_type=f32)
    router_probs = jax.nn.softmax(logits, axis=-1)
    experts = router_full.shape[1]
    capacity = row_count * routes.shape[1] // experts
    slot_table, kept = slot_tables(routes, fill_order[0], live_rows, experts, capacity)
    gates = jnp.where(kept, router_probs, 0.0)

    sent = jnp.stack([gates, slot_table.astype(f32)], axis=0).transpose(2, 0, 1)
    given = lax.all_to_all(sent, "ex", split_axis=0, concat_axis=0, tiled=True)
    moe_all = lax.all_gather(moe_in, "ex", axis=0)
    gate_rows, slot_rows = given[:, 0], given[:, 1]
    slots = jnp.arange(capacity, dtype=jnp.int32).astype(f32)
    picked = slot_rows[:, None, :] == slots[None, :, None]
    picked_low = picked.astype(bf16)
    slot_gate = jnp.sum(jnp.where(picked, gate_rows[:, None, :], 0.0), axis=2).reshape(-1, 1)

    def pick(rows):
        chosen = jnp.einsum("sct,std->scd", picked_low, rows, preferred_element_type=f32)
        return chosen.astype(bf16).reshape(-1, model_width)

    def spread(rows):
        rows = rows.reshape(group_size, capacity, model_width)
        return jnp.einsum("sct,scd->std", picked_low, rows, preferred_element_type=f32).astype(bf16)

    rows_in, rows_cot = pick(moe_all), pick(cot_all)
    gate_pre = jnp.dot(rows_in, gate_full, preferred_element_type=f32)
    up_pre = jnp.dot(rows_in, up_full, preferred_element_type=f32)
    sigma = jax.nn.sigmoid(gate_pre)
    silu = gate_pre * sigma
    middle = (silu * up_pre).astype(bf16)
    expert_out = jnp.dot(middle, down_full, preferred_element_type=f32).astype(bf16)
    slot_grad = jnp.sum(rows_cot.astype(f32) * expert_out.astype(f32), axis=1)
    weighted = (slot_gate * expert_out.astype(f32)).astype(bf16)
    grad_expert_out = (slot_gate * rows_cot.astype(f32)).astype(bf16)
    grad_middle = jnp.dot(grad_expert_out, down_full.T, preferred_element_type=f32)
    grad_down_full = jnp.dot(middle.T, grad_expert_out, preferred_element_type=f32)
    grad_gate_low = (grad_middle * up_pre * sigma * (1.0 + gate_pre * (1.0 - sigma))).astype(bf16)
    grad_up_low = (grad_middle * silu).astype(bf16)
    grad_gate_full = jnp.dot(rows_in.T, grad_gate_low, preferred_element_type=f32)
    grad_up_full = jnp.dot(rows_in.T, grad_up_low, preferred_element_type=f32)
    grad_rows = jnp.dot(grad_gate_low, gate_full.T, preferred_element_type=f32)
    grad_rows = (
        grad_rows + jnp.dot(grad_up_low, up_full.T, preferred_element_type=f32)
    ).astype(bf16)
    slot_grad = slot_grad.reshape(group_size, capacity, 1)
    grad_back = jnp.sum(jnp.where(picked, slot_grad, 0.0), axis=1)
    grad_moe_in = lax.psum_scatter(spread(grad_rows), "ex", scatter_dimension=0).astype(f32)
    mixture = lax.psum_scatter(spread(weighted), "ex", scatter_dimension=0).astype(f32)
    grad_rprobs = lax.all_to_all(grad_back, "ex", split_axis=0, concat_axis=0, tiled=True).T
    output = (after_attn + mixture).astype(bf16)
    owned_gate, owned_up, owned_down = (
        lax.psum_scatter(g.astype(bf16), "rep", scatter_dimension=0, tiled=True).astype(f32)[None]
        for g in (grad_gate_full, grad_up_full, grad_down_full)
    )

    grad_out = cot_in.astype(f32)
    grad_logits = router_probs * (
        grad_rprobs - jnp.sum(router_probs * grad_rprobs, axis=-1, keepdims=True)
    )
    grad_moe_in = grad_moe_in + jnp.dot(
        grad_logits, router_full.T, precision=lax.Precision.HIGHEST, preferred_element_type=f32
    )
    grad_router = jnp.dot(
        moe_in.T, grad_logits, precision=lax.Precision.HIGHEST, preferred_element_type=f32
    )
    grad_moe_scale = jnp.sum(grad_moe_in * normed_moe, axis=0)
    grad_after = grad_out + norm_back(grad_moe_in * moe_scale, normed_moe, scale_moe)
    grad_branch = (live_column * grad_after).astype(bf16)
    grad_output_full = jnp.dot(mixed.T, grad_branch, preferred_element_type=f32)
    grad_mixed = (
        jnp.dot(grad_branch, output_full.T, preferred_element_type=f32)
        .astype(bf16)
        .reshape(row_count, HEADS, HEAD_DIM)
    )
    grad_value = jnp.einsum("hqk,qhd->khd", probs_low, grad_mixed, preferred_element_type=f32)
    grad_att = jnp.einsum("qhd,khd->hqk", grad_mixed, value_low, preferred_element_type=f32)
    grad_scores = (probs * (grad_att - jnp.sum(probs * grad_att, axis=-1, keepdims=True))).astype(
        bf16
    )
    grad_query_rot = jnp.einsum(
        "hqk,khd->qhd", grad_scores, key_low, preferred_element_type=f32
    ) * HEAD_DIM ** (-0.5)
    grad_key_rot = jnp.einsum(
        "hqk,qhd->khd", grad_scores, query_low, preferred_element_type=f32
    ) * HEAD_DIM ** (-0.5)
    grad_query_normed = (grad_query_rot * cosine + rotate_back(grad_query_rot * sine)).reshape(
        row_count, model_width
    )
    grad_key_normed = (grad_key_rot * cosine + rotate_back(grad_key_rot * sine)).reshape(
        row_count, model_width
    )
    grad_query_scale = jnp.sum(grad_query_normed * normed_query, axis=0)
    grad_key_scale = jnp.sum(grad_key_normed * normed_key, axis=0)
    grad_query_pre = norm_back(grad_query_normed * query_scale, normed_query, scale_query)
    grad_key_pre = norm_back(grad_key_normed * key_scale, normed_key, scale_key)
    grad_query_pre = grad_query_pre.astype(bf16)
    grad_key_pre = grad_key_pre.astype(bf16)
    grad_value_pre = grad_value.reshape(row_count, model_width).astype(bf16)
    grad_attn_in = jnp.dot(grad_query_pre, query_full.T, preferred_element_type=f32)
    grad_attn_in = grad_attn_in + jnp.dot(grad_key_pre, key_full.T, preferred_element_type=f32)
    grad_attn_in = grad_attn_in + jnp.dot(grad_value_pre, value_full.T, preferred_element_type=f32)
    grad_query_full = jnp.dot(attn_in.T, grad_query_pre, preferred_element_type=f32)
    grad_key_full = jnp.dot(attn_in.T, grad_key_pre, preferred_element_type=f32)
    grad_value_full = jnp.dot(attn_in.T, grad_value_pre, preferred_element_type=f32)
    grad_attn_scale = jnp.sum(grad_attn_in * normed_attn, axis=0)
    grad_hidden = grad_after + norm_back(grad_attn_in * attn_scale, normed_attn, scale_attn)

    owned_query, owned_key, owned_value, owned_output = (
        lax.psum_scatter(g.astype(bf16), both, scatter_dimension=0, tiled=True).astype(f32)
        for g in (grad_query_full, grad_key_full, grad_value_full, grad_output_full)
    )
    small = jnp.concatenate(
        [
            jnp.stack([grad_query_scale, grad_key_scale, grad_attn_scale, grad_moe_scale], axis=1),
            grad_router,
        ],
        axis=1,
    )
    small = lax.psum_scatter(small, both, scatter_dimension=0, tiled=True)
    outbound = jnp.concatenate([output, grad_hidden.astype(bf16)], axis=1)
    outbound = lax.all_to_all(outbound, "ex", split_axis=0, concat_axis=0, tiled=True)
    outbound = jnp.dot(to_send.T, outbound, preferred_element_type=f32).astype(bf16)
    return (
        outbound[:, :model_width],
        outbound[:, model_width:],
        owned_query,
        owned_key,
        owned_value,
        owned_output,
        small[:, 0],
        small[:, 1],
        small[:, 2],
        small[:, 3],
        small[:, 4:],
        owned_gate,
        owned_up,
        owned_down,
    )


def solution(mesh):
    rows, row = P(("rep", "ex"), None), P(("rep", "ex"))
    expert = P("ex", "rep", None)
    return jax.shard_map(
        body,
        mesh=mesh,
        in_specs=(rows, rows, row) + (rows,) * 7 + (row,) * 4 + (rows,) + (expert,) * 3,
        out_specs=(rows,) * 6 + (row,) * 4 + (rows,) + (expert,) * 3,
        check_vma=False,
    )
```

```python
import functools

import jax
import jax.numpy as jnp
from jax import lax
from jax.experimental import pallas as pl
from jax.experimental.pallas import tpu as pltpu
from jax.sharding import PartitionSpec as P

HEADS = 16
HEAD_DIM = 128

epsilon = 1e-05
rope_base = 10000.0
masked_score = -1e30
bf16 = jnp.bfloat16
f32 = jnp.float32


def normalize(values):
    scale = lax.rsqrt(jnp.mean(values * values, axis=-1, keepdims=True) + epsilon)
    return (values * scale, scale)


def norm_back(grad_normed, normed, scale):
    return scale * (grad_normed - normed * jnp.mean(grad_normed * normed, axis=-1, keepdims=True))


def rotate_half(values):
    middle = values.shape[-1] // 2
    return jnp.concatenate([-values[..., middle:], values[..., :middle]], axis=-1)


def rotate_back(values):
    middle = values.shape[-1] // 2
    return jnp.concatenate([values[..., middle:], -values[..., :middle]], axis=-1)


def rope_tables(position):
    steps = jnp.arange(HEAD_DIM // 2, dtype=f32) * (2.0 / HEAD_DIM)
    inverse = rope_base ** (-steps)
    angle = position.astype(f32)[:, None] * inverse[None, :]
    cosine = jnp.concatenate([jnp.cos(angle), jnp.cos(angle)], axis=-1)[:, None, :]
    sine = jnp.concatenate([jnp.sin(angle), jnp.sin(angle)], axis=-1)[:, None, :]
    return (cosine, sine)


def segment_tables(lengths, row_count):
    count = lengths.shape[0]
    numbers = jnp.arange(count, dtype=jnp.int32)
    before = (numbers[None, :] < numbers[:, None]).astype(jnp.int32)
    starts = jnp.sum(before * lengths[None, :], axis=1)
    ends = starts + lengths
    row_index = jnp.arange(row_count, dtype=jnp.int32)
    segment = jnp.sum((row_index[:, None] >= ends[None, :]).astype(jnp.int32), axis=1)
    begin = jnp.sum(jnp.where(segment[:, None] == numbers[None, :], starts[None, :], 0), axis=1)
    return (segment, row_index - begin, segment < count - 1)


def slot_tables(routes, filling, live_rows, experts, capacity):
    row_count, top_count = routes.shape
    order = jnp.arange(row_count * top_count, dtype=jnp.int32)
    rows = jnp.arange(row_count, dtype=jnp.int32)
    hot_row = (filling[None, :] // top_count == rows[:, None]).astype(bf16)
    hot_choice = (filling % top_count)[:, None] == jnp.arange(top_count, dtype=jnp.int32)[None, :]
    high = jnp.where(hot_choice, (order // 64)[:, None], 0).astype(bf16)
    lower = jnp.where(hot_choice, (order % 64)[:, None], 0).astype(bf16)
    ranks = jnp.dot(
        hot_row, jnp.concatenate([high, lower], axis=1), preferred_element_type=f32
    ).astype(jnp.int32)
    rank = ranks[:, :top_count] * 64 + ranks[:, top_count:]
    chosen = routes[:, :, None] == jnp.arange(experts, dtype=jnp.int32)[None, None, :]
    rank_table = jnp.sum(jnp.where(chosen, rank[:, :, None], 0), axis=1)
    counted = jnp.any(chosen, axis=1) & live_rows[:, None]
    earlier = counted[:, None, :] & (rank_table[:, None, :] < rank_table[None, :, :])
    slot = jnp.sum(earlier.astype(jnp.int32), axis=0)
    kept = counted & (slot < capacity)
    return (jnp.where(kept, slot, -1), kept)


def attention_scores(query_low, key_low, visible):
    scores = jnp.einsum(
        "qhd,khd->hqk", query_low, key_low, preferred_element_type=f32
    ) * HEAD_DIM ** (-0.5)
    return jnp.where(visible[None], scores, masked_score)


MESH = pl.DeviceIdType.MESH


class Place:
    def __init__(self):
        self.rep, self.ex = lax.axis_index("rep"), lax.axis_index("ex")
        self.x, self.y, self.z = self.ex % 2, self.ex // 2 % 2, self.ex // 4
        self.other_x = (self.rep, self.ex + 1 - 2 * self.x)
        self.other_y = (self.rep, self.ex + 2 - 4 * self.y)
        self.other_core = (1 - self.rep, self.ex)
        self.other_z = [(self.rep, (self.ex + 4 * k) % 16) for k in range(1, 4)]
        self.peers = [(self.rep, (self.ex + k) % 16) for k in range(1, 16)]


def enter(devices):
    barrier = pltpu.get_barrier_semaphore()
    for device in devices:
        pl.semaphore_signal(barrier, inc=1, device_id=device, device_id_type=MESH)
    pl.semaphore_wait(barrier, len(devices))


class Copies:
    def __init__(self, send_sems, recv_sems):
        self.send_sems, self.recv_sems, self.made = send_sems, recv_sems, []

    def start(self, source, target, device):
        at = len(self.made)
        copy = pltpu.make_async_remote_copy(
            src_ref=source,
            dst_ref=target,
            send_sem=self.send_sems.at[at],
            recv_sem=self.recv_sems.at[at],
            device_id=device,
            device_id_type=MESH,
        )
        copy.start()
        self.made.append(copy)
        return copy

    def finish(self):
        for copy in self.made:
            copy.wait_send()


def gather_kernel(pieces, with_core, shards, spread_in, *refs):
    count, moved = len(shards), len(spread_in)
    ins, refs = refs[:count], refs[count:]
    from_all, refs = refs[:moved], refs[moved:]
    outs, refs = refs[:count], refs[count:]
    to_all, refs = refs[:moved], refs[moved:]
    send_sems, recv_sems, local_sems = refs
    here = Place()
    rep, x, y, z = here.rep, here.x, here.y, here.z
    enter(here.peers + ([here.other_core] if with_core else []))
    copies = Copies(send_sems, recv_sems)
    local, exchanged = [], []

    def keep(source, target):
        copy = pltpu.make_async_copy(source, target, local_sems.at[len(local)])
        copy.start()
        local.append(copy)
        return copy

    for source, target in zip(from_all, to_all):
        keep(source.at[here.ex], target.at[here.ex])
        for peer in here.peers:
            exchanged.append(copies.start(source.at[peer[1]], target.at[here.ex], peer))

    parts = []
    for i in range(count):
        rows = shards[i][0] // pieces[i]
        parts += [(i, k * rows, rows) for k in range(pieces[i])]

    def stage_z(part):
        i, first, rows = part
        source, full = ins[i].at[pl.ds(first, rows)], outs[i].at[rep]
        target = full.at[z, y, x, pl.ds(first, rows)]
        waits = [copies.start(source, target, device) for device in here.other_z]
        return waits, keep(source, target)

    def stage_one(part, waits, kept):
        i, first, rows = part
        full, half = outs[i].at[rep], rows // 2
        kept.wait()
        for copy in waits:
            copy.wait_recv()
        upper, lower = pl.ds(first, half), pl.ds(first + half, half)
        a = full.at[:, y, x, upper]
        b = full.at[:, y, x, lower]
        one = copies.start(a, a, here.other_x), copies.start(b, b, here.other_y)
        own = full.at[:, y, x, pl.ds(first, rows)]
        cores = [copies.start(own, own, here.other_core)] if with_core else []
        return one, cores

    def stage_two(part, one, cores):
        i, first, rows = part
        full, half = outs[i].at[rep], rows // 2
        upper, lower = pl.ds(first, half), pl.ds(first + half, half)
        one[0].wait_recv()
        a = full.at[:, y, :, upper]
        two_a = copies.start(a, a, here.other_y)
        one[1].wait_recv()
        b = full.at[:, :, x, lower]
        two_b = copies.start(b, b, here.other_x)
        if with_core:
            a, b = full.at[:, y, 1 - x, upper], full.at[:, 1 - y, x, lower]
            cores += [copies.start(a, a, here.other_core), copies.start(b, b, here.other_core)]
        return (two_a, two_b), cores

    def stage_three(part, two, cores):
        i, first, rows = part
        full, half = outs[i].at[rep], rows // 2
        upper, lower = pl.ds(first, half), pl.ds(first + half, half)
        two[0].wait_recv()
        a = full.at[:, 1 - y, :, upper]
        if with_core:
            cores += [copies.start(a, a, here.other_core)]
        two[1].wait_recv()
        b = full.at[:, :, 1 - x, lower]
        if with_core:
            cores += [copies.start(b, b, here.other_core)]
        return cores

    held, arrivals, count = {}, [], len(parts)
    for step in range(count + 3):
        if step < count:
            held[step] = stage_z(parts[step])
        if 0 <= step - 1 < count:
            held[step - 1] = stage_one(parts[step - 1], *held[step - 1])
        if 0 <= step - 2 < count:
            held[step - 2] = stage_two(parts[step - 2], *held[step - 2])
        if 0 <= step - 3 < count:
            arrivals += stage_three(parts[step - 3], *held[step - 3])
    for copy in arrivals + exchanged:
        copy.wait_recv()
    copies.finish()
    for copy in local[:len(from_all)]:
        copy.wait()


def gather(shards, spread_in, with_core, pieces, collective_id):
    copies = sum(pieces) * (12 if with_core else 7) + 15 * len(spread_in)
    local = sum(pieces) + len(spread_in)
    out_shape = [jax.ShapeDtypeStruct((2, 4, 2, 2) + a.shape, a.dtype) for a in shards]
    out_shape += [jax.ShapeDtypeStruct(a.shape, a.dtype) for a in spread_in]
    anywhere = pl.BlockSpec(memory_space=pl.ANY)
    shapes = [a.shape for a in shards]
    return pl.pallas_call(
        functools.partial(gather_kernel, pieces, with_core, shapes, [a.shape for a in spread_in]),
        out_shape=out_shape,
        in_specs=[anywhere] * (len(shards) + len(spread_in)),
        out_specs=[anywhere] * len(out_shape),
        scratch_shapes=[
            pltpu.SemaphoreType.DMA((copies,)),
            pltpu.SemaphoreType.DMA((copies,)),
            pltpu.SemaphoreType.DMA((local,)),
        ],
        compiler_params=pltpu.CompilerParams(collective_id=collective_id, has_side_effects=True),
    )(*shards, *spread_in)


def accumulate(target, blocks, arrived):
    def add(z, carry):
        for into, source in blocks:
            value = target[(z,) + into].astype(f32) + arrived[(z,) + source].astype(f32)
            target[(z,) + into] = value.astype(target.dtype)
        return carry
    lax.fori_loop(0, 4, add, 0)


def reduce_kernel(plan, with_core, moved, n_in, *refs):
    parts = len(plan)
    ins, refs = refs[:n_in], refs[n_in:]
    from_all, refs = refs[:moved], refs[moved:]
    n_out = len({p["out"] for p in plan})
    outs, refs = refs[:n_out], refs[n_out:]
    to_all, refs = refs[:moved], refs[moved:]
    slots = max(p["slot"] for p in plan) + 1
    owns, refs = refs[:slots], refs[slots:]
    if with_core:
        away_slots = max(p["away"] for p in plan) + 1
        aways, refs = refs[:away_slots], refs[away_slots:]
    per = 6 if with_core else 5
    landing, refs = refs[:per * parts], refs[per * parts:]
    send_sems, recv_sems, local_sems = refs
    here = Place()
    rep, x, y, z = here.rep, here.x, here.y, here.z
    enter(here.peers + ([here.other_core] if with_core else []))
    copies = Copies(send_sems, recv_sems)
    local, exchanged = [], []
    for source, target in zip(from_all, to_all):
        copy = pltpu.make_async_copy(
            source.at[here.ex], target.at[here.ex], local_sems.at[len(local)]
        )
        copy.start()
        local.append(copy)
        for peer in here.peers:
            exchanged.append(copies.start(source.at[peer[1]], target.at[here.ex], peer))

    def halves(j):
        half = plan[j]["rows"] // 2
        return pl.ds(0, half), pl.ds(half, half)

    core_copies, one, two, last = {}, {}, {}, {}
    sent = set()

    def done_sending(copy):
        if id(copy) not in sent:
            sent.add(id(copy))
            copy.wait_send()

    def stage_fill(j):
        p = plan[j]
        if not with_core:
            p["fill"](ins, owns[p["slot"]], rep, None)
            return
        away = aways[p["away"]]
        for k in range(j):
            if plan[k]["away"] == p["away"]:
                done_sending(core_copies[k])
        p["fill"](ins, away, 1 - rep, None)
        core_copies[j] = copies.start(away, landing[per * j + 5], here.other_core)

    def stage_one(j):
        p = plan[j]
        own, (upper, lower) = owns[p["slot"]], halves(j)
        if with_core:
            core_copies[j].wait_recv()
            p["fill"](ins, own, rep, landing[per * j + 5])
        one[j] = (
            copies.start(own.at[:, 1 - y, :, upper], landing[per * j], here.other_y),
            copies.start(own.at[:, :, 1 - x, lower], landing[per * j + 1], here.other_x),
        )

    def stage_two(j):
        own, (upper, lower) = owns[plan[j]["slot"]], halves(j)
        from_y, from_x = landing[per * j], landing[per * j + 1]
        one[j][0].wait_recv()
        accumulate(own, [((y, 1 - x, upper), (1 - x,))], from_y)
        a = copies.start(own.at[:, y, 1 - x, upper], landing[per * j + 2], here.other_x)
        one[j][1].wait_recv()
        accumulate(own, [((1 - y, x, lower), (1 - y,))], from_x)
        b = copies.start(own.at[:, 1 - y, x, lower], landing[per * j + 3], here.other_y)
        accumulate(own, [((y, x, upper), (x,))], from_y)
        accumulate(own, [((y, x, lower), (y,))], from_x)
        two[j] = a, b

    def stage_three(j):
        own, (upper, lower) = owns[plan[j]["slot"]], halves(j)
        two[j][0].wait_recv()
        accumulate(own, [((y, x, upper), ())], landing[per * j + 2])
        two[j][1].wait_recv()
        accumulate(own, [((y, x, lower), ())], landing[per * j + 3])
        last[j] = [
            copies.start(own.at[(z + k) % 4, y, x], landing[per * j + 4].at[k - 1], here.other_z[k - 1])
            for k in range(1, 4)
        ]

    def stage_four(j):
        own, arrived = owns[plan[j]["slot"]], landing[per * j + 4]
        for copy in last[j]:
            copy.wait_recv()
        total = own[z, y, x].astype(f32) + arrived[0].astype(f32)
        total = total + arrived[1].astype(f32) + arrived[2].astype(f32)
        plan[j]["finish"](outs[plan[j]["out"]], total)
        for copy in (*one[j], *two[j], *last[j]):
            done_sending(copy)

    for step in range(parts + 4):
        for behind, stage in enumerate((stage_fill, stage_one, stage_two, stage_three, stage_four)):
            if 0 <= step - behind < parts:
                stage(step - behind)
    for copy in core_copies.values():
        done_sending(copy)
    for copy in exchanged:
        copy.wait_recv()
        done_sending(copy)
    for copy in local:
        copy.wait()


def reduce(plan, ins, spread_in, out_shapes, with_core, collective_id):
    parts = len(plan)
    scratch, slot_shape, away_shape = [], {}, {}
    for p in plan:
        shape = (4, 2, 2, p["rows"], p["columns"])
        slot_shape[p["slot"]] = pltpu.VMEM(shape, p["dtype"])
        if with_core:
            away_shape[p["away"]] = pltpu.VMEM(shape, p["dtype"])
    scratch += [slot_shape[i] for i in range(len(slot_shape))]
    scratch += [away_shape[i] for i in range(len(away_shape))]
    for p in plan:
        rows, columns, dtype = p["rows"], p["columns"], p["dtype"]
        shapes = [
            (4, 2, rows // 2, columns),
            (4, 2, rows // 2, columns),
            (4, rows // 2, columns),
            (4, rows // 2, columns),
            (3, rows, columns),
        ] + ([(4, 2, 2, rows, columns)] if with_core else [])
        scratch += [pltpu.VMEM(shape, dtype) for shape in shapes]
    copies = (8 if with_core else 7) * parts + 15 * len(spread_in)
    vmem, anywhere = pl.BlockSpec(memory_space=pltpu.VMEM), pl.BlockSpec(memory_space=pl.ANY)
    return pl.pallas_call(
        functools.partial(reduce_kernel, plan, with_core, len(spread_in), len(ins)),
        out_shape=out_shapes + [jax.ShapeDtypeStruct(a.shape, a.dtype) for a in spread_in],
        in_specs=[vmem] * len(ins) + [anywhere] * len(spread_in),
        out_specs=[vmem] * len(out_shapes) + [anywhere] * len(spread_in),
        scratch_shapes=scratch + [
            pltpu.SemaphoreType.DMA((copies,)),
            pltpu.SemaphoreType.DMA((copies,)),
            pltpu.SemaphoreType.DMA((max(len(spread_in), 1),)),
        ],
        compiler_params=pltpu.CompilerParams(
            collective_id=collective_id, has_side_effects=True, vmem_limit_bytes=62 * 2**20
        ),
    )(*ins, *spread_in)


def put(first, columns):
    def finish(out, total):
        out[:, pl.ds(first, columns)] = total
    return finish


def reduce_weights(pairs, small, outbound, pieces=2, collective_id=2):
    lefts = {}
    for left, _ in pairs:
        lefts.setdefault(id(left), (len(lefts), left))
    ins = [v[1].T.reshape(2, 8, 128, left_rows(v[1])) for v in lefts.values()]
    ins += [right for _, right in pairs] + [small]
    plan, columns = [], pairs[0][1].shape[1] // pieces
    for i, (left, _) in enumerate(pairs):
        for k in range(pieces):
            def fill(ins, own, rep, arrived, at=lefts[id(left)][0], right=len(lefts) + i, first=k * columns):
                def block(n, carry):
                    value = jnp.dot(
                        ins[at][rep, n], ins[right][:, pl.ds(first, columns)], preferred_element_type=f32
                    ).reshape(2, 64, columns)
                    if arrived is not None:
                        value = value + arrived[n // 2, n % 2].astype(f32)
                    own[n // 2, n % 2] = value.astype(own.dtype)
                    return carry
                lax.fori_loop(0, 8, block, 0)
            at = len(plan)
            plan.append(dict(rows=64, columns=columns, dtype=bf16, fill=fill, finish=put(k * columns, columns), out=i, slot=at % 5, away=at % 2))
    def fill_small(ins, own, rep, arrived):
        def block(n, carry):
            value = ins[-1][rep, n]
            if arrived is not None:
                value = value + arrived[n]
            own[n] = value
            return carry
        lax.fori_loop(0, 4, block, 0)
    plan.append(dict(rows=64, columns=small.shape[-1], dtype=f32, fill=fill_small, finish=put(0, small.shape[-1]), out=len(pairs), slot=min(5, len(plan)), away=2))
    out_shapes = [jax.ShapeDtypeStruct((64, b.shape[1]), f32) for _, b in pairs] + [jax.ShapeDtypeStruct((64, small.shape[-1]), f32)]
    return reduce(plan, ins, outbound, out_shapes, True, collective_id)


def left_rows(a):
    return a.shape[0]


def reduce_tokens(picked_low, arrays, back, pieces=2, collective_id=4):
    group, capacity, rows = picked_low.shape
    ins = [picked_low.transpose(0, 2, 1)] + [a.reshape(group, capacity, -1) for a in arrays]
    plan, columns = [], ins[1].shape[-1] // pieces
    for i in range(len(arrays)):
        for k in range(pieces):
            def fill(ins, own, rep, arrived, at=1 + i, first=k * columns):
                def block(n, carry):
                    value = jnp.dot(ins[0][n], ins[at][n, :, pl.ds(first, columns)], preferred_element_type=f32)
                    own[n // 4, n // 2 % 2, n % 2] = value.astype(own.dtype)
                    return carry
                lax.fori_loop(0, group, block, 0)
            plan.append(dict(rows=rows, columns=columns, dtype=bf16, fill=fill, finish=put(k * columns, columns), out=i, slot=len(plan) % 4))
    out_shapes = [jax.ShapeDtypeStruct((rows, ins[1].shape[-1]), f32)] * len(arrays)
    return reduce(plan, ins, back, out_shapes, False, collective_id)

def has_kernels():
    return (lax.axis_size("rep"), lax.axis_size("ex")) == (2, 16)


def exchange(array):
    return lax.all_to_all(array, "ex", split_axis=0, concat_axis=0, tiled=True)


def gather_weights(shards, outbound):
    if has_kernels():
        *full, inbound = gather(shards, [outbound], True, [2] * (len(shards) - 1) + [1], 1)
        return [a.reshape(-1, a.shape[-1]) for a in full], inbound
    full = [lax.all_gather(a, ("rep", "ex"), axis=0, tiled=True) for a in shards]
    return full, exchange(outbound)


def gather_tokens(arrays, table):
    if has_kernels():
        wide = jnp.pad(table, ((0, 0), (0, 8 - table.shape[1]), (0, 0)))
        *full, given = gather(arrays, [wide], False, [2] * len(arrays), 2)
        full = [a[lax.axis_index("rep")].reshape(16, *a.shape[-2:]) for a in full]
        return full, given[:, : table.shape[1]]
    return [lax.all_gather(a, "ex", axis=0) for a in arrays], exchange(table)


def sum_tokens(picked_low, arrays, back):
    if has_kernels():
        wide = jnp.broadcast_to(back[:, None, :], (back.shape[0], 8, back.shape[1]))
        *sums, given = reduce_tokens(picked_low, arrays, [wide], 2, 3)
        return sums, given[:, 0]
    group, capacity, _ = picked_low.shape
    sums = []
    for rows in arrays:
        rows = rows.reshape(group, capacity, -1)
        spread = jnp.einsum("sct,scd->std", picked_low, rows, preferred_element_type=f32)
        spread = spread.astype(bf16)
        sums.append(lax.psum_scatter(spread, "ex", scatter_dimension=0).astype(f32))
    return sums, exchange(back)


def sum_weights(pairs, small, outbound):
    if has_kernels():
        width = small.shape[1]
        wide = jnp.pad(small, ((0, 0), (0, 128 - width))).reshape(2, 4, 2, 2, 64, 128)
        *sums, summed, given = reduce_weights(pairs, wide, [outbound], 2, 4)
        return sums, summed[:, :width], given
    both = ("rep", "ex")
    sums = []
    for left, right in pairs:
        grad = jnp.dot(left.T, right, preferred_element_type=f32).astype(bf16)
        sums.append(lax.psum_scatter(grad, both, scatter_dimension=0, tiled=True).astype(f32))
    summed = lax.psum_scatter(small, both, scatter_dimension=0, tiled=True)
    return sums, summed, exchange(outbound)


def body(
    tokens,
    out_cot,
    destination,
    doc_lengths,
    routes,
    fill_order,
    query_weight,
    key_weight,
    value_weight,
    output_weight,
    query_gain,
    key_gain,
    attn_gain,
    moe_gain,
    router_weight,
    expert_gate,
    expert_up,
    expert_down,
):
    group_size = lax.axis_size("ex")
    row_count, model_width = tokens.shape
    block_rows = row_count // group_size
    row_index = jnp.arange(row_count, dtype=jnp.int32)
    placed = destination // row_count % group_size * block_rows + destination % block_rows
    to_send = (placed[None, :] == row_index[:, None]).astype(bf16)
    inbound = jnp.dot(
        to_send, jnp.concatenate([tokens, out_cot], axis=1), preferred_element_type=f32
    ).astype(bf16)
    gains = jnp.concatenate(
        [jnp.stack([query_gain, key_gain, attn_gain, moe_gain], axis=1), router_weight], axis=1
    )
    extra = gains.shape[1]
    gains = jnp.pad(gains, ((0, 0), (0, -extra % 128)))
    full, packed = gather_weights(
        [query_weight, key_weight, value_weight, output_weight, gains],
        inbound.reshape(group_size, block_rows, 2 * model_width),
    )
    query_full, key_full, value_full, output_full, gains = full
    packed = packed.reshape(row_count, 2 * model_width)
    hidden_in, cot_in = packed[:, :model_width], packed[:, model_width:]
    query_scale, key_scale, attn_scale, moe_scale = (gains[:, i].astype(f32) for i in range(4))
    router_full = gains[:, 4:extra]
    gate_full = lax.all_gather(expert_gate[0], "rep", axis=0, tiled=True)
    up_full = lax.all_gather(expert_up[0], "rep", axis=0, tiled=True)
    down_full = lax.all_gather(expert_down[0], "rep", axis=0, tiled=True)

    segment, position, live_rows = segment_tables(doc_lengths[0], row_count)
    live_column = live_rows.astype(f32)[:, None]
    hidden = hidden_in.astype(f32)
    normed_attn, scale_attn = normalize(hidden)
    attn_in = (normed_attn * attn_scale).astype(bf16)
    query_pre = jnp.dot(attn_in, query_full, preferred_element_type=f32)
    key_pre = jnp.dot(attn_in, key_full, preferred_element_type=f32)
    value_pre = jnp.dot(attn_in, value_full, preferred_element_type=f32)
    normed_query, scale_query = normalize(query_pre)
    normed_key, scale_key = normalize(key_pre)
    cosine, sine = rope_tables(position)
    query_norm = (normed_query * query_scale).reshape(row_count, HEADS, HEAD_DIM)
    key_norm = (normed_key * key_scale).reshape(row_count, HEADS, HEAD_DIM)
    query_low = (query_norm * cosine + rotate_half(query_norm) * sine).astype(bf16)
    key_low = (key_norm * cosine + rotate_half(key_norm) * sine).astype(bf16)
    value_low = value_pre.astype(bf16).reshape(row_count, HEADS, HEAD_DIM)
    visible = (segment[:, None] == segment[None, :]) & (row_index[None, :] <= row_index[:, None])
    scores = attention_scores(query_low, key_low, visible)
    peak = jnp.max(scores, axis=-1, keepdims=True)
    weights_exp = jnp.exp(scores - peak)
    probs = weights_exp / jnp.sum(weights_exp, axis=-1, keepdims=True)
    probs_low = probs.astype(bf16)
    mixed = jnp.einsum("hqk,khd->qhd", probs_low, value_low, preferred_element_type=f32)
    mixed = mixed.reshape(row_count, model_width).astype(bf16)
    branch = jnp.dot(mixed, output_full, preferred_element_type=f32)
    after_attn = hidden + live_column * branch
    normed_moe, scale_moe = normalize(after_attn)
    moe_in = (normed_moe * moe_scale).astype(bf16)
    logits = jnp.dot(moe_in, router_full, preferred_element_type=f32)
    router_probs = jax.nn.softmax(logits, axis=-1)
    experts = router_full.shape[1]
    capacity = row_count * routes.shape[1] // experts
    slot_table, kept = slot_tables(routes, fill_order[0], live_rows, experts, capacity)
    gates = jnp.where(kept, router_probs, 0.0)

    sent = jnp.stack([gates, slot_table.astype(f32)], axis=0).transpose(2, 0, 1)
    (moe_all, cot_all), given = gather_tokens([moe_in, cot_in], sent)
    gate_rows, slot_rows = given[:, 0], given[:, 1]
    slots = jnp.arange(capacity, dtype=jnp.int32).astype(f32)
    picked = slot_rows[:, None, :] == slots[None, :, None]
    picked_low = picked.astype(bf16)
    slot_gate = jnp.sum(jnp.where(picked, gate_rows[:, None, :], 0.0), axis=2).reshape(-1, 1)

    def pick(rows):
        chosen = jnp.einsum("sct,std->scd", picked_low, rows, preferred_element_type=f32)
        return chosen.astype(bf16).reshape(-1, model_width)

    rows_in, rows_cot = pick(moe_all), pick(cot_all)
    gate_pre = jnp.dot(rows_in, gate_full, preferred_element_type=f32)
    up_pre = jnp.dot(rows_in, up_full, preferred_element_type=f32)
    sigma = jax.nn.sigmoid(gate_pre)
    silu = gate_pre * sigma
    middle = (silu * up_pre).astype(bf16)
    expert_out = jnp.dot(middle, down_full, preferred_element_type=f32).astype(bf16)
    slot_grad = jnp.sum(rows_cot.astype(f32) * expert_out.astype(f32), axis=1)
    weighted = (slot_gate * expert_out.astype(f32)).astype(bf16)
    grad_expert_out = (slot_gate * rows_cot.astype(f32)).astype(bf16)
    grad_middle = jnp.dot(grad_expert_out, down_full.T, preferred_element_type=f32)
    grad_down_full = jnp.dot(middle.T, grad_expert_out, preferred_element_type=f32)
    grad_gate_low = (grad_middle * up_pre * sigma * (1.0 + gate_pre * (1.0 - sigma))).astype(bf16)
    grad_up_low = (grad_middle * silu).astype(bf16)
    grad_gate_full = jnp.dot(rows_in.T, grad_gate_low, preferred_element_type=f32)
    grad_up_full = jnp.dot(rows_in.T, grad_up_low, preferred_element_type=f32)
    grad_rows = jnp.dot(grad_gate_low, gate_full.T, preferred_element_type=f32)
    grad_rows = (
        grad_rows + jnp.dot(grad_up_low, up_full.T, preferred_element_type=f32)
    ).astype(bf16)
    slot_grad = slot_grad.reshape(group_size, capacity, 1)
    grad_back = jnp.sum(jnp.where(picked, slot_grad, 0.0), axis=1)
    (grad_moe_in, mixture), grad_rprobs = sum_tokens(picked_low, [grad_rows, weighted], grad_back)
    grad_rprobs = grad_rprobs.T
    output = (after_attn + mixture).astype(bf16)
    owned_gate, owned_up, owned_down = (
        lax.psum_scatter(g.astype(bf16), "rep", scatter_dimension=0, tiled=True).astype(f32)[None]
        for g in (grad_gate_full, grad_up_full, grad_down_full)
    )

    grad_out = cot_in.astype(f32)
    grad_logits = router_probs * (
        grad_rprobs - jnp.sum(router_probs * grad_rprobs, axis=-1, keepdims=True)
    )
    grad_moe_in = grad_moe_in + jnp.dot(
        grad_logits, router_full.T, precision=lax.Precision.HIGHEST, preferred_element_type=f32
    )
    grad_router = jnp.dot(
        moe_in.T, grad_logits, precision=lax.Precision.HIGHEST, preferred_element_type=f32
    )
    grad_moe_scale = jnp.sum(grad_moe_in * normed_moe, axis=0)
    grad_after = grad_out + norm_back(grad_moe_in * moe_scale, normed_moe, scale_moe)
    grad_branch = (live_column * grad_after).astype(bf16)
    grad_mixed = (
        jnp.dot(grad_branch, output_full.T, preferred_element_type=f32)
        .astype(bf16)
        .reshape(row_count, HEADS, HEAD_DIM)
    )
    grad_value = jnp.einsum("hqk,qhd->khd", probs_low, grad_mixed, preferred_element_type=f32)
    grad_att = jnp.einsum("qhd,khd->hqk", grad_mixed, value_low, preferred_element_type=f32)
    grad_scores = (probs * (grad_att - jnp.sum(probs * grad_att, axis=-1, keepdims=True))).astype(
        bf16
    )
    grad_query_rot = jnp.einsum(
        "hqk,khd->qhd", grad_scores, key_low, preferred_element_type=f32
    ) * HEAD_DIM ** (-0.5)
    grad_key_rot = jnp.einsum(
        "hqk,qhd->khd", grad_scores, query_low, preferred_element_type=f32
    ) * HEAD_DIM ** (-0.5)
    grad_query_normed = (grad_query_rot * cosine + rotate_back(grad_query_rot * sine)).reshape(
        row_count, model_width
    )
    grad_key_normed = (grad_key_rot * cosine + rotate_back(grad_key_rot * sine)).reshape(
        row_count, model_width
    )
    grad_query_scale = jnp.sum(grad_query_normed * normed_query, axis=0)
    grad_key_scale = jnp.sum(grad_key_normed * normed_key, axis=0)
    grad_query_pre = norm_back(grad_query_normed * query_scale, normed_query, scale_query)
    grad_key_pre = norm_back(grad_key_normed * key_scale, normed_key, scale_key)
    grad_query_pre = grad_query_pre.astype(bf16)
    grad_key_pre = grad_key_pre.astype(bf16)
    grad_value_pre = grad_value.reshape(row_count, model_width).astype(bf16)
    grad_attn_in = jnp.dot(grad_query_pre, query_full.T, preferred_element_type=f32)
    grad_attn_in = grad_attn_in + jnp.dot(grad_key_pre, key_full.T, preferred_element_type=f32)
    grad_attn_in = grad_attn_in + jnp.dot(grad_value_pre, value_full.T, preferred_element_type=f32)
    grad_attn_scale = jnp.sum(grad_attn_in * normed_attn, axis=0)
    grad_hidden = grad_after + norm_back(grad_attn_in * attn_scale, normed_attn, scale_attn)

    small = jnp.concatenate(
        [
            jnp.stack([grad_query_scale, grad_key_scale, grad_attn_scale, grad_moe_scale], axis=1),
            grad_router,
        ],
        axis=1,
    )
    outbound = jnp.concatenate([output, grad_hidden.astype(bf16)], axis=1)
    pairs = [
        (attn_in, grad_query_pre),
        (attn_in, grad_key_pre),
        (attn_in, grad_value_pre),
        (mixed, grad_branch),
    ]
    sums, small, outbound = sum_weights(
        pairs, small, outbound.reshape(group_size, block_rows, 2 * model_width)
    )
    owned_query, owned_key, owned_value, owned_output = sums
    outbound = outbound.reshape(row_count, 2 * model_width)
    outbound = jnp.dot(to_send.T, outbound, preferred_element_type=f32).astype(bf16)
    return (
        outbound[:, :model_width],
        outbound[:, model_width:],
        owned_query,
        owned_key,
        owned_value,
        owned_output,
        small[:, 0],
        small[:, 1],
        small[:, 2],
        small[:, 3],
        small[:, 4:],
        owned_gate,
        owned_up,
        owned_down,
    )


def solution(mesh):
    rows, row = P(("rep", "ex"), None), P(("rep", "ex"))
    expert = P("ex", "rep", None)
    return jax.shard_map(
        body,
        mesh=mesh,
        in_specs=(rows, rows, row) + (rows,) * 7 + (row,) * 4 + (rows,) + (expert,) * 3,
        out_specs=(rows,) * 6 + (row,) * 4 + (rows,) + (expert,) * 3,
        check_vma=False,
    )
```

```python
import functools

import jax
import jax.numpy as jnp
from jax import lax
from jax.experimental import pallas as pl
from jax.experimental.pallas import tpu as pltpu
from jax.sharding import PartitionSpec as P

HEADS = 16
HEAD_DIM = 128

epsilon = 1e-05
rope_base = 10000.0
masked_score = -1e30
bf16 = jnp.bfloat16
f32 = jnp.float32


def normalize(values):
    scale = lax.rsqrt(jnp.mean(values * values, axis=-1, keepdims=True) + epsilon)
    return (values * scale, scale)


def norm_back(grad_normed, normed, scale):
    return scale * (grad_normed - normed * jnp.mean(grad_normed * normed, axis=-1, keepdims=True))


def rotate_half(values):
    middle = values.shape[-1] // 2
    return jnp.concatenate([-values[..., middle:], values[..., :middle]], axis=-1)


def rotate_back(values):
    middle = values.shape[-1] // 2
    return jnp.concatenate([values[..., middle:], -values[..., :middle]], axis=-1)


def rope_tables(position):
    steps = jnp.arange(HEAD_DIM // 2, dtype=f32) * (2.0 / HEAD_DIM)
    inverse = rope_base ** (-steps)
    angle = position.astype(f32)[:, None] * inverse[None, :]
    cosine = jnp.concatenate([jnp.cos(angle), jnp.cos(angle)], axis=-1)[:, None, :]
    sine = jnp.concatenate([jnp.sin(angle), jnp.sin(angle)], axis=-1)[:, None, :]
    return (cosine, sine)


def segment_tables(lengths, row_count):
    count = lengths.shape[0]
    numbers = jnp.arange(count, dtype=jnp.int32)
    before = (numbers[None, :] < numbers[:, None]).astype(jnp.int32)
    starts = jnp.sum(before * lengths[None, :], axis=1)
    ends = starts + lengths
    row_index = jnp.arange(row_count, dtype=jnp.int32)
    segment = jnp.sum((row_index[:, None] >= ends[None, :]).astype(jnp.int32), axis=1)
    begin = jnp.sum(jnp.where(segment[:, None] == numbers[None, :], starts[None, :], 0), axis=1)
    return (segment, row_index - begin, segment < count - 1)


def slot_tables(routes, filling, live_rows, experts, capacity):
    row_count, top_count = routes.shape
    order = jnp.arange(row_count * top_count, dtype=jnp.int32)
    rows = jnp.arange(row_count, dtype=jnp.int32)
    hot_row = (filling[None, :] // top_count == rows[:, None]).astype(bf16)
    hot_choice = (filling % top_count)[:, None] == jnp.arange(top_count, dtype=jnp.int32)[None, :]
    high = jnp.where(hot_choice, (order // 64)[:, None], 0).astype(bf16)
    lower = jnp.where(hot_choice, (order % 64)[:, None], 0).astype(bf16)
    ranks = jnp.dot(
        hot_row, jnp.concatenate([high, lower], axis=1), preferred_element_type=f32
    ).astype(jnp.int32)
    rank = ranks[:, :top_count] * 64 + ranks[:, top_count:]
    chosen = routes[:, :, None] == jnp.arange(experts, dtype=jnp.int32)[None, None, :]
    rank_table = jnp.sum(jnp.where(chosen, rank[:, :, None], 0), axis=1)
    counted = jnp.any(chosen, axis=1) & live_rows[:, None]
    earlier = counted[:, None, :] & (rank_table[:, None, :] < rank_table[None, :, :])
    slot = jnp.sum(earlier.astype(jnp.int32), axis=0)
    kept = counted & (slot < capacity)
    return (jnp.where(kept, slot, -1), kept)


def attention_scores(query_low, key_low, visible):
    scores = jnp.einsum(
        "qhd,khd->hqk", query_low, key_low, preferred_element_type=f32
    ) * HEAD_DIM ** (-0.5)
    return jnp.where(visible[None], scores, masked_score)


MESH = pl.DeviceIdType.MESH


class Place:
    def __init__(self):
        self.rep, self.ex = lax.axis_index("rep"), lax.axis_index("ex")
        self.x, self.y, self.z = self.ex % 2, self.ex // 2 % 2, self.ex // 4
        self.other_x = (self.rep, self.ex + 1 - 2 * self.x)
        self.other_y = (self.rep, self.ex + 2 - 4 * self.y)
        self.other_core = (1 - self.rep, self.ex)
        self.other_z = [(self.rep, (self.ex + 4 * k) % 16) for k in range(1, 4)]
        self.peers = [(self.rep, (self.ex + k) % 16) for k in range(1, 16)]


def enter(devices):
    barrier = pltpu.get_barrier_semaphore()
    for device in devices:
        pl.semaphore_signal(barrier, inc=1, device_id=device, device_id_type=MESH)
    pl.semaphore_wait(barrier, len(devices))


class Copies:
    def __init__(self, send_sems, recv_sems):
        self.send_sems, self.recv_sems, self.made = send_sems, recv_sems, []

    def start(self, source, target, device):
        at = len(self.made)
        copy = pltpu.make_async_remote_copy(
            src_ref=source,
            dst_ref=target,
            send_sem=self.send_sems.at[at],
            recv_sem=self.recv_sems.at[at],
            device_id=device,
            device_id_type=MESH,
        )
        copy.start()
        self.made.append(copy)
        return copy

    def finish(self):
        for copy in self.made:
            copy.wait_send()


def gather_kernel(pieces, with_core, shards, spread_in, *refs):
    count, moved = len(shards), len(spread_in)
    ins, refs = refs[:count], refs[count:]
    from_all, refs = refs[:moved], refs[moved:]
    outs, refs = refs[:count], refs[count:]
    to_all, refs = refs[:moved], refs[moved:]
    send_sems, recv_sems, local_sems = refs
    here = Place()
    rep, x, y, z = here.rep, here.x, here.y, here.z
    enter(here.peers + ([here.other_core] if with_core else []))
    copies = Copies(send_sems, recv_sems)
    local, exchanged = [], []

    def keep(source, target):
        copy = pltpu.make_async_copy(source, target, local_sems.at[len(local)])
        copy.start()
        local.append(copy)
        return copy

    for source, target in zip(from_all, to_all):
        keep(source.at[here.ex], target.at[here.ex])
        for peer in here.peers:
            exchanged.append(copies.start(source.at[peer[1]], target.at[here.ex], peer))

    parts = []
    for i in range(count):
        rows = shards[i][0] // pieces[i]
        parts += [(i, k * rows, rows) for k in range(pieces[i])]

    def stage_z(part):
        i, first, rows = part
        source, full = ins[i].at[pl.ds(first, rows)], outs[i].at[rep]
        target = full.at[z, y, x, pl.ds(first, rows)]
        waits = [copies.start(source, target, device) for device in here.other_z]
        return waits, keep(source, target)

    def stage_one(part, waits, kept):
        i, first, rows = part
        full, half = outs[i].at[rep], rows // 2
        kept.wait()
        for copy in waits:
            copy.wait_recv()
        upper, lower = pl.ds(first, half), pl.ds(first + half, half)
        a = full.at[:, y, x, upper]
        b = full.at[:, y, x, lower]
        one = copies.start(a, a, here.other_x), copies.start(b, b, here.other_y)
        own = full.at[:, y, x, pl.ds(first, rows)]
        cores = [copies.start(own, own, here.other_core)] if with_core else []
        return one, cores

    def stage_two(part, one, cores):
        i, first, rows = part
        full, half = outs[i].at[rep], rows // 2
        upper, lower = pl.ds(first, half), pl.ds(first + half, half)
        one[0].wait_recv()
        a = full.at[:, y, :, upper]
        two_a = copies.start(a, a, here.other_y)
        one[1].wait_recv()
        b = full.at[:, :, x, lower]
        two_b = copies.start(b, b, here.other_x)
        if with_core:
            a, b = full.at[:, y, 1 - x, upper], full.at[:, 1 - y, x, lower]
            cores += [copies.start(a, a, here.other_core), copies.start(b, b, here.other_core)]
        return (two_a, two_b), cores

    def stage_three(part, two, cores):
        i, first, rows = part
        full, half = outs[i].at[rep], rows // 2
        upper, lower = pl.ds(first, half), pl.ds(first + half, half)
        two[0].wait_recv()
        a = full.at[:, 1 - y, :, upper]
        if with_core:
            cores += [copies.start(a, a, here.other_core)]
        two[1].wait_recv()
        b = full.at[:, :, 1 - x, lower]
        if with_core:
            cores += [copies.start(b, b, here.other_core)]
        return cores

    held, arrivals, count = {}, [], len(parts)
    for step in range(count + 3):
        if step < count:
            held[step] = stage_z(parts[step])
        if 0 <= step - 1 < count:
            held[step - 1] = stage_one(parts[step - 1], *held[step - 1])
        if 0 <= step - 2 < count:
            held[step - 2] = stage_two(parts[step - 2], *held[step - 2])
        if 0 <= step - 3 < count:
            arrivals += stage_three(parts[step - 3], *held[step - 3])
    for copy in arrivals + exchanged:
        copy.wait_recv()
    copies.finish()
    for copy in local[:len(from_all)]:
        copy.wait()


def gather(shards, spread_in, with_core, pieces, collective_id):
    copies = sum(pieces) * (12 if with_core else 7) + 15 * len(spread_in)
    local = sum(pieces) + len(spread_in)
    out_shape = [jax.ShapeDtypeStruct((2, 4, 2, 2) + a.shape, a.dtype) for a in shards]
    out_shape += [jax.ShapeDtypeStruct(a.shape, a.dtype) for a in spread_in]
    anywhere = pl.BlockSpec(memory_space=pl.ANY)
    shapes = [a.shape for a in shards]
    return pl.pallas_call(
        functools.partial(gather_kernel, pieces, with_core, shapes, [a.shape for a in spread_in]),
        out_shape=out_shape,
        in_specs=[anywhere] * (len(shards) + len(spread_in)),
        out_specs=[anywhere] * len(out_shape),
        scratch_shapes=[
            pltpu.SemaphoreType.DMA((copies,)),
            pltpu.SemaphoreType.DMA((copies,)),
            pltpu.SemaphoreType.DMA((local,)),
        ],
        compiler_params=pltpu.CompilerParams(collective_id=collective_id, has_side_effects=True),
    )(*shards, *spread_in)


def accumulate(target, blocks, arrived):
    def add(z, carry):
        for into, source in blocks:
            value = target[(z,) + into].astype(f32) + arrived[(z,) + source].astype(f32)
            target[(z,) + into] = value.astype(target.dtype)
        return carry
    lax.fori_loop(0, 4, add, 0)


def reduce_kernel(plan, with_core, moved, n_in, *refs):
    parts = len(plan)
    ins, refs = refs[:n_in], refs[n_in:]
    from_all, refs = refs[:moved], refs[moved:]
    n_out = len({p["out"] for p in plan})
    outs, refs = refs[:n_out], refs[n_out:]
    to_all, refs = refs[:moved], refs[moved:]
    slots = max(p["slot"] for p in plan) + 1
    owns, refs = refs[:slots], refs[slots:]
    if with_core:
        away_slots = max(p["away"] for p in plan) + 1
        aways, refs = refs[:away_slots], refs[away_slots:]
    per = 6 if with_core else 5
    landing, refs = refs[:per * parts], refs[per * parts:]
    send_sems, recv_sems, local_sems = refs
    here = Place()
    rep, x, y, z = here.rep, here.x, here.y, here.z
    enter(here.peers + ([here.other_core] if with_core else []))
    copies = Copies(send_sems, recv_sems)
    local, exchanged = [], []
    for source, target in zip(from_all, to_all):
        copy = pltpu.make_async_copy(
            source.at[here.ex], target.at[here.ex], local_sems.at[len(local)]
        )
        copy.start()
        local.append(copy)
        for peer in here.peers:
            exchanged.append(copies.start(source.at[peer[1]], target.at[here.ex], peer))

    def halves(j):
        half = plan[j]["rows"] // 2
        return pl.ds(0, half), pl.ds(half, half)

    core_copies, one, two, last = {}, {}, {}, {}
    sent = set()

    def done_sending(copy):
        if id(copy) not in sent:
            sent.add(id(copy))
            copy.wait_send()

    def stage_fill(j):
        p = plan[j]
        if not with_core:
            p["fill"](ins, owns[p["slot"]], rep, None)
            return
        away = aways[p["away"]]
        for k in range(j):
            if plan[k]["away"] == p["away"]:
                done_sending(core_copies[k])
        p["fill"](ins, away, 1 - rep, None)
        core_copies[j] = copies.start(away, landing[per * j + 5], here.other_core)

    def stage_one(j):
        p = plan[j]
        own, (upper, lower) = owns[p["slot"]], halves(j)
        if with_core:
            core_copies[j].wait_recv()
            p["fill"](ins, own, rep, landing[per * j + 5])
        one[j] = (
            copies.start(own.at[:, 1 - y, :, upper], landing[per * j], here.other_y),
            copies.start(own.at[:, :, 1 - x, lower], landing[per * j + 1], here.other_x),
        )

    def stage_two(j):
        own, (upper, lower) = owns[plan[j]["slot"]], halves(j)
        from_y, from_x = landing[per * j], landing[per * j + 1]
        one[j][0].wait_recv()
        accumulate(own, [((y, 1 - x, upper), (1 - x,))], from_y)
        a = copies.start(own.at[:, y, 1 - x, upper], landing[per * j + 2], here.other_x)
        one[j][1].wait_recv()
        accumulate(own, [((1 - y, x, lower), (1 - y,))], from_x)
        b = copies.start(own.at[:, 1 - y, x, lower], landing[per * j + 3], here.other_y)
        accumulate(own, [((y, x, upper), (x,))], from_y)
        accumulate(own, [((y, x, lower), (y,))], from_x)
        two[j] = a, b

    def stage_three(j):
        own, (upper, lower) = owns[plan[j]["slot"]], halves(j)
        two[j][0].wait_recv()
        accumulate(own, [((y, x, upper), ())], landing[per * j + 2])
        two[j][1].wait_recv()
        accumulate(own, [((y, x, lower), ())], landing[per * j + 3])
        last[j] = [
            copies.start(own.at[(z + k) % 4, y, x], landing[per * j + 4].at[k - 1], here.other_z[k - 1])
            for k in range(1, 4)
        ]

    def stage_four(j):
        own, arrived = owns[plan[j]["slot"]], landing[per * j + 4]
        for copy in last[j]:
            copy.wait_recv()
        total = own[z, y, x].astype(f32) + arrived[0].astype(f32)
        total = total + arrived[1].astype(f32) + arrived[2].astype(f32)
        plan[j]["finish"](outs[plan[j]["out"]], total)
        for copy in (*one[j], *two[j], *last[j]):
            done_sending(copy)

    for step in range(parts + 4):
        for behind, stage in enumerate((stage_fill, stage_one, stage_two, stage_three, stage_four)):
            if 0 <= step - behind < parts:
                stage(step - behind)
    for copy in core_copies.values():
        done_sending(copy)
    for copy in exchanged:
        copy.wait_recv()
        done_sending(copy)
    for copy in local:
        copy.wait()


def reduce(plan, ins, spread_in, out_shapes, with_core, collective_id):
    parts = len(plan)
    scratch, slot_shape, away_shape = [], {}, {}
    for p in plan:
        shape = (4, 2, 2, p["rows"], p["columns"])
        slot_shape[p["slot"]] = pltpu.VMEM(shape, p["dtype"])
        if with_core:
            away_shape[p["away"]] = pltpu.VMEM(shape, p["dtype"])
    scratch += [slot_shape[i] for i in range(len(slot_shape))]
    scratch += [away_shape[i] for i in range(len(away_shape))]
    for p in plan:
        rows, columns, dtype = p["rows"], p["columns"], p["dtype"]
        shapes = [
            (4, 2, rows // 2, columns),
            (4, 2, rows // 2, columns),
            (4, rows // 2, columns),
            (4, rows // 2, columns),
            (3, rows, columns),
        ] + ([(4, 2, 2, rows, columns)] if with_core else [])
        scratch += [pltpu.VMEM(shape, dtype) for shape in shapes]
    copies = (8 if with_core else 7) * parts + 15 * len(spread_in)
    vmem, anywhere = pl.BlockSpec(memory_space=pltpu.VMEM), pl.BlockSpec(memory_space=pl.ANY)
    return pl.pallas_call(
        functools.partial(reduce_kernel, plan, with_core, len(spread_in), len(ins)),
        out_shape=out_shapes + [jax.ShapeDtypeStruct(a.shape, a.dtype) for a in spread_in],
        in_specs=[vmem] * len(ins) + [anywhere] * len(spread_in),
        out_specs=[vmem] * len(out_shapes) + [anywhere] * len(spread_in),
        scratch_shapes=scratch + [
            pltpu.SemaphoreType.DMA((copies,)),
            pltpu.SemaphoreType.DMA((copies,)),
            pltpu.SemaphoreType.DMA((max(len(spread_in), 1),)),
        ],
        compiler_params=pltpu.CompilerParams(
            collective_id=collective_id, has_side_effects=True, vmem_limit_bytes=62 * 2**20
        ),
    )(*ins, *spread_in)


def put(first, columns):
    def finish(out, total):
        out[:, pl.ds(first, columns)] = total
    return finish


def reduce_weights(pairs, small, outbound, pieces=2, collective_id=2):
    lefts = {}
    for left, _ in pairs:
        lefts.setdefault(id(left), (len(lefts), left))
    ins = [v[1].T.reshape(2, 8, 128, left_rows(v[1])) for v in lefts.values()]
    ins += [right for _, right in pairs] + [small]
    plan, columns = [], pairs[0][1].shape[1] // pieces
    for i, (left, _) in enumerate(pairs):
        for k in range(pieces):
            def fill(ins, own, rep, arrived, at=lefts[id(left)][0], right=len(lefts) + i, first=k * columns):
                def block(n, carry):
                    value = jnp.dot(
                        ins[at][rep, n], ins[right][:, pl.ds(first, columns)], preferred_element_type=f32
                    ).reshape(2, 64, columns)
                    if arrived is not None:
                        value = value + arrived[n // 2, n % 2].astype(f32)
                    own[n // 2, n % 2] = value.astype(own.dtype)
                    return carry
                lax.fori_loop(0, 8, block, 0)
            at = len(plan)
            plan.append(dict(rows=64, columns=columns, dtype=bf16, fill=fill, finish=put(k * columns, columns), out=i, slot=at % 5, away=at % 2))
    def fill_small(ins, own, rep, arrived):
        def block(n, carry):
            value = ins[-1][rep, n]
            if arrived is not None:
                value = value + arrived[n]
            own[n] = value
            return carry
        lax.fori_loop(0, 4, block, 0)
    plan.append(dict(rows=64, columns=small.shape[-1], dtype=f32, fill=fill_small, finish=put(0, small.shape[-1]), out=len(pairs), slot=min(5, len(plan)), away=2))
    out_shapes = [jax.ShapeDtypeStruct((64, b.shape[1]), f32) for _, b in pairs] + [jax.ShapeDtypeStruct((64, small.shape[-1]), f32)]
    return reduce(plan, ins, outbound, out_shapes, True, collective_id)


def left_rows(a):
    return a.shape[0]


def hot_slots(table, expert, capacity):
    experts, rows = table.shape
    lane = lax.broadcasted_iota(jnp.int32, (capacity, experts), 1)
    mine = jnp.where(lane == expert, 1.0, 0.0).astype(bf16)
    slot = jnp.dot(mine, table.astype(bf16), preferred_element_type=f32)
    wanted = lax.broadcasted_iota(jnp.int32, (capacity, rows), 0).astype(f32)
    return jnp.where(slot == wanted, 1.0, 0.0).astype(bf16)


def hot_rows(table, expert, capacity):
    rows, experts = table.shape
    sublane = lax.broadcasted_iota(jnp.int32, (experts, capacity), 0)
    mine = jnp.where(sublane == expert, 1.0, 0.0).astype(bf16)
    slot = jnp.dot(table.astype(bf16), mine, preferred_element_type=f32)
    wanted = lax.broadcasted_iota(jnp.int32, (rows, capacity), 1).astype(f32)
    return jnp.where(slot == wanted, 1.0, 0.0).astype(bf16)


def exact(left, right):
    return jnp.dot(left, right, preferred_element_type=f32).astype(bf16)


def pick_kernel(count, pieces, capacity, *refs):
    table, refs = refs[0], refs[1:]
    ins, refs = refs[:count], refs[count:]
    tables, refs = refs[0], refs[1:]
    outs, refs = refs[:count], refs[count:]
    hot, refs = refs[0], refs[1:]
    parts = count * pieces
    buffers, refs = refs[:5 * parts], refs[5 * parts:]
    send_sems, recv_sems, local_sems = refs
    here = Place()
    rep, x, y, z, ex = here.rep, here.x, here.y, here.z, here.ex
    by_y, by_x = here.other_y[1], here.other_x[1]
    experts = table.shape[0] // 2
    width = ins[0].shape[1] // pieces
    half = width // 2
    enter(here.peers)
    copies = Copies(send_sems, recv_sems)
    local = []

    def keep(source, target):
        copy = pltpu.make_async_copy(source, target, local_sems.at[len(local)])
        copy.start()
        local.append(copy)
        return copy

    def of(j):
        first = j % pieces * width
        return buffers[5 * j:5 * j + 5], ins[j // pieces], outs[j // pieces], first

    def stage_z(j):
        (column, *_), source, _, first = of(j)
        source = source.at[:, pl.ds(first, width)]
        sent = [copies.start(source, column.at[z], device) for device in here.other_z]
        return sent, keep(source, column.at[z])

    def stage_one(j, sent, kept):
        (column, from_x, from_y, _, _), _, _, _ = of(j)
        kept.wait()
        for copy in sent:
            copy.wait_recv()
        return (
            copies.start(column.at[:, :, pl.ds(0, half)], from_x, here.other_x),
            copies.start(column.at[:, :, pl.ds(half, half)], from_y, here.other_y),
        )

    def block(zz, yy, xx):
        return (zz * 2 + yy) * 2 + xx

    def pick_own(j):
        (column, *_), _, out, first = of(j)
        def body(n, carry):
            out[n, y, x, :, pl.ds(first, width)] = exact(hot[0, block(n, y, x)], column[n])
            return carry
        lax.fori_loop(0, 4, body, 0)

    def pick_moved(j):
        (_, from_x, from_y, _, _), _, out, first = of(j)
        def body(n, carry):
            out[n, y, 1 - x, :, pl.ds(first, half)] = exact(hot[0, block(n, y, 1 - x)], from_x[n])
            out[n, 1 - y, x, :, pl.ds(first + half, half)] = exact(hot[0, block(n, 1 - y, x)], from_y[n])
            return carry
        lax.fori_loop(0, 4, body, 0)

    def stage_two(j, one):
        (column, from_x, from_y, to_y, to_x), _, out, first = of(j)
        def own_part(n, carry):
            to_y[n, x] = exact(hot[1, block(n, y, x)], column[n, :, pl.ds(0, half)])
            to_x[n, y] = exact(hot[2, block(n, y, x)], column[n, :, pl.ds(half, half)])
            return carry
        lax.fori_loop(0, 4, own_part, 0)
        one[0].wait_recv()
        def x_part(n, carry):
            to_y[n, 1 - x] = exact(hot[1, block(n, y, 1 - x)], from_x[n])
            return carry
        lax.fori_loop(0, 4, x_part, 0)
        a = copies.start(to_y, out.at[:, y, :, :, pl.ds(first, half)], here.other_y)
        one[1].wait_recv()
        def y_part(n, carry):
            to_x[n, 1 - y] = exact(hot[2, block(n, 1 - y, x)], from_y[n])
            return carry
        lax.fori_loop(0, 4, y_part, 0)
        b = copies.start(to_x, out.at[:, :, x, :, pl.ds(first + half, half)], here.other_x)
        return a, b

    told = [copies.start(table, tables.at[ex], peer) for peer in here.peers]
    kept_table = keep(table, tables.at[ex])
    held, arrivals = {}, []
    for step in range(parts + 2):
        if step < parts:
            held[step] = stage_z(step)
        if step == 1:
            kept_table.wait()
            for copy in told:
                copy.wait_recv()
            def build(n, carry):
                for k, expert in enumerate((ex, by_y, by_x)):
                    hot[k, n] = hot_slots(tables[n, pl.ds(experts, experts)], expert, capacity)
                return carry
            lax.fori_loop(0, 16, build, 0)
        if 0 <= step - 1 < parts:
            held[step - 1] = stage_one(step - 1, *held[step - 1])
        if 0 <= step - 2 < parts:
            arrivals += stage_two(step - 2, held[step - 2])
        if 0 <= step - 1 < parts:
            pick_own(step - 1)
        if 0 <= step - 2 < parts:
            pick_moved(step - 2)
    for copy in arrivals:
        copy.wait_recv()
    copies.finish()


def pick_tokens(arrays, table, capacity, pieces, collective_id):
    count, (rows, model_width) = len(arrays), arrays[0].shape
    parts, width = count * pieces, model_width // pieces
    scratch = [pltpu.VMEM((3, 16, capacity, rows), bf16)]
    for _ in range(parts):
        scratch += [
            pltpu.VMEM((4, rows, width), bf16),
            pltpu.VMEM((4, rows, width // 2), bf16),
            pltpu.VMEM((4, rows, width // 2), bf16),
            pltpu.VMEM((4, 2, capacity, width // 2), bf16),
            pltpu.VMEM((4, 2, capacity, width // 2), bf16),
        ]
    copies = 7 * parts + 15
    vmem = pl.BlockSpec(memory_space=pltpu.VMEM)
    tables, *picked = pl.pallas_call(
        functools.partial(pick_kernel, count, pieces, capacity),
        out_shape=[jax.ShapeDtypeStruct((16, *table.shape), table.dtype)]
        + [jax.ShapeDtypeStruct((4, 2, 2, capacity, model_width), bf16)] * count,
        in_specs=[vmem] * (1 + count),
        out_specs=[vmem] * (1 + count),
        scratch_shapes=scratch
        + [
            pltpu.SemaphoreType.DMA((copies,)),
            pltpu.SemaphoreType.DMA((copies,)),
            pltpu.SemaphoreType.DMA((parts + 1,)),
        ],
        compiler_params=pltpu.CompilerParams(
            collective_id=collective_id, has_side_effects=True, vmem_limit_bytes=60 * 2**20
        ),
    )(table, *arrays)
    return tables, [a.reshape(-1, model_width) for a in picked]


def spread_kernel(count, pieces, capacity, *refs):
    tables, back, refs = refs[0], refs[1], refs[2:]
    ins, refs = refs[:count], refs[count:]
    given, refs = refs[0], refs[1:]
    outs, refs = refs[:count], refs[count:]
    hot, refs = refs[0], refs[1:]
    parts = count * pieces
    buffers, refs = refs[:8 * parts], refs[8 * parts:]
    send_sems, recv_sems, local_sems = refs
    here = Place()
    rep, x, y, z, ex = here.rep, here.x, here.y, here.z, here.ex
    by_y, by_x = here.other_y[1], here.other_x[1]
    width = ins[0].shape[-1] // pieces
    half = width // 2
    enter(here.peers)
    copies = Copies(send_sems, recv_sems)

    def of(j):
        first = j % pieces * width
        cols = pl.ds(first, half), pl.ds(first + half, half)
        return buffers[8 * j:8 * j + 8], ins[j // pieces], outs[j // pieces], first, cols

    def block(zz, yy, xx):
        return (zz * 2 + yy) * 2 + xx

    def term(which, at, rows):
        return jnp.dot(hot[which, at], rows, preferred_element_type=f32)

    def stage_one(j):
        (from_y, from_x, *_), source, _, _, (a, b) = of(j)
        return (
            copies.start(source.at[:, 1 - y, :, :, a], from_y, here.other_y),
            copies.start(source.at[:, :, 1 - x, :, b], from_x, here.other_x),
        )

    def stage_two(j, one):
        (from_y, from_x, to_x, to_y, *_), source, _, _, (a, b) = of(j)
        to_x_from, to_y_from = of(j)[0][4:6]
        one[0].wait_recv()
        def x_part(n, carry):
            at = block(n, y, 1 - x)
            total = term(0, at, source[n, y, 1 - x, :, a]) + term(1, at, from_y[n, 1 - x])
            to_x[n] = total.astype(bf16)
            return carry
        lax.fori_loop(0, 4, x_part, 0)
        first = copies.start(to_x, to_x_from, here.other_x)
        one[1].wait_recv()
        def y_part(n, carry):
            at = block(n, 1 - y, x)
            total = term(0, at, source[n, 1 - y, x, :, b]) + term(2, at, from_x[n, 1 - y])
            to_y[n] = total.astype(bf16)
            return carry
        lax.fori_loop(0, 4, y_part, 0)
        return first, copies.start(to_y, to_y_from, here.other_y)

    def stage_three(j, two):
        (from_y, from_x, _, _, more_a, more_b, column, from_z), source, _, _, (a, b) = of(j)
        two[0].wait_recv()
        two[1].wait_recv()
        def body(n, carry):
            at = block(n, y, x)
            total = term(0, at, source[n, y, x, :, a]) + term(1, at, from_y[n, x])
            column[n, :, pl.ds(0, half)] = (total + more_a[n].astype(f32)).astype(bf16)
            total = term(0, at, source[n, y, x, :, b]) + term(2, at, from_x[n, y])
            column[n, :, pl.ds(half, half)] = (total + more_b[n].astype(f32)).astype(bf16)
            return carry
        lax.fori_loop(0, 4, body, 0)
        return [
            copies.start(column.at[(z + k) % 4], from_z.at[k - 1], here.other_z[k - 1])
            for k in range(1, 4)
        ]

    def stage_four(j, last):
        (*_, column, from_z), _, out, first, _ = of(j)
        for copy in last:
            copy.wait_recv()
        total = column[z].astype(f32) + from_z[0].astype(f32)
        out[:, pl.ds(first, width)] = total + from_z[1].astype(f32) + from_z[2].astype(f32)

    told = [copies.start(back.at[peer[1]], given.at[ex], peer) for peer in here.peers]
    kept = pltpu.make_async_copy(back.at[ex], given.at[ex], local_sems.at[0])
    kept.start()
    held = {}
    for step in range(parts + 3):
        if step < parts:
            held[step] = stage_one(step)
        if step == 0:
            def build(n, carry):
                for k, expert in enumerate((ex, by_y, by_x)):
                    hot[k, n] = hot_rows(tables[n], expert, capacity)
                return carry
            lax.fori_loop(0, 16, build, 0)
        if 0 <= step - 1 < parts:
            held[step - 1] = stage_two(step - 1, held[step - 1])
        if 0 <= step - 2 < parts:
            held[step - 2] = stage_three(step - 2, held[step - 2])
        if 0 <= step - 3 < parts:
            stage_four(step - 3, held[step - 3])
    for copy in told:
        copy.wait_recv()
    copies.finish()
    kept.wait()


def spread_tokens(arrays, tables, back, pieces, collective_id):
    count, rows = len(arrays), tables.shape[1]
    model_width, capacity = arrays[0].shape[1], arrays[0].shape[0] // 16
    parts, width = count * pieces, model_width // pieces
    half = width // 2
    scratch = [pltpu.VMEM((3, 16, rows, capacity), bf16)]
    for _ in range(parts):
        scratch += [
            pltpu.VMEM((4, 2, capacity, half), bf16),
            pltpu.VMEM((4, 2, capacity, half), bf16),
            pltpu.VMEM((4, rows, half), bf16),
            pltpu.VMEM((4, rows, half), bf16),
            pltpu.VMEM((4, rows, half), bf16),
            pltpu.VMEM((4, rows, half), bf16),
            pltpu.VMEM((4, rows, width), bf16),
            pltpu.VMEM((3, rows, width), bf16),
        ]
    copies = 7 * parts + 15
    vmem = pl.BlockSpec(memory_space=pltpu.VMEM)
    given, *sums = pl.pallas_call(
        functools.partial(spread_kernel, count, pieces, capacity),
        out_shape=[jax.ShapeDtypeStruct(back.shape, back.dtype)]
        + [jax.ShapeDtypeStruct((rows, model_width), f32)] * count,
        in_specs=[vmem] * (2 + count),
        out_specs=[vmem] * (1 + count),
        scratch_shapes=scratch
        + [
            pltpu.SemaphoreType.DMA((copies,)),
            pltpu.SemaphoreType.DMA((copies,)),
            pltpu.SemaphoreType.DMA((1,)),
        ],
        compiler_params=pltpu.CompilerParams(
            collective_id=collective_id, has_side_effects=True, vmem_limit_bytes=60 * 2**20
        ),
    )(tables, back, *[a.reshape(4, 2, 2, capacity, model_width) for a in arrays])
    return given, sums


def has_kernels():
    return (lax.axis_size("rep"), lax.axis_size("ex")) == (2, 16)


def exchange(array):
    return lax.all_to_all(array, "ex", split_axis=0, concat_axis=0, tiled=True)


def gather_weights(shards, outbound):
    if has_kernels():
        *full, inbound = gather(shards, [outbound], True, [4] * (len(shards) - 1) + [1], 1)
        return [a.reshape(-1, a.shape[-1]) for a in full], inbound
    full = [lax.all_gather(a, ("rep", "ex"), axis=0, tiled=True) for a in shards]
    return full, exchange(outbound)


def slots_of(tables, capacity):
    experts, me = tables.shape[1] // 2, lax.axis_index("ex")
    gates = lax.dynamic_index_in_dim(tables, me, 1, keepdims=True)
    slots = lax.dynamic_index_in_dim(tables, experts + me, 1, keepdims=True)
    return slots == jnp.arange(capacity, dtype=f32)[None, :, None], gates


def dispatch(arrays, table, capacity):
    if has_kernels():
        return pick_tokens(arrays, table, capacity, 4, 2)
    tables = lax.all_gather(table, "ex", axis=0)
    picked_low = slots_of(tables, capacity)[0].astype(bf16)
    chosen = []
    for rows in arrays:
        rows = lax.all_gather(rows, "ex", axis=0)
        rows = jnp.einsum("sct,std->scd", picked_low, rows, preferred_element_type=f32)
        chosen.append(rows.astype(bf16).reshape(-1, rows.shape[-1]))
    return tables, chosen


def combine(arrays, tables, back, capacity):
    if has_kernels():
        wide = jnp.broadcast_to(back[:, None, :], (back.shape[0], 8, back.shape[1]))
        slots = tables[:, tables.shape[1] // 2 :].transpose(0, 2, 1)
        given, sums = spread_tokens(arrays, slots, wide, 4, 3)
        return given[:, 0], sums
    picked_low = slots_of(tables, capacity)[0].astype(bf16)
    sums = []
    for rows in arrays:
        rows = rows.reshape(*picked_low.shape[:2], -1)
        spread = jnp.einsum("sct,scd->std", picked_low, rows, preferred_element_type=f32)
        spread = spread.astype(bf16)
        sums.append(lax.psum_scatter(spread, "ex", scatter_dimension=0).astype(f32))
    return exchange(back), sums


def sum_weights(pairs, small, outbound):
    if has_kernels():
        width = small.shape[1]
        wide = jnp.pad(small, ((0, 0), (0, 128 - width))).reshape(2, 4, 2, 2, 64, 128)
        *sums, summed, given = reduce_weights(pairs, wide, [outbound], 4, 4)
        return sums, summed[:, :width], given
    both = ("rep", "ex")
    sums = []
    for left, right in pairs:
        grad = jnp.dot(left.T, right, preferred_element_type=f32).astype(bf16)
        sums.append(lax.psum_scatter(grad, both, scatter_dimension=0, tiled=True).astype(f32))
    summed = lax.psum_scatter(small, both, scatter_dimension=0, tiled=True)
    return sums, summed, exchange(outbound)


def body(
    tokens,
    out_cot,
    destination,
    doc_lengths,
    routes,
    fill_order,
    query_weight,
    key_weight,
    value_weight,
    output_weight,
    query_gain,
    key_gain,
    attn_gain,
    moe_gain,
    router_weight,
    expert_gate,
    expert_up,
    expert_down,
):
    group_size = lax.axis_size("ex")
    row_count, model_width = tokens.shape
    block_rows = row_count // group_size
    row_index = jnp.arange(row_count, dtype=jnp.int32)
    placed = destination // row_count % group_size * block_rows + destination % block_rows
    to_send = (placed[None, :] == row_index[:, None]).astype(bf16)
    inbound = jnp.dot(
        to_send, jnp.concatenate([tokens, out_cot], axis=1), preferred_element_type=f32
    ).astype(bf16)
    gains = jnp.concatenate(
        [jnp.stack([query_gain, key_gain, attn_gain, moe_gain], axis=1), router_weight], axis=1
    )
    extra = gains.shape[1]
    gains = jnp.pad(gains, ((0, 0), (0, -extra % 128)))
    full, packed = gather_weights(
        [query_weight, key_weight, value_weight, output_weight, gains],
        inbound.reshape(group_size, block_rows, 2 * model_width),
    )
    query_full, key_full, value_full, output_full, gains = full
    packed = packed.reshape(row_count, 2 * model_width)
    hidden_in, cot_in = packed[:, :model_width], packed[:, model_width:]
    query_scale, key_scale, attn_scale, moe_scale = (gains[:, i].astype(f32) for i in range(4))
    router_full = gains[:, 4:extra]
    gate_full = lax.all_gather(expert_gate[0], "rep", axis=0, tiled=True)
    up_full = lax.all_gather(expert_up[0], "rep", axis=0, tiled=True)
    down_full = lax.all_gather(expert_down[0], "rep", axis=0, tiled=True)

    segment, position, live_rows = segment_tables(doc_lengths[0], row_count)
    live_column = live_rows.astype(f32)[:, None]
    hidden = hidden_in.astype(f32)
    normed_attn, scale_attn = normalize(hidden)
    attn_in = (normed_attn * attn_scale).astype(bf16)
    query_pre = jnp.dot(attn_in, query_full, preferred_element_type=f32)
    key_pre = jnp.dot(attn_in, key_full, preferred_element_type=f32)
    value_pre = jnp.dot(attn_in, value_full, preferred_element_type=f32)
    normed_query, scale_query = normalize(query_pre)
    normed_key, scale_key = normalize(key_pre)
    cosine, sine = rope_tables(position)
    query_norm = (normed_query * query_scale).reshape(row_count, HEADS, HEAD_DIM)
    key_norm = (normed_key * key_scale).reshape(row_count, HEADS, HEAD_DIM)
    query_low = (query_norm * cosine + rotate_half(query_norm) * sine).astype(bf16)
    key_low = (key_norm * cosine + rotate_half(key_norm) * sine).astype(bf16)
    value_low = value_pre.astype(bf16).reshape(row_count, HEADS, HEAD_DIM)
    visible = (segment[:, None] == segment[None, :]) & (row_index[None, :] <= row_index[:, None])
    scores = attention_scores(query_low, key_low, visible)
    peak = jnp.max(scores, axis=-1, keepdims=True)
    weights_exp = jnp.exp(scores - peak)
    probs = weights_exp / jnp.sum(weights_exp, axis=-1, keepdims=True)
    probs_low = probs.astype(bf16)
    mixed = jnp.einsum("hqk,khd->qhd", probs_low, value_low, preferred_element_type=f32)
    mixed = mixed.reshape(row_count, model_width).astype(bf16)
    branch = jnp.dot(mixed, output_full, preferred_element_type=f32)
    after_attn = hidden + live_column * branch
    normed_moe, scale_moe = normalize(after_attn)
    moe_in = (normed_moe * moe_scale).astype(bf16)
    logits = jnp.dot(moe_in, router_full, preferred_element_type=f32)
    router_probs = jax.nn.softmax(logits, axis=-1)
    experts = router_full.shape[1]
    capacity = row_count * routes.shape[1] // experts
    slot_table, kept = slot_tables(routes, fill_order[0], live_rows, experts, capacity)
    gates = jnp.where(kept, router_probs, 0.0)

    table = jnp.concatenate([gates.T, slot_table.T.astype(f32)], axis=0)
    tables, (rows_in, rows_cot) = dispatch([moe_in, cot_in], table, capacity)
    picked, gate_rows = slots_of(tables, capacity)
    slot_gate = jnp.sum(jnp.where(picked, gate_rows, 0.0), axis=2).reshape(-1, 1)
    gate_pre = jnp.dot(rows_in, gate_full, preferred_element_type=f32)
    up_pre = jnp.dot(rows_in, up_full, preferred_element_type=f32)
    sigma = jax.nn.sigmoid(gate_pre)
    silu = gate_pre * sigma
    middle = (silu * up_pre).astype(bf16)
    expert_out = jnp.dot(middle, down_full, preferred_element_type=f32).astype(bf16)
    slot_grad = jnp.sum(rows_cot.astype(f32) * expert_out.astype(f32), axis=1)
    weighted = (slot_gate * expert_out.astype(f32)).astype(bf16)
    grad_expert_out = (slot_gate * rows_cot.astype(f32)).astype(bf16)
    grad_middle = jnp.dot(grad_expert_out, down_full.T, preferred_element_type=f32)
    grad_down_full = jnp.dot(middle.T, grad_expert_out, preferred_element_type=f32)
    grad_gate_low = (grad_middle * up_pre * sigma * (1.0 + gate_pre * (1.0 - sigma))).astype(bf16)
    grad_up_low = (grad_middle * silu).astype(bf16)
    grad_gate_full = jnp.dot(rows_in.T, grad_gate_low, preferred_element_type=f32)
    grad_up_full = jnp.dot(rows_in.T, grad_up_low, preferred_element_type=f32)
    grad_rows = jnp.dot(grad_gate_low, gate_full.T, preferred_element_type=f32)
    grad_rows = (
        grad_rows + jnp.dot(grad_up_low, up_full.T, preferred_element_type=f32)
    ).astype(bf16)
    slot_grad = slot_grad.reshape(group_size, capacity, 1)
    grad_back = jnp.sum(jnp.where(picked, slot_grad, 0.0), axis=1)
    grad_rprobs, (grad_moe_in, mixture) = combine([grad_rows, weighted], tables, grad_back, capacity)
    grad_rprobs = grad_rprobs.T
    output = (after_attn + mixture).astype(bf16)
    owned_gate, owned_up, owned_down = (
        lax.psum_scatter(g.astype(bf16), "rep", scatter_dimension=0, tiled=True).astype(f32)[None]
        for g in (grad_gate_full, grad_up_full, grad_down_full)
    )

    grad_out = cot_in.astype(f32)
    grad_logits = router_probs * (
        grad_rprobs - jnp.sum(router_probs * grad_rprobs, axis=-1, keepdims=True)
    )
    grad_moe_in = grad_moe_in + jnp.dot(
        grad_logits, router_full.T, precision=lax.Precision.HIGHEST, preferred_element_type=f32
    )
    grad_router = jnp.dot(
        moe_in.T, grad_logits, precision=lax.Precision.HIGHEST, preferred_element_type=f32
    )
    grad_moe_scale = jnp.sum(grad_moe_in * normed_moe, axis=0)
    grad_after = grad_out + norm_back(grad_moe_in * moe_scale, normed_moe, scale_moe)
    grad_branch = (live_column * grad_after).astype(bf16)
    grad_mixed = (
        jnp.dot(grad_branch, output_full.T, preferred_element_type=f32)
        .astype(bf16)
        .reshape(row_count, HEADS, HEAD_DIM)
    )
    grad_value = jnp.einsum("hqk,qhd->khd", probs_low, grad_mixed, preferred_element_type=f32)
    grad_att = jnp.einsum("qhd,khd->hqk", grad_mixed, value_low, preferred_element_type=f32)
    grad_scores = (probs * (grad_att - jnp.sum(probs * grad_att, axis=-1, keepdims=True))).astype(
        bf16
    )
    grad_query_rot = jnp.einsum(
        "hqk,khd->qhd", grad_scores, key_low, preferred_element_type=f32
    ) * HEAD_DIM ** (-0.5)
    grad_key_rot = jnp.einsum(
        "hqk,qhd->khd", grad_scores, query_low, preferred_element_type=f32
    ) * HEAD_DIM ** (-0.5)
    grad_query_normed = (grad_query_rot * cosine + rotate_back(grad_query_rot * sine)).reshape(
        row_count, model_width
    )
    grad_key_normed = (grad_key_rot * cosine + rotate_back(grad_key_rot * sine)).reshape(
        row_count, model_width
    )
    grad_query_scale = jnp.sum(grad_query_normed * normed_query, axis=0)
    grad_key_scale = jnp.sum(grad_key_normed * normed_key, axis=0)
    grad_query_pre = norm_back(grad_query_normed * query_scale, normed_query, scale_query)
    grad_key_pre = norm_back(grad_key_normed * key_scale, normed_key, scale_key)
    grad_query_pre = grad_query_pre.astype(bf16)
    grad_key_pre = grad_key_pre.astype(bf16)
    grad_value_pre = grad_value.reshape(row_count, model_width).astype(bf16)
    grad_attn_in = jnp.dot(grad_query_pre, query_full.T, preferred_element_type=f32)
    grad_attn_in = grad_attn_in + jnp.dot(grad_key_pre, key_full.T, preferred_element_type=f32)
    grad_attn_in = grad_attn_in + jnp.dot(grad_value_pre, value_full.T, preferred_element_type=f32)
    grad_attn_scale = jnp.sum(grad_attn_in * normed_attn, axis=0)
    grad_hidden = grad_after + norm_back(grad_attn_in * attn_scale, normed_attn, scale_attn)

    small = jnp.concatenate(
        [
            jnp.stack([grad_query_scale, grad_key_scale, grad_attn_scale, grad_moe_scale], axis=1),
            grad_router,
        ],
        axis=1,
    )
    outbound = jnp.concatenate([output, grad_hidden.astype(bf16)], axis=1)
    pairs = [
        (attn_in, grad_query_pre),
        (attn_in, grad_key_pre),
        (attn_in, grad_value_pre),
        (mixed, grad_branch),
    ]
    sums, small, outbound = sum_weights(
        pairs, small, outbound.reshape(group_size, block_rows, 2 * model_width)
    )
    owned_query, owned_key, owned_value, owned_output = sums
    outbound = outbound.reshape(row_count, 2 * model_width)
    outbound = jnp.dot(to_send.T, outbound, preferred_element_type=f32).astype(bf16)
    return (
        outbound[:, :model_width],
        outbound[:, model_width:],
        owned_query,
        owned_key,
        owned_value,
        owned_output,
        small[:, 0],
        small[:, 1],
        small[:, 2],
        small[:, 3],
        small[:, 4:],
        owned_gate,
        owned_up,
        owned_down,
    )


def solution(mesh):
    rows, row = P(("rep", "ex"), None), P(("rep", "ex"))
    expert = P("ex", "rep", None)
    return jax.shard_map(
        body,
        mesh=mesh,
        in_specs=(rows, rows, row) + (rows,) * 7 + (row,) * 4 + (rows,) + (expert,) * 3,
        out_specs=(rows,) * 6 + (row,) * 4 + (rows,) + (expert,) * 3,
        check_vma=False,
    )
```

```python
import functools

import jax
import jax.numpy as jnp
from jax import lax
from jax.experimental import pallas as pl
from jax.experimental.pallas import tpu as pltpu
from jax.sharding import PartitionSpec as P

HEADS = 16
HEAD_DIM = 128

epsilon = 1e-05
rope_base = 10000.0
masked_score = -1e30
bf16 = jnp.bfloat16
f32 = jnp.float32


def normalize(values):
    scale = lax.rsqrt(jnp.mean(values * values, axis=-1, keepdims=True) + epsilon)
    return (values * scale, scale)


def norm_back(grad_normed, normed, scale):
    return scale * (grad_normed - normed * jnp.mean(grad_normed * normed, axis=-1, keepdims=True))


def rotate_half(values):
    middle = values.shape[-1] // 2
    return jnp.concatenate([-values[..., middle:], values[..., :middle]], axis=-1)


def rotate_back(values):
    middle = values.shape[-1] // 2
    return jnp.concatenate([values[..., middle:], -values[..., :middle]], axis=-1)


def rope_tables(position):
    steps = jnp.arange(HEAD_DIM // 2, dtype=f32) * (2.0 / HEAD_DIM)
    inverse = rope_base ** (-steps)
    angle = position.astype(f32)[:, None] * inverse[None, :]
    cosine = jnp.concatenate([jnp.cos(angle), jnp.cos(angle)], axis=-1)[:, None, :]
    sine = jnp.concatenate([jnp.sin(angle), jnp.sin(angle)], axis=-1)[:, None, :]
    return (cosine, sine)


def segment_tables(lengths, row_count):
    count = lengths.shape[0]
    numbers = jnp.arange(count, dtype=jnp.int32)
    before = (numbers[None, :] < numbers[:, None]).astype(jnp.int32)
    starts = jnp.sum(before * lengths[None, :], axis=1)
    ends = starts + lengths
    row_index = jnp.arange(row_count, dtype=jnp.int32)
    segment = jnp.sum((row_index[:, None] >= ends[None, :]).astype(jnp.int32), axis=1)
    begin = jnp.sum(jnp.where(segment[:, None] == numbers[None, :], starts[None, :], 0), axis=1)
    return (segment, row_index - begin, segment < count - 1)


def slot_tables(routes, filling, live_rows, experts, capacity):
    row_count, top_count = routes.shape
    order = jnp.arange(row_count * top_count, dtype=jnp.int32)
    rows = jnp.arange(row_count, dtype=jnp.int32)
    hot_row = (filling[None, :] // top_count == rows[:, None]).astype(bf16)
    hot_choice = (filling % top_count)[:, None] == jnp.arange(top_count, dtype=jnp.int32)[None, :]
    high = jnp.where(hot_choice, (order // 64)[:, None], 0).astype(bf16)
    lower = jnp.where(hot_choice, (order % 64)[:, None], 0).astype(bf16)
    ranks = jnp.dot(
        hot_row, jnp.concatenate([high, lower], axis=1), preferred_element_type=f32
    ).astype(jnp.int32)
    rank = ranks[:, :top_count] * 64 + ranks[:, top_count:]
    chosen = routes[:, :, None] == jnp.arange(experts, dtype=jnp.int32)[None, None, :]
    rank_table = jnp.sum(jnp.where(chosen, rank[:, :, None], 0), axis=1)
    counted = jnp.any(chosen, axis=1) & live_rows[:, None]
    earlier = counted[:, None, :] & (rank_table[:, None, :] < rank_table[None, :, :])
    slot = jnp.sum(earlier.astype(jnp.int32), axis=0)
    kept = counted & (slot < capacity)
    return (jnp.where(kept, slot, -1), kept)


def attention_scores(query_low, key_low, visible):
    scores = jnp.einsum(
        "qhd,khd->hqk", query_low, key_low, preferred_element_type=f32
    ) * HEAD_DIM ** (-0.5)
    return jnp.where(visible[None], scores, masked_score)


MESH = pl.DeviceIdType.MESH


class Place:
    def __init__(self):
        self.rep, self.ex = lax.axis_index("rep"), lax.axis_index("ex")
        self.x, self.y, self.z = self.ex % 2, self.ex // 2 % 2, self.ex // 4
        self.other_x = (self.rep, self.ex + 1 - 2 * self.x)
        self.other_y = (self.rep, self.ex + 2 - 4 * self.y)
        self.other_core = (1 - self.rep, self.ex)
        self.other_z = [(self.rep, (self.ex + 4 * k) % 16) for k in range(1, 4)]
        self.peers = [(self.rep, (self.ex + k) % 16) for k in range(1, 16)]


def enter(devices):
    barrier = pltpu.get_barrier_semaphore()
    for device in devices:
        pl.semaphore_signal(barrier, inc=1, device_id=device, device_id_type=MESH)
    pl.semaphore_wait(barrier, len(devices))


class Copies:
    def __init__(self, send_sems, recv_sems):
        self.send_sems, self.recv_sems, self.made = send_sems, recv_sems, []
        self.done = set()

    def start(self, source, target, device):
        at = len(self.made)
        copy = pltpu.make_async_remote_copy(
            src_ref=source,
            dst_ref=target,
            send_sem=self.send_sems.at[at],
            recv_sem=self.recv_sems.at[at],
            device_id=device,
            device_id_type=MESH,
        )
        copy.start()
        self.made.append(copy)
        return copy

    def sent(self, copy):
        if id(copy) not in self.done:
            self.done.add(id(copy))
            copy.wait_send()

    def finish(self):
        for copy in self.made:
            self.sent(copy)


def gather_kernel(pieces, with_core, shards, spread_in, *refs):
    count, moved = len(shards), len(spread_in)
    ins, refs = refs[:count], refs[count:]
    from_all, refs = refs[:moved], refs[moved:]
    outs, refs = refs[:count], refs[count:]
    to_all, refs = refs[:moved], refs[moved:]
    send_sems, recv_sems, local_sems = refs
    here = Place()
    rep, x, y, z = here.rep, here.x, here.y, here.z
    enter(here.peers + ([here.other_core] if with_core else []))
    copies = Copies(send_sems, recv_sems)
    local, exchanged = [], []

    def keep(source, target):
        copy = pltpu.make_async_copy(source, target, local_sems.at[len(local)])
        copy.start()
        local.append(copy)
        return copy

    for source, target in zip(from_all, to_all):
        keep(source.at[here.ex], target.at[here.ex])
        for peer in here.peers:
            exchanged.append(copies.start(source.at[peer[1]], target.at[here.ex], peer))

    parts = []
    for i in range(count):
        rows = shards[i][0] // pieces[i]
        parts += [(i, k * rows, rows) for k in range(pieces[i])]

    def stage_z(part):
        i, first, rows = part
        source, full = ins[i].at[pl.ds(first, rows)], outs[i].at[rep]
        target = full.at[z, y, x, pl.ds(first, rows)]
        waits = [copies.start(source, target, device) for device in here.other_z]
        return waits, keep(source, target)

    def stage_one(part, waits, kept):
        i, first, rows = part
        full, half = outs[i].at[rep], rows // 2
        kept.wait()
        for copy in waits:
            copy.wait_recv()
        upper, lower = pl.ds(first, half), pl.ds(first + half, half)
        a = full.at[:, y, x, upper]
        b = full.at[:, y, x, lower]
        one = copies.start(a, a, here.other_x), copies.start(b, b, here.other_y)
        own = full.at[:, y, x, pl.ds(first, rows)]
        cores = [copies.start(own, own, here.other_core)] if with_core else []
        return one, cores

    def stage_two(part, one, cores):
        i, first, rows = part
        full, half = outs[i].at[rep], rows // 2
        upper, lower = pl.ds(first, half), pl.ds(first + half, half)
        one[0].wait_recv()
        a = full.at[:, y, :, upper]
        two_a = copies.start(a, a, here.other_y)
        one[1].wait_recv()
        b = full.at[:, :, x, lower]
        two_b = copies.start(b, b, here.other_x)
        if with_core:
            a, b = full.at[:, y, 1 - x, upper], full.at[:, 1 - y, x, lower]
            cores += [copies.start(a, a, here.other_core), copies.start(b, b, here.other_core)]
        return (two_a, two_b), cores

    def stage_three(part, two, cores):
        i, first, rows = part
        full, half = outs[i].at[rep], rows // 2
        upper, lower = pl.ds(first, half), pl.ds(first + half, half)
        two[0].wait_recv()
        a = full.at[:, 1 - y, :, upper]
        if with_core:
            cores += [copies.start(a, a, here.other_core)]
        two[1].wait_recv()
        b = full.at[:, :, 1 - x, lower]
        if with_core:
            cores += [copies.start(b, b, here.other_core)]
        return cores

    held, arrivals, count = {}, [], len(parts)
    for step in range(count + 3):
        if step < count:
            held[step] = stage_z(parts[step])
        if 0 <= step - 1 < count:
            held[step - 1] = stage_one(parts[step - 1], *held[step - 1])
        if 0 <= step - 2 < count:
            held[step - 2] = stage_two(parts[step - 2], *held[step - 2])
        if 0 <= step - 3 < count:
            arrivals += stage_three(parts[step - 3], *held[step - 3])
    for copy in arrivals + exchanged:
        copy.wait_recv()
    copies.finish()
    for copy in local[:len(from_all)]:
        copy.wait()


def gather(shards, spread_in, with_core, pieces, collective_id):
    copies = sum(pieces) * (12 if with_core else 7) + 15 * len(spread_in)
    local = sum(pieces) + len(spread_in)
    out_shape = [jax.ShapeDtypeStruct((2, 4, 2, 2) + a.shape, a.dtype) for a in shards]
    out_shape += [jax.ShapeDtypeStruct(a.shape, a.dtype) for a in spread_in]
    anywhere = pl.BlockSpec(memory_space=pl.ANY)
    shapes = [a.shape for a in shards]
    return pl.pallas_call(
        functools.partial(gather_kernel, pieces, with_core, shapes, [a.shape for a in spread_in]),
        out_shape=out_shape,
        in_specs=[anywhere] * (len(shards) + len(spread_in)),
        out_specs=[anywhere] * len(out_shape),
        scratch_shapes=[
            pltpu.SemaphoreType.DMA((copies,)),
            pltpu.SemaphoreType.DMA((copies,)),
            pltpu.SemaphoreType.DMA((local,)),
        ],
        compiler_params=pltpu.CompilerParams(collective_id=collective_id, has_side_effects=True),
    )(*shards, *spread_in)


def accumulate(target, blocks, arrived):
    def add(z, carry):
        for into, source in blocks:
            value = target[(z,) + into].astype(f32) + arrived[(z,) + source].astype(f32)
            target[(z,) + into] = value.astype(target.dtype)
        return carry
    lax.fori_loop(0, 4, add, 0)


def reduce_kernel(plan, with_core, moved, n_in, *refs):
    parts = len(plan)
    ins, refs = refs[:n_in], refs[n_in:]
    from_all, refs = refs[:moved], refs[moved:]
    n_out = len({p["out"] for p in plan})
    outs, refs = refs[:n_out], refs[n_out:]
    to_all, refs = refs[:moved], refs[moved:]
    slots = max(p["slot"] for p in plan) + 1
    owns, refs = refs[:slots], refs[slots:]
    if with_core:
        away_slots = max(p["away"] for p in plan) + 1
        aways, refs = refs[:away_slots], refs[away_slots:]
    per = 6 if with_core else 5
    landing, refs = refs[:per * parts], refs[per * parts:]
    send_sems, recv_sems, local_sems = refs
    here = Place()
    rep, x, y, z = here.rep, here.x, here.y, here.z
    enter(here.peers + ([here.other_core] if with_core else []))
    copies = Copies(send_sems, recv_sems)
    local, exchanged = [], []
    for source, target in zip(from_all, to_all):
        copy = pltpu.make_async_copy(
            source.at[here.ex], target.at[here.ex], local_sems.at[len(local)]
        )
        copy.start()
        local.append(copy)
        for peer in here.peers:
            exchanged.append(copies.start(source.at[peer[1]], target.at[here.ex], peer))

    def halves(j):
        half = plan[j]["rows"] // 2
        return pl.ds(0, half), pl.ds(half, half)

    core_copies, one, two, last = {}, {}, {}, {}
    sent = set()

    def done_sending(copy):
        if id(copy) not in sent:
            sent.add(id(copy))
            copy.wait_send()

    def stage_fill(j):
        p = plan[j]
        if not with_core:
            p["fill"](ins, owns[p["slot"]], rep, None)
            return
        away = aways[p["away"]]
        for k in range(j):
            if plan[k]["away"] == p["away"]:
                done_sending(core_copies[k])
        p["fill"](ins, away, 1 - rep, None)
        core_copies[j] = copies.start(away, landing[per * j + 5], here.other_core)

    def stage_one(j):
        p = plan[j]
        own, (upper, lower) = owns[p["slot"]], halves(j)
        if with_core:
            core_copies[j].wait_recv()
            p["fill"](ins, own, rep, landing[per * j + 5])
        one[j] = (
            copies.start(own.at[:, 1 - y, :, upper], landing[per * j], here.other_y),
            copies.start(own.at[:, :, 1 - x, lower], landing[per * j + 1], here.other_x),
        )

    def stage_two(j):
        own, (upper, lower) = owns[plan[j]["slot"]], halves(j)
        from_y, from_x = landing[per * j], landing[per * j + 1]
        one[j][0].wait_recv()
        accumulate(own, [((y, 1 - x, upper), (1 - x,))], from_y)
        a = copies.start(own.at[:, y, 1 - x, upper], landing[per * j + 2], here.other_x)
        one[j][1].wait_recv()
        accumulate(own, [((1 - y, x, lower), (1 - y,))], from_x)
        b = copies.start(own.at[:, 1 - y, x, lower], landing[per * j + 3], here.other_y)
        accumulate(own, [((y, x, upper), (x,))], from_y)
        accumulate(own, [((y, x, lower), (y,))], from_x)
        two[j] = a, b

    def stage_three(j):
        own, (upper, lower) = owns[plan[j]["slot"]], halves(j)
        two[j][0].wait_recv()
        accumulate(own, [((y, x, upper), ())], landing[per * j + 2])
        two[j][1].wait_recv()
        accumulate(own, [((y, x, lower), ())], landing[per * j + 3])
        last[j] = [
            copies.start(own.at[(z + k) % 4, y, x], landing[per * j + 4].at[k - 1], here.other_z[k - 1])
            for k in range(1, 4)
        ]

    def stage_four(j):
        own, arrived = owns[plan[j]["slot"]], landing[per * j + 4]
        for copy in last[j]:
            copy.wait_recv()
        total = own[z, y, x].astype(f32) + arrived[0].astype(f32)
        total = total + arrived[1].astype(f32) + arrived[2].astype(f32)
        plan[j]["finish"](outs[plan[j]["out"]], total)
        for copy in (*one[j], *two[j], *last[j]):
            done_sending(copy)

    for step in range(parts + 4):
        for behind, stage in enumerate((stage_fill, stage_one, stage_two, stage_three, stage_four)):
            if 0 <= step - behind < parts:
                stage(step - behind)
    for copy in core_copies.values():
        done_sending(copy)
    for copy in exchanged:
        copy.wait_recv()
        done_sending(copy)
    for copy in local:
        copy.wait()


def reduce(plan, ins, spread_in, out_shapes, with_core, collective_id):
    parts = len(plan)
    scratch, slot_shape, away_shape = [], {}, {}
    for p in plan:
        shape = (4, 2, 2, p["rows"], p["columns"])
        slot_shape[p["slot"]] = pltpu.VMEM(shape, p["dtype"])
        if with_core:
            away_shape[p["away"]] = pltpu.VMEM(shape, p["dtype"])
    scratch += [slot_shape[i] for i in range(len(slot_shape))]
    scratch += [away_shape[i] for i in range(len(away_shape))]
    for p in plan:
        rows, columns, dtype = p["rows"], p["columns"], p["dtype"]
        shapes = [
            (4, 2, rows // 2, columns),
            (4, 2, rows // 2, columns),
            (4, rows // 2, columns),
            (4, rows // 2, columns),
            (3, rows, columns),
        ] + ([(4, 2, 2, rows, columns)] if with_core else [])
        scratch += [pltpu.VMEM(shape, dtype) for shape in shapes]
    copies = (8 if with_core else 7) * parts + 15 * len(spread_in)
    vmem, anywhere = pl.BlockSpec(memory_space=pltpu.VMEM), pl.BlockSpec(memory_space=pl.ANY)
    return pl.pallas_call(
        functools.partial(reduce_kernel, plan, with_core, len(spread_in), len(ins)),
        out_shape=out_shapes + [jax.ShapeDtypeStruct(a.shape, a.dtype) for a in spread_in],
        in_specs=[vmem] * len(ins) + [anywhere] * len(spread_in),
        out_specs=[vmem] * len(out_shapes) + [anywhere] * len(spread_in),
        scratch_shapes=scratch + [
            pltpu.SemaphoreType.DMA((copies,)),
            pltpu.SemaphoreType.DMA((copies,)),
            pltpu.SemaphoreType.DMA((max(len(spread_in), 1),)),
        ],
        compiler_params=pltpu.CompilerParams(
            collective_id=collective_id, has_side_effects=True, vmem_limit_bytes=62 * 2**20
        ),
    )(*ins, *spread_in)


def put(first, columns):
    def finish(out, total):
        out[:, pl.ds(first, columns)] = total
    return finish


def reduce_weights(pairs, small, outbound, pieces=2, collective_id=2):
    lefts = {}
    for left, _ in pairs:
        lefts.setdefault(id(left), (len(lefts), left))
    ins = [v[1].T.reshape(2, 8, 128, left_rows(v[1])) for v in lefts.values()]
    ins += [right for _, right in pairs] + [small]
    plan, columns = [], pairs[0][1].shape[1] // pieces
    for i, (left, _) in enumerate(pairs):
        for k in range(pieces):
            def fill(ins, own, rep, arrived, at=lefts[id(left)][0], right=len(lefts) + i, first=k * columns):
                def block(n, carry):
                    value = jnp.dot(
                        ins[at][rep, n], ins[right][:, pl.ds(first, columns)], preferred_element_type=f32
                    ).reshape(2, 64, columns)
                    if arrived is not None:
                        value = value + arrived[n // 2, n % 2].astype(f32)
                    own[n // 2, n % 2] = value.astype(own.dtype)
                    return carry
                lax.fori_loop(0, 8, block, 0)
            at = len(plan)
            plan.append(dict(rows=64, columns=columns, dtype=bf16, fill=fill, finish=put(k * columns, columns), out=i, slot=at % 5, away=at % 2))
    def fill_small(ins, own, rep, arrived):
        def block(n, carry):
            value = ins[-1][rep, n]
            if arrived is not None:
                value = value + arrived[n]
            own[n] = value
            return carry
        lax.fori_loop(0, 4, block, 0)
    plan.append(dict(rows=64, columns=small.shape[-1], dtype=f32, fill=fill_small, finish=put(0, small.shape[-1]), out=len(pairs), slot=min(5, len(plan)), away=2))
    out_shapes = [jax.ShapeDtypeStruct((64, b.shape[1]), f32) for _, b in pairs] + [jax.ShapeDtypeStruct((64, small.shape[-1]), f32)]
    return reduce(plan, ins, outbound, out_shapes, True, collective_id)


def left_rows(a):
    return a.shape[0]


def nt(left, right):
    return lax.dot_general(left, right, (((1,), (1,)), ((), ())), preferred_element_type=f32)


def nn(left, right):
    return jnp.dot(left, right, preferred_element_type=f32)


def hot_slots(table, expert, capacity):
    experts, rows = table.shape
    lane = lax.broadcasted_iota(jnp.int32, (capacity, experts), 1)
    mine = jnp.where(lane == expert, 1.0, 0.0).astype(bf16)
    slot = nn(mine, table.astype(bf16))
    wanted = lax.broadcasted_iota(jnp.int32, (capacity, rows), 0).astype(f32)
    return jnp.where(slot == wanted, 1.0, 0.0).astype(bf16)


PIECES = 4


def expert_kernel(capacity, *refs):
    table, moe, cot, gate_w, up_w, down_w = refs[:6]
    grad_out, mix_out, given, *kept_outs = refs[6:14]
    refs = refs[14:]
    tables, hot, hot_row, hot_gate, gate_col, grad_col, back = refs[:7]
    rows_in, rows_cot, acc, to_gate, to_up, middle, result = refs[7:14]
    gu_slots, down_slots, to_slots, send_slots, column_slots = refs[14:19]
    parts = 2 * PIECES
    pick_buffers = [refs[19 + 3 * j : 22 + 3 * j] for j in range(parts)]
    refs = refs[19 + 3 * parts :]
    spread_buffers = [refs[2 * j : 2 * j + 2] for j in range(parts)]
    send_sems, recv_sems, local_sems, load_sems, ready = refs[2 * parts :]
    here = Place()
    x, y, z, ex = here.x, here.y, here.z, here.ex
    by_y, by_x = here.other_y[1], here.other_x[1]
    experts = table.shape[0] // 2
    units = gate_w.shape[1]
    width = moe.shape[1] // PIECES
    half = width // 2
    enter(here.peers)
    copies = Copies(send_sems, recv_sems)
    local = []

    def keep(source, target):
        copy = pltpu.make_async_copy(source, target, local_sems.at[len(local)])
        copy.start()
        local.append(copy)
        return copy

    def block(zz, yy, xx):
        return (zz * 2 + yy) * 2 + xx

    def piece(j):
        return j % PIECES * width

    gu_loads, down_loads = {}, {}

    def load_gu(n):
        if n < parts:
            rows = pl.ds(piece(n), width)
            gu_loads[n] = [
                pltpu.make_async_copy(w.at[rows], gu_slots.at[n % 2, k], load_sems.at[n % 2, k])
                for k, w in enumerate((gate_w, up_w))
            ]
            for copy in gu_loads[n]:
                copy.start()

    def load_down(n):
        if n < parts:
            columns = pl.ds(piece(n), width)
            down_loads[n] = pltpu.make_async_copy(
                down_w.at[:, columns], down_slots.at[n % 2], load_sems.at[n % 2, 2]
            )
            down_loads[n].start()

    def stage_z(j):
        source = (moe if j < PIECES else cot).at[:, pl.ds(piece(j), width)]
        target = pick_buffers[j][0].at[z]
        return [copies.start(source, target, peer) for peer in here.other_z], keep(source, target)

    def stage_one(j, sent, kept):
        column, from_x, from_y = pick_buffers[j]
        kept.wait()
        for copy in sent:
            copy.wait_recv()
        return (
            copies.start(column.at[:, :, pl.ds(0, half)], from_x, here.other_x),
            copies.start(column.at[:, :, pl.ds(half, half)], from_y, here.other_y),
        )

    def landing(j):
        return rows_in if j < PIECES else rows_cot

    def pick_own(j):
        column, into = pick_buffers[j][0], landing(j)
        def body(n, carry):
            picked = nn(hot[0, block(n, y, x)], column[n])
            into[n, y, x, :, pl.ds(piece(j), width)] = picked.astype(bf16)
            return carry
        lax.fori_loop(0, 4, body, 0)

    def pick_moved(j):
        (_, from_x, from_y), into, first = pick_buffers[j], landing(j), piece(j)
        def body(n, carry):
            picked = nn(hot[0, block(n, y, 1 - x)], from_x[n])
            into[n, y, 1 - x, :, pl.ds(first, half)] = picked.astype(bf16)
            picked = nn(hot[0, block(n, 1 - y, x)], from_y[n])
            into[n, 1 - y, x, :, pl.ds(first + half, half)] = picked.astype(bf16)
            return carry
        lax.fori_loop(0, 4, body, 0)

    second = {}

    def stage_two(j, one):
        (column, from_x, from_y), into, first = pick_buffers[j], landing(j), piece(j)
        to_y, to_x = to_slots.at[j % 2, 0], to_slots.at[j % 2, 1]
        if j >= 2:
            copies.sent(second[j - 2][0])
            copies.sent(second[j - 2][1])
        def own_part(n, carry):
            at = block(n, y, x)
            to_y[n, x] = nn(hot[1, at], column[n, :, pl.ds(0, half)]).astype(bf16)
            to_x[n, y] = nn(hot[2, at], column[n, :, pl.ds(half, half)]).astype(bf16)
            return carry
        lax.fori_loop(0, 4, own_part, 0)
        one[0].wait_recv()
        def x_part(n, carry):
            to_y[n, 1 - x] = nn(hot[1, block(n, y, 1 - x)], from_x[n]).astype(bf16)
            return carry
        lax.fori_loop(0, 4, x_part, 0)
        a = copies.start(to_y, into.at[:, y, :, :, pl.ds(first, half)], here.other_y)
        one[1].wait_recv()
        def y_part(n, carry):
            to_x[n, 1 - y] = nn(hot[2, block(n, 1 - y, x)], from_y[n]).astype(bf16)
            return carry
        lax.fori_loop(0, 4, y_part, 0)
        b = copies.start(to_x, into.at[:, :, x, :, pl.ds(first + half, half)], here.other_x)
        second[j] = a, b

    def build(n, carry):
        both = tables[n]
        for k, expert in enumerate((ex, by_y, by_x)):
            hot[k, n] = hot_slots(both[experts:], expert, capacity)
        turned = both.T
        lane = lax.broadcasted_iota(jnp.int32, turned.shape, 1)
        wanted = lax.broadcasted_iota(jnp.int32, (turned.shape[0], capacity), 1).astype(f32)
        for k, expert in enumerate((ex, by_y, by_x)):
            slot = jnp.sum(jnp.where(lane == experts + expert, turned, 0.0), axis=1, keepdims=True)
            gate = jnp.sum(jnp.where(lane == expert, turned, 0.0), axis=1, keepdims=True)
            hot_row[k, n] = jnp.where(slot == wanted, 1.0, 0.0).astype(bf16)
            hot_gate[k, n] = jnp.where(slot == wanted, gate, 0.0).astype(bf16)
        row = lax.broadcasted_iota(jnp.int32, (experts, both.shape[1]), 0)
        gates = jnp.sum(jnp.where(row == ex, both[:experts], 0.0), axis=0, keepdims=True)
        gate_col[n] = jnp.sum(hot[0, n].astype(f32) * gates, axis=1, keepdims=True)
        grad_col[n] = jnp.zeros((capacity, 1), f32)
        return carry

    def flat(ref, first, size):
        return ref[:, :, :, :, pl.ds(first, size)].reshape(-1, size)

    def grow(k, columns, value, fresh):
        acc[k, :, columns] = value if fresh else acc[k, :, columns] + value

    def tile(n):
        return pl.ds(pl.multiple_of(n * 256, 256), 256)

    def gate_and_up(p):
        for copy in gu_loads[p]:
            copy.wait()
        def body(n, carry):
            left = flat(rows_in, piece(p), width)
            for k in range(2):
                grow(k, tile(n), nn(left, gu_slots[p % 2, k, :, tile(n)]), p == 0)
            return carry
        lax.fori_loop(0, units // 256, body, 0)
        load_gu(p + 2)

    def activate(n, carry):
        rows = pl.ds(pl.multiple_of(n * 32, 32), 32)
        gate, up = acc[0, rows], acc[1, rows]
        sigma = 1.0 / (1.0 + jnp.exp(-gate))
        silu = gate * sigma
        middle[rows] = (silu * up).astype(bf16)
        to_gate[rows] = (up * sigma * (1.0 + gate * (1.0 - sigma))).astype(bf16)
        to_up[rows] = silu.astype(bf16)
        return carry

    def store(first, value):
        result[:, :, :, :, pl.ds(first, 256)] = value.astype(bf16).reshape(4, 2, 2, capacity, 256)

    def down(p):
        down_loads[p].wait()
        for n in range(width // 256):
            store(piece(p) + n * 256, nn(middle[...], down_slots[p % 2, :, pl.ds(n * 256, 256)]))
        load_down(p + 2)

    def back_down(p):
        n_load = p + PIECES
        columns = pl.ds(piece(p), width)
        def rows(n, carry):
            at = (n // 4, n // 2 % 2, n % 2, slice(None), columns)
            mine = rows_cot[at].astype(f32)
            dots = jnp.sum(mine * result[at].astype(f32), axis=1, keepdims=True)
            grad_col[n] = grad_col[n] + dots
            rows_cot[at] = (gate_col[n] * mine).astype(bf16)
            return carry
        lax.fori_loop(0, 16, rows, 0)
        down_loads[n_load].wait()
        def body(n, carry):
            value = nt(flat(rows_cot, piece(p), width), down_slots[n_load % 2, tile(n)])
            grow(0, tile(n), value, p == 0)
            return carry
        lax.fori_loop(0, units // 256, body, 0)
        load_down(n_load + 2)

    def back_activate(n, carry):
        rows = pl.ds(pl.multiple_of(n * 32, 32), 32)
        grad = acc[0, rows]
        to_gate[rows] = (grad * to_gate[rows].astype(f32)).astype(bf16)
        to_up[rows] = (grad * to_up[rows].astype(f32)).astype(bf16)
        return carry

    def back_rows(p):
        n_load = p + PIECES
        for copy in spread_one[p]:
            copies.sent(copy)
        for copy in gu_loads[n_load]:
            copy.wait()
        for n in range(width // 256):
            rows = pl.ds(n * 256, 256)
            value = nt(to_gate[...], gu_slots[n_load % 2, 0, rows])
            store(piece(p) + n * 256, value + nt(to_up[...], gu_slots[n_load % 2, 1, rows]))
        load_gu(n_load + 2)

    def give_back(n, carry):
        grads = jnp.sum(hot[0, n].astype(f32) * grad_col[n], axis=0, keepdims=True)
        back[n] = jnp.broadcast_to(grads, back.shape[1:])
        return carry

    spread_one, spread_two, spread_three = {}, {}, {}

    def cols(j):
        return pl.ds(piece(j), half), pl.ds(piece(j) + half, half)

    def term(j, which, at, rows):
        return nn((hot_gate if j < PIECES else hot_row)[which, at], rows)

    def send_one(j):
        (from_y, from_x), (a, b) = spread_buffers[j], cols(j)
        spread_one[j] = (
            copies.start(result.at[:, 1 - y, :, :, a], from_y, here.other_y),
            copies.start(result.at[:, :, 1 - x, :, b], from_x, here.other_x),
        )

    def send_two(j):
        (from_y, from_x), (a, b) = spread_buffers[j], cols(j)
        to_x, to_y = send_slots.at[j % 2, 0], send_slots.at[j % 2, 1]
        if j >= 2:
            copies.sent(spread_two[j - 2][0])
            copies.sent(spread_two[j - 2][1])
        if j % PIECES == 0:
            pl.semaphore_wait(ready.at[j // PIECES], 5)
        spread_one[j][0].wait_recv()
        def x_part(n, carry):
            at = block(n, y, 1 - x)
            total = term(j, 0, at, result[n, y, 1 - x, :, a]) + term(j, 1, at, from_y[n, 1 - x])
            to_x[n] = total.astype(bf16)
            return carry
        lax.fori_loop(0, 4, x_part, 0)
        first = copies.start(to_x, pick_buffers[j][1], here.other_x)
        spread_one[j][1].wait_recv()
        def y_part(n, carry):
            at = block(n, 1 - y, x)
            total = term(j, 0, at, result[n, 1 - y, x, :, b]) + term(j, 2, at, from_x[n, 1 - y])
            to_y[n] = total.astype(bf16)
            return carry
        lax.fori_loop(0, 4, y_part, 0)
        spread_two[j] = first, copies.start(to_y, pick_buffers[j][2], here.other_y)

    def send_three(j):
        (from_y, from_x), (a, b) = spread_buffers[j], cols(j)
        from_z, more_a, more_b = pick_buffers[j]
        column = column_slots.at[j % 3]
        if j >= 3:
            for copy in spread_three[j - 3]:
                copies.sent(copy)
        for copy in spread_two[j]:
            copy.wait_recv()
        def body(n, carry):
            at = block(n, y, x)
            total = term(j, 0, at, result[n, y, x, :, a]) + term(j, 1, at, from_y[n, x])
            column[n, :, pl.ds(0, half)] = (total + more_a[n].astype(f32)).astype(bf16)
            total = term(j, 0, at, result[n, y, x, :, b]) + term(j, 2, at, from_x[n, y])
            column[n, :, pl.ds(half, half)] = (total + more_b[n].astype(f32)).astype(bf16)
            return carry
        lax.fori_loop(0, 4, body, 0)
        spread_three[j] = [
            copies.start(column.at[(z + k) % 4], from_z.at[k - 1], here.other_z[k - 1])
            for k in range(1, 4)
        ]

    def send_four(j):
        from_z = pick_buffers[j][0]
        for copy in spread_three[j]:
            copy.wait_recv()
        total = column_slots[j % 3, z].astype(f32) + from_z[0].astype(f32)
        total = total + from_z[1].astype(f32) + from_z[2].astype(f32)
        (mix_out if j < PIECES else grad_out)[:, pl.ds(piece(j), width)] = total

    told = [copies.start(table, tables.at[ex], peer) for peer in here.peers]
    kept_table = keep(table, tables.at[ex])
    held, ones, written, returned = {}, {}, [], []
    for n in range(2):
        load_gu(n)
        load_down(n)
    for step in range(2 * parts + 3):
        if step < parts:
            held[step] = stage_z(step)
        if step == 1:
            kept_table.wait()
            for copy in told:
                copy.wait_recv()
            lax.fori_loop(0, 16, build, 0)
        if 0 <= step - 1 < parts:
            ones[step - 1] = stage_one(step - 1, *held[step - 1])
        if 0 <= step - 2 < parts:
            stage_two(step - 2, ones[step - 2])
        for behind, send in enumerate((send_one, send_two, send_three, send_four)):
            if 0 <= step - parts - behind < parts:
                send(step - parts - behind)
        if 0 <= step - 1 < parts:
            pick_own(step - 1)
        if 0 <= step - 2 < parts:
            pick_moved(step - 2)
            if (step - 2) % PIECES == PIECES - 1:
                for j in range(step - 1 - PIECES, step - 1):
                    copies.sent(ones[j][0])
                    copies.sent(ones[j][1])
                for device in (here.other_x, here.other_y, *here.other_z):
                    pl.semaphore_signal(
                        ready.at[(step - 2) // PIECES], inc=1, device_id=device, device_id_type=MESH
                    )
        p = step - 3
        if 0 <= p < parts:
            second[p][0].wait_recv()
            second[p][1].wait_recv()
        if 0 <= p < PIECES:
            gate_and_up(p)
        if p == PIECES - 1:
            lax.fori_loop(0, acc.shape[1] // 32, activate, 0)
            written.append(keep(rows_in, kept_outs[0]))
            written.append(keep(middle, kept_outs[2]))
            for n in range(PIECES):
                down(n)
        if PIECES <= p < parts:
            back_down(p - PIECES)
        if p == parts - 1:
            lax.fori_loop(0, acc.shape[1] // 32, back_activate, 0)
            written.append(keep(rows_cot, kept_outs[1]))
            written.append(keep(to_gate, kept_outs[3]))
            written.append(keep(to_up, kept_outs[4]))
            lax.fori_loop(0, 16, give_back, 0)
            returned = [copies.start(back.at[peer[1]], given.at[ex], peer) for peer in here.peers]
            written.append(keep(back.at[ex], given.at[ex]))
        if 0 <= step - 3 - parts < PIECES:
            back_rows(step - 3 - parts)
    for copy in returned:
        copy.wait_recv()
    for copy in written:
        copy.wait()
    copies.finish()


def run_experts(moe_in, cot_in, table, gate_full, up_full, down_full, capacity, collective_id):
    rows, model_width = moe_in.shape
    units, parts = gate_full.shape[1], 2 * PIECES
    width = model_width // PIECES
    half, slots = width // 2, 16 * capacity
    vmem, anywhere = pl.BlockSpec(memory_space=pltpu.VMEM), pl.BlockSpec(memory_space=pl.ANY)
    compact = (4, 2, 2, capacity, model_width)
    scratch = [
        pltpu.VMEM((16, *table.shape), f32),
        pltpu.VMEM((3, 16, capacity, rows), bf16),
        pltpu.VMEM((3, 16, rows, capacity), bf16),
        pltpu.VMEM((3, 16, rows, capacity), bf16),
        pltpu.VMEM((16, capacity, 1), f32),
        pltpu.VMEM((16, capacity, 1), f32),
        pltpu.VMEM((16, 8, rows), f32),
        pltpu.VMEM(compact, bf16),
        pltpu.VMEM(compact, bf16),
        pltpu.VMEM((2, slots, units), f32),
        pltpu.VMEM((slots, units), bf16),
        pltpu.VMEM((slots, units), bf16),
        pltpu.VMEM((slots, units), bf16),
        pltpu.VMEM(compact, bf16),
        pltpu.VMEM((2, 2, width, units), bf16),
        pltpu.VMEM((2, units, width), bf16),
        pltpu.VMEM((2, 2, 4, 2, capacity, half), bf16),
        pltpu.VMEM((2, 2, 4, rows, half), bf16),
        pltpu.VMEM((3, 4, rows, width), bf16),
    ]
    for _ in range(parts):
        scratch += [
            pltpu.VMEM((4, rows, width), bf16),
            pltpu.VMEM((4, rows, half), bf16),
            pltpu.VMEM((4, rows, half), bf16),
        ]
    scratch += [pltpu.VMEM((4, 2, capacity, half), bf16)] * (2 * parts)
    copies = 14 * parts + 30
    shape = jax.ShapeDtypeStruct
    grad, mixture, given, rows_in, rows_grad, *units_out = pl.pallas_call(
        functools.partial(expert_kernel, capacity),
        out_shape=[shape((rows, model_width), f32)] * 2
        + [shape((16, 8, rows), f32)]
        + [shape(compact, bf16)] * 2
        + [shape((slots, units), bf16)] * 3,
        in_specs=[vmem] * 3 + [anywhere] * 3,
        out_specs=[vmem] * 3 + [anywhere] * 5,
        scratch_shapes=scratch
        + [
            pltpu.SemaphoreType.DMA((copies,)),
            pltpu.SemaphoreType.DMA((copies,)),
            pltpu.SemaphoreType.DMA((parts + 7,)),
            pltpu.SemaphoreType.DMA((2, 3)),
            pltpu.SemaphoreType.REGULAR((2,)),
        ],
        compiler_params=pltpu.CompilerParams(
            collective_id=collective_id, has_side_effects=True, vmem_limit_bytes=62 * 2**20
        ),
    )(table, moe_in, cot_in, gate_full, up_full, down_full)
    rows_in, rows_grad = rows_in.reshape(slots, -1), rows_grad.reshape(slots, -1)
    return grad, mixture, given[:, 0], rows_in, rows_grad, *units_out


def has_kernels():
    return (lax.axis_size("rep"), lax.axis_size("ex")) == (2, 16)


def exchange(array):
    return lax.all_to_all(array, "ex", split_axis=0, concat_axis=0, tiled=True)


def gather_weights(shards, outbound):
    if has_kernels():
        *full, inbound = gather(shards, [outbound], True, [4] * (len(shards) - 1) + [1], 1)
        return [a.reshape(-1, a.shape[-1]) for a in full], inbound
    full = [lax.all_gather(a, ("rep", "ex"), axis=0, tiled=True) for a in shards]
    return full, exchange(outbound)


def slots_of(tables, capacity):
    experts, me = tables.shape[1] // 2, lax.axis_index("ex")
    gates = lax.dynamic_index_in_dim(tables, me, 1, keepdims=True)
    slots = lax.dynamic_index_in_dim(tables, experts + me, 1, keepdims=True)
    return slots == jnp.arange(capacity, dtype=f32)[None, :, None], gates


def experts_of_group(moe_in, cot_in, table, gate_full, up_full, down_full, capacity):
    if has_kernels():
        return run_experts(moe_in, cot_in, table, gate_full, up_full, down_full, capacity, 2)
    tables = lax.all_gather(table, "ex", axis=0)
    picked, gate_rows = slots_of(tables, capacity)
    picked_low = picked.astype(bf16)
    slot_gate = jnp.sum(jnp.where(picked, gate_rows, 0.0), axis=2).reshape(-1, 1)

    def pick(rows):
        rows = lax.all_gather(rows, "ex", axis=0)
        rows = jnp.einsum("sct,std->scd", picked_low, rows, preferred_element_type=f32)
        return rows.astype(bf16).reshape(-1, rows.shape[-1])

    def spread(rows):
        rows = rows.reshape(*picked_low.shape[:2], -1)
        rows = jnp.einsum("sct,scd->std", picked_low, rows, preferred_element_type=f32)
        return lax.psum_scatter(rows.astype(bf16), "ex", scatter_dimension=0).astype(f32)

    rows_in, rows_cot = pick(moe_in), pick(cot_in)
    gate_pre = jnp.dot(rows_in, gate_full, preferred_element_type=f32)
    up_pre = jnp.dot(rows_in, up_full, preferred_element_type=f32)
    sigma = jax.nn.sigmoid(gate_pre)
    silu = gate_pre * sigma
    middle = (silu * up_pre).astype(bf16)
    expert_out = jnp.dot(middle, down_full, preferred_element_type=f32).astype(bf16)
    slot_grad = jnp.sum(rows_cot.astype(f32) * expert_out.astype(f32), axis=1)
    rows_grad = (slot_gate * rows_cot.astype(f32)).astype(bf16)
    grad_middle = jnp.dot(rows_grad, down_full.T, preferred_element_type=f32)
    grad_gate_low = (grad_middle * up_pre * sigma * (1.0 + gate_pre * (1.0 - sigma))).astype(bf16)
    grad_up_low = (grad_middle * silu).astype(bf16)
    grad_rows = jnp.dot(grad_gate_low, gate_full.T, preferred_element_type=f32)
    grad_rows = grad_rows + jnp.dot(grad_up_low, up_full.T, preferred_element_type=f32)
    weighted = slot_gate * expert_out.astype(f32)
    slot_grad = slot_grad.reshape(*picked.shape[:2], 1)
    back = exchange(jnp.sum(jnp.where(picked, slot_grad, 0.0), axis=1))
    sums = spread(grad_rows.astype(bf16)), spread(weighted.astype(bf16))
    return *sums, back, rows_in, rows_grad, middle, grad_gate_low, grad_up_low


def sum_weights(pairs, small, outbound):
    if has_kernels():
        width = small.shape[1]
        wide = jnp.pad(small, ((0, 0), (0, 128 - width))).reshape(2, 4, 2, 2, 64, 128)
        *sums, summed, given = reduce_weights(pairs, wide, [outbound], 4, 3)
        return sums, summed[:, :width], given
    both = ("rep", "ex")
    sums = []
    for left, right in pairs:
        grad = jnp.dot(left.T, right, preferred_element_type=f32).astype(bf16)
        sums.append(lax.psum_scatter(grad, both, scatter_dimension=0, tiled=True).astype(f32))
    summed = lax.psum_scatter(small, both, scatter_dimension=0, tiled=True)
    return sums, summed, exchange(outbound)


def body(
    tokens,
    out_cot,
    destination,
    doc_lengths,
    routes,
    fill_order,
    query_weight,
    key_weight,
    value_weight,
    output_weight,
    query_gain,
    key_gain,
    attn_gain,
    moe_gain,
    router_weight,
    expert_gate,
    expert_up,
    expert_down,
):
    group_size = lax.axis_size("ex")
    row_count, model_width = tokens.shape
    block_rows = row_count // group_size
    row_index = jnp.arange(row_count, dtype=jnp.int32)
    placed = destination // row_count % group_size * block_rows + destination % block_rows
    to_send = (placed[None, :] == row_index[:, None]).astype(bf16)
    inbound = jnp.dot(
        to_send, jnp.concatenate([tokens, out_cot], axis=1), preferred_element_type=f32
    ).astype(bf16)
    gains = jnp.concatenate(
        [jnp.stack([query_gain, key_gain, attn_gain, moe_gain], axis=1), router_weight], axis=1
    )
    extra = gains.shape[1]
    gains = jnp.pad(gains, ((0, 0), (0, -extra % 128)))
    full, packed = gather_weights(
        [query_weight, key_weight, value_weight, output_weight, gains],
        inbound.reshape(group_size, block_rows, 2 * model_width),
    )
    query_full, key_full, value_full, output_full, gains = full
    packed = packed.reshape(row_count, 2 * model_width)
    hidden_in, cot_in = packed[:, :model_width], packed[:, model_width:]
    query_scale, key_scale, attn_scale, moe_scale = (gains[:, i].astype(f32) for i in range(4))
    router_full = gains[:, 4:extra]
    gate_full = lax.all_gather(expert_gate[0], "rep", axis=0, tiled=True)
    up_full = lax.all_gather(expert_up[0], "rep", axis=0, tiled=True)
    down_full = lax.all_gather(expert_down[0], "rep", axis=0, tiled=True)

    segment, position, live_rows = segment_tables(doc_lengths[0], row_count)
    live_column = live_rows.astype(f32)[:, None]
    hidden = hidden_in.astype(f32)
    normed_attn, scale_attn = normalize(hidden)
    attn_in = (normed_attn * attn_scale).astype(bf16)
    query_pre = jnp.dot(attn_in, query_full, preferred_element_type=f32)
    key_pre = jnp.dot(attn_in, key_full, preferred_element_type=f32)
    value_pre = jnp.dot(attn_in, value_full, preferred_element_type=f32)
    normed_query, scale_query = normalize(query_pre)
    normed_key, scale_key = normalize(key_pre)
    cosine, sine = rope_tables(position)
    query_norm = (normed_query * query_scale).reshape(row_count, HEADS, HEAD_DIM)
    key_norm = (normed_key * key_scale).reshape(row_count, HEADS, HEAD_DIM)
    query_low = (query_norm * cosine + rotate_half(query_norm) * sine).astype(bf16)
    key_low = (key_norm * cosine + rotate_half(key_norm) * sine).astype(bf16)
    value_low = value_pre.astype(bf16).reshape(row_count, HEADS, HEAD_DIM)
    visible = (segment[:, None] == segment[None, :]) & (row_index[None, :] <= row_index[:, None])
    scores = attention_scores(query_low, key_low, visible)
    peak = jnp.max(scores, axis=-1, keepdims=True)
    weights_exp = jnp.exp(scores - peak)
    probs = weights_exp / jnp.sum(weights_exp, axis=-1, keepdims=True)
    probs_low = probs.astype(bf16)
    mixed = jnp.einsum("hqk,khd->qhd", probs_low, value_low, preferred_element_type=f32)
    mixed = mixed.reshape(row_count, model_width).astype(bf16)
    branch = jnp.dot(mixed, output_full, preferred_element_type=f32)
    after_attn = hidden + live_column * branch
    normed_moe, scale_moe = normalize(after_attn)
    moe_in = (normed_moe * moe_scale).astype(bf16)
    logits = jnp.dot(moe_in, router_full, preferred_element_type=f32)
    router_probs = jax.nn.softmax(logits, axis=-1)
    experts = router_full.shape[1]
    capacity = row_count * routes.shape[1] // experts
    slot_table, kept = slot_tables(routes, fill_order[0], live_rows, experts, capacity)
    gates = jnp.where(kept, router_probs, 0.0)

    table = jnp.concatenate([gates.T, slot_table.T.astype(f32)], axis=0)
    (
        grad_moe_in,
        mixture,
        grad_rprobs,
        rows_in,
        rows_grad,
        middle,
        grad_gate_low,
        grad_up_low,
    ) = experts_of_group(moe_in, cot_in, table, gate_full, up_full, down_full, capacity)
    grad_down_full = jnp.dot(middle.T, rows_grad, preferred_element_type=f32)
    grad_gate_full = jnp.dot(rows_in.T, grad_gate_low, preferred_element_type=f32)
    grad_up_full = jnp.dot(rows_in.T, grad_up_low, preferred_element_type=f32)
    grad_rprobs = grad_rprobs.T
    output = (after_attn + mixture).astype(bf16)
    owned_gate, owned_up, owned_down = (
        lax.psum_scatter(g.astype(bf16), "rep", scatter_dimension=0, tiled=True).astype(f32)[None]
        for g in (grad_gate_full, grad_up_full, grad_down_full)
    )

    grad_out = cot_in.astype(f32)
    grad_logits = router_probs * (
        grad_rprobs - jnp.sum(router_probs * grad_rprobs, axis=-1, keepdims=True)
    )
    grad_moe_in = grad_moe_in + jnp.dot(
        grad_logits, router_full.T, precision=lax.Precision.HIGHEST, preferred_element_type=f32
    )
    grad_router = jnp.dot(
        moe_in.T, grad_logits, precision=lax.Precision.HIGHEST, preferred_element_type=f32
    )
    grad_moe_scale = jnp.sum(grad_moe_in * normed_moe, axis=0)
    grad_after = grad_out + norm_back(grad_moe_in * moe_scale, normed_moe, scale_moe)
    grad_branch = (live_column * grad_after).astype(bf16)
    grad_mixed = (
        jnp.dot(grad_branch, output_full.T, preferred_element_type=f32)
        .astype(bf16)
        .reshape(row_count, HEADS, HEAD_DIM)
    )
    grad_value = jnp.einsum("hqk,qhd->khd", probs_low, grad_mixed, preferred_element_type=f32)
    grad_att = jnp.einsum("qhd,khd->hqk", grad_mixed, value_low, preferred_element_type=f32)
    grad_scores = (probs * (grad_att - jnp.sum(probs * grad_att, axis=-1, keepdims=True))).astype(
        bf16
    )
    grad_query_rot = jnp.einsum(
        "hqk,khd->qhd", grad_scores, key_low, preferred_element_type=f32
    ) * HEAD_DIM ** (-0.5)
    grad_key_rot = jnp.einsum(
        "hqk,qhd->khd", grad_scores, query_low, preferred_element_type=f32
    ) * HEAD_DIM ** (-0.5)
    grad_query_normed = (grad_query_rot * cosine + rotate_back(grad_query_rot * sine)).reshape(
        row_count, model_width
    )
    grad_key_normed = (grad_key_rot * cosine + rotate_back(grad_key_rot * sine)).reshape(
        row_count, model_width
    )
    grad_query_scale = jnp.sum(grad_query_normed * normed_query, axis=0)
    grad_key_scale = jnp.sum(grad_key_normed * normed_key, axis=0)
    grad_query_pre = norm_back(grad_query_normed * query_scale, normed_query, scale_query)
    grad_key_pre = norm_back(grad_key_normed * key_scale, normed_key, scale_key)
    grad_query_pre = grad_query_pre.astype(bf16)
    grad_key_pre = grad_key_pre.astype(bf16)
    grad_value_pre = grad_value.reshape(row_count, model_width).astype(bf16)
    grad_attn_in = jnp.dot(grad_query_pre, query_full.T, preferred_element_type=f32)
    grad_attn_in = grad_attn_in + jnp.dot(grad_key_pre, key_full.T, preferred_element_type=f32)
    grad_attn_in = grad_attn_in + jnp.dot(grad_value_pre, value_full.T, preferred_element_type=f32)
    grad_attn_scale = jnp.sum(grad_attn_in * normed_attn, axis=0)
    grad_hidden = grad_after + norm_back(grad_attn_in * attn_scale, normed_attn, scale_attn)

    small = jnp.concatenate(
        [
            jnp.stack([grad_query_scale, grad_key_scale, grad_attn_scale, grad_moe_scale], axis=1),
            grad_router,
        ],
        axis=1,
    )
    outbound = jnp.concatenate([output, grad_hidden.astype(bf16)], axis=1)
    pairs = [
        (attn_in, grad_query_pre),
        (attn_in, grad_key_pre),
        (attn_in, grad_value_pre),
        (mixed, grad_branch),
    ]
    sums, small, outbound = sum_weights(
        pairs, small, outbound.reshape(group_size, block_rows, 2 * model_width)
    )
    owned_query, owned_key, owned_value, owned_output = sums
    outbound = outbound.reshape(row_count, 2 * model_width)
    outbound = jnp.dot(to_send.T, outbound, preferred_element_type=f32).astype(bf16)
    return (
        outbound[:, :model_width],
        outbound[:, model_width:],
        owned_query,
        owned_key,
        owned_value,
        owned_output,
        small[:, 0],
        small[:, 1],
        small[:, 2],
        small[:, 3],
        small[:, 4:],
        owned_gate,
        owned_up,
        owned_down,
    )


def solution(mesh):
    rows, row = P(("rep", "ex"), None), P(("rep", "ex"))
    expert = P("ex", "rep", None)
    return jax.shard_map(
        body,
        mesh=mesh,
        in_specs=(rows, rows, row) + (rows,) * 7 + (row,) * 4 + (rows,) + (expert,) * 3,
        out_specs=(rows,) * 6 + (row,) * 4 + (rows,) + (expert,) * 3,
        check_vma=False,
    )
```

```python
import functools

import jax
import jax.numpy as jnp
from jax import lax
from jax.experimental import pallas as pl
from jax.experimental.pallas import tpu as pltpu
from jax.sharding import PartitionSpec as P

HEADS = 16
HEAD_DIM = 128

epsilon = 1e-05
rope_base = 10000.0
masked_score = -1e30
bf16 = jnp.bfloat16
f32 = jnp.float32


def normalize(values):
    scale = lax.rsqrt(jnp.mean(values * values, axis=-1, keepdims=True) + epsilon)
    return (values * scale, scale)


def norm_back(grad_normed, normed, scale):
    return scale * (grad_normed - normed * jnp.mean(grad_normed * normed, axis=-1, keepdims=True))


def rotate_half(values):
    middle = values.shape[-1] // 2
    return jnp.concatenate([-values[..., middle:], values[..., :middle]], axis=-1)


def rotate_back(values):
    middle = values.shape[-1] // 2
    return jnp.concatenate([values[..., middle:], -values[..., :middle]], axis=-1)


def rope_tables(position):
    steps = jnp.arange(HEAD_DIM // 2, dtype=f32) * (2.0 / HEAD_DIM)
    inverse = rope_base ** (-steps)
    angle = position.astype(f32)[:, None] * inverse[None, :]
    cosine = jnp.concatenate([jnp.cos(angle), jnp.cos(angle)], axis=-1)[:, None, :]
    sine = jnp.concatenate([jnp.sin(angle), jnp.sin(angle)], axis=-1)[:, None, :]
    return (cosine, sine)


def segment_tables(lengths, row_count):
    count = lengths.shape[0]
    numbers = jnp.arange(count, dtype=jnp.int32)
    before = (numbers[None, :] < numbers[:, None]).astype(jnp.int32)
    starts = jnp.sum(before * lengths[None, :], axis=1)
    ends = starts + lengths
    row_index = jnp.arange(row_count, dtype=jnp.int32)
    segment = jnp.sum((row_index[:, None] >= ends[None, :]).astype(jnp.int32), axis=1)
    begin = jnp.sum(jnp.where(segment[:, None] == numbers[None, :], starts[None, :], 0), axis=1)
    return (segment, row_index - begin, segment < count - 1)


def slot_tables(routes, filling, live_rows, experts, capacity):
    row_count, top_count = routes.shape
    order = jnp.arange(row_count * top_count, dtype=jnp.int32)
    rows = jnp.arange(row_count, dtype=jnp.int32)
    hot_row = (filling[None, :] // top_count == rows[:, None]).astype(bf16)
    hot_choice = (filling % top_count)[:, None] == jnp.arange(top_count, dtype=jnp.int32)[None, :]
    high = jnp.where(hot_choice, (order // 64)[:, None], 0).astype(bf16)
    lower = jnp.where(hot_choice, (order % 64)[:, None], 0).astype(bf16)
    ranks = jnp.dot(
        hot_row, jnp.concatenate([high, lower], axis=1), preferred_element_type=f32
    ).astype(jnp.int32)
    rank = ranks[:, :top_count] * 64 + ranks[:, top_count:]
    chosen = routes[:, :, None] == jnp.arange(experts, dtype=jnp.int32)[None, None, :]
    rank_table = jnp.sum(jnp.where(chosen, rank[:, :, None], 0), axis=1)
    counted = jnp.any(chosen, axis=1) & live_rows[:, None]
    earlier = counted[:, None, :] & (rank_table[:, None, :] < rank_table[None, :, :])
    slot = jnp.sum(earlier.astype(jnp.int32), axis=0)
    kept = counted & (slot < capacity)
    return (jnp.where(kept, slot, -1), kept)


def attention_scores(query_low, key_low, visible):
    scores = jnp.einsum(
        "qhd,khd->hqk", query_low, key_low, preferred_element_type=f32
    ) * HEAD_DIM ** (-0.5)
    return jnp.where(visible[None], scores, masked_score)


MESH = pl.DeviceIdType.MESH


class Place:
    def __init__(self):
        self.rep, self.ex = lax.axis_index("rep"), lax.axis_index("ex")
        self.x, self.y, self.z = self.ex % 2, self.ex // 2 % 2, self.ex // 4
        self.other_x = (self.rep, self.ex + 1 - 2 * self.x)
        self.other_y = (self.rep, self.ex + 2 - 4 * self.y)
        self.other_core = (1 - self.rep, self.ex)
        self.other_z = [(self.rep, (self.ex + 4 * k) % 16) for k in range(1, 4)]
        self.peers = [(self.rep, (self.ex + k) % 16) for k in range(1, 16)]


def enter(devices):
    barrier = pltpu.get_barrier_semaphore()
    for device in devices:
        pl.semaphore_signal(barrier, inc=1, device_id=device, device_id_type=MESH)
    pl.semaphore_wait(barrier, len(devices))


class Copies:
    def __init__(self, send_sems, recv_sems):
        self.send_sems, self.recv_sems, self.made = send_sems, recv_sems, []
        self.done = set()

    def start(self, source, target, device):
        at = len(self.made)
        copy = pltpu.make_async_remote_copy(
            src_ref=source,
            dst_ref=target,
            send_sem=self.send_sems.at[at],
            recv_sem=self.recv_sems.at[at],
            device_id=device,
            device_id_type=MESH,
        )
        copy.start()
        self.made.append(copy)
        return copy

    def sent(self, copy):
        if id(copy) not in self.done:
            self.done.add(id(copy))
            copy.wait_send()

    def finish(self):
        for copy in self.made:
            self.sent(copy)


def gather_kernel(pieces, with_core, shards, spread_in, *refs):
    count, moved = len(shards), len(spread_in)
    ins, refs = refs[:count], refs[count:]
    from_all, refs = refs[:moved], refs[moved:]
    outs, refs = refs[:count], refs[count:]
    to_all, refs = refs[:moved], refs[moved:]
    send_sems, recv_sems, local_sems = refs
    here = Place()
    rep, x, y, z = here.rep, here.x, here.y, here.z
    enter(here.peers + ([here.other_core] if with_core else []))
    copies = Copies(send_sems, recv_sems)
    local, exchanged = [], []

    def keep(source, target):
        copy = pltpu.make_async_copy(source, target, local_sems.at[len(local)])
        copy.start()
        local.append(copy)
        return copy

    for source, target in zip(from_all, to_all):
        keep(source.at[here.ex], target.at[here.ex])
        for peer in here.peers:
            exchanged.append(copies.start(source.at[peer[1]], target.at[here.ex], peer))

    parts = []
    for i in range(count):
        rows = shards[i][0] // pieces[i]
        parts += [(i, k * rows, rows) for k in range(pieces[i])]

    def stage_z(part):
        i, first, rows = part
        source, full = ins[i].at[pl.ds(first, rows)], outs[i].at[rep]
        target = full.at[z, y, x, pl.ds(first, rows)]
        waits = [copies.start(source, target, device) for device in here.other_z]
        return waits, keep(source, target)

    def stage_one(part, waits, kept):
        i, first, rows = part
        full, half = outs[i].at[rep], rows // 2
        kept.wait()
        for copy in waits:
            copy.wait_recv()
        upper, lower = pl.ds(first, half), pl.ds(first + half, half)
        a = full.at[:, y, x, upper]
        b = full.at[:, y, x, lower]
        one = copies.start(a, a, here.other_x), copies.start(b, b, here.other_y)
        own = full.at[:, y, x, pl.ds(first, rows)]
        cores = [copies.start(own, own, here.other_core)] if with_core else []
        return one, cores

    def stage_two(part, one, cores):
        i, first, rows = part
        full, half = outs[i].at[rep], rows // 2
        upper, lower = pl.ds(first, half), pl.ds(first + half, half)
        one[0].wait_recv()
        a = full.at[:, y, :, upper]
        two_a = copies.start(a, a, here.other_y)
        one[1].wait_recv()
        b = full.at[:, :, x, lower]
        two_b = copies.start(b, b, here.other_x)
        if with_core:
            a, b = full.at[:, y, 1 - x, upper], full.at[:, 1 - y, x, lower]
            cores += [copies.start(a, a, here.other_core), copies.start(b, b, here.other_core)]
        return (two_a, two_b), cores

    def stage_three(part, two, cores):
        i, first, rows = part
        full, half = outs[i].at[rep], rows // 2
        upper, lower = pl.ds(first, half), pl.ds(first + half, half)
        two[0].wait_recv()
        a = full.at[:, 1 - y, :, upper]
        if with_core:
            cores += [copies.start(a, a, here.other_core)]
        two[1].wait_recv()
        b = full.at[:, :, 1 - x, lower]
        if with_core:
            cores += [copies.start(b, b, here.other_core)]
        return cores

    held, arrivals, count = {}, [], len(parts)
    for step in range(count + 3):
        if step < count:
            held[step] = stage_z(parts[step])
        if 0 <= step - 1 < count:
            held[step - 1] = stage_one(parts[step - 1], *held[step - 1])
        if 0 <= step - 2 < count:
            held[step - 2] = stage_two(parts[step - 2], *held[step - 2])
        if 0 <= step - 3 < count:
            arrivals += stage_three(parts[step - 3], *held[step - 3])
    for copy in arrivals + exchanged:
        copy.wait_recv()
    copies.finish()
    for copy in local[:len(from_all)]:
        copy.wait()


def gather(shards, spread_in, with_core, pieces, collective_id):
    copies = sum(pieces) * (12 if with_core else 7) + 15 * len(spread_in)
    local = sum(pieces) + len(spread_in)
    out_shape = [jax.ShapeDtypeStruct((2, 4, 2, 2) + a.shape, a.dtype) for a in shards]
    out_shape += [jax.ShapeDtypeStruct(a.shape, a.dtype) for a in spread_in]
    anywhere = pl.BlockSpec(memory_space=pl.ANY)
    shapes = [a.shape for a in shards]
    return pl.pallas_call(
        functools.partial(gather_kernel, pieces, with_core, shapes, [a.shape for a in spread_in]),
        out_shape=out_shape,
        in_specs=[anywhere] * (len(shards) + len(spread_in)),
        out_specs=[anywhere] * len(out_shape),
        scratch_shapes=[
            pltpu.SemaphoreType.DMA((copies,)),
            pltpu.SemaphoreType.DMA((copies,)),
            pltpu.SemaphoreType.DMA((local,)),
        ],
        compiler_params=pltpu.CompilerParams(collective_id=collective_id, has_side_effects=True),
    )(*shards, *spread_in)


def nt(left, right):
    return lax.dot_general(left, right, (((1,), (1,)), ((), ())), preferred_element_type=f32)


def nn(left, right):
    return jnp.dot(left, right, preferred_element_type=f32)


def hot_slots(table, expert, capacity):
    experts, rows = table.shape
    lane = lax.broadcasted_iota(jnp.int32, (capacity, experts), 1)
    mine = jnp.where(lane == expert, 1.0, 0.0).astype(bf16)
    slot = nn(mine, table.astype(bf16))
    wanted = lax.broadcasted_iota(jnp.int32, (capacity, rows), 0).astype(f32)
    return jnp.where(slot == wanted, 1.0, 0.0).astype(bf16)


PIECES = 4


def expert_kernel(capacity, *refs):
    table, moe, cot, gate_w, up_w, down_w = refs[:6]
    grad_out, mix_out, given, *kept_outs = refs[6:14]
    refs = refs[14:]
    tables, hot, hot_row, hot_gate, gate_col, grad_col, back = refs[:7]
    rows_in, rows_cot, acc, to_gate, to_up, middle, result = refs[7:14]
    gu_slots, down_slots, to_slots, send_slots, column_slots = refs[14:19]
    parts = 2 * PIECES
    pick_buffers = [refs[19 + 3 * j : 22 + 3 * j] for j in range(parts)]
    refs = refs[19 + 3 * parts :]
    spread_buffers = [refs[2 * j : 2 * j + 2] for j in range(parts)]
    send_sems, recv_sems, local_sems, load_sems, ready = refs[2 * parts :]
    here = Place()
    x, y, z, ex = here.x, here.y, here.z, here.ex
    by_y, by_x = here.other_y[1], here.other_x[1]
    experts = table.shape[0] // 2
    units = gate_w.shape[1]
    width = moe.shape[1] // PIECES
    half = width // 2
    enter(here.peers)
    copies = Copies(send_sems, recv_sems)
    local = []

    def keep(source, target):
        copy = pltpu.make_async_copy(source, target, local_sems.at[len(local)])
        copy.start()
        local.append(copy)
        return copy

    def block(zz, yy, xx):
        return (zz * 2 + yy) * 2 + xx

    def piece(j):
        return j % PIECES * width

    gu_loads, down_loads = {}, {}

    def load_gu(n):
        if n < parts:
            rows = pl.ds(piece(n), width)
            gu_loads[n] = [
                pltpu.make_async_copy(w.at[rows], gu_slots.at[n % 2, k], load_sems.at[n % 2, k])
                for k, w in enumerate((gate_w, up_w))
            ]
            for copy in gu_loads[n]:
                copy.start()

    def load_down(n):
        if n < parts:
            columns = pl.ds(piece(n), width)
            down_loads[n] = pltpu.make_async_copy(
                down_w.at[:, columns], down_slots.at[n % 2], load_sems.at[n % 2, 2]
            )
            down_loads[n].start()

    def stage_z(j):
        source = (moe if j < PIECES else cot).at[:, pl.ds(piece(j), width)]
        target = pick_buffers[j][0].at[z]
        return [copies.start(source, target, peer) for peer in here.other_z], keep(source, target)

    def stage_one(j, sent, kept):
        column, from_x, from_y = pick_buffers[j]
        kept.wait()
        for copy in sent:
            copy.wait_recv()
        return (
            copies.start(column.at[:, :, pl.ds(0, half)], from_x, here.other_x),
            copies.start(column.at[:, :, pl.ds(half, half)], from_y, here.other_y),
        )

    def landing(j):
        return rows_in if j < PIECES else rows_cot

    def pick_own(j):
        column, into = pick_buffers[j][0], landing(j)
        def body(n, carry):
            picked = nn(hot[0, block(n, y, x)], column[n])
            into[n, y, x, :, pl.ds(piece(j), width)] = picked.astype(bf16)
            return carry
        lax.fori_loop(0, 4, body, 0)

    def pick_moved(j):
        (_, from_x, from_y), into, first = pick_buffers[j], landing(j), piece(j)
        def body(n, carry):
            picked = nn(hot[0, block(n, y, 1 - x)], from_x[n])
            into[n, y, 1 - x, :, pl.ds(first, half)] = picked.astype(bf16)
            picked = nn(hot[0, block(n, 1 - y, x)], from_y[n])
            into[n, 1 - y, x, :, pl.ds(first + half, half)] = picked.astype(bf16)
            return carry
        lax.fori_loop(0, 4, body, 0)

    second = {}

    def stage_two(j, one):
        (column, from_x, from_y), into, first = pick_buffers[j], landing(j), piece(j)
        to_y, to_x = to_slots.at[j % 2, 0], to_slots.at[j % 2, 1]
        if j >= 2:
            copies.sent(second[j - 2][0])
            copies.sent(second[j - 2][1])
        def own_part(n, carry):
            at = block(n, y, x)
            to_y[n, x] = nn(hot[1, at], column[n, :, pl.ds(0, half)]).astype(bf16)
            to_x[n, y] = nn(hot[2, at], column[n, :, pl.ds(half, half)]).astype(bf16)
            return carry
        lax.fori_loop(0, 4, own_part, 0)
        one[0].wait_recv()
        def x_part(n, carry):
            to_y[n, 1 - x] = nn(hot[1, block(n, y, 1 - x)], from_x[n]).astype(bf16)
            return carry
        lax.fori_loop(0, 4, x_part, 0)
        a = copies.start(to_y, into.at[:, y, :, :, pl.ds(first, half)], here.other_y)
        one[1].wait_recv()
        def y_part(n, carry):
            to_x[n, 1 - y] = nn(hot[2, block(n, 1 - y, x)], from_y[n]).astype(bf16)
            return carry
        lax.fori_loop(0, 4, y_part, 0)
        b = copies.start(to_x, into.at[:, :, x, :, pl.ds(first + half, half)], here.other_x)
        second[j] = a, b

    def build(n, carry):
        both = tables[n]
        for k, expert in enumerate((ex, by_y, by_x)):
            hot[k, n] = hot_slots(both[experts:], expert, capacity)
        turned = both.T
        lane = lax.broadcasted_iota(jnp.int32, turned.shape, 1)
        wanted = lax.broadcasted_iota(jnp.int32, (turned.shape[0], capacity), 1).astype(f32)
        for k, expert in enumerate((ex, by_y, by_x)):
            slot = jnp.sum(jnp.where(lane == experts + expert, turned, 0.0), axis=1, keepdims=True)
            gate = jnp.sum(jnp.where(lane == expert, turned, 0.0), axis=1, keepdims=True)
            hot_row[k, n] = jnp.where(slot == wanted, 1.0, 0.0).astype(bf16)
            hot_gate[k, n] = jnp.where(slot == wanted, gate, 0.0).astype(bf16)
        row = lax.broadcasted_iota(jnp.int32, (experts, both.shape[1]), 0)
        gates = jnp.sum(jnp.where(row == ex, both[:experts], 0.0), axis=0, keepdims=True)
        gate_col[n] = jnp.sum(hot[0, n].astype(f32) * gates, axis=1, keepdims=True)
        grad_col[n] = jnp.zeros((capacity, 1), f32)
        return carry

    def flat(ref, first, size):
        return ref[:, :, :, :, pl.ds(first, size)].reshape(-1, size)

    def grow(k, columns, value, fresh):
        acc[k, :, columns] = value if fresh else acc[k, :, columns] + value

    def tile(n):
        return pl.ds(pl.multiple_of(n * 256, 256), 256)

    def gate_and_up(p):
        for copy in gu_loads[p]:
            copy.wait()
        def body(n, carry):
            left = flat(rows_in, piece(p), width)
            for k in range(2):
                grow(k, tile(n), nn(left, gu_slots[p % 2, k, :, tile(n)]), p == 0)
            return carry
        lax.fori_loop(0, units // 256, body, 0)
        load_gu(p + 2)

    def activate(n, carry):
        rows = pl.ds(pl.multiple_of(n * 32, 32), 32)
        gate, up = acc[0, rows], acc[1, rows]
        sigma = 1.0 / (1.0 + jnp.exp(-gate))
        silu = gate * sigma
        middle[rows] = (silu * up).astype(bf16)
        to_gate[rows] = (up * sigma * (1.0 + gate * (1.0 - sigma))).astype(bf16)
        to_up[rows] = silu.astype(bf16)
        return carry

    def store(first, value):
        result[:, :, :, :, pl.ds(first, 256)] = value.astype(bf16).reshape(4, 2, 2, capacity, 256)

    def down(p):
        down_loads[p].wait()
        for n in range(width // 256):
            store(piece(p) + n * 256, nn(middle[...], down_slots[p % 2, :, pl.ds(n * 256, 256)]))
        load_down(p + 2)

    def back_down(p):
        n_load = p + PIECES
        columns = pl.ds(piece(p), width)
        def rows(n, carry):
            at = (n // 4, n // 2 % 2, n % 2, slice(None), columns)
            mine = rows_cot[at].astype(f32)
            dots = jnp.sum(mine * result[at].astype(f32), axis=1, keepdims=True)
            grad_col[n] = grad_col[n] + dots
            rows_cot[at] = (gate_col[n] * mine).astype(bf16)
            return carry
        lax.fori_loop(0, 16, rows, 0)
        down_loads[n_load].wait()
        def body(n, carry):
            value = nt(flat(rows_cot, piece(p), width), down_slots[n_load % 2, tile(n)])
            grow(0, tile(n), value, p == 0)
            return carry
        lax.fori_loop(0, units // 256, body, 0)
        load_down(n_load + 2)

    def back_activate(n, carry):
        rows = pl.ds(pl.multiple_of(n * 32, 32), 32)
        grad = acc[0, rows]
        to_gate[rows] = (grad * to_gate[rows].astype(f32)).astype(bf16)
        to_up[rows] = (grad * to_up[rows].astype(f32)).astype(bf16)
        return carry

    def back_rows(p):
        n_load = p + PIECES
        for copy in spread_one[p]:
            copies.sent(copy)
        for copy in gu_loads[n_load]:
            copy.wait()
        for n in range(width // 256):
            rows = pl.ds(n * 256, 256)
            value = nt(to_gate[...], gu_slots[n_load % 2, 0, rows])
            store(piece(p) + n * 256, value + nt(to_up[...], gu_slots[n_load % 2, 1, rows]))
        load_gu(n_load + 2)

    def give_back(n, carry):
        grads = jnp.sum(hot[0, n].astype(f32) * grad_col[n], axis=0, keepdims=True)
        back[n] = jnp.broadcast_to(grads, back.shape[1:])
        return carry

    spread_one, spread_two, spread_three = {}, {}, {}

    def cols(j):
        return pl.ds(piece(j), half), pl.ds(piece(j) + half, half)

    def term(j, which, at, rows):
        return nn((hot_gate if j < PIECES else hot_row)[which, at], rows)

    def send_one(j):
        (from_y, from_x), (a, b) = spread_buffers[j], cols(j)
        spread_one[j] = (
            copies.start(result.at[:, 1 - y, :, :, a], from_y, here.other_y),
            copies.start(result.at[:, :, 1 - x, :, b], from_x, here.other_x),
        )

    def send_two(j):
        (from_y, from_x), (a, b) = spread_buffers[j], cols(j)
        to_x, to_y = send_slots.at[j % 2, 0], send_slots.at[j % 2, 1]
        if j >= 2:
            copies.sent(spread_two[j - 2][0])
            copies.sent(spread_two[j - 2][1])
        if j % PIECES == 0:
            pl.semaphore_wait(ready.at[j // PIECES], 5)
        spread_one[j][0].wait_recv()
        def x_part(n, carry):
            at = block(n, y, 1 - x)
            total = term(j, 0, at, result[n, y, 1 - x, :, a]) + term(j, 1, at, from_y[n, 1 - x])
            to_x[n] = total.astype(bf16)
            return carry
        lax.fori_loop(0, 4, x_part, 0)
        first = copies.start(to_x, pick_buffers[j][1], here.other_x)
        spread_one[j][1].wait_recv()
        def y_part(n, carry):
            at = block(n, 1 - y, x)
            total = term(j, 0, at, result[n, 1 - y, x, :, b]) + term(j, 2, at, from_x[n, 1 - y])
            to_y[n] = total.astype(bf16)
            return carry
        lax.fori_loop(0, 4, y_part, 0)
        spread_two[j] = first, copies.start(to_y, pick_buffers[j][2], here.other_y)

    def send_three(j):
        (from_y, from_x), (a, b) = spread_buffers[j], cols(j)
        from_z, more_a, more_b = pick_buffers[j]
        column = column_slots.at[j % 3]
        if j >= 3:
            for copy in spread_three[j - 3]:
                copies.sent(copy)
        for copy in spread_two[j]:
            copy.wait_recv()
        def body(n, carry):
            at = block(n, y, x)
            total = term(j, 0, at, result[n, y, x, :, a]) + term(j, 1, at, from_y[n, x])
            column[n, :, pl.ds(0, half)] = (total + more_a[n].astype(f32)).astype(bf16)
            total = term(j, 0, at, result[n, y, x, :, b]) + term(j, 2, at, from_x[n, y])
            column[n, :, pl.ds(half, half)] = (total + more_b[n].astype(f32)).astype(bf16)
            return carry
        lax.fori_loop(0, 4, body, 0)
        spread_three[j] = [
            copies.start(column.at[(z + k) % 4], from_z.at[k - 1], here.other_z[k - 1])
            for k in range(1, 4)
        ]

    def send_four(j):
        from_z = pick_buffers[j][0]
        for copy in spread_three[j]:
            copy.wait_recv()
        total = column_slots[j % 3, z].astype(f32) + from_z[0].astype(f32)
        total = total + from_z[1].astype(f32) + from_z[2].astype(f32)
        (mix_out if j < PIECES else grad_out)[:, pl.ds(piece(j), width)] = total

    told = [copies.start(table, tables.at[ex], peer) for peer in here.peers]
    kept_table = keep(table, tables.at[ex])
    held, ones, written, returned = {}, {}, [], []
    for n in range(2):
        load_gu(n)
        load_down(n)
    for step in range(2 * parts + 3):
        if step < parts:
            held[step] = stage_z(step)
        if step == 1:
            kept_table.wait()
            for copy in told:
                copy.wait_recv()
            lax.fori_loop(0, 16, build, 0)
        if 0 <= step - 1 < parts:
            ones[step - 1] = stage_one(step - 1, *held[step - 1])
        if 0 <= step - 2 < parts:
            stage_two(step - 2, ones[step - 2])
        for behind, send in enumerate((send_one, send_two, send_three, send_four)):
            if 0 <= step - parts - behind < parts:
                send(step - parts - behind)
        if 0 <= step - 1 < parts:
            pick_own(step - 1)
        if 0 <= step - 2 < parts:
            pick_moved(step - 2)
            if (step - 2) % PIECES == PIECES - 1:
                for j in range(step - 1 - PIECES, step - 1):
                    copies.sent(ones[j][0])
                    copies.sent(ones[j][1])
                for device in (here.other_x, here.other_y, *here.other_z):
                    pl.semaphore_signal(
                        ready.at[(step - 2) // PIECES], inc=1, device_id=device, device_id_type=MESH
                    )
        p = step - 3
        if 0 <= p < parts:
            second[p][0].wait_recv()
            second[p][1].wait_recv()
        if 0 <= p < PIECES:
            gate_and_up(p)
        if p == PIECES - 1:
            lax.fori_loop(0, acc.shape[1] // 32, activate, 0)
            written.append(keep(rows_in, kept_outs[0]))
            written.append(keep(middle, kept_outs[2]))
            for n in range(PIECES):
                down(n)
        if PIECES <= p < parts:
            back_down(p - PIECES)
        if p == parts - 1:
            lax.fori_loop(0, acc.shape[1] // 32, back_activate, 0)
            written.append(keep(rows_cot, kept_outs[1]))
            written.append(keep(to_gate, kept_outs[3]))
            written.append(keep(to_up, kept_outs[4]))
            lax.fori_loop(0, 16, give_back, 0)
            returned = [copies.start(back.at[peer[1]], given.at[ex], peer) for peer in here.peers]
            written.append(keep(back.at[ex], given.at[ex]))
        if 0 <= step - 3 - parts < PIECES:
            back_rows(step - 3 - parts)
    for copy in returned:
        copy.wait_recv()
    for copy in written:
        copy.wait()
    copies.finish()


def run_experts(moe_in, cot_in, table, gate_full, up_full, down_full, capacity, collective_id):
    rows, model_width = moe_in.shape
    units, parts = gate_full.shape[1], 2 * PIECES
    width = model_width // PIECES
    half, slots = width // 2, 16 * capacity
    vmem, anywhere = pl.BlockSpec(memory_space=pltpu.VMEM), pl.BlockSpec(memory_space=pl.ANY)
    compact = (4, 2, 2, capacity, model_width)
    scratch = [
        pltpu.VMEM((16, *table.shape), f32),
        pltpu.VMEM((3, 16, capacity, rows), bf16),
        pltpu.VMEM((3, 16, rows, capacity), bf16),
        pltpu.VMEM((3, 16, rows, capacity), bf16),
        pltpu.VMEM((16, capacity, 1), f32),
        pltpu.VMEM((16, capacity, 1), f32),
        pltpu.VMEM((16, 8, rows), f32),
        pltpu.VMEM(compact, bf16),
        pltpu.VMEM(compact, bf16),
        pltpu.VMEM((2, slots, units), f32),
        pltpu.VMEM((slots, units), bf16),
        pltpu.VMEM((slots, units), bf16),
        pltpu.VMEM((slots, units), bf16),
        pltpu.VMEM(compact, bf16),
        pltpu.VMEM((2, 2, width, units), bf16),
        pltpu.VMEM((2, units, width), bf16),
        pltpu.VMEM((2, 2, 4, 2, capacity, half), bf16),
        pltpu.VMEM((2, 2, 4, rows, half), bf16),
        pltpu.VMEM((3, 4, rows, width), bf16),
    ]
    for _ in range(parts):
        scratch += [
            pltpu.VMEM((4, rows, width), bf16),
            pltpu.VMEM((4, rows, half), bf16),
            pltpu.VMEM((4, rows, half), bf16),
        ]
    scratch += [pltpu.VMEM((4, 2, capacity, half), bf16)] * (2 * parts)
    copies = 14 * parts + 30
    shape = jax.ShapeDtypeStruct
    grad, mixture, given, rows_in, rows_grad, *units_out = pl.pallas_call(
        functools.partial(expert_kernel, capacity),
        out_shape=[shape((rows, model_width), f32)] * 2
        + [shape((16, 8, rows), f32)]
        + [shape(compact, bf16)] * 2
        + [shape((slots, units), bf16)] * 3,
        in_specs=[vmem] * 3 + [anywhere] * 3,
        out_specs=[vmem] * 3 + [anywhere] * 5,
        scratch_shapes=scratch
        + [
            pltpu.SemaphoreType.DMA((copies,)),
            pltpu.SemaphoreType.DMA((copies,)),
            pltpu.SemaphoreType.DMA((parts + 7,)),
            pltpu.SemaphoreType.DMA((2, 3)),
            pltpu.SemaphoreType.REGULAR((2,)),
        ],
        compiler_params=pltpu.CompilerParams(
            collective_id=collective_id, has_side_effects=True, vmem_limit_bytes=62 * 2**20
        ),
    )(table, moe_in, cot_in, gate_full, up_full, down_full)
    rows_in, rows_grad = rows_in.reshape(slots, -1), rows_grad.reshape(slots, -1)
    return grad, mixture, given[:, 0], rows_in, rows_grad, *units_out


def tn(left, right):
    return lax.dot_general(left, right, (((0,), (0,)), ((), ())), preferred_element_type=f32)


def accumulate(target, blocks, arrived):
    def add(n, carry):
        for into, source in blocks:
            value = target[(n,) + into].astype(f32) + arrived[(n,) + source].astype(f32)
            target[(n,) + into] = value.astype(target.dtype)
        return carry
    lax.fori_loop(0, 4, add, 0)


ROW = 16


def finish_kernel(*refs):
    (
        grad_branch, mixed, attn_in, hidden_in, query, key, value, normed_query, normed_key,
        scale_query, scale_key, hidden_mask, cosine, sine, grad_after, gains, small_in, out_rows,
        query_w, key_w, value_w, output_w, rows_in, rows_grad, middle, grad_gate, grad_up,
    ) = refs[:27]
    weight_outs, small_out, given_out, given_grad = refs[27:31], *refs[31:34]
    gate_out, up_out, down_out, expert_landing = refs[34:38]
    refs = refs[38:]
    sides, lefts, grads, mixed_grad, query_normed, key_normed, attn_grad, grad_rows = refs[:8]
    owns, small_buf, small_own, small_core, w_slots = refs[8:13]
    left_slots, right_slots, send_slots, came, result = refs[13:18]
    parts = 17
    landing, refs = refs[18 : 18 + 5 * parts], refs[18 + 5 * parts :]
    send_sems, recv_sems, local_sems, load_sems = refs
    here = Place()
    rep, x, y, z, ex = here.rep, here.x, here.y, here.z, here.ex
    model_width = grad_branch.shape[1]
    columns = model_width // 4
    enter([*here.peers, here.other_core])
    copies = Copies(send_sems, recv_sems)
    local = []

    def keep(source, target):
        copy = pltpu.make_async_copy(source, target, local_sems.at[len(local)])
        copy.start()
        local.append(copy)
        return copy

    returned = []

    def give(source, target):
        keep(source.at[ex], target.at[ex])
        for peer in here.peers:
            returned.append(copies.start(source.at[peer[1]], target.at[ex], peer))

    mine, theirs = (pl.ds(pl.multiple_of(r * 1024, 1024), 1024) for r in (rep, 1 - rep))
    core_left = [
        copies.start(ref.at[:, theirs], sides.at[n], here.other_core)
        for n, ref in enumerate((mixed, attn_in))
    ]
    core_grad = {}

    def share(n):
        core_grad[n] = copies.start(
            grads.at[n, pl.ds(0, 128)], grads.at[n, pl.ds(128, 128)], here.other_core
        )

    def turn_left(n, ref):
        core_left[n].wait_recv()
        def body(k, carry):
            at = pl.multiple_of(rep * 1024 + k * 128, 128)
            lefts[n, k, :, pl.ds(0, 128)] = ref[:, pl.ds(at, 128)].astype(f32).T.astype(bf16)
            at = pl.multiple_of(k * 128, 128)
            lefts[n, k, :, pl.ds(128, 128)] = sides[n, :, pl.ds(at, 128)].astype(f32).T.astype(bf16)
            return carry
        lax.fori_loop(0, 8, body, 0)

    stream, loads = [(w, n) for w in (output_w, value_w, query_w, key_w) for n in range(4)], {}

    def load(n):
        if n < len(stream):
            w, k = stream[n]
            loads[n] = pltpu.make_async_copy(
                w.at[pl.ds(k * columns, columns)], w_slots.at[n % 2], load_sems.at[n % 2]
            )
            loads[n].start()

    def back_mixed():
        for k in range(4):
            loads[k].wait()
            at = pl.ds(k * columns, columns)
            mixed_grad[:, at] = nt(grad_branch[...], w_slots[k % 2]).astype(bf16)
            load(k + 2)

    def unrotate(grad):
        turned = grad * sine[...]
        lane = lax.broadcasted_iota(jnp.int32, turned.shape, 1)
        sign = jnp.where(lane < HEAD_DIM // 2, 1.0, -1.0)
        return grad * cosine[...] + sign * pltpu.roll(turned, HEAD_DIM // 2, 1)

    def heads(first, count):
        def body(n, carry):
            at = pl.ds(pl.multiple_of((first + n) * HEAD_DIM, HEAD_DIM), HEAD_DIM)
            q, k, v, grad = query[:, at], key[:, at], value[:, at], mixed_grad[:, at]
            scores = jnp.where(hidden_mask[...] > 0, nt(q, k) * HEAD_DIM ** (-0.5), masked_score)
            weights = jnp.exp(scores - jnp.max(scores, axis=1, keepdims=True))
            probs = weights / jnp.sum(weights, axis=1, keepdims=True)
            grads[2, pl.ds(0, 128), at] = tn(probs.astype(bf16), grad).astype(bf16)
            grad_att = nt(grad, v)
            grad_scores = probs * (grad_att - jnp.sum(probs * grad_att, axis=1, keepdims=True))
            grad_scores = grad_scores.astype(bf16)
            query_normed[:, at] = unrotate(nn(grad_scores, k) * HEAD_DIM ** (-0.5))
            key_normed[:, at] = unrotate(tn(grad_scores, q) * HEAD_DIM ** (-0.5))
            return carry
        lax.fori_loop(0, count, body, 0)

    sums = {}

    def back_norm(n, grad_ref, normed_ref, scale_ref):
        def body(k, total):
            rows = pl.ds(pl.multiple_of(k * ROW, ROW), ROW)
            grad, normed = grad_ref[rows], normed_ref[rows]
            total = total + jnp.sum(grad * normed, axis=0, keepdims=True)
            grad = grad * gains[pl.ds(n, 1)]
            mean = jnp.mean(grad * normed, axis=1, keepdims=True)
            grads[n, rows] = (scale_ref[rows] * (grad - normed * mean)).astype(bf16)
            return total
        start = jnp.zeros((1, model_width), f32)
        sums[n] = lax.fori_loop(0, 128 // ROW, body, start)

    def back_attn(n, at_stream, fresh):
        for k in range(4):
            loads[at_stream + k].wait()
            at = pl.ds(k * columns, columns)
            grad = nt(grads[n, pl.ds(0, 128)], w_slots[(at_stream + k) % 2])
            attn_grad[:, at] = grad if fresh else attn_grad[:, at] + grad
            load(at_stream + k + 2)

    def back_hidden():
        def body(k, total):
            rows = pl.ds(pl.multiple_of(k * ROW, ROW), ROW)
            hidden, grad = hidden_in[rows].astype(f32), attn_grad[rows]
            scale = lax.rsqrt(jnp.mean(hidden * hidden, axis=1, keepdims=True) + epsilon)
            normed = hidden * scale
            total = total + jnp.sum(grad * normed, axis=0, keepdims=True)
            grad = grad * gains[pl.ds(2, 1)]
            mean = jnp.mean(grad * normed, axis=1, keepdims=True)
            grad = grad_after[rows] + scale * (grad - normed * mean)
            grad = grad.astype(bf16).reshape(2, 8, model_width)
            grad_rows[pl.ds(2 * k, 2)] = grad
            return total
        start = jnp.zeros((1, model_width), f32)
        sums[2] = lax.fori_loop(0, 128 // ROW, body, start)
        give(grad_rows, given_grad)
        pad = jnp.zeros((125, 128), f32)
        for k in range(model_width // 128):
            rows = [sums[n][:, k * 128 : k * 128 + 128] for n in range(3)]
            block = jnp.concatenate([*rows, pad], axis=0).T.reshape(2, 64, 128)
            at = (k // 8, k // 2 % 4, k % 2)
            small_buf[at] = small_in[at] + block

    def halves():
        return pl.ds(0, 32), pl.ds(32, 32)

    one, two, last = {}, {}, {}

    def own_of(j):
        return owns.at[j % 4] if j < 16 else small_own

    def sum_one(j):
        own, (upper, lower) = own_of(j), halves()
        if j < 16:
            n, which = (3, 0) if j < 4 else ((2, 1), (0, 1), (1, 1))[j // 4 - 1]
            at = pl.ds(j % 4 * columns, columns)
            if j % 4 == 0:
                core_grad[n].wait_recv()
            if j >= 4:
                for copy in (*one[j - 4], *two[j - 4], *last[j - 4]):
                    copies.sent(copy)
            def body(k, carry):
                own[k // 2, k % 2] = nn(lefts[which, k], grads[n, :, at]).astype(bf16).reshape(2, 64, columns)
                return carry
            lax.fori_loop(0, 8, body, 0)
        else:
            core_grad["small"].wait_recv()
            def add(k, carry):
                own[k] = small_buf[rep, k] + small_core[k]
                return carry
            lax.fori_loop(0, 4, add, 0)
        one[j] = (
            copies.start(own.at[:, 1 - y, :, upper], landing[5 * j], here.other_y),
            copies.start(own.at[:, :, 1 - x, lower], landing[5 * j + 1], here.other_x),
        )

    def sum_two(j):
        own, (upper, lower) = own_of(j), halves()
        from_y, from_x = landing[5 * j], landing[5 * j + 1]
        one[j][0].wait_recv()
        accumulate(own, [((y, 1 - x, upper), (1 - x,))], from_y)
        a = copies.start(own.at[:, y, 1 - x, upper], landing[5 * j + 2], here.other_x)
        one[j][1].wait_recv()
        accumulate(own, [((1 - y, x, lower), (1 - y,))], from_x)
        b = copies.start(own.at[:, 1 - y, x, lower], landing[5 * j + 3], here.other_y)
        accumulate(own, [((y, x, upper), (x,)), ], from_y)
        accumulate(own, [((y, x, lower), (y,)), ], from_x)
        two[j] = a, b

    def sum_three(j):
        own, (upper, lower) = own_of(j), halves()
        two[j][0].wait_recv()
        accumulate(own, [((y, x, upper), ())], landing[5 * j + 2])
        two[j][1].wait_recv()
        accumulate(own, [((y, x, lower), ())], landing[5 * j + 3])
        last[j] = [
            copies.start(own.at[(z + k) % 4, y, x], landing[5 * j + 4].at[k - 1], here.other_z[k - 1])
            for k in range(1, 4)
        ]

    def sum_four(j):
        own, arrived = own_of(j), landing[5 * j + 4]
        for copy in last[j]:
            copy.wait_recv()
        total = own[z, y, x].astype(f32) + arrived[0].astype(f32)
        total = total + arrived[1].astype(f32) + arrived[2].astype(f32)
        if j == 16:
            small_out[...] = total
        else:
            n = (3, 2, 0, 1)[j // 4]
            weight_outs[n][:, pl.ds(j % 4 * columns, columns)] = total

    tasks, task_loads, sent_halves, stored = [], {}, {}, {}
    for side in range(2):
        for k in range(2):
            for kind in range(3):
                tasks.append((side, k, kind))

    def task_load(n):
        if n < len(tasks):
            side, k, kind = tasks[n]
            whose = rep if side else 1 - rep
            if kind < 2:
                left = rows_in.at[:, pl.ds(pl.multiple_of(whose * 1024 + k * 512, 512), 512)]
                right = (grad_gate, grad_up)[kind]
            else:
                left = middle.at[:, pl.ds(pl.multiple_of(whose * 512, 512), 512)]
                right = rows_grad.at[:, pl.ds(k * 1024, 1024)]
            task_loads[n] = (
                pltpu.make_async_copy(left, left_slots.at[n % 2], load_sems.at[2 + n % 2]),
                pltpu.make_async_copy(right, right_slots.at[n % 2], load_sems.at[4 + n % 2]),
            )
            for copy in task_loads[n]:
                copy.start()

    def task(n):
        side, k, kind = tasks[n]
        for copy in task_loads[n]:
            copy.wait()
        left, right = left_slots.at[n % 2], right_slots.at[n % 2]
        if side == 0:
            target = send_slots.at[n % 2]
            if n >= 2:
                copies.sent(sent_halves[n - 2])
            def body(m, carry):
                at = pl.ds(pl.multiple_of(m * 256, 256), 256)
                target[at] = tn(left[:, at], right[...]).astype(bf16)
                return carry
            lax.fori_loop(0, 2, body, 0)
            sent_halves[n] = copies.start(target, expert_landing.at[n], here.other_core)
        else:
            at = n - len(tasks) // 2
            sent_halves[at].wait_recv()
            back = pltpu.make_async_copy(expert_landing.at[at], came, load_sems.at[6])
            back.start()
            if n - 1 in stored:
                stored[n - 1].wait()
            back.wait()
            def body(m, carry):
                rows = pl.ds(pl.multiple_of(m * 256, 256), 256)
                result[rows] = tn(left[:, rows], right[...]) + came[rows].astype(f32)
                return carry
            lax.fori_loop(0, 2, body, 0)
            if kind < 2:
                target = (gate_out, up_out)[kind].at[pl.ds(k * 512, 512)]
            else:
                target = down_out.at[:, pl.ds(k * 1024, 1024)]
            stored[n] = pltpu.make_async_copy(result, target, load_sems.at[7])
            stored[n].start()
        task_load(n + 2)

    grads[3, pl.ds(0, 128)] = grad_branch[...]
    share(3)
    for n in range(2):
        load(n)
        task_load(n)
    turn_left(0, mixed)
    for step in range(parts + 3):
        for behind, stage in enumerate((sum_one, sum_two, sum_three, sum_four)):
            if 0 <= step - behind < parts:
                stage(step - behind)
        if step == 0:
            give(out_rows, given_out)
            back_mixed()
            turn_left(1, attn_in)
        elif step == 1:
            heads(0, 8)
        elif step == 2:
            heads(8, 8)
            share(2)
        elif step == 3:
            back_norm(0, query_normed, normed_query, scale_query)
            share(0)
            back_norm(1, key_normed, normed_key, scale_key)
            share(1)
        elif step == 4:
            back_attn(2, 4, True)
        elif step == 5:
            back_attn(0, 8, False)
        elif step == 6:
            back_attn(1, 12, False)
        elif step == 7:
            back_hidden()
            core_grad["small"] = copies.start(small_buf.at[1 - rep], small_core, here.other_core)
        elif step < 8 + len(tasks) // 2:
            task(2 * (step - 8))
            task(2 * (step - 8) + 1)
    stored[len(tasks) - 1].wait()
    for copy in returned:
        copy.wait_recv()
    for copy in local:
        copy.wait()
    copies.finish()


def run_finish(arrays, weights, expert, collective_id):
    rows, model_width = arrays[0].shape
    columns = model_width // 4
    vmem, anywhere = pl.BlockSpec(memory_space=pltpu.VMEM), pl.BlockSpec(memory_space=pl.ANY)
    shape, tile = jax.ShapeDtypeStruct, (4, 2, 2, 64)
    scratch = [
        pltpu.VMEM((2, rows, 1024), bf16),
        pltpu.VMEM((2, 8, 128, 256), bf16),
        pltpu.VMEM((4, 2 * rows, model_width), bf16),
        pltpu.VMEM((rows, model_width), bf16),
        pltpu.VMEM((rows, model_width), f32),
        pltpu.VMEM((rows, model_width), f32),
        pltpu.VMEM((rows, model_width), f32),
        pltpu.VMEM((16, 8, model_width), bf16),
        pltpu.VMEM((4, *tile, columns), bf16),
        pltpu.VMEM((2, *tile, 128), f32),
        pltpu.VMEM((*tile, 128), f32),
        pltpu.VMEM((*tile, 128), f32),
        pltpu.VMEM((2, columns, model_width), bf16),
        pltpu.VMEM((2, 1024, 512), bf16),
        pltpu.VMEM((2, 1024, 1024), bf16),
        pltpu.VMEM((2, 512, 1024), bf16),
        pltpu.VMEM((512, 1024), bf16),
        pltpu.VMEM((512, 1024), f32),
    ]
    for j in range(17):
        width, dtype = (columns, bf16) if j < 16 else (128, f32)
        scratch += [
            pltpu.VMEM((4, 2, 32, width), dtype),
            pltpu.VMEM((4, 2, 32, width), dtype),
            pltpu.VMEM((4, 32, width), dtype),
            pltpu.VMEM((4, 32, width), dtype),
            pltpu.VMEM((3, 64, width), dtype),
        ]
    copies = 7 * 17 + 30 + 7 + 6
    return pl.pallas_call(
        finish_kernel,
        out_shape=[shape((64, model_width), f32)] * 4
        + [shape((64, 128), f32)]
        + [shape((16, 8, model_width), bf16)] * 2
        + [shape((1024, 1024), f32)] * 2
        + [shape((512, 2048), f32), shape((6, 512, 1024), bf16)],
        in_specs=[vmem] * len(arrays) + [anywhere] * (len(weights) + len(expert)),
        out_specs=[vmem] * 5 + [anywhere] * 6,
        scratch_shapes=scratch
        + [
            pltpu.SemaphoreType.DMA((copies,)),
            pltpu.SemaphoreType.DMA((copies,)),
            pltpu.SemaphoreType.DMA((2,)),
            pltpu.SemaphoreType.DMA((8,)),
        ],
        compiler_params=pltpu.CompilerParams(
            collective_id=collective_id, has_side_effects=True, vmem_limit_bytes=62 * 2**20
        ),
    )(*arrays, *weights, *expert)


def has_kernels():
    return (lax.axis_size("rep"), lax.axis_size("ex")) == (2, 16)


def exchange(array):
    return lax.all_to_all(array, "ex", split_axis=0, concat_axis=0, tiled=True)


def gather_weights(shards, outbound):
    if has_kernels():
        *full, inbound = gather(shards, [outbound], True, [4] * (len(shards) - 1) + [1], 1)
        return [a.reshape(-1, a.shape[-1]) for a in full], inbound
    full = [lax.all_gather(a, ("rep", "ex"), axis=0, tiled=True) for a in shards]
    return full, exchange(outbound)


def slots_of(tables, capacity):
    experts, me = tables.shape[1] // 2, lax.axis_index("ex")
    gates = lax.dynamic_index_in_dim(tables, me, 1, keepdims=True)
    slots = lax.dynamic_index_in_dim(tables, experts + me, 1, keepdims=True)
    return slots == jnp.arange(capacity, dtype=f32)[None, :, None], gates


def experts_of_group(moe_in, cot_in, table, gate_full, up_full, down_full, capacity):
    if has_kernels():
        return run_experts(moe_in, cot_in, table, gate_full, up_full, down_full, capacity, 2)
    tables = lax.all_gather(table, "ex", axis=0)
    picked, gate_rows = slots_of(tables, capacity)
    picked_low = picked.astype(bf16)
    slot_gate = jnp.sum(jnp.where(picked, gate_rows, 0.0), axis=2).reshape(-1, 1)

    def pick(rows):
        rows = lax.all_gather(rows, "ex", axis=0)
        rows = jnp.einsum("sct,std->scd", picked_low, rows, preferred_element_type=f32)
        return rows.astype(bf16).reshape(-1, rows.shape[-1])

    def spread(rows):
        rows = rows.reshape(*picked_low.shape[:2], -1)
        rows = jnp.einsum("sct,scd->std", picked_low, rows, preferred_element_type=f32)
        return lax.psum_scatter(rows.astype(bf16), "ex", scatter_dimension=0).astype(f32)

    rows_in, rows_cot = pick(moe_in), pick(cot_in)
    gate_pre = jnp.dot(rows_in, gate_full, preferred_element_type=f32)
    up_pre = jnp.dot(rows_in, up_full, preferred_element_type=f32)
    sigma = jax.nn.sigmoid(gate_pre)
    silu = gate_pre * sigma
    middle = (silu * up_pre).astype(bf16)
    expert_out = jnp.dot(middle, down_full, preferred_element_type=f32).astype(bf16)
    slot_grad = jnp.sum(rows_cot.astype(f32) * expert_out.astype(f32), axis=1)
    rows_grad = (slot_gate * rows_cot.astype(f32)).astype(bf16)
    grad_middle = jnp.dot(rows_grad, down_full.T, preferred_element_type=f32)
    grad_gate_low = (grad_middle * up_pre * sigma * (1.0 + gate_pre * (1.0 - sigma))).astype(bf16)
    grad_up_low = (grad_middle * silu).astype(bf16)
    grad_rows = jnp.dot(grad_gate_low, gate_full.T, preferred_element_type=f32)
    grad_rows = grad_rows + jnp.dot(grad_up_low, up_full.T, preferred_element_type=f32)
    weighted = slot_gate * expert_out.astype(f32)
    slot_grad = slot_grad.reshape(*picked.shape[:2], 1)
    back = exchange(jnp.sum(jnp.where(picked, slot_grad, 0.0), axis=1))
    sums = spread(grad_rows.astype(bf16)), spread(weighted.astype(bf16))
    return *sums, back, rows_in, rows_grad, middle, grad_gate_low, grad_up_low


def finish(
    grad_branch, mixed, attn_in, hidden_in, query_low, key_low, value_low, normed_query, normed_key,
    scale_query, scale_key, visible, cosine, sine, grad_after, query_scale, key_scale, attn_scale,
    small, output, query_full, key_full, value_full, output_full,
    rows_in, rows_grad, middle, grad_gate_low, grad_up_low,
):
    row_count, model_width = mixed.shape
    group_size = lax.axis_size("ex")
    block_rows = row_count // group_size
    if has_kernels():
        wide = jnp.pad(small, ((0, 0), (3, 128 - 3 - small.shape[1])))
        gains = jnp.stack([query_scale, key_scale, attn_scale], axis=0)
        arrays = [
            grad_branch, mixed, attn_in, hidden_in,
            *(a.reshape(row_count, model_width) for a in (query_low, key_low, value_low)),
            normed_query, normed_key, scale_query, scale_key, visible.astype(f32),
            cosine[:, 0], sine[:, 0], grad_after, jnp.pad(gains, ((0, 5), (0, 0))),
            wide.reshape(2, 4, 2, 2, 64, 128), output.reshape(group_size, block_rows, model_width),
        ]
        *weights, summed, given_out, given_grad, gate, up, down, _ = run_finish(
            arrays,
            [query_full, key_full, value_full, output_full],
            [rows_in, rows_grad, middle, grad_gate_low, grad_up_low],
            3,
        )
        rows = [a.reshape(row_count, model_width) for a in (given_out, given_grad)]
        return weights, summed[:, : 3 + small.shape[1]], rows, (gate, up, down)
    both = ("rep", "ex")
    scores = attention_scores(query_low, key_low, visible)
    probs = jax.nn.softmax(scores, axis=-1)
    probs_low = probs.astype(bf16)
    normed_attn, scale_attn = normalize(hidden_in.astype(f32))
    grad_mixed = (
        jnp.dot(grad_branch, output_full.T, preferred_element_type=f32)
        .astype(bf16)
        .reshape(row_count, HEADS, HEAD_DIM)
    )
    grad_value = jnp.einsum("hqk,qhd->khd", probs_low, grad_mixed, preferred_element_type=f32)
    grad_att = jnp.einsum("qhd,khd->hqk", grad_mixed, value_low, preferred_element_type=f32)
    grad_scores = (probs * (grad_att - jnp.sum(probs * grad_att, axis=-1, keepdims=True))).astype(
        bf16
    )
    grad_query_rot = jnp.einsum(
        "hqk,khd->qhd", grad_scores, key_low, preferred_element_type=f32
    ) * HEAD_DIM ** (-0.5)
    grad_key_rot = jnp.einsum(
        "hqk,qhd->khd", grad_scores, query_low, preferred_element_type=f32
    ) * HEAD_DIM ** (-0.5)
    grad_query_normed = (grad_query_rot * cosine + rotate_back(grad_query_rot * sine)).reshape(
        row_count, model_width
    )
    grad_key_normed = (grad_key_rot * cosine + rotate_back(grad_key_rot * sine)).reshape(
        row_count, model_width
    )
    grad_query_scale = jnp.sum(grad_query_normed * normed_query, axis=0)
    grad_key_scale = jnp.sum(grad_key_normed * normed_key, axis=0)
    grad_query_pre = norm_back(grad_query_normed * query_scale, normed_query, scale_query)
    grad_key_pre = norm_back(grad_key_normed * key_scale, normed_key, scale_key)
    grad_query_pre = grad_query_pre.astype(bf16)
    grad_key_pre = grad_key_pre.astype(bf16)
    grad_value_pre = grad_value.reshape(row_count, model_width).astype(bf16)
    grad_attn_in = jnp.dot(grad_query_pre, query_full.T, preferred_element_type=f32)
    grad_attn_in = grad_attn_in + jnp.dot(grad_key_pre, key_full.T, preferred_element_type=f32)
    grad_attn_in = grad_attn_in + jnp.dot(grad_value_pre, value_full.T, preferred_element_type=f32)
    grad_attn_scale = jnp.sum(grad_attn_in * normed_attn, axis=0)
    grad_hidden = grad_after + norm_back(grad_attn_in * attn_scale, normed_attn, scale_attn)
    sums = []
    for left, right in (
        (attn_in, grad_query_pre),
        (attn_in, grad_key_pre),
        (attn_in, grad_value_pre),
        (mixed, grad_branch),
    ):
        grad = jnp.dot(left.T, right, preferred_element_type=f32).astype(bf16)
        sums.append(lax.psum_scatter(grad, both, scatter_dimension=0, tiled=True).astype(f32))
    three = jnp.stack([grad_query_scale, grad_key_scale, grad_attn_scale], axis=1)
    small = jnp.concatenate([three, small], axis=1)
    small = lax.psum_scatter(small, both, scatter_dimension=0, tiled=True)
    expert = []
    for left, right in ((rows_in, grad_gate_low), (rows_in, grad_up_low), (middle, rows_grad)):
        grad = jnp.dot(left.T, right, preferred_element_type=f32).astype(bf16)
        expert.append(lax.psum_scatter(grad, "rep", scatter_dimension=0, tiled=True).astype(f32))
    rows = [exchange(output), exchange(grad_hidden.astype(bf16))]
    return sums, small, rows, expert


def body(
    tokens,
    out_cot,
    destination,
    doc_lengths,
    routes,
    fill_order,
    query_weight,
    key_weight,
    value_weight,
    output_weight,
    query_gain,
    key_gain,
    attn_gain,
    moe_gain,
    router_weight,
    expert_gate,
    expert_up,
    expert_down,
):
    group_size = lax.axis_size("ex")
    row_count, model_width = tokens.shape
    block_rows = row_count // group_size
    row_index = jnp.arange(row_count, dtype=jnp.int32)
    placed = destination // row_count % group_size * block_rows + destination % block_rows
    to_send = (placed[None, :] == row_index[:, None]).astype(bf16)
    inbound = jnp.dot(
        to_send, jnp.concatenate([tokens, out_cot], axis=1), preferred_element_type=f32
    ).astype(bf16)
    gains = jnp.concatenate(
        [jnp.stack([query_gain, key_gain, attn_gain, moe_gain], axis=1), router_weight], axis=1
    )
    extra = gains.shape[1]
    gains = jnp.pad(gains, ((0, 0), (0, -extra % 128)))
    full, packed = gather_weights(
        [query_weight, key_weight, value_weight, output_weight, gains],
        inbound.reshape(group_size, block_rows, 2 * model_width),
    )
    query_full, key_full, value_full, output_full, gains = full
    packed = packed.reshape(row_count, 2 * model_width)
    hidden_in, cot_in = packed[:, :model_width], packed[:, model_width:]
    query_scale, key_scale, attn_scale, moe_scale = (gains[:, i].astype(f32) for i in range(4))
    router_full = gains[:, 4:extra]
    gate_full = lax.all_gather(expert_gate[0], "rep", axis=0, tiled=True)
    up_full = lax.all_gather(expert_up[0], "rep", axis=0, tiled=True)
    down_full = lax.all_gather(expert_down[0], "rep", axis=0, tiled=True)

    segment, position, live_rows = segment_tables(doc_lengths[0], row_count)
    live_column = live_rows.astype(f32)[:, None]
    hidden = hidden_in.astype(f32)
    normed_attn, scale_attn = normalize(hidden)
    attn_in = (normed_attn * attn_scale).astype(bf16)
    query_pre = jnp.dot(attn_in, query_full, preferred_element_type=f32)
    key_pre = jnp.dot(attn_in, key_full, preferred_element_type=f32)
    value_pre = jnp.dot(attn_in, value_full, preferred_element_type=f32)
    normed_query, scale_query = normalize(query_pre)
    normed_key, scale_key = normalize(key_pre)
    cosine, sine = rope_tables(position)
    query_norm = (normed_query * query_scale).reshape(row_count, HEADS, HEAD_DIM)
    key_norm = (normed_key * key_scale).reshape(row_count, HEADS, HEAD_DIM)
    query_low = (query_norm * cosine + rotate_half(query_norm) * sine).astype(bf16)
    key_low = (key_norm * cosine + rotate_half(key_norm) * sine).astype(bf16)
    value_low = value_pre.astype(bf16).reshape(row_count, HEADS, HEAD_DIM)
    visible = (segment[:, None] == segment[None, :]) & (row_index[None, :] <= row_index[:, None])
    scores = attention_scores(query_low, key_low, visible)
    peak = jnp.max(scores, axis=-1, keepdims=True)
    weights_exp = jnp.exp(scores - peak)
    probs = weights_exp / jnp.sum(weights_exp, axis=-1, keepdims=True)
    probs_low = probs.astype(bf16)
    mixed = jnp.einsum("hqk,khd->qhd", probs_low, value_low, preferred_element_type=f32)
    mixed = mixed.reshape(row_count, model_width).astype(bf16)
    branch = jnp.dot(mixed, output_full, preferred_element_type=f32)
    after_attn = hidden + live_column * branch
    normed_moe, scale_moe = normalize(after_attn)
    moe_in = (normed_moe * moe_scale).astype(bf16)
    logits = jnp.dot(moe_in, router_full, preferred_element_type=f32)
    router_probs = jax.nn.softmax(logits, axis=-1)
    experts = router_full.shape[1]
    capacity = row_count * routes.shape[1] // experts
    slot_table, kept = slot_tables(routes, fill_order[0], live_rows, experts, capacity)
    gates = jnp.where(kept, router_probs, 0.0)

    table = jnp.concatenate([gates.T, slot_table.T.astype(f32)], axis=0)
    (
        grad_moe_in,
        mixture,
        grad_rprobs,
        rows_in,
        rows_grad,
        middle,
        grad_gate_low,
        grad_up_low,
    ) = experts_of_group(moe_in, cot_in, table, gate_full, up_full, down_full, capacity)
    grad_rprobs = grad_rprobs.T
    output = (after_attn + mixture).astype(bf16)

    grad_out = cot_in.astype(f32)
    grad_logits = router_probs * (
        grad_rprobs - jnp.sum(router_probs * grad_rprobs, axis=-1, keepdims=True)
    )
    grad_moe_in = grad_moe_in + jnp.dot(
        grad_logits, router_full.T, precision=lax.Precision.HIGHEST, preferred_element_type=f32
    )
    grad_router = jnp.dot(
        moe_in.T, grad_logits, precision=lax.Precision.HIGHEST, preferred_element_type=f32
    )
    grad_moe_scale = jnp.sum(grad_moe_in * normed_moe, axis=0)
    grad_after = grad_out + norm_back(grad_moe_in * moe_scale, normed_moe, scale_moe)
    grad_branch = (live_column * grad_after).astype(bf16)
    small = jnp.concatenate([grad_moe_scale[:, None], grad_router], axis=1)
    sums, small, rows, expert = finish(
        grad_branch, mixed, attn_in, hidden_in, query_low, key_low, value_low, normed_query,
        normed_key, scale_query, scale_key, visible, cosine, sine, grad_after, query_scale,
        key_scale, attn_scale, small, output, query_full, key_full, value_full, output_full,
        rows_in, rows_grad, middle, grad_gate_low, grad_up_low,
    )
    owned_query, owned_key, owned_value, owned_output = sums
    owned_gate, owned_up, owned_down = (a[None] for a in expert)
    outbound = jnp.dot(
        to_send.T, jnp.concatenate(rows, axis=1), preferred_element_type=f32
    ).astype(bf16)
    return (
        outbound[:, :model_width],
        outbound[:, model_width:],
        owned_query,
        owned_key,
        owned_value,
        owned_output,
        small[:, 0],
        small[:, 1],
        small[:, 2],
        small[:, 3],
        small[:, 4:],
        owned_gate,
        owned_up,
        owned_down,
    )


def solution(mesh):
    rows, row = P(("rep", "ex"), None), P(("rep", "ex"))
    expert = P("ex", "rep", None)
    return jax.shard_map(
        body,
        mesh=mesh,
        in_specs=(rows, rows, row) + (rows,) * 7 + (row,) * 4 + (rows,) + (expert,) * 3,
        out_specs=(rows,) * 6 + (row,) * 4 + (rows,) + (expert,) * 3,
        check_vma=False,
    )
```

```python
import functools

import jax
import jax.numpy as jnp
from jax import lax
from jax.experimental import pallas as pl
from jax.experimental.pallas import tpu as pltpu
from jax.sharding import PartitionSpec as P

HEADS = 16
HEAD_DIM = 128

epsilon = 1e-05
rope_base = 10000.0
masked_score = -1e30
bf16 = jnp.bfloat16
f32 = jnp.float32


def normalize(values):
    scale = lax.rsqrt(jnp.mean(values * values, axis=-1, keepdims=True) + epsilon)
    return (values * scale, scale)


def norm_back(grad_normed, normed, scale):
    return scale * (grad_normed - normed * jnp.mean(grad_normed * normed, axis=-1, keepdims=True))


def rotate_half(values):
    middle = values.shape[-1] // 2
    return jnp.concatenate([-values[..., middle:], values[..., :middle]], axis=-1)


def rotate_back(values):
    middle = values.shape[-1] // 2
    return jnp.concatenate([values[..., middle:], -values[..., :middle]], axis=-1)


def rope_tables(position):
    steps = jnp.arange(HEAD_DIM // 2, dtype=f32) * (2.0 / HEAD_DIM)
    inverse = rope_base ** (-steps)
    angle = position.astype(f32)[:, None] * inverse[None, :]
    cosine = jnp.concatenate([jnp.cos(angle), jnp.cos(angle)], axis=-1)[:, None, :]
    sine = jnp.concatenate([jnp.sin(angle), jnp.sin(angle)], axis=-1)[:, None, :]
    return (cosine, sine)


def segment_tables(lengths, row_count):
    count = lengths.shape[0]
    numbers = jnp.arange(count, dtype=jnp.int32)
    before = (numbers[None, :] < numbers[:, None]).astype(jnp.int32)
    starts = jnp.sum(before * lengths[None, :], axis=1)
    ends = starts + lengths
    row_index = jnp.arange(row_count, dtype=jnp.int32)
    segment = jnp.sum((row_index[:, None] >= ends[None, :]).astype(jnp.int32), axis=1)
    begin = jnp.sum(jnp.where(segment[:, None] == numbers[None, :], starts[None, :], 0), axis=1)
    return (segment, row_index - begin, segment < count - 1)


def slot_tables(routes, filling, live_rows, experts, capacity):
    row_count, top_count = routes.shape
    order = jnp.arange(row_count * top_count, dtype=jnp.int32)
    rows = jnp.arange(row_count, dtype=jnp.int32)
    hot_row = (filling[None, :] // top_count == rows[:, None]).astype(bf16)
    hot_choice = (filling % top_count)[:, None] == jnp.arange(top_count, dtype=jnp.int32)[None, :]
    high = jnp.where(hot_choice, (order // 64)[:, None], 0).astype(bf16)
    lower = jnp.where(hot_choice, (order % 64)[:, None], 0).astype(bf16)
    ranks = jnp.dot(
        hot_row, jnp.concatenate([high, lower], axis=1), preferred_element_type=f32
    ).astype(jnp.int32)
    rank = ranks[:, :top_count] * 64 + ranks[:, top_count:]
    chosen = routes[:, :, None] == jnp.arange(experts, dtype=jnp.int32)[None, None, :]
    rank_table = jnp.sum(jnp.where(chosen, rank[:, :, None], 0), axis=1)
    counted = jnp.any(chosen, axis=1) & live_rows[:, None]
    earlier = counted[:, None, :] & (rank_table[:, None, :] < rank_table[None, :, :])
    slot = jnp.sum(earlier.astype(jnp.int32), axis=0)
    kept = counted & (slot < capacity)
    return (jnp.where(kept, slot, -1), kept)


def attention_scores(query_low, key_low, visible):
    scores = jnp.einsum(
        "qhd,khd->hqk", query_low, key_low, preferred_element_type=f32
    ) * HEAD_DIM ** (-0.5)
    return jnp.where(visible[None], scores, masked_score)


MESH = pl.DeviceIdType.MESH


class Place:
    def __init__(self):
        self.rep, self.ex = lax.axis_index("rep"), lax.axis_index("ex")
        self.x, self.y, self.z = self.ex % 2, self.ex // 2 % 2, self.ex // 4
        self.other_x = (self.rep, self.ex + 1 - 2 * self.x)
        self.other_y = (self.rep, self.ex + 2 - 4 * self.y)
        self.other_core = (1 - self.rep, self.ex)
        self.other_z = [(self.rep, (self.ex + 4 * k) % 16) for k in range(1, 4)]
        self.middle = (self.z == 1) | (self.z == 2)
        self.end = jnp.logical_not(self.middle)
        near = jnp.where(self.z < 2, 1, 2)
        self.end_z = jnp.where(self.z < 2, 0, 3)
        self.near, self.far, self.across, self.own_end, self.far_end = (
            (self.rep, zz * 4 + self.ex % 4) for zz in (near, 3 - near, 3 - self.z, self.end_z, 3 - self.end_z)
        )
        self.peers = [(self.rep, (self.ex + k) % 16) for k in range(1, 16)]


def enter(devices):
    barrier = pltpu.get_barrier_semaphore()
    for device in devices:
        pl.semaphore_signal(barrier, inc=1, device_id=device, device_id_type=MESH)
    pl.semaphore_wait(barrier, len(devices))


class Copies:
    def __init__(self, send_sems, recv_sems):
        self.send_sems, self.recv_sems, self.made = send_sems, recv_sems, []
        self.done, self.whens = set(), {}

    def start(self, source, target, device, when=None):
        at = len(self.made)
        copy = pltpu.make_async_remote_copy(
            src_ref=source,
            dst_ref=target,
            send_sem=self.send_sems.at[at],
            recv_sem=self.recv_sems.at[at],
            device_id=device,
            device_id_type=MESH,
        )
        if when is None:
            copy.start()
        else:
            pl.when(when)(copy.start)
        self.made.append(copy)
        self.whens[id(copy)] = when
        return copy

    def sent(self, copy):
        if id(copy) not in self.done:
            self.done.add(id(copy))
            when = self.whens[id(copy)]
            if when is None:
                copy.wait_send()
            else:
                pl.when(when)(copy.wait_send)

    def finish(self):
        for copy in self.made:
            self.sent(copy)


def nt(left, right):
    return lax.dot_general(left, right, (((1,), (1,)), ((), ())), preferred_element_type=f32)


def nn(left, right):
    return jnp.dot(left, right, preferred_element_type=f32)


def hot_slots(table, expert, capacity):
    experts, rows = table.shape
    lane = lax.broadcasted_iota(jnp.int32, (capacity, experts), 1)
    mine = jnp.where(lane == expert, 1.0, 0.0).astype(bf16)
    slot = nn(mine, table.astype(bf16))
    wanted = lax.broadcasted_iota(jnp.int32, (capacity, rows), 0).astype(f32)
    return jnp.where(slot == wanted, 1.0, 0.0).astype(bf16)


PIECES = 4


def expert_kernel(capacity, *refs):
    table, moe, cot, gate_w, up_w, down_w = refs[:6]
    grad_out, mix_out, given, *kept_outs = refs[6:14]
    refs = refs[14:]
    tables, hot, hot_row, hot_gate, gate_col, grad_col, back = refs[:7]
    rows_in, rows_cot, acc, to_gate, to_up, middle, result = refs[7:14]
    gu_slots, down_slots, to_slots, send_slots, column_slots = refs[14:19]
    parts = 2 * PIECES
    pick_buffers = [refs[19 + 3 * j : 22 + 3 * j] for j in range(parts)]
    refs = refs[19 + 3 * parts :]
    spread_buffers = [refs[2 * j : 2 * j + 2] for j in range(parts)]
    send_sems, recv_sems, local_sems, load_sems, ready = refs[2 * parts :]
    here = Place()
    x, y, z, ex = here.x, here.y, here.z, here.ex
    by_y, by_x = here.other_y[1], here.other_x[1]
    experts = table.shape[0] // 2
    units = gate_w.shape[1]
    width = moe.shape[1] // PIECES
    half = width // 2
    enter(here.peers)
    copies = Copies(send_sems, recv_sems)
    local = []

    def keep(source, target):
        copy = pltpu.make_async_copy(source, target, local_sems.at[len(local)])
        copy.start()
        local.append(copy)
        return copy

    def block(zz, yy, xx):
        return (zz * 2 + yy) * 2 + xx

    def piece(j):
        return j % PIECES * width

    gu_loads, down_loads = {}, {}

    def load_gu(n):
        if n < parts:
            rows = pl.ds(piece(n), width)
            gu_loads[n] = [
                pltpu.make_async_copy(w.at[rows], gu_slots.at[n % 2, k], load_sems.at[n % 2, k])
                for k, w in enumerate((gate_w, up_w))
            ]
            for copy in gu_loads[n]:
                copy.start()

    def load_down(n):
        if n < parts:
            columns = pl.ds(piece(n), width)
            down_loads[n] = pltpu.make_async_copy(
                down_w.at[:, columns], down_slots.at[n % 2], load_sems.at[n % 2, 2]
            )
            down_loads[n].start()

    def stage_z(j):
        source = (moe if j < PIECES else cot).at[:, pl.ds(piece(j), width)]
        target = pick_buffers[j][0].at[z]
        to_near = copies.start(source, target, here.near, here.end)
        to_far = copies.start(source, target, here.far, here.end)
        across = copies.start(source, target, here.across, here.middle)
        to_end = copies.start(source, target, here.own_end, here.middle)
        return [to_near, to_far, across, to_end], keep(source, target)

    def relay(j):
        (_, to_far, across, _), _ = held[j]
        def arrived():
            to_far.wait_recv()
            across.wait_recv()
        pl.when(here.middle)(arrived)
        blocks = pick_buffers[j][0].at[pl.ds(jnp.where(z == 1, 2, 0), 2)]
        held[j][0].append(copies.start(blocks, blocks, here.own_end, here.middle))

    def stage_one(j, sent, kept):
        column, from_x, from_y = pick_buffers[j]
        to_near, _, _, to_end, relayed = sent
        kept.wait()
        pl.when(here.middle)(to_near.wait_recv)
        def arrived():
            to_end.wait_recv()
            relayed.wait_recv()
        pl.when(here.end)(arrived)
        return (
            copies.start(column.at[:, :, pl.ds(0, half)], from_x, here.other_x),
            copies.start(column.at[:, :, pl.ds(half, half)], from_y, here.other_y),
        )

    def landing(j):
        return rows_in if j < PIECES else rows_cot

    def pick_own(j):
        column, into = pick_buffers[j][0], landing(j)
        def body(n, carry):
            picked = nn(hot[0, block(n, y, x)], column[n])
            into[n, y, x, :, pl.ds(piece(j), width)] = picked.astype(bf16)
            return carry
        lax.fori_loop(0, 4, body, 0)

    def pick_moved(j):
        (_, from_x, from_y), into, first = pick_buffers[j], landing(j), piece(j)
        def body(n, carry):
            picked = nn(hot[0, block(n, y, 1 - x)], from_x[n])
            into[n, y, 1 - x, :, pl.ds(first, half)] = picked.astype(bf16)
            picked = nn(hot[0, block(n, 1 - y, x)], from_y[n])
            into[n, 1 - y, x, :, pl.ds(first + half, half)] = picked.astype(bf16)
            return carry
        lax.fori_loop(0, 4, body, 0)

    second = {}

    def stage_two(j, one):
        (column, from_x, from_y), into, first = pick_buffers[j], landing(j), piece(j)
        to_y, to_x = to_slots.at[j % 2, 0], to_slots.at[j % 2, 1]
        if j >= 2:
            copies.sent(second[j - 2][0])
            copies.sent(second[j - 2][1])
        def own_part(n, carry):
            at = block(n, y, x)
            to_y[n, x] = nn(hot[1, at], column[n, :, pl.ds(0, half)]).astype(bf16)
            to_x[n, y] = nn(hot[2, at], column[n, :, pl.ds(half, half)]).astype(bf16)
            return carry
        lax.fori_loop(0, 4, own_part, 0)
        one[0].wait_recv()
        def x_part(n, carry):
            to_y[n, 1 - x] = nn(hot[1, block(n, y, 1 - x)], from_x[n]).astype(bf16)
            return carry
        lax.fori_loop(0, 4, x_part, 0)
        a = copies.start(to_y, into.at[:, y, :, :, pl.ds(first, half)], here.other_y)
        one[1].wait_recv()
        def y_part(n, carry):
            to_x[n, 1 - y] = nn(hot[2, block(n, 1 - y, x)], from_y[n]).astype(bf16)
            return carry
        lax.fori_loop(0, 4, y_part, 0)
        b = copies.start(to_x, into.at[:, :, x, :, pl.ds(first + half, half)], here.other_x)
        second[j] = a, b

    def build(n, carry):
        both = tables[n]
        for k, expert in enumerate((ex, by_y, by_x)):
            hot[k, n] = hot_slots(both[experts:], expert, capacity)
        turned = both.T
        lane = lax.broadcasted_iota(jnp.int32, turned.shape, 1)
        wanted = lax.broadcasted_iota(jnp.int32, (turned.shape[0], capacity), 1).astype(f32)
        for k, expert in enumerate((ex, by_y, by_x)):
            slot = jnp.sum(jnp.where(lane == experts + expert, turned, 0.0), axis=1, keepdims=True)
            gate = jnp.sum(jnp.where(lane == expert, turned, 0.0), axis=1, keepdims=True)
            hot_row[k, n] = jnp.where(slot == wanted, 1.0, 0.0).astype(bf16)
            hot_gate[k, n] = jnp.where(slot == wanted, gate, 0.0).astype(bf16)
        row = lax.broadcasted_iota(jnp.int32, (experts, both.shape[1]), 0)
        gates = jnp.sum(jnp.where(row == ex, both[:experts], 0.0), axis=0, keepdims=True)
        gate_col[n] = jnp.sum(hot[0, n].astype(f32) * gates, axis=1, keepdims=True)
        grad_col[n] = jnp.zeros((capacity, 1), f32)
        return carry

    def flat(ref, first, size):
        return ref[:, :, :, :, pl.ds(first, size)].reshape(-1, size)

    def grow(k, columns, value, fresh):
        acc[k, :, columns] = value if fresh else acc[k, :, columns] + value

    def tile(n):
        return pl.ds(pl.multiple_of(n * 256, 256), 256)

    def gate_and_up(p):
        for copy in gu_loads[p]:
            copy.wait()
        def body(n, carry):
            left = flat(rows_in, piece(p), width)
            for k in range(2):
                grow(k, tile(n), nn(left, gu_slots[p % 2, k, :, tile(n)]), p == 0)
            return carry
        lax.fori_loop(0, units // 256, body, 0)
        load_gu(p + 2)

    def activate(n, carry):
        rows = pl.ds(pl.multiple_of(n * 32, 32), 32)
        gate, up = acc[0, rows], acc[1, rows]
        sigma = 1.0 / (1.0 + jnp.exp(-gate))
        silu = gate * sigma
        middle[rows] = (silu * up).astype(bf16)
        to_gate[rows] = (up * sigma * (1.0 + gate * (1.0 - sigma))).astype(bf16)
        to_up[rows] = silu.astype(bf16)
        return carry

    def store(first, value):
        result[:, :, :, :, pl.ds(first, 256)] = value.astype(bf16).reshape(4, 2, 2, capacity, 256)

    def down(p):
        down_loads[p].wait()
        for n in range(width // 256):
            store(piece(p) + n * 256, nn(middle[...], down_slots[p % 2, :, pl.ds(n * 256, 256)]))
        load_down(p + 2)

    def back_down(p):
        n_load = p + PIECES
        columns = pl.ds(piece(p), width)
        def rows(n, carry):
            at = (n // 4, n // 2 % 2, n % 2, slice(None), columns)
            mine = rows_cot[at].astype(f32)
            dots = jnp.sum(mine * result[at].astype(f32), axis=1, keepdims=True)
            grad_col[n] = grad_col[n] + dots
            rows_cot[at] = (gate_col[n] * mine).astype(bf16)
            return carry
        lax.fori_loop(0, 16, rows, 0)
        down_loads[n_load].wait()
        def body(n, carry):
            value = nt(flat(rows_cot, piece(p), width), down_slots[n_load % 2, tile(n)])
            grow(0, tile(n), value, p == 0)
            return carry
        lax.fori_loop(0, units // 256, body, 0)
        load_down(n_load + 2)

    def back_activate(n, carry):
        rows = pl.ds(pl.multiple_of(n * 32, 32), 32)
        grad = acc[0, rows]
        to_gate[rows] = (grad * to_gate[rows].astype(f32)).astype(bf16)
        to_up[rows] = (grad * to_up[rows].astype(f32)).astype(bf16)
        return carry

    def back_rows(p):
        n_load = p + PIECES
        for copy in spread_one[p]:
            copies.sent(copy)
        for copy in gu_loads[n_load]:
            copy.wait()
        for n in range(width // 256):
            rows = pl.ds(n * 256, 256)
            value = nt(to_gate[...], gu_slots[n_load % 2, 0, rows])
            store(piece(p) + n * 256, value + nt(to_up[...], gu_slots[n_load % 2, 1, rows]))
        load_gu(n_load + 2)

    def give_back(n, carry):
        grads = jnp.sum(hot[0, n].astype(f32) * grad_col[n], axis=0, keepdims=True)
        back[n] = jnp.broadcast_to(grads, back.shape[1:])
        return carry

    spread_one, spread_two, spread_three = {}, {}, {}

    def cols(j):
        return pl.ds(piece(j), half), pl.ds(piece(j) + half, half)

    def term(j, which, at, rows):
        return nn((hot_gate if j < PIECES else hot_row)[which, at], rows)

    def send_one(j):
        (from_y, from_x), (a, b) = spread_buffers[j], cols(j)
        spread_one[j] = (
            copies.start(result.at[:, 1 - y, :, :, a], from_y, here.other_y),
            copies.start(result.at[:, :, 1 - x, :, b], from_x, here.other_x),
        )

    def send_two(j):
        (from_y, from_x), (a, b) = spread_buffers[j], cols(j)
        to_x, to_y = send_slots.at[j % 2, 0], send_slots.at[j % 2, 1]
        if j >= 2:
            copies.sent(spread_two[j - 2][0])
            copies.sent(spread_two[j - 2][1])
        if j % PIECES == 0:
            pl.semaphore_wait(ready.at[j // PIECES], 5)
        spread_one[j][0].wait_recv()
        def x_part(n, carry):
            at = block(n, y, 1 - x)
            total = term(j, 0, at, result[n, y, 1 - x, :, a]) + term(j, 1, at, from_y[n, 1 - x])
            to_x[n] = total.astype(bf16)
            return carry
        lax.fori_loop(0, 4, x_part, 0)
        first = copies.start(to_x, pick_buffers[j][1], here.other_x)
        spread_one[j][1].wait_recv()
        def y_part(n, carry):
            at = block(n, 1 - y, x)
            total = term(j, 0, at, result[n, 1 - y, x, :, b]) + term(j, 2, at, from_x[n, 1 - y])
            to_y[n] = total.astype(bf16)
            return carry
        lax.fori_loop(0, 4, y_part, 0)
        spread_two[j] = first, copies.start(to_y, pick_buffers[j][2], here.other_y)

    def send_three(j):
        (from_y, from_x), (a, b) = spread_buffers[j], cols(j)
        from_z, more_a, more_b = pick_buffers[j]
        column = column_slots.at[j % 3]
        if j >= 3:
            for copy in spread_three[j - 3]:
                copies.sent(copy)
        for copy in spread_two[j]:
            copy.wait_recv()
        def body(n, carry):
            at = block(n, y, x)
            total = term(j, 0, at, result[n, y, x, :, a]) + term(j, 1, at, from_y[n, x])
            column[n, :, pl.ds(0, half)] = (total + more_a[n].astype(f32)).astype(bf16)
            total = term(j, 0, at, result[n, y, x, :, b]) + term(j, 2, at, from_x[n, y])
            column[n, :, pl.ds(half, half)] = (total + more_b[n].astype(f32)).astype(bf16)
            return carry
        lax.fori_loop(0, 4, body, 0)
        spread_three[j] = [
            copies.start(
                column.at[pl.ds(jnp.where(z == 0, 1, 0), 3)], from_z.at[pl.ds(0, 3)], here.near, here.end
            ),
            copies.start(column.at[here.end_z], from_z.at[0], here.own_end, here.middle),
        ]

    def send_merged(j):
        column, from_z = column_slots.at[j % 3], pick_buffers[j][0]
        def merge():
            spread_three[j][0].wait_recv()
            first, came = jnp.where(z == 1, 2, 0), jnp.where(z == 1, 1, 0)
            for k in range(2):
                total = column[first + k].astype(f32) + from_z[came + k].astype(f32)
                column[first + k] = total.astype(bf16)
        pl.when(here.middle)(merge)
        spread_three[j] += [
            copies.start(column.at[3 - z], from_z.at[3], here.across, here.middle),
            copies.start(column.at[3 - here.end_z], from_z.at[1], here.far_end, here.middle),
        ]

    def send_four(j):
        from_z, out = pick_buffers[j][0], mix_out if j < PIECES else grad_out
        columns = pl.ds(piece(j), width)
        _, to_end, across, to_far_end = spread_three[j]
        def in_middle():
            across.wait_recv()
            total = column_slots[j % 3, z].astype(f32) + from_z[jnp.where(z == 1, 0, 2)].astype(f32)
            out[:, columns] = total + from_z[3].astype(f32)
        pl.when(here.middle)(in_middle)
        def at_end():
            to_end.wait_recv()
            to_far_end.wait_recv()
            total = column_slots[j % 3, z].astype(f32) + from_z[0].astype(f32)
            out[:, columns] = total + from_z[1].astype(f32)
        pl.when(here.end)(at_end)

    told = [copies.start(table, tables.at[ex], peer) for peer in here.peers]
    kept_table = keep(table, tables.at[ex])
    held, ones, written, returned = {}, {}, [], []
    for n in range(2):
        load_gu(n)
        load_down(n)
    for step in range(2 * parts + 4):
        if step == 0:
            held[0] = stage_z(0)
        if step + 1 < parts:
            held[step + 1] = stage_z(step + 1)
        if step < parts:
            relay(step)
        if step == 1:
            kept_table.wait()
            for copy in told:
                copy.wait_recv()
            lax.fori_loop(0, 16, build, 0)
        if 0 <= step - 1 < parts:
            ones[step - 1] = stage_one(step - 1, *held[step - 1])
        if 0 <= step - 2 < parts:
            stage_two(step - 2, ones[step - 2])
        for behind, send in enumerate((send_one, send_two, send_three, send_merged, send_four)):
            if 0 <= step - parts - behind < parts:
                send(step - parts - behind)
        if 0 <= step - 1 < parts:
            pick_own(step - 1)
        if 0 <= step - 2 < parts:
            pick_moved(step - 2)
            if (step - 2) % PIECES == PIECES - 1:
                for j in range(step - 1 - PIECES, step - 1):
                    for copy in (*ones[j], held[j][0][4]):
                        copies.sent(copy)
                for device in (here.other_x, here.other_y, *here.other_z):
                    pl.semaphore_signal(
                        ready.at[(step - 2) // PIECES], inc=1, device_id=device, device_id_type=MESH
                    )
        p = step - 3
        if 0 <= p < parts:
            second[p][0].wait_recv()
            second[p][1].wait_recv()
        if 0 <= p < PIECES:
            gate_and_up(p)
        if p == PIECES - 1:
            lax.fori_loop(0, acc.shape[1] // 32, activate, 0)
            written.append(keep(rows_in, kept_outs[0]))
            written.append(keep(middle, kept_outs[2]))
            for n in range(PIECES):
                down(n)
        if PIECES <= p < parts:
            back_down(p - PIECES)
        if p == parts - 1:
            lax.fori_loop(0, acc.shape[1] // 32, back_activate, 0)
            written.append(keep(rows_cot, kept_outs[1]))
            written.append(keep(to_gate, kept_outs[3]))
            written.append(keep(to_up, kept_outs[4]))
            lax.fori_loop(0, 16, give_back, 0)
            returned = [copies.start(back.at[peer[1]], given.at[ex], peer) for peer in here.peers]
            written.append(keep(back.at[ex], given.at[ex]))
        if 0 <= step - 3 - parts < PIECES:
            back_rows(step - 3 - parts)
    for copy in returned:
        copy.wait_recv()
    for copy in written:
        copy.wait()
    copies.finish()


def run_experts(moe_in, cot_in, table, gate_full, up_full, down_full, capacity, collective_id):
    rows, model_width = moe_in.shape
    units, parts = gate_full.shape[1], 2 * PIECES
    width = model_width // PIECES
    half, slots = width // 2, 16 * capacity
    vmem, anywhere = pl.BlockSpec(memory_space=pltpu.VMEM), pl.BlockSpec(memory_space=pl.ANY)
    compact = (4, 2, 2, capacity, model_width)
    scratch = [
        pltpu.VMEM((16, *table.shape), f32),
        pltpu.VMEM((3, 16, capacity, rows), bf16),
        pltpu.VMEM((3, 16, rows, capacity), bf16),
        pltpu.VMEM((3, 16, rows, capacity), bf16),
        pltpu.VMEM((16, capacity, 1), f32),
        pltpu.VMEM((16, capacity, 1), f32),
        pltpu.VMEM((16, 8, rows), f32),
        pltpu.VMEM(compact, bf16),
        pltpu.VMEM(compact, bf16),
        pltpu.VMEM((2, slots, units), f32),
        pltpu.VMEM((slots, units), bf16),
        pltpu.VMEM((slots, units), bf16),
        pltpu.VMEM((slots, units), bf16),
        pltpu.VMEM(compact, bf16),
        pltpu.VMEM((2, 2, width, units), bf16),
        pltpu.VMEM((2, units, width), bf16),
        pltpu.VMEM((2, 2, 4, 2, capacity, half), bf16),
        pltpu.VMEM((2, 2, 4, rows, half), bf16),
        pltpu.VMEM((3, 4, rows, width), bf16),
    ]
    for _ in range(parts):
        scratch += [
            pltpu.VMEM((4, rows, width), bf16),
            pltpu.VMEM((4, rows, half), bf16),
            pltpu.VMEM((4, rows, half), bf16),
        ]
    scratch += [pltpu.VMEM((4, 2, capacity, half), bf16)] * (2 * parts)
    copies = 17 * parts + 30
    shape = jax.ShapeDtypeStruct
    grad, mixture, given, rows_in, rows_grad, *units_out = pl.pallas_call(
        functools.partial(expert_kernel, capacity),
        out_shape=[shape((rows, model_width), f32)] * 2
        + [shape((16, 8, rows), f32)]
        + [shape(compact, bf16)] * 2
        + [shape((slots, units), bf16)] * 3,
        in_specs=[vmem] * 3 + [anywhere] * 3,
        out_specs=[vmem] * 3 + [anywhere] * 5,
        scratch_shapes=scratch
        + [
            pltpu.SemaphoreType.DMA((copies,)),
            pltpu.SemaphoreType.DMA((copies,)),
            pltpu.SemaphoreType.DMA((parts + 7,)),
            pltpu.SemaphoreType.DMA((2, 3)),
            pltpu.SemaphoreType.REGULAR((2,)),
        ],
        compiler_params=pltpu.CompilerParams(
            collective_id=collective_id, has_side_effects=True, vmem_limit_bytes=62 * 2**20
        ),
    )(table, moe_in, cot_in, gate_full, up_full, down_full)
    rows_in, rows_grad = rows_in.reshape(slots, -1), rows_grad.reshape(slots, -1)
    return grad, mixture, given[:, 0], rows_in, rows_grad, *units_out


def tn(left, right):
    return lax.dot_general(left, right, (((0,), (0,)), ((), ())), preferred_element_type=f32)


def accumulate(target, blocks, arrived):
    def add(n, carry):
        for into, source in blocks:
            value = target[(n,) + into].astype(f32) + arrived[(n,) + source].astype(f32)
            target[(n,) + into] = value.astype(target.dtype)
        return carry
    lax.fori_loop(0, 4, add, 0)


ROW = 16


def finish_kernel(*refs):
    (
        grad_branch, mixed, attn_in, hidden_in, query, key, value, normed_query, normed_key,
        scale_query, scale_key, seen, cosine, sine, grad_after, gains, small_in, out_rows,
        query_w, key_w, value_w, output_w, rows_in, rows_grad, middle, grad_gate, grad_up,
    ) = refs[:27]
    weight_outs, small_out, given_out, given_grad = refs[27:31], *refs[31:34]
    gate_out, up_out, down_out, expert_landing = refs[34:38]
    refs = refs[38:]
    sides, lefts, grads, mixed_grad, query_normed, key_normed, attn_grad, grad_rows = refs[:8]
    owns, small_buf, small_own, small_core, w_slots = refs[8:13]
    left_slots, right_slots, send_slots, came, result = refs[13:18]
    parts = 17
    landing, refs = refs[18 : 18 + 5 * parts], refs[18 + 5 * parts :]
    send_sems, recv_sems, local_sems, load_sems = refs
    here = Place()
    rep, x, y, z, ex = here.rep, here.x, here.y, here.z, here.ex
    model_width = grad_branch.shape[1]
    columns = model_width // 4
    enter([*here.peers, here.other_core])
    copies = Copies(send_sems, recv_sems)
    local = []

    def keep(source, target):
        copy = pltpu.make_async_copy(source, target, local_sems.at[len(local)])
        copy.start()
        local.append(copy)
        return copy

    returned = []

    def give(source, target):
        keep(source.at[ex], target.at[ex])
        for peer in here.peers:
            returned.append(copies.start(source.at[peer[1]], target.at[ex], peer))

    mine, theirs = (pl.ds(pl.multiple_of(r * 1024, 1024), 1024) for r in (rep, 1 - rep))
    core_left = [
        copies.start(ref.at[:, theirs], sides.at[n], here.other_core)
        for n, ref in enumerate((mixed, attn_in))
    ]
    core_grad = {}

    def share(n):
        core_grad[n] = copies.start(
            grads.at[n, pl.ds(0, 128)], grads.at[n, pl.ds(128, 128)], here.other_core
        )

    def turn_left(n, ref):
        core_left[n].wait_recv()
        def body(k, carry):
            at = pl.multiple_of(rep * 1024 + k * 128, 128)
            lefts[n, k, :, pl.ds(0, 128)] = ref[:, pl.ds(at, 128)].astype(f32).T.astype(bf16)
            at = pl.multiple_of(k * 128, 128)
            lefts[n, k, :, pl.ds(128, 128)] = sides[n, :, pl.ds(at, 128)].astype(f32).T.astype(bf16)
            return carry
        lax.fori_loop(0, 8, body, 0)

    stream, loads = [(w, n) for w in (output_w, value_w, query_w, key_w) for n in range(4)], {}

    def load(n):
        if n < len(stream):
            w, k = stream[n]
            loads[n] = pltpu.make_async_copy(
                w.at[pl.ds(k * columns, columns)], w_slots.at[n % 2], load_sems.at[n % 2]
            )
            loads[n].start()

    def back_mixed():
        for k in range(4):
            loads[k].wait()
            at = pl.ds(k * columns, columns)
            mixed_grad[:, at] = nt(grad_branch[...], w_slots[k % 2]).astype(bf16)
            load(k + 2)

    def unrotate(grad):
        turned = grad * sine[...]
        lane = lax.broadcasted_iota(jnp.int32, turned.shape, 1)
        sign = jnp.where(lane < HEAD_DIM // 2, 1.0, -1.0)
        return grad * cosine[...] + sign * pltpu.roll(turned, HEAD_DIM // 2, 1)

    def heads(first, count):
        def body(n, carry):
            at = pl.ds(pl.multiple_of((first + n) * HEAD_DIM, HEAD_DIM), HEAD_DIM)
            q, k, v, grad = query[:, at], key[:, at], value[:, at], mixed_grad[:, at]
            scores = jnp.where(seen[...] > 0, nt(q, k) * HEAD_DIM ** (-0.5), masked_score)
            weights = jnp.exp(scores - jnp.max(scores, axis=1, keepdims=True))
            probs = weights / jnp.sum(weights, axis=1, keepdims=True)
            grads[2, pl.ds(0, 128), at] = tn(probs.astype(bf16), grad).astype(bf16)
            grad_att = nt(grad, v)
            grad_scores = probs * (grad_att - jnp.sum(probs * grad_att, axis=1, keepdims=True))
            grad_scores = grad_scores.astype(bf16)
            query_normed[:, at] = unrotate(nn(grad_scores, k) * HEAD_DIM ** (-0.5))
            key_normed[:, at] = unrotate(tn(grad_scores, q) * HEAD_DIM ** (-0.5))
            return carry
        lax.fori_loop(0, count, body, 0)

    sums = {}

    def back_norm(n, grad_ref, normed_ref, scale_ref):
        def body(k, total):
            rows = pl.ds(pl.multiple_of(k * ROW, ROW), ROW)
            grad, normed = grad_ref[rows], normed_ref[rows]
            total = total + jnp.sum(grad * normed, axis=0, keepdims=True)
            grad = grad * gains[pl.ds(n, 1)]
            mean = jnp.mean(grad * normed, axis=1, keepdims=True)
            grads[n, rows] = (scale_ref[rows] * (grad - normed * mean)).astype(bf16)
            return total
        start = jnp.zeros((1, model_width), f32)
        sums[n] = lax.fori_loop(0, 128 // ROW, body, start)

    def back_attn(n, at_stream, fresh):
        for k in range(4):
            loads[at_stream + k].wait()
            at = pl.ds(k * columns, columns)
            grad = nt(grads[n, pl.ds(0, 128)], w_slots[(at_stream + k) % 2])
            attn_grad[:, at] = grad if fresh else attn_grad[:, at] + grad
            load(at_stream + k + 2)

    def back_hidden():
        def body(k, total):
            rows = pl.ds(pl.multiple_of(k * ROW, ROW), ROW)
            hidden, grad = hidden_in[rows].astype(f32), attn_grad[rows]
            scale = lax.rsqrt(jnp.mean(hidden * hidden, axis=1, keepdims=True) + epsilon)
            normed = hidden * scale
            total = total + jnp.sum(grad * normed, axis=0, keepdims=True)
            grad = grad * gains[pl.ds(2, 1)]
            mean = jnp.mean(grad * normed, axis=1, keepdims=True)
            grad = grad_after[rows] + scale * (grad - normed * mean)
            grad = grad.astype(bf16).reshape(2, 8, model_width)
            grad_rows[pl.ds(2 * k, 2)] = grad
            return total
        start = jnp.zeros((1, model_width), f32)
        sums[2] = lax.fori_loop(0, 128 // ROW, body, start)
        give(grad_rows, given_grad)
        pad = jnp.zeros((125, 128), f32)
        for k in range(model_width // 128):
            rows = [sums[n][:, k * 128 : k * 128 + 128] for n in range(3)]
            block = jnp.concatenate([*rows, pad], axis=0).T.reshape(2, 64, 128)
            at = (k // 8, k // 2 % 4, k % 2)
            small_buf[at] = small_in[at] + block

    def halves():
        return pl.ds(0, 32), pl.ds(32, 32)

    one, two, last = {}, {}, {}

    def own_of(j):
        return owns.at[j % 4] if j < 16 else small_own

    def sum_one(j):
        own, (upper, lower) = own_of(j), halves()
        if j < 16:
            n, which = (3, 0) if j < 4 else ((2, 1), (0, 1), (1, 1))[j // 4 - 1]
            at = pl.ds(j % 4 * columns, columns)
            if j % 4 == 0:
                core_grad[n].wait_recv()
            if j >= 4:
                for copy in (*one[j - 4], *two[j - 4], *last[j - 4]):
                    copies.sent(copy)
            def body(k, carry):
                own[k // 2, k % 2] = nn(lefts[which, k], grads[n, :, at]).astype(bf16).reshape(2, 64, columns)
                return carry
            lax.fori_loop(0, 8, body, 0)
        else:
            core_grad["small"].wait_recv()
            def add(k, carry):
                own[k] = small_buf[rep, k] + small_core[k]
                return carry
            lax.fori_loop(0, 4, add, 0)
        one[j] = (
            copies.start(own.at[:, 1 - y, :, upper], landing[5 * j], here.other_y),
            copies.start(own.at[:, :, 1 - x, lower], landing[5 * j + 1], here.other_x),
        )

    def sum_two(j):
        own, (upper, lower) = own_of(j), halves()
        from_y, from_x = landing[5 * j], landing[5 * j + 1]
        one[j][0].wait_recv()
        accumulate(own, [((y, 1 - x, upper), (1 - x,))], from_y)
        a = copies.start(own.at[:, y, 1 - x, upper], landing[5 * j + 2], here.other_x)
        one[j][1].wait_recv()
        accumulate(own, [((1 - y, x, lower), (1 - y,))], from_x)
        b = copies.start(own.at[:, 1 - y, x, lower], landing[5 * j + 3], here.other_y)
        accumulate(own, [((y, x, upper), (x,)), ], from_y)
        accumulate(own, [((y, x, lower), (y,)), ], from_x)
        two[j] = a, b

    def sum_three(j):
        own, (upper, lower) = own_of(j), halves()
        two[j][0].wait_recv()
        accumulate(own, [((y, x, upper), ())], landing[5 * j + 2])
        two[j][1].wait_recv()
        accumulate(own, [((y, x, lower), ())], landing[5 * j + 3])
        last[j] = [
            copies.start(own.at[(z + k) % 4, y, x], landing[5 * j + 4].at[k - 1], here.other_z[k - 1])
            for k in range(1, 4)
        ]

    def sum_four(j):
        own, arrived = own_of(j), landing[5 * j + 4]
        for copy in last[j]:
            copy.wait_recv()
        total = own[z, y, x].astype(f32) + arrived[0].astype(f32)
        total = total + arrived[1].astype(f32) + arrived[2].astype(f32)
        if j == 16:
            small_out[...] = total
        else:
            n = (3, 2, 0, 1)[j // 4]
            weight_outs[n][:, pl.ds(j % 4 * columns, columns)] = total

    tasks, task_loads, sent_halves, stored = [], {}, {}, {}
    for side in range(2):
        for k in range(2):
            for kind in range(3):
                tasks.append((side, k, kind))

    def task_load(n):
        if n < len(tasks):
            side, k, kind = tasks[n]
            whose = rep if side else 1 - rep
            if kind < 2:
                left = rows_in.at[:, pl.ds(pl.multiple_of(whose * 1024 + k * 512, 512), 512)]
                right = (grad_gate, grad_up)[kind]
            else:
                left = middle.at[:, pl.ds(pl.multiple_of(whose * 512, 512), 512)]
                right = rows_grad.at[:, pl.ds(k * 1024, 1024)]
            task_loads[n] = (
                pltpu.make_async_copy(left, left_slots.at[n % 2], load_sems.at[2 + n % 2]),
                pltpu.make_async_copy(right, right_slots.at[n % 2], load_sems.at[4 + n % 2]),
            )
            for copy in task_loads[n]:
                copy.start()

    def task(n):
        side, k, kind = tasks[n]
        for copy in task_loads[n]:
            copy.wait()
        left, right = left_slots.at[n % 2], right_slots.at[n % 2]
        if side == 0:
            target = send_slots.at[n % 2]
            if n >= 2:
                copies.sent(sent_halves[n - 2])
            def body(m, carry):
                at = pl.ds(pl.multiple_of(m * 256, 256), 256)
                target[at] = tn(left[:, at], right[...]).astype(bf16)
                return carry
            lax.fori_loop(0, 2, body, 0)
            sent_halves[n] = copies.start(target, expert_landing.at[n], here.other_core)
        else:
            at = n - len(tasks) // 2
            sent_halves[at].wait_recv()
            back = pltpu.make_async_copy(expert_landing.at[at], came, load_sems.at[6])
            back.start()
            if n - 1 in stored:
                stored[n - 1].wait()
            back.wait()
            def body(m, carry):
                rows = pl.ds(pl.multiple_of(m * 256, 256), 256)
                result[rows] = tn(left[:, rows], right[...]) + came[rows].astype(f32)
                return carry
            lax.fori_loop(0, 2, body, 0)
            if kind < 2:
                target = (gate_out, up_out)[kind].at[pl.ds(k * 512, 512)]
            else:
                target = down_out.at[:, pl.ds(k * 1024, 1024)]
            stored[n] = pltpu.make_async_copy(result, target, load_sems.at[7])
            stored[n].start()
        task_load(n + 2)

    grads[3, pl.ds(0, 128)] = grad_branch[...]
    share(3)
    for n in range(2):
        load(n)
        task_load(n)
    turn_left(0, mixed)
    for step in range(parts + 3):
        for behind, stage in enumerate((sum_one, sum_two, sum_three, sum_four)):
            if 0 <= step - behind < parts:
                stage(step - behind)
        if step == 0:
            give(out_rows, given_out)
            back_mixed()
            turn_left(1, attn_in)
        elif step == 1:
            heads(0, 8)
        elif step == 2:
            heads(8, 8)
            share(2)
        elif step == 3:
            back_norm(0, query_normed, normed_query, scale_query)
            share(0)
            back_norm(1, key_normed, normed_key, scale_key)
            share(1)
        elif step == 4:
            back_attn(2, 4, True)
        elif step == 5:
            back_attn(0, 8, False)
        elif step == 6:
            back_attn(1, 12, False)
        elif step == 7:
            back_hidden()
            core_grad["small"] = copies.start(small_buf.at[1 - rep], small_core, here.other_core)
        elif step < 8 + len(tasks) // 2:
            task(2 * (step - 8))
            task(2 * (step - 8) + 1)
    stored[len(tasks) - 1].wait()
    for copy in returned:
        copy.wait_recv()
    for copy in local:
        copy.wait()
    copies.finish()


def run_finish(arrays, weights, expert, collective_id):
    rows, model_width = arrays[0].shape
    columns = model_width // 4
    vmem, anywhere = pl.BlockSpec(memory_space=pltpu.VMEM), pl.BlockSpec(memory_space=pl.ANY)
    shape, tile = jax.ShapeDtypeStruct, (4, 2, 2, 64)
    scratch = [
        pltpu.VMEM((2, rows, 1024), bf16),
        pltpu.VMEM((2, 8, 128, 256), bf16),
        pltpu.VMEM((4, 2 * rows, model_width), bf16),
        pltpu.VMEM((rows, model_width), bf16),
        pltpu.VMEM((rows, model_width), f32),
        pltpu.VMEM((rows, model_width), f32),
        pltpu.VMEM((rows, model_width), f32),
        pltpu.VMEM((16, 8, model_width), bf16),
        pltpu.VMEM((4, *tile, columns), bf16),
        pltpu.VMEM((2, *tile, 128), f32),
        pltpu.VMEM((*tile, 128), f32),
        pltpu.VMEM((*tile, 128), f32),
        pltpu.VMEM((2, columns, model_width), bf16),
        pltpu.VMEM((2, 1024, 512), bf16),
        pltpu.VMEM((2, 1024, 1024), bf16),
        pltpu.VMEM((2, 512, 1024), bf16),
        pltpu.VMEM((512, 1024), bf16),
        pltpu.VMEM((512, 1024), f32),
    ]
    for j in range(17):
        width, dtype = (columns, bf16) if j < 16 else (128, f32)
        scratch += [
            pltpu.VMEM((4, 2, 32, width), dtype),
            pltpu.VMEM((4, 2, 32, width), dtype),
            pltpu.VMEM((4, 32, width), dtype),
            pltpu.VMEM((4, 32, width), dtype),
            pltpu.VMEM((3, 64, width), dtype),
        ]
    copies = 7 * 17 + 30 + 7 + 6
    return pl.pallas_call(
        finish_kernel,
        out_shape=[shape((64, model_width), f32)] * 4
        + [shape((64, 128), f32)]
        + [shape((16, 8, model_width), bf16)] * 2
        + [shape((1024, 1024), f32)] * 2
        + [shape((512, 2048), f32), shape((6, 512, 1024), bf16)],
        in_specs=[vmem] * len(arrays) + [anywhere] * (len(weights) + len(expert)),
        out_specs=[vmem] * 5 + [anywhere] * 6,
        scratch_shapes=scratch
        + [
            pltpu.SemaphoreType.DMA((copies,)),
            pltpu.SemaphoreType.DMA((copies,)),
            pltpu.SemaphoreType.DMA((2,)),
            pltpu.SemaphoreType.DMA((8,)),
        ],
        compiler_params=pltpu.CompilerParams(
            collective_id=collective_id, has_side_effects=True, vmem_limit_bytes=62 * 2**20
        ),
    )(*arrays, *weights, *expert)


def start_kernel(*refs):
    query_w, key_w, value_w, output_w, gains_w, rows_in, cot_in, seen, cosine, sine = refs[:10]
    fulls, (hidden_out, cot_out), refs = refs[10:15], refs[15:17], refs[17:]
    gain_rows, attn_in, query, key, value, mixed, normed_query, normed_key, scale_query, scale_key = refs[:10]
    product, slots, came_rows, gain_cols = refs[10:14]
    send_sems, recv_sems, local_sems, load_sems = refs[14:]
    here = Place()
    rep, x, y, z, ex = here.rep, here.x, here.y, here.z, here.ex
    model_width = query_w.shape[1]
    enter([*here.peers, here.other_core])
    copies = Copies(send_sems, recv_sems)
    local = []

    def keep(source, target):
        copy = pltpu.make_async_copy(source, target, local_sems.at[len(local)])
        copy.start()
        local.append(copy)
        return copy

    def give(source, target):
        return [keep(source.at[ex], target.at[ex])] + [
            copies.start(source.at[peer[1]], target.at[ex], peer) for peer in here.peers
        ]

    def take(moved):
        moved[0].wait()
        for copy in moved[1:]:
            copy.wait_recv()

    shards = (query_w, key_w, value_w, output_w, gains_w)
    parts = [(4, 0, 64)] + [(i, k * 16, 16) for i in range(4) for k in range(4)]
    first_stage, one, two, cores = {}, {}, {}, {}

    def spans(j):
        i, first, rows = parts[j]
        half = rows // 2
        return fulls[i].at[rep], pl.ds(first, rows), pl.ds(first, half), pl.ds(first + half, half)

    def stage_z(j):
        full, rows, _, _ = spans(j)
        source, target = shards[parts[j][0]].at[rows], full.at[z, y, x, rows]
        sent = [copies.start(source, target, device) for device in here.other_z]
        first_stage[j] = sent, keep(source, target)

    def stage_one(j):
        full, rows, upper, lower = spans(j)
        sent, kept = first_stage[j]
        kept.wait()
        for copy in sent:
            copy.wait_recv()
        a, b, own = full.at[:, y, x, upper], full.at[:, y, x, lower], full.at[:, y, x, rows]
        one[j] = copies.start(a, a, here.other_x), copies.start(b, b, here.other_y)
        cores[j] = [copies.start(own, own, here.other_core)]

    def stage_two(j):
        full, _, upper, lower = spans(j)
        one[j][0].wait_recv()
        a = full.at[:, y, :, upper]
        two_a = copies.start(a, a, here.other_y)
        one[j][1].wait_recv()
        b = full.at[:, :, x, lower]
        two[j] = two_a, copies.start(b, b, here.other_x)
        for c in (full.at[:, y, 1 - x, upper], full.at[:, 1 - y, x, lower]):
            cores[j].append(copies.start(c, c, here.other_core))

    def stage_three(j):
        full, _, upper, lower = spans(j)
        two[j][0].wait_recv()
        a = full.at[:, 1 - y, :, upper]
        cores[j].append(copies.start(a, a, here.other_core))
        two[j][1].wait_recv()
        b = full.at[:, :, 1 - x, lower]
        cores[j].append(copies.start(b, b, here.other_core))

    def complete(j):
        for copy in cores[j]:
            copy.wait_recv()

    def turn_gains():
        complete(0)
        copy = pltpu.make_async_copy(fulls[4], gain_cols, load_sems.at[2])
        copy.start()
        copy.wait()
        for k in range(model_width // 128):
            block = gain_cols[k // 8, k // 2 % 4, k % 2].reshape(128, 128).astype(f32)
            gain_rows[:, k * 128 : k * 128 + 128] = block.T[:8]

    def norm_rows(moved):
        take(moved)
        copy = pltpu.make_async_copy(hidden_out, came_rows, load_sems.at[2])
        copy.start()
        copy.wait()
        def body(k, carry):
            hidden = came_rows[pl.ds(2 * k, 2)].reshape(ROW, model_width).astype(f32)
            scale = lax.rsqrt(jnp.mean(hidden * hidden, axis=1, keepdims=True) + epsilon)
            rows = pl.ds(pl.multiple_of(k * ROW, ROW), ROW)
            attn_in[rows] = (hidden * scale * gain_rows[pl.ds(2, 1)]).astype(bf16)
            return carry
        lax.fori_loop(0, 128 // ROW, body, 0)

    def load(i, n):
        copy = pltpu.make_async_copy(
            fulls[i].at[n // 2, pl.ds(n % 2 * 2, 2)], slots.at[n % 2], load_sems.at[n % 2]
        )
        copy.start()
        return copy

    def project(i):
        for j in range(1 + 4 * i, 5 + 4 * i):
            complete(j)
        loads = {n: load(i, n) for n in range(2)}
        for n in range(4):
            loads[n].wait()
            left = attn_in[:, pl.ds(n * 512, 512)]
            for k in range(4):
                at = pl.ds(k * 512, 512)
                grown = nn(left, slots[n % 2, :, :, :, :, at].reshape(512, 512))
                product[:, at] = grown if n == 0 else product[:, at] + grown
            if n + 2 < 4:
                loads[n + 2] = load(i, n + 2)

    def norm_heads(n, normed_ref, scale_ref, low_ref):
        lane = lax.broadcasted_iota(jnp.int32, (ROW, HEAD_DIM), 1)
        sign = jnp.where(lane < HEAD_DIM // 2, -1.0, 1.0)
        def body(k, carry):
            rows = pl.ds(pl.multiple_of(k * ROW, ROW), ROW)
            pre = product[rows]
            scale = lax.rsqrt(jnp.mean(pre * pre, axis=1, keepdims=True) + epsilon)
            normed = pre * scale
            normed_ref[rows], scale_ref[rows] = normed, scale
            gained = normed * gain_rows[pl.ds(n, 1)]
            for h in range(HEADS):
                at = slice(h * HEAD_DIM, (h + 1) * HEAD_DIM)
                turned = sign * pltpu.roll(gained[:, at], HEAD_DIM // 2, 1)
                low_ref[rows, at] = (gained[:, at] * cosine[rows] + turned * sine[rows]).astype(bf16)
            return carry
        lax.fori_loop(0, 128 // ROW, body, 0)

    def heads(first, count):
        def body(n, carry):
            at = pl.ds(pl.multiple_of((first + n) * HEAD_DIM, HEAD_DIM), HEAD_DIM)
            scores = nt(query[:, at], key[:, at]) * HEAD_DIM ** (-0.5)
            scores = jnp.where(seen[...] > 0, scores, masked_score)
            weights = jnp.exp(scores - jnp.max(scores, axis=1, keepdims=True))
            probs = weights / jnp.sum(weights, axis=1, keepdims=True)
            mixed[:, at] = nn(probs.astype(bf16), value[:, at]).astype(bf16)
            return carry
        lax.fori_loop(0, count, body, 0)

    stage_z(0)
    stage_z(1)
    moved_rows = give(rows_in, hidden_out)
    moved_cot = []
    for step in range(len(parts) + 3):
        if 2 <= step < len(parts):
            stage_z(step)
        for behind, stage in ((1, stage_one), (2, stage_two), (3, stage_three)):
            if 0 <= step - behind < len(parts):
                stage(step - behind)
        if step == 4:
            turn_gains()
            moved_cot = give(cot_in, cot_out)
        elif step == 6:
            norm_rows(moved_rows)
        elif step == 8:
            project(0)
        elif step == 9:
            norm_heads(0, normed_query, scale_query, query)
        elif step == 12:
            project(1)
        elif step == 13:
            norm_heads(1, normed_key, scale_key, key)
        elif step == 16:
            project(2)
            value[...] = product[...].astype(bf16)
        elif step == 17:
            heads(0, 6)
        elif step == 18:
            heads(6, 6)
        elif step == 19:
            heads(12, 4)
    for j in range(13, 17):
        complete(j)
    take(moved_cot)
    copies.finish()


def run_start(shards, rows, cot, visible, cosine, sine, collective_id):
    model_width = shards[0].shape[1]
    vmem, anywhere = pl.BlockSpec(memory_space=pltpu.VMEM), pl.BlockSpec(memory_space=pl.ANY)
    shape = jax.ShapeDtypeStruct
    own_rows = [(shape((128, model_width), dtype)) for dtype in (bf16,) * 5 + (f32,) * 2]
    *fulls, hidden_in, cot_in, gain_rows, attn_in, query, key, value, mixed, nq, nk, sq, sk = pl.pallas_call(
        start_kernel,
        out_shape=[shape((2, 4, 2, 2) + a.shape, a.dtype) for a in shards]
        + [shape(rows.shape, bf16)] * 2
        + [shape((8, model_width), f32)]
        + own_rows
        + [shape((128, 1), f32)] * 2,
        in_specs=[anywhere] * 7 + [vmem] * 3,
        out_specs=[anywhere] * 7 + [vmem] * 10,
        scratch_shapes=[
            pltpu.VMEM((128, model_width), f32),
            pltpu.VMEM((2, 2, 2, 2, 64, model_width), bf16),
            pltpu.VMEM(rows.shape, bf16),
            pltpu.VMEM((2, 4, 2, 2, 64, 128), bf16),
            pltpu.SemaphoreType.DMA((12 * 17 + 30,)),
            pltpu.SemaphoreType.DMA((12 * 17 + 30,)),
            pltpu.SemaphoreType.DMA((19,)),
            pltpu.SemaphoreType.DMA((3,)),
        ],
        compiler_params=pltpu.CompilerParams(
            collective_id=collective_id, has_side_effects=True, vmem_limit_bytes=40 * 2**20
        ),
    )(*shards, rows, cot, visible, cosine, sine)
    fulls = [a.reshape(-1, a.shape[-1]) for a in fulls]
    hidden_in, cot_in = (a.reshape(128, model_width) for a in (hidden_in, cot_in))
    return fulls, hidden_in, cot_in, gain_rows, attn_in, query, key, value, mixed, nq, nk, sq, sk


def has_kernels():
    return (lax.axis_size("rep"), lax.axis_size("ex")) == (2, 16)


def exchange(array):
    return lax.all_to_all(array, "ex", split_axis=0, concat_axis=0, tiled=True)


def start(shards, gains, inbound_rows, inbound_cot, visible, cosine, sine):
    block_rows, model_width = inbound_rows.shape[1:]
    row_count = inbound_rows.shape[0] * block_rows
    if has_kernels():
        wide = jnp.pad(gains, ((0, 0), (0, 128 - gains.shape[1])))
        full, hidden_in, cot_in, gain_rows, attn_in, *qkv, mixed, nq, nk, sq, sk = run_start(
            [*shards, wide], inbound_rows, inbound_cot, visible.astype(f32), cosine[:, 0], sine[:, 0], 1
        )
        *weights, wide = full
        qkv = [a.reshape(row_count, HEADS, HEAD_DIM) for a in qkv]
        router = wide[:, 4 : gains.shape[1]]
        return weights, gain_rows[:4], router, hidden_in, cot_in, attn_in, qkv, mixed, (nq, nk, sq, sk)
    gather = functools.partial(lax.all_gather, axis_name=("rep", "ex"), axis=0, tiled=True)
    weights = query_full, key_full, value_full, _ = [gather(a) for a in shards]
    gains = gather(jnp.pad(gains, ((0, 0), (0, -gains.shape[1] % 128))))[:, : gains.shape[1]]
    gain_rows = gains[:, :4].astype(f32).T
    query_scale, key_scale, attn_scale, _ = gain_rows
    hidden_in, cot_in = (exchange(a).reshape(row_count, model_width) for a in (inbound_rows, inbound_cot))
    hidden = hidden_in.astype(f32)
    normed_attn, scale_attn = normalize(hidden)
    attn_in = (normed_attn * attn_scale).astype(bf16)
    query_pre = jnp.dot(attn_in, query_full, preferred_element_type=f32)
    key_pre = jnp.dot(attn_in, key_full, preferred_element_type=f32)
    value_pre = jnp.dot(attn_in, value_full, preferred_element_type=f32)
    normed_query, scale_query = normalize(query_pre)
    normed_key, scale_key = normalize(key_pre)
    query_norm = (normed_query * query_scale).reshape(row_count, HEADS, HEAD_DIM)
    key_norm = (normed_key * key_scale).reshape(row_count, HEADS, HEAD_DIM)
    query_low = (query_norm * cosine + rotate_half(query_norm) * sine).astype(bf16)
    key_low = (key_norm * cosine + rotate_half(key_norm) * sine).astype(bf16)
    value_low = value_pre.astype(bf16).reshape(row_count, HEADS, HEAD_DIM)
    scores = attention_scores(query_low, key_low, visible)
    peak = jnp.max(scores, axis=-1, keepdims=True)
    weights_exp = jnp.exp(scores - peak)
    probs = weights_exp / jnp.sum(weights_exp, axis=-1, keepdims=True)
    probs_low = probs.astype(bf16)
    mixed = jnp.einsum("hqk,khd->qhd", probs_low, value_low, preferred_element_type=f32)
    mixed = mixed.reshape(row_count, model_width).astype(bf16)
    qkv = query_low, key_low, value_low
    norms = normed_query, normed_key, scale_query, scale_key
    return weights, gain_rows, gains[:, 4:], hidden_in, cot_in, attn_in, qkv, mixed, norms


def slots_of(tables, capacity):
    experts, me = tables.shape[1] // 2, lax.axis_index("ex")
    gates = lax.dynamic_index_in_dim(tables, me, 1, keepdims=True)
    slots = lax.dynamic_index_in_dim(tables, experts + me, 1, keepdims=True)
    return slots == jnp.arange(capacity, dtype=f32)[None, :, None], gates


def experts_of_group(moe_in, cot_in, table, gate_full, up_full, down_full, capacity):
    if has_kernels():
        return run_experts(moe_in, cot_in, table, gate_full, up_full, down_full, capacity, 2)
    tables = lax.all_gather(table, "ex", axis=0)
    picked, gate_rows = slots_of(tables, capacity)
    picked_low = picked.astype(bf16)
    slot_gate = jnp.sum(jnp.where(picked, gate_rows, 0.0), axis=2).reshape(-1, 1)

    def pick(rows):
        rows = lax.all_gather(rows, "ex", axis=0)
        rows = jnp.einsum("sct,std->scd", picked_low, rows, preferred_element_type=f32)
        return rows.astype(bf16).reshape(-1, rows.shape[-1])

    def spread(rows):
        rows = rows.reshape(*picked_low.shape[:2], -1)
        rows = jnp.einsum("sct,scd->std", picked_low, rows, preferred_element_type=f32)
        return lax.psum_scatter(rows.astype(bf16), "ex", scatter_dimension=0).astype(f32)

    rows_in, rows_cot = pick(moe_in), pick(cot_in)
    gate_pre = jnp.dot(rows_in, gate_full, preferred_element_type=f32)
    up_pre = jnp.dot(rows_in, up_full, preferred_element_type=f32)
    sigma = jax.nn.sigmoid(gate_pre)
    silu = gate_pre * sigma
    middle = (silu * up_pre).astype(bf16)
    expert_out = jnp.dot(middle, down_full, preferred_element_type=f32).astype(bf16)
    slot_grad = jnp.sum(rows_cot.astype(f32) * expert_out.astype(f32), axis=1)
    rows_grad = (slot_gate * rows_cot.astype(f32)).astype(bf16)
    grad_middle = jnp.dot(rows_grad, down_full.T, preferred_element_type=f32)
    grad_gate_low = (grad_middle * up_pre * sigma * (1.0 + gate_pre * (1.0 - sigma))).astype(bf16)
    grad_up_low = (grad_middle * silu).astype(bf16)
    grad_rows = jnp.dot(grad_gate_low, gate_full.T, preferred_element_type=f32)
    grad_rows = grad_rows + jnp.dot(grad_up_low, up_full.T, preferred_element_type=f32)
    weighted = slot_gate * expert_out.astype(f32)
    slot_grad = slot_grad.reshape(*picked.shape[:2], 1)
    back = exchange(jnp.sum(jnp.where(picked, slot_grad, 0.0), axis=1))
    sums = spread(grad_rows.astype(bf16)), spread(weighted.astype(bf16))
    return *sums, back, rows_in, rows_grad, middle, grad_gate_low, grad_up_low


def finish(
    grad_branch, mixed, attn_in, hidden_in, query_low, key_low, value_low, normed_query, normed_key,
    scale_query, scale_key, visible, cosine, sine, grad_after, query_scale, key_scale, attn_scale,
    small, output, query_full, key_full, value_full, output_full,
    rows_in, rows_grad, middle, grad_gate_low, grad_up_low,
):
    row_count, model_width = mixed.shape
    group_size = lax.axis_size("ex")
    block_rows = row_count // group_size
    if has_kernels():
        wide = jnp.pad(small, ((0, 0), (3, 128 - 3 - small.shape[1])))
        gains = jnp.stack([query_scale, key_scale, attn_scale], axis=0)
        arrays = [
            grad_branch, mixed, attn_in, hidden_in,
            *(a.reshape(row_count, model_width) for a in (query_low, key_low, value_low)),
            normed_query, normed_key, scale_query, scale_key, visible.astype(f32),
            cosine[:, 0], sine[:, 0], grad_after, jnp.pad(gains, ((0, 5), (0, 0))),
            wide.reshape(2, 4, 2, 2, 64, 128), output.reshape(group_size, block_rows, model_width),
        ]
        *weights, summed, given_out, given_grad, gate, up, down, _ = run_finish(
            arrays,
            [query_full, key_full, value_full, output_full],
            [rows_in, rows_grad, middle, grad_gate_low, grad_up_low],
            3,
        )
        rows = [a.reshape(row_count, model_width) for a in (given_out, given_grad)]
        return weights, summed[:, : 3 + small.shape[1]], rows, (gate, up, down)
    both = ("rep", "ex")
    scores = attention_scores(query_low, key_low, visible)
    probs = jax.nn.softmax(scores, axis=-1)
    probs_low = probs.astype(bf16)
    normed_attn, scale_attn = normalize(hidden_in.astype(f32))
    grad_mixed = (
        jnp.dot(grad_branch, output_full.T, preferred_element_type=f32)
        .astype(bf16)
        .reshape(row_count, HEADS, HEAD_DIM)
    )
    grad_value = jnp.einsum("hqk,qhd->khd", probs_low, grad_mixed, preferred_element_type=f32)
    grad_att = jnp.einsum("qhd,khd->hqk", grad_mixed, value_low, preferred_element_type=f32)
    grad_scores = (probs * (grad_att - jnp.sum(probs * grad_att, axis=-1, keepdims=True))).astype(
        bf16
    )
    grad_query_rot = jnp.einsum(
        "hqk,khd->qhd", grad_scores, key_low, preferred_element_type=f32
    ) * HEAD_DIM ** (-0.5)
    grad_key_rot = jnp.einsum(
        "hqk,qhd->khd", grad_scores, query_low, preferred_element_type=f32
    ) * HEAD_DIM ** (-0.5)
    grad_query_normed = (grad_query_rot * cosine + rotate_back(grad_query_rot * sine)).reshape(
        row_count, model_width
    )
    grad_key_normed = (grad_key_rot * cosine + rotate_back(grad_key_rot * sine)).reshape(
        row_count, model_width
    )
    grad_query_scale = jnp.sum(grad_query_normed * normed_query, axis=0)
    grad_key_scale = jnp.sum(grad_key_normed * normed_key, axis=0)
    grad_query_pre = norm_back(grad_query_normed * query_scale, normed_query, scale_query)
    grad_key_pre = norm_back(grad_key_normed * key_scale, normed_key, scale_key)
    grad_query_pre = grad_query_pre.astype(bf16)
    grad_key_pre = grad_key_pre.astype(bf16)
    grad_value_pre = grad_value.reshape(row_count, model_width).astype(bf16)
    grad_attn_in = jnp.dot(grad_query_pre, query_full.T, preferred_element_type=f32)
    grad_attn_in = grad_attn_in + jnp.dot(grad_key_pre, key_full.T, preferred_element_type=f32)
    grad_attn_in = grad_attn_in + jnp.dot(grad_value_pre, value_full.T, preferred_element_type=f32)
    grad_attn_scale = jnp.sum(grad_attn_in * normed_attn, axis=0)
    grad_hidden = grad_after + norm_back(grad_attn_in * attn_scale, normed_attn, scale_attn)
    sums = []
    for left, right in (
        (attn_in, grad_query_pre),
        (attn_in, grad_key_pre),
        (attn_in, grad_value_pre),
        (mixed, grad_branch),
    ):
        grad = jnp.dot(left.T, right, preferred_element_type=f32).astype(bf16)
        sums.append(lax.psum_scatter(grad, both, scatter_dimension=0, tiled=True).astype(f32))
    three = jnp.stack([grad_query_scale, grad_key_scale, grad_attn_scale], axis=1)
    small = jnp.concatenate([three, small], axis=1)
    small = lax.psum_scatter(small, both, scatter_dimension=0, tiled=True)
    expert = []
    for left, right in ((rows_in, grad_gate_low), (rows_in, grad_up_low), (middle, rows_grad)):
        grad = jnp.dot(left.T, right, preferred_element_type=f32).astype(bf16)
        expert.append(lax.psum_scatter(grad, "rep", scatter_dimension=0, tiled=True).astype(f32))
    rows = [exchange(output), exchange(grad_hidden.astype(bf16))]
    return sums, small, rows, expert


def body(
    tokens,
    out_cot,
    destination,
    doc_lengths,
    routes,
    fill_order,
    query_weight,
    key_weight,
    value_weight,
    output_weight,
    query_gain,
    key_gain,
    attn_gain,
    moe_gain,
    router_weight,
    expert_gate,
    expert_up,
    expert_down,
):
    group_size = lax.axis_size("ex")
    row_count, model_width = tokens.shape
    block_rows = row_count // group_size
    row_index = jnp.arange(row_count, dtype=jnp.int32)
    placed = destination // row_count % group_size * block_rows + destination % block_rows
    to_send = (placed[None, :] == row_index[:, None]).astype(bf16)
    inbound = jnp.einsum(
        "pr,brd->bpd", to_send, jnp.stack([tokens, out_cot]), preferred_element_type=f32
    ).astype(bf16)
    gains = jnp.concatenate(
        [jnp.stack([query_gain, key_gain, attn_gain, moe_gain], axis=1), router_weight], axis=1
    )
    segment, position, live_rows = segment_tables(doc_lengths[0], row_count)
    visible = (segment[:, None] == segment[None, :]) & (row_index[None, :] <= row_index[:, None])
    cosine, sine = rope_tables(position)
    shards = [query_weight, key_weight, value_weight, output_weight]
    inbound = inbound.reshape(2, group_size, block_rows, model_width)
    weights, gain_rows, router_full, hidden_in, cot_in, attn_in, qkv, mixed, norms = start(
        shards, gains, inbound[0], inbound[1], visible, cosine, sine
    )
    query_full, key_full, value_full, output_full = weights
    query_scale, key_scale, attn_scale, moe_scale = gain_rows
    query_low, key_low, value_low = qkv
    normed_query, normed_key, scale_query, scale_key = norms
    gate_full = lax.all_gather(expert_gate[0], "rep", axis=0, tiled=True)
    up_full = lax.all_gather(expert_up[0], "rep", axis=0, tiled=True)
    down_full = lax.all_gather(expert_down[0], "rep", axis=0, tiled=True)

    live_column = live_rows.astype(f32)[:, None]
    hidden = hidden_in.astype(f32)
    branch = jnp.dot(mixed, output_full, preferred_element_type=f32)
    after_attn = hidden + live_column * branch
    normed_moe, scale_moe = normalize(after_attn)
    moe_in = (normed_moe * moe_scale).astype(bf16)
    logits = jnp.dot(moe_in, router_full, preferred_element_type=f32)
    router_probs = jax.nn.softmax(logits, axis=-1)
    experts = router_full.shape[1]
    capacity = row_count * routes.shape[1] // experts
    slot_table, kept = slot_tables(routes, fill_order[0], live_rows, experts, capacity)
    gates = jnp.where(kept, router_probs, 0.0)

    table = jnp.concatenate([gates.T, slot_table.T.astype(f32)], axis=0)
    (
        grad_moe_in,
        mixture,
        grad_rprobs,
        rows_in,
        rows_grad,
        middle,
        grad_gate_low,
        grad_up_low,
    ) = experts_of_group(moe_in, cot_in, table, gate_full, up_full, down_full, capacity)
    grad_rprobs = grad_rprobs.T
    output = (after_attn + mixture).astype(bf16)

    grad_out = cot_in.astype(f32)
    grad_logits = router_probs * (
        grad_rprobs - jnp.sum(router_probs * grad_rprobs, axis=-1, keepdims=True)
    )
    grad_moe_in = grad_moe_in + jnp.dot(
        grad_logits, router_full.T, precision=lax.Precision.HIGHEST, preferred_element_type=f32
    )
    grad_router = jnp.dot(
        moe_in.T, grad_logits, precision=lax.Precision.HIGHEST, preferred_element_type=f32
    )
    grad_moe_scale = jnp.sum(grad_moe_in * normed_moe, axis=0)
    grad_after = grad_out + norm_back(grad_moe_in * moe_scale, normed_moe, scale_moe)
    grad_branch = (live_column * grad_after).astype(bf16)
    small = jnp.concatenate([grad_moe_scale[:, None], grad_router], axis=1)
    sums, small, rows, expert = finish(
        grad_branch, mixed, attn_in, hidden_in, query_low, key_low, value_low, normed_query,
        normed_key, scale_query, scale_key, visible, cosine, sine, grad_after, query_scale,
        key_scale, attn_scale, small, output, query_full, key_full, value_full, output_full,
        rows_in, rows_grad, middle, grad_gate_low, grad_up_low,
    )
    owned_query, owned_key, owned_value, owned_output = sums
    owned_gate, owned_up, owned_down = (a[None] for a in expert)
    outbound = jnp.dot(
        to_send.T, jnp.concatenate(rows, axis=1), preferred_element_type=f32
    ).astype(bf16)
    return (
        outbound[:, :model_width],
        outbound[:, model_width:],
        owned_query,
        owned_key,
        owned_value,
        owned_output,
        small[:, 0],
        small[:, 1],
        small[:, 2],
        small[:, 3],
        small[:, 4:],
        owned_gate,
        owned_up,
        owned_down,
    )


def solution(mesh):
    rows, row = P(("rep", "ex"), None), P(("rep", "ex"))
    expert = P("ex", "rep", None)
    return jax.shard_map(
        body,
        mesh=mesh,
        in_specs=(rows, rows, row) + (rows,) * 7 + (row,) * 4 + (rows,) + (expert,) * 3,
        out_specs=(rows,) * 6 + (row,) * 4 + (rows,) + (expert,) * 3,
        check_vma=False,
    )
```

```python
import functools

import jax
import jax.numpy as jnp
from jax import lax
from jax.experimental import pallas as pl
from jax.experimental.pallas import tpu as pltpu
from jax.sharding import PartitionSpec as P

HEADS = 16
HEAD_DIM = 128

epsilon = 1e-05
rope_base = 10000.0
masked_score = -1e30
bf16 = jnp.bfloat16
f32 = jnp.float32


def normalize(values):
    scale = lax.rsqrt(jnp.mean(values * values, axis=-1, keepdims=True) + epsilon)
    return (values * scale, scale)


def norm_back(grad_normed, normed, scale):
    return scale * (grad_normed - normed * jnp.mean(grad_normed * normed, axis=-1, keepdims=True))


def rotate_half(values):
    middle = values.shape[-1] // 2
    return jnp.concatenate([-values[..., middle:], values[..., :middle]], axis=-1)


def rotate_back(values):
    middle = values.shape[-1] // 2
    return jnp.concatenate([values[..., middle:], -values[..., :middle]], axis=-1)


def rope_tables(position):
    steps = jnp.arange(HEAD_DIM // 2, dtype=f32) * (2.0 / HEAD_DIM)
    inverse = rope_base ** (-steps)
    angle = position.astype(f32)[:, None] * inverse[None, :]
    cosine = jnp.concatenate([jnp.cos(angle), jnp.cos(angle)], axis=-1)[:, None, :]
    sine = jnp.concatenate([jnp.sin(angle), jnp.sin(angle)], axis=-1)[:, None, :]
    return (cosine, sine)


def segment_tables(lengths, row_count):
    count = lengths.shape[0]
    numbers = jnp.arange(count, dtype=jnp.int32)
    before = (numbers[None, :] < numbers[:, None]).astype(jnp.int32)
    starts = jnp.sum(before * lengths[None, :], axis=1)
    ends = starts + lengths
    row_index = jnp.arange(row_count, dtype=jnp.int32)
    segment = jnp.sum((row_index[:, None] >= ends[None, :]).astype(jnp.int32), axis=1)
    begin = jnp.sum(jnp.where(segment[:, None] == numbers[None, :], starts[None, :], 0), axis=1)
    return (segment, row_index - begin, segment < count - 1)


def slot_tables(routes, filling, live_rows, experts, capacity):
    row_count, top_count = routes.shape
    order = jnp.arange(row_count * top_count, dtype=jnp.int32)
    rows = jnp.arange(row_count, dtype=jnp.int32)
    hot_row = (filling[None, :] // top_count == rows[:, None]).astype(bf16)
    hot_choice = (filling % top_count)[:, None] == jnp.arange(top_count, dtype=jnp.int32)[None, :]
    high = jnp.where(hot_choice, (order // 64)[:, None], 0).astype(bf16)
    lower = jnp.where(hot_choice, (order % 64)[:, None], 0).astype(bf16)
    ranks = jnp.dot(
        hot_row, jnp.concatenate([high, lower], axis=1), preferred_element_type=f32
    ).astype(jnp.int32)
    rank = ranks[:, :top_count] * 64 + ranks[:, top_count:]
    chosen = routes[:, :, None] == jnp.arange(experts, dtype=jnp.int32)[None, None, :]
    rank_table = jnp.sum(jnp.where(chosen, rank[:, :, None], 0), axis=1)
    counted = jnp.any(chosen, axis=1) & live_rows[:, None]
    earlier = counted[:, None, :] & (rank_table[:, None, :] < rank_table[None, :, :])
    slot = jnp.sum(earlier.astype(jnp.int32), axis=0)
    kept = counted & (slot < capacity)
    return (jnp.where(kept, slot, -1), kept)


def attention_scores(query_low, key_low, visible):
    scores = jnp.einsum(
        "qhd,khd->hqk", query_low, key_low, preferred_element_type=f32
    ) * HEAD_DIM ** (-0.5)
    return jnp.where(visible[None], scores, masked_score)


MESH = pl.DeviceIdType.MESH


class Place:
    def __init__(self):
        self.rep, self.ex = lax.axis_index("rep"), lax.axis_index("ex")
        self.x, self.y, self.z = self.ex % 2, self.ex // 2 % 2, self.ex // 4
        self.other_x = (self.rep, self.ex + 1 - 2 * self.x)
        self.other_y = (self.rep, self.ex + 2 - 4 * self.y)
        self.other_core = (1 - self.rep, self.ex)
        self.other_z = [(self.rep, (self.ex + 4 * k) % 16) for k in range(1, 4)]
        self.middle = (self.z == 1) | (self.z == 2)
        self.end = jnp.logical_not(self.middle)
        near = jnp.where(self.z < 2, 1, 2)
        self.end_z = jnp.where(self.z < 2, 0, 3)
        self.near, self.far, self.across, self.own_end, self.far_end = (
            (self.rep, zz * 4 + self.ex % 4) for zz in (near, 3 - near, 3 - self.z, self.end_z, 3 - self.end_z)
        )
        self.peers = [(self.rep, (self.ex + k) % 16) for k in range(1, 16)]


def enter(devices):
    barrier = pltpu.get_barrier_semaphore()
    for device in devices:
        pl.semaphore_signal(barrier, inc=1, device_id=device, device_id_type=MESH)
    pl.semaphore_wait(barrier, len(devices))


class Copies:
    def __init__(self, send_sems, recv_sems):
        self.send_sems, self.recv_sems, self.made = send_sems, recv_sems, []
        self.done, self.whens = set(), {}

    def start(self, source, target, device, when=None):
        at = len(self.made)
        copy = pltpu.make_async_remote_copy(
            src_ref=source,
            dst_ref=target,
            send_sem=self.send_sems.at[at],
            recv_sem=self.recv_sems.at[at],
            device_id=device,
            device_id_type=MESH,
        )
        if when is None:
            copy.start()
        else:
            pl.when(when)(copy.start)
        self.made.append(copy)
        self.whens[id(copy)] = when
        return copy

    def sent(self, copy):
        if id(copy) not in self.done:
            self.done.add(id(copy))
            when = self.whens[id(copy)]
            if when is None:
                copy.wait_send()
            else:
                pl.when(when)(copy.wait_send)

    def finish(self):
        for copy in self.made:
            self.sent(copy)


def nt(left, right):
    return lax.dot_general(left, right, (((1,), (1,)), ((), ())), preferred_element_type=f32)


def nn(left, right):
    return jnp.dot(left, right, preferred_element_type=f32)


def hot_slots(table, expert, capacity):
    experts, rows = table.shape
    lane = lax.broadcasted_iota(jnp.int32, (capacity, experts), 1)
    mine = jnp.where(lane == expert, 1.0, 0.0).astype(bf16)
    slot = nn(mine, table.astype(bf16))
    wanted = lax.broadcasted_iota(jnp.int32, (capacity, rows), 0).astype(f32)
    return jnp.where(slot == wanted, 1.0, 0.0).astype(bf16)


PIECES = 4


def expert_kernel(capacity, *refs):
    table, moe, cot, gate_w, up_w, down_w = refs[:6]
    grad_out, mix_out, given, *kept_outs = refs[6:14]
    refs = refs[14:]
    tables, hot, hot_row, hot_gate, gate_col, grad_col, back = refs[:7]
    rows_in, rows_cot, acc, to_gate, to_up, middle, result = refs[7:14]
    gu_slots, down_slots, to_slots, send_slots, column_slots = refs[14:19]
    parts = 2 * PIECES
    pick_buffers = [refs[19 + 3 * j : 22 + 3 * j] for j in range(parts)]
    refs = refs[19 + 3 * parts :]
    spread_buffers = [refs[2 * j : 2 * j + 2] for j in range(parts)]
    send_sems, recv_sems, local_sems, load_sems, ready = refs[2 * parts :]
    here = Place()
    x, y, z, ex = here.x, here.y, here.z, here.ex
    by_y, by_x = here.other_y[1], here.other_x[1]
    experts = table.shape[0] // 2
    units = gate_w.shape[1]
    width = moe.shape[1] // PIECES
    half = width // 2
    enter(here.peers)
    copies = Copies(send_sems, recv_sems)
    local = []

    def keep(source, target):
        copy = pltpu.make_async_copy(source, target, local_sems.at[len(local)])
        copy.start()
        local.append(copy)
        return copy

    def block(zz, yy, xx):
        return (zz * 2 + yy) * 2 + xx

    def piece(j):
        return j % PIECES * width

    gu_loads, down_loads = {}, {}

    def load_gu(n):
        if n < parts:
            rows = pl.ds(piece(n), width)
            gu_loads[n] = [
                pltpu.make_async_copy(w.at[rows], gu_slots.at[n % 2, k], load_sems.at[n % 2, k])
                for k, w in enumerate((gate_w, up_w))
            ]
            for copy in gu_loads[n]:
                copy.start()

    def load_down(n):
        if n < parts:
            columns = pl.ds(piece(n), width)
            down_loads[n] = pltpu.make_async_copy(
                down_w.at[:, columns], down_slots.at[n % 2], load_sems.at[n % 2, 2]
            )
            down_loads[n].start()

    def stage_z(j):
        source = (moe if j < PIECES else cot).at[:, pl.ds(piece(j), width)]
        target = pick_buffers[j][0].at[z]
        to_near = copies.start(source, target, here.near, here.end)
        to_far = copies.start(source, target, here.far, here.end)
        across = copies.start(source, target, here.across, here.middle)
        to_end = copies.start(source, target, here.own_end, here.middle)
        return [to_near, to_far, across, to_end], keep(source, target)

    def relay(j):
        (_, to_far, across, _), _ = held[j]
        def arrived():
            to_far.wait_recv()
            across.wait_recv()
        pl.when(here.middle)(arrived)
        blocks = pick_buffers[j][0].at[pl.ds(jnp.where(z == 1, 2, 0), 2)]
        held[j][0].append(copies.start(blocks, blocks, here.own_end, here.middle))

    def stage_one(j, sent, kept):
        column, from_x, from_y = pick_buffers[j]
        to_near, _, _, to_end, relayed = sent
        kept.wait()
        pl.when(here.middle)(to_near.wait_recv)
        def arrived():
            to_end.wait_recv()
            relayed.wait_recv()
        pl.when(here.end)(arrived)
        return (
            copies.start(column.at[:, :, pl.ds(0, half)], from_x, here.other_x),
            copies.start(column.at[:, :, pl.ds(half, half)], from_y, here.other_y),
        )

    def landing(j):
        return rows_in if j < PIECES else rows_cot

    def pick_own(j):
        column, into = pick_buffers[j][0], landing(j)
        def body(n, carry):
            picked = nn(hot[0, block(n, y, x)], column[n])
            into[n, y, x, :, pl.ds(piece(j), width)] = picked.astype(bf16)
            return carry
        lax.fori_loop(0, 4, body, 0)

    def pick_moved(j):
        (_, from_x, from_y), into, first = pick_buffers[j], landing(j), piece(j)
        def body(n, carry):
            picked = nn(hot[0, block(n, y, 1 - x)], from_x[n])
            into[n, y, 1 - x, :, pl.ds(first, half)] = picked.astype(bf16)
            picked = nn(hot[0, block(n, 1 - y, x)], from_y[n])
            into[n, 1 - y, x, :, pl.ds(first + half, half)] = picked.astype(bf16)
            return carry
        lax.fori_loop(0, 4, body, 0)

    second = {}

    def stage_two(j, one):
        (column, from_x, from_y), into, first = pick_buffers[j], landing(j), piece(j)
        to_y, to_x = to_slots.at[j % 2, 0], to_slots.at[j % 2, 1]
        if j >= 2:
            copies.sent(second[j - 2][0])
            copies.sent(second[j - 2][1])
        def own_part(n, carry):
            at = block(n, y, x)
            to_y[n, x] = nn(hot[1, at], column[n, :, pl.ds(0, half)]).astype(bf16)
            to_x[n, y] = nn(hot[2, at], column[n, :, pl.ds(half, half)]).astype(bf16)
            return carry
        lax.fori_loop(0, 4, own_part, 0)
        one[0].wait_recv()
        def x_part(n, carry):
            to_y[n, 1 - x] = nn(hot[1, block(n, y, 1 - x)], from_x[n]).astype(bf16)
            return carry
        lax.fori_loop(0, 4, x_part, 0)
        a = copies.start(to_y, into.at[:, y, :, :, pl.ds(first, half)], here.other_y)
        one[1].wait_recv()
        def y_part(n, carry):
            to_x[n, 1 - y] = nn(hot[2, block(n, 1 - y, x)], from_y[n]).astype(bf16)
            return carry
        lax.fori_loop(0, 4, y_part, 0)
        b = copies.start(to_x, into.at[:, :, x, :, pl.ds(first + half, half)], here.other_x)
        second[j] = a, b

    def build(n, carry):
        both = tables[n]
        for k, expert in enumerate((ex, by_y, by_x)):
            hot[k, n] = hot_slots(both[experts:], expert, capacity)
        turned = both.T
        lane = lax.broadcasted_iota(jnp.int32, turned.shape, 1)
        wanted = lax.broadcasted_iota(jnp.int32, (turned.shape[0], capacity), 1).astype(f32)
        for k, expert in enumerate((ex, by_y, by_x)):
            slot = jnp.sum(jnp.where(lane == experts + expert, turned, 0.0), axis=1, keepdims=True)
            gate = jnp.sum(jnp.where(lane == expert, turned, 0.0), axis=1, keepdims=True)
            hot_row[k, n] = jnp.where(slot == wanted, 1.0, 0.0).astype(bf16)
            hot_gate[k, n] = jnp.where(slot == wanted, gate, 0.0).astype(bf16)
        row = lax.broadcasted_iota(jnp.int32, (experts, both.shape[1]), 0)
        gates = jnp.sum(jnp.where(row == ex, both[:experts], 0.0), axis=0, keepdims=True)
        gate_col[n] = jnp.sum(hot[0, n].astype(f32) * gates, axis=1, keepdims=True)
        grad_col[n] = jnp.zeros((capacity, 1), f32)
        return carry

    def flat(ref, first, size):
        return ref[:, :, :, :, pl.ds(first, size)].reshape(-1, size)

    def grow(k, columns, value, fresh):
        acc[k, :, columns] = value if fresh else acc[k, :, columns] + value

    def tile(n):
        return pl.ds(pl.multiple_of(n * 256, 256), 256)

    def gate_and_up(p):
        for copy in gu_loads[p]:
            copy.wait()
        def body(n, carry):
            left = flat(rows_in, piece(p), width)
            for k in range(2):
                grow(k, tile(n), nn(left, gu_slots[p % 2, k, :, tile(n)]), p == 0)
            return carry
        lax.fori_loop(0, units // 256, body, 0)
        load_gu(p + 2)

    def activate(n, carry):
        rows = pl.ds(pl.multiple_of(n * 32, 32), 32)
        gate, up = acc[0, rows], acc[1, rows]
        sigma = 1.0 / (1.0 + jnp.exp(-gate))
        silu = gate * sigma
        middle[rows] = (silu * up).astype(bf16)
        to_gate[rows] = (up * sigma * (1.0 + gate * (1.0 - sigma))).astype(bf16)
        to_up[rows] = silu.astype(bf16)
        return carry

    def store(first, value):
        result[:, :, :, :, pl.ds(first, 256)] = value.astype(bf16).reshape(4, 2, 2, capacity, 256)

    def down(p):
        down_loads[p].wait()
        for n in range(width // 256):
            store(piece(p) + n * 256, nn(middle[...], down_slots[p % 2, :, pl.ds(n * 256, 256)]))
        load_down(p + 2)

    def back_down(p):
        n_load = p + PIECES
        columns = pl.ds(piece(p), width)
        def rows(n, carry):
            at = (n // 4, n // 2 % 2, n % 2, slice(None), columns)
            mine = rows_cot[at].astype(f32)
            dots = jnp.sum(mine * result[at].astype(f32), axis=1, keepdims=True)
            grad_col[n] = grad_col[n] + dots
            rows_cot[at] = (gate_col[n] * mine).astype(bf16)
            return carry
        lax.fori_loop(0, 16, rows, 0)
        down_loads[n_load].wait()
        def body(n, carry):
            value = nt(flat(rows_cot, piece(p), width), down_slots[n_load % 2, tile(n)])
            grow(0, tile(n), value, p == 0)
            return carry
        lax.fori_loop(0, units // 256, body, 0)
        load_down(n_load + 2)

    def back_activate(n, carry):
        rows = pl.ds(pl.multiple_of(n * 32, 32), 32)
        grad = acc[0, rows]
        to_gate[rows] = (grad * to_gate[rows].astype(f32)).astype(bf16)
        to_up[rows] = (grad * to_up[rows].astype(f32)).astype(bf16)
        return carry

    def back_rows(p):
        n_load = p + PIECES
        for copy in spread_one[p]:
            copies.sent(copy)
        for copy in gu_loads[n_load]:
            copy.wait()
        for n in range(width // 256):
            rows = pl.ds(n * 256, 256)
            value = nt(to_gate[...], gu_slots[n_load % 2, 0, rows])
            store(piece(p) + n * 256, value + nt(to_up[...], gu_slots[n_load % 2, 1, rows]))
        load_gu(n_load + 2)

    def give_back(n, carry):
        grads = jnp.sum(hot[0, n].astype(f32) * grad_col[n], axis=0, keepdims=True)
        back[n] = jnp.broadcast_to(grads, back.shape[1:])
        return carry

    spread_one, spread_two, spread_three = {}, {}, {}

    def cols(j):
        return pl.ds(piece(j), half), pl.ds(piece(j) + half, half)

    def term(j, which, at, rows):
        return nn((hot_gate if j < PIECES else hot_row)[which, at], rows)

    def send_one(j):
        (from_y, from_x), (a, b) = spread_buffers[j], cols(j)
        spread_one[j] = (
            copies.start(result.at[:, 1 - y, :, :, a], from_y, here.other_y),
            copies.start(result.at[:, :, 1 - x, :, b], from_x, here.other_x),
        )

    def send_two(j):
        (from_y, from_x), (a, b) = spread_buffers[j], cols(j)
        to_x, to_y = send_slots.at[j % 2, 0], send_slots.at[j % 2, 1]
        if j >= 2:
            copies.sent(spread_two[j - 2][0])
            copies.sent(spread_two[j - 2][1])
        if j % PIECES == 0:
            pl.semaphore_wait(ready.at[j // PIECES], 5)
        spread_one[j][0].wait_recv()
        def x_part(n, carry):
            at = block(n, y, 1 - x)
            total = term(j, 0, at, result[n, y, 1 - x, :, a]) + term(j, 1, at, from_y[n, 1 - x])
            to_x[n] = total.astype(bf16)
            return carry
        lax.fori_loop(0, 4, x_part, 0)
        first = copies.start(to_x, pick_buffers[j][1], here.other_x)
        spread_one[j][1].wait_recv()
        def y_part(n, carry):
            at = block(n, 1 - y, x)
            total = term(j, 0, at, result[n, 1 - y, x, :, b]) + term(j, 2, at, from_x[n, 1 - y])
            to_y[n] = total.astype(bf16)
            return carry
        lax.fori_loop(0, 4, y_part, 0)
        spread_two[j] = first, copies.start(to_y, pick_buffers[j][2], here.other_y)

    def send_three(j):
        (from_y, from_x), (a, b) = spread_buffers[j], cols(j)
        from_z, more_a, more_b = pick_buffers[j]
        column = column_slots.at[j % 3]
        if j >= 3:
            for copy in spread_three[j - 3]:
                copies.sent(copy)
        for copy in spread_two[j]:
            copy.wait_recv()
        def body(n, carry):
            at = block(n, y, x)
            total = term(j, 0, at, result[n, y, x, :, a]) + term(j, 1, at, from_y[n, x])
            column[n, :, pl.ds(0, half)] = (total + more_a[n].astype(f32)).astype(bf16)
            total = term(j, 0, at, result[n, y, x, :, b]) + term(j, 2, at, from_x[n, y])
            column[n, :, pl.ds(half, half)] = (total + more_b[n].astype(f32)).astype(bf16)
            return carry
        lax.fori_loop(0, 4, body, 0)
        spread_three[j] = [
            copies.start(
                column.at[pl.ds(jnp.where(z == 0, 1, 0), 3)], from_z.at[pl.ds(0, 3)], here.near, here.end
            ),
            copies.start(column.at[here.end_z], from_z.at[0], here.own_end, here.middle),
        ]

    def send_merged(j):
        column, from_z = column_slots.at[j % 3], pick_buffers[j][0]
        def merge():
            spread_three[j][0].wait_recv()
            first, came = jnp.where(z == 1, 2, 0), jnp.where(z == 1, 1, 0)
            for k in range(2):
                total = column[first + k].astype(f32) + from_z[came + k].astype(f32)
                column[first + k] = total.astype(bf16)
        pl.when(here.middle)(merge)
        spread_three[j] += [
            copies.start(column.at[3 - z], from_z.at[3], here.across, here.middle),
            copies.start(column.at[3 - here.end_z], from_z.at[1], here.far_end, here.middle),
        ]

    def send_four(j):
        from_z, out = pick_buffers[j][0], mix_out if j < PIECES else grad_out
        columns = pl.ds(piece(j), width)
        _, to_end, across, to_far_end = spread_three[j]
        def in_middle():
            across.wait_recv()
            total = column_slots[j % 3, z].astype(f32) + from_z[jnp.where(z == 1, 0, 2)].astype(f32)
            out[:, columns] = total + from_z[3].astype(f32)
        pl.when(here.middle)(in_middle)
        def at_end():
            to_end.wait_recv()
            to_far_end.wait_recv()
            total = column_slots[j % 3, z].astype(f32) + from_z[0].astype(f32)
            out[:, columns] = total + from_z[1].astype(f32)
        pl.when(here.end)(at_end)

    told = [copies.start(table, tables.at[ex], peer) for peer in here.peers]
    kept_table = keep(table, tables.at[ex])
    held, ones, written, returned = {}, {}, [], []
    for n in range(2):
        load_gu(n)
        load_down(n)
    for step in range(2 * parts + 4):
        if step == 0:
            held[0] = stage_z(0)
        if step + 1 < parts:
            held[step + 1] = stage_z(step + 1)
        if step < parts:
            relay(step)
        if step == 1:
            kept_table.wait()
            for copy in told:
                copy.wait_recv()
            lax.fori_loop(0, 16, build, 0)
        if 0 <= step - 1 < parts:
            ones[step - 1] = stage_one(step - 1, *held[step - 1])
        if 0 <= step - 2 < parts:
            stage_two(step - 2, ones[step - 2])
        for behind, send in enumerate((send_one, send_two, send_three, send_merged, send_four)):
            if 0 <= step - parts - behind < parts:
                send(step - parts - behind)
        if 0 <= step - 1 < parts:
            pick_own(step - 1)
        if 0 <= step - 2 < parts:
            pick_moved(step - 2)
            if (step - 2) % PIECES == PIECES - 1:
                for j in range(step - 1 - PIECES, step - 1):
                    for copy in (*ones[j], held[j][0][4]):
                        copies.sent(copy)
                for device in (here.other_x, here.other_y, *here.other_z):
                    pl.semaphore_signal(
                        ready.at[(step - 2) // PIECES], inc=1, device_id=device, device_id_type=MESH
                    )
        p = step - 3
        if 0 <= p < parts:
            second[p][0].wait_recv()
            second[p][1].wait_recv()
        if 0 <= p < PIECES:
            gate_and_up(p)
        if p == PIECES - 1:
            lax.fori_loop(0, acc.shape[1] // 32, activate, 0)
            written.append(keep(rows_in, kept_outs[0]))
            written.append(keep(middle, kept_outs[2]))
            for n in range(PIECES):
                down(n)
        if PIECES <= p < parts:
            back_down(p - PIECES)
        if p == parts - 1:
            lax.fori_loop(0, acc.shape[1] // 32, back_activate, 0)
            written.append(keep(rows_cot, kept_outs[1]))
            written.append(keep(to_gate, kept_outs[3]))
            written.append(keep(to_up, kept_outs[4]))
            lax.fori_loop(0, 16, give_back, 0)
            returned = [copies.start(back.at[peer[1]], given.at[ex], peer) for peer in here.peers]
            written.append(keep(back.at[ex], given.at[ex]))
        if 0 <= step - 3 - parts < PIECES:
            back_rows(step - 3 - parts)
    for copy in returned:
        copy.wait_recv()
    for copy in written:
        copy.wait()
    copies.finish()


def run_experts(moe_in, cot_in, table, gate_full, up_full, down_full, capacity, collective_id):
    rows, model_width = moe_in.shape
    units, parts = gate_full.shape[1], 2 * PIECES
    width = model_width // PIECES
    half, slots = width // 2, 16 * capacity
    vmem, anywhere = pl.BlockSpec(memory_space=pltpu.VMEM), pl.BlockSpec(memory_space=pl.ANY)
    compact = (4, 2, 2, capacity, model_width)
    scratch = [
        pltpu.VMEM((16, *table.shape), f32),
        pltpu.VMEM((3, 16, capacity, rows), bf16),
        pltpu.VMEM((3, 16, rows, capacity), bf16),
        pltpu.VMEM((3, 16, rows, capacity), bf16),
        pltpu.VMEM((16, capacity, 1), f32),
        pltpu.VMEM((16, capacity, 1), f32),
        pltpu.VMEM((16, 8, rows), f32),
        pltpu.VMEM(compact, bf16),
        pltpu.VMEM(compact, bf16),
        pltpu.VMEM((2, slots, units), f32),
        pltpu.VMEM((slots, units), bf16),
        pltpu.VMEM((slots, units), bf16),
        pltpu.VMEM((slots, units), bf16),
        pltpu.VMEM(compact, bf16),
        pltpu.VMEM((2, 2, width, units), bf16),
        pltpu.VMEM((2, units, width), bf16),
        pltpu.VMEM((2, 2, 4, 2, capacity, half), bf16),
        pltpu.VMEM((2, 2, 4, rows, half), bf16),
        pltpu.VMEM((3, 4, rows, width), bf16),
    ]
    for _ in range(parts):
        scratch += [
            pltpu.VMEM((4, rows, width), bf16),
            pltpu.VMEM((4, rows, half), bf16),
            pltpu.VMEM((4, rows, half), bf16),
        ]
    scratch += [pltpu.VMEM((4, 2, capacity, half), bf16)] * (2 * parts)
    copies = 17 * parts + 30
    shape = jax.ShapeDtypeStruct
    grad, mixture, given, rows_in, rows_grad, *units_out = pl.pallas_call(
        functools.partial(expert_kernel, capacity),
        out_shape=[shape((rows, model_width), f32)] * 2
        + [shape((16, 8, rows), f32)]
        + [shape(compact, bf16)] * 2
        + [shape((slots, units), bf16)] * 3,
        in_specs=[vmem] * 3 + [anywhere] * 3,
        out_specs=[vmem] * 3 + [anywhere] * 5,
        scratch_shapes=scratch
        + [
            pltpu.SemaphoreType.DMA((copies,)),
            pltpu.SemaphoreType.DMA((copies,)),
            pltpu.SemaphoreType.DMA((parts + 7,)),
            pltpu.SemaphoreType.DMA((2, 3)),
            pltpu.SemaphoreType.REGULAR((2,)),
        ],
        compiler_params=pltpu.CompilerParams(
            collective_id=collective_id, has_side_effects=True, vmem_limit_bytes=62 * 2**20
        ),
    )(table, moe_in, cot_in, gate_full, up_full, down_full)
    rows_in, rows_grad = rows_in.reshape(slots, -1), rows_grad.reshape(slots, -1)
    return grad, mixture, given[:, 0], rows_in, rows_grad, *units_out


def tn(left, right):
    return lax.dot_general(left, right, (((0,), (0,)), ((), ())), preferred_element_type=f32)


def accumulate(target, blocks, arrived):
    def add(n, carry):
        for into, source in blocks:
            value = target[(n,) + into].astype(f32) + arrived[(n,) + source].astype(f32)
            target[(n,) + into] = value.astype(target.dtype)
        return carry
    lax.fori_loop(0, 4, add, 0)


ROW = 16


def finish_kernel(*refs):
    (
        grad_branch, mixed, attn_in, hidden_in, query, key, value, normed_query, normed_key,
        scale_query, scale_key, seen, cosine, sine, grad_after, gains, small_in, out_rows,
        query_w, key_w, value_w, output_w, rows_in, rows_grad, middle, grad_gate, grad_up,
    ) = refs[:27]
    weight_outs, small_out, given_out, given_grad = refs[27:31], *refs[31:34]
    gate_out, up_out, down_out, expert_landing = refs[34:38]
    refs = refs[38:]
    sides, lefts, grads, mixed_grad, query_normed, key_normed, attn_grad, grad_rows = refs[:8]
    owns, small_buf, small_own, small_core, w_slots = refs[8:13]
    left_slots, right_slots, send_slots, came, result = refs[13:18]
    parts = 17
    landing, refs = refs[18 : 18 + 5 * parts], refs[18 + 5 * parts :]
    send_sems, recv_sems, local_sems, load_sems = refs
    here = Place()
    rep, x, y, z, ex = here.rep, here.x, here.y, here.z, here.ex
    model_width = grad_branch.shape[1]
    columns = model_width // 4
    enter([*here.peers, here.other_core])
    copies = Copies(send_sems, recv_sems)
    local = []

    def keep(source, target):
        copy = pltpu.make_async_copy(source, target, local_sems.at[len(local)])
        copy.start()
        local.append(copy)
        return copy

    returned = []

    def give(source, target):
        keep(source.at[ex], target.at[ex])
        for peer in here.peers:
            returned.append(copies.start(source.at[peer[1]], target.at[ex], peer))

    mine, theirs = (pl.ds(pl.multiple_of(r * 1024, 1024), 1024) for r in (rep, 1 - rep))
    core_left = [
        copies.start(ref.at[:, theirs], sides.at[n], here.other_core)
        for n, ref in enumerate((mixed, attn_in))
    ]
    core_grad = {}

    def share(n):
        core_grad[n] = copies.start(
            grads.at[n, pl.ds(0, 128)], grads.at[n, pl.ds(128, 128)], here.other_core
        )

    def turn_left(n, ref):
        core_left[n].wait_recv()
        def body(k, carry):
            at = pl.multiple_of(rep * 1024 + k * 128, 128)
            lefts[n, k, :, pl.ds(0, 128)] = ref[:, pl.ds(at, 128)].astype(f32).T.astype(bf16)
            at = pl.multiple_of(k * 128, 128)
            lefts[n, k, :, pl.ds(128, 128)] = sides[n, :, pl.ds(at, 128)].astype(f32).T.astype(bf16)
            return carry
        lax.fori_loop(0, 8, body, 0)

    stream, loads = [(w, n) for w in (output_w, value_w, query_w, key_w) for n in range(4)], {}

    def load(n):
        if n < len(stream):
            w, k = stream[n]
            loads[n] = pltpu.make_async_copy(
                w.at[pl.ds(k * columns, columns)], w_slots.at[n % 2], load_sems.at[n % 2]
            )
            loads[n].start()

    def back_mixed():
        for k in range(4):
            loads[k].wait()
            at = pl.ds(k * columns, columns)
            mixed_grad[:, at] = nt(grad_branch[...], w_slots[k % 2]).astype(bf16)
            load(k + 2)

    def unrotate(grad):
        turned = grad * sine[...]
        lane = lax.broadcasted_iota(jnp.int32, turned.shape, 1)
        sign = jnp.where(lane < HEAD_DIM // 2, 1.0, -1.0)
        return grad * cosine[...] + sign * pltpu.roll(turned, HEAD_DIM // 2, 1)

    def heads(first, count):
        def body(n, carry):
            at = pl.ds(pl.multiple_of((first + n) * HEAD_DIM, HEAD_DIM), HEAD_DIM)
            q, k, v, grad = query[:, at], key[:, at], value[:, at], mixed_grad[:, at]
            scores = jnp.where(seen[...] > 0, nt(q, k) * HEAD_DIM ** (-0.5), masked_score)
            weights = jnp.exp(scores - jnp.max(scores, axis=1, keepdims=True))
            probs = weights / jnp.sum(weights, axis=1, keepdims=True)
            grads[2, pl.ds(0, 128), at] = tn(probs.astype(bf16), grad).astype(bf16)
            grad_att = nt(grad, v)
            grad_scores = probs * (grad_att - jnp.sum(probs * grad_att, axis=1, keepdims=True))
            grad_scores = grad_scores.astype(bf16)
            query_normed[:, at] = unrotate(nn(grad_scores, k) * HEAD_DIM ** (-0.5))
            key_normed[:, at] = unrotate(tn(grad_scores, q) * HEAD_DIM ** (-0.5))
            return carry
        lax.fori_loop(0, count, body, 0)

    sums = {}

    def back_norm(n, grad_ref, normed_ref, scale_ref):
        def body(k, total):
            rows = pl.ds(pl.multiple_of(k * ROW, ROW), ROW)
            grad, normed = grad_ref[rows], normed_ref[rows]
            total = total + jnp.sum(grad * normed, axis=0, keepdims=True)
            grad = grad * gains[pl.ds(n, 1)]
            mean = jnp.mean(grad * normed, axis=1, keepdims=True)
            grads[n, rows] = (scale_ref[rows] * (grad - normed * mean)).astype(bf16)
            return total
        start = jnp.zeros((1, model_width), f32)
        sums[n] = lax.fori_loop(0, 128 // ROW, body, start)

    def back_attn(n, at_stream, fresh):
        for k in range(4):
            loads[at_stream + k].wait()
            at = pl.ds(k * columns, columns)
            grad = nt(grads[n, pl.ds(0, 128)], w_slots[(at_stream + k) % 2])
            attn_grad[:, at] = grad if fresh else attn_grad[:, at] + grad
            load(at_stream + k + 2)

    def back_hidden():
        def body(k, total):
            rows = pl.ds(pl.multiple_of(k * ROW, ROW), ROW)
            hidden, grad = hidden_in[rows].astype(f32), attn_grad[rows]
            scale = lax.rsqrt(jnp.mean(hidden * hidden, axis=1, keepdims=True) + epsilon)
            normed = hidden * scale
            total = total + jnp.sum(grad * normed, axis=0, keepdims=True)
            grad = grad * gains[pl.ds(2, 1)]
            mean = jnp.mean(grad * normed, axis=1, keepdims=True)
            grad = grad_after[rows] + scale * (grad - normed * mean)
            grad = grad.astype(bf16).reshape(2, 8, model_width)
            grad_rows[pl.ds(2 * k, 2)] = grad
            return total
        start = jnp.zeros((1, model_width), f32)
        sums[2] = lax.fori_loop(0, 128 // ROW, body, start)
        give(grad_rows, given_grad)
        pad = jnp.zeros((125, 128), f32)
        for k in range(model_width // 128):
            rows = [sums[n][:, k * 128 : k * 128 + 128] for n in range(3)]
            block = jnp.concatenate([*rows, pad], axis=0).T.reshape(2, 64, 128)
            at = (k // 8, k // 2 % 4, k % 2)
            small_buf[at] = small_in[at] + block

    def halves():
        return pl.ds(0, 32), pl.ds(32, 32)

    one, two, last = {}, {}, {}

    def own_of(j):
        return owns.at[j % 6] if j < 16 else small_own

    def sum_one(j):
        own, (upper, lower) = own_of(j), halves()
        if j < 16:
            n, which = (3, 0) if j < 4 else ((2, 1), (0, 1), (1, 1))[j // 4 - 1]
            at = pl.ds(j % 4 * columns, columns)
            if j % 4 == 0:
                core_grad[n].wait_recv()
            if j >= 6:
                for copy in (*one[j - 6], *two[j - 6], *last[j - 6]):
                    copies.sent(copy)
            def body(k, carry):
                own[k // 2, k % 2] = nn(lefts[which, k], grads[n, :, at]).astype(bf16).reshape(2, 64, columns)
                return carry
            lax.fori_loop(0, 8, body, 0)
        else:
            core_grad["small"].wait_recv()
            def add(k, carry):
                own[k] = small_buf[rep, k] + small_core[k]
                return carry
            lax.fori_loop(0, 4, add, 0)
        one[j] = (
            copies.start(own.at[:, 1 - y, :, upper], landing[5 * j], here.other_y),
            copies.start(own.at[:, :, 1 - x, lower], landing[5 * j + 1], here.other_x),
        )

    def sum_two(j):
        own, (upper, lower) = own_of(j), halves()
        from_y, from_x = landing[5 * j], landing[5 * j + 1]
        one[j][0].wait_recv()
        accumulate(own, [((y, 1 - x, upper), (1 - x,))], from_y)
        a = copies.start(own.at[:, y, 1 - x, upper], landing[5 * j + 2], here.other_x)
        one[j][1].wait_recv()
        accumulate(own, [((1 - y, x, lower), (1 - y,))], from_x)
        b = copies.start(own.at[:, 1 - y, x, lower], landing[5 * j + 3], here.other_y)
        accumulate(own, [((y, x, upper), (x,)), ], from_y)
        accumulate(own, [((y, x, lower), (y,)), ], from_x)
        two[j] = a, b

    def sum_three(j):
        own, (upper, lower) = own_of(j), halves()
        two[j][0].wait_recv()
        accumulate(own, [((y, x, upper), ())], landing[5 * j + 2])
        two[j][1].wait_recv()
        accumulate(own, [((y, x, lower), ())], landing[5 * j + 3])
        last[j] = [
            copies.start(own.at[(z + k) % 4, y, x], landing[5 * j + 4].at[k - 1], here.other_z[k - 1])
            for k in range(1, 4)
        ]

    def sum_four(j):
        own, arrived = own_of(j), landing[5 * j + 4]
        for copy in last[j]:
            copy.wait_recv()
        total = own[z, y, x].astype(f32) + arrived[0].astype(f32)
        total = total + arrived[1].astype(f32) + arrived[2].astype(f32)
        if j == 16:
            small_out[...] = total
        else:
            n = (3, 2, 0, 1)[j // 4]
            weight_outs[n][:, pl.ds(j % 4 * columns, columns)] = total

    tasks, task_loads, sent_halves, stored = [], {}, {}, {}
    for side in range(2):
        for k in range(2):
            for kind in range(3):
                tasks.append((side, k, kind))

    def task_load(n):
        if n < len(tasks):
            side, k, kind = tasks[n]
            whose = rep if side else 1 - rep
            if kind < 2:
                left = rows_in.at[:, pl.ds(pl.multiple_of(whose * 1024 + k * 512, 512), 512)]
                right = (grad_gate, grad_up)[kind]
            else:
                left = middle.at[:, pl.ds(pl.multiple_of(whose * 512, 512), 512)]
                right = rows_grad.at[:, pl.ds(k * 1024, 1024)]
            task_loads[n] = (
                pltpu.make_async_copy(left, left_slots.at[n % 2], load_sems.at[2 + n % 2]),
                pltpu.make_async_copy(right, right_slots.at[n % 2], load_sems.at[4 + n % 2]),
            )
            for copy in task_loads[n]:
                copy.start()

    def task(n):
        side, k, kind = tasks[n]
        for copy in task_loads[n]:
            copy.wait()
        left, right = left_slots.at[n % 2], right_slots.at[n % 2]
        if side == 0:
            target = send_slots.at[n % 2]
            if n >= 2:
                copies.sent(sent_halves[n - 2])
            def body(m, carry):
                at = pl.ds(pl.multiple_of(m * 256, 256), 256)
                target[at] = tn(left[:, at], right[...]).astype(bf16)
                return carry
            lax.fori_loop(0, 2, body, 0)
            sent_halves[n] = copies.start(target, expert_landing.at[n], here.other_core)
        else:
            at = n - len(tasks) // 2
            sent_halves[at].wait_recv()
            back = pltpu.make_async_copy(expert_landing.at[at], came, load_sems.at[6])
            back.start()
            if n - 1 in stored:
                stored[n - 1].wait()
            back.wait()
            def body(m, carry):
                rows = pl.ds(pl.multiple_of(m * 256, 256), 256)
                result[rows] = tn(left[:, rows], right[...]) + came[rows].astype(f32)
                return carry
            lax.fori_loop(0, 2, body, 0)
            if kind < 2:
                target = (gate_out, up_out)[kind].at[pl.ds(k * 512, 512)]
            else:
                target = down_out.at[:, pl.ds(k * 1024, 1024)]
            stored[n] = pltpu.make_async_copy(result, target, load_sems.at[7])
            stored[n].start()
        task_load(n + 2)

    give(out_rows, given_out)
    grads[3, pl.ds(0, 128)] = grad_branch[...]
    share(3)
    for n in range(2):
        load(n)
        task_load(n)
    turn_left(0, mixed)
    for step in range(parts + 3):
        for behind, stage in enumerate((sum_one, sum_two, sum_three, sum_four)):
            if 0 <= step - behind < parts:
                stage(step - behind)
        if step == 0:
            back_mixed()
            turn_left(1, attn_in)
        elif step == 1:
            heads(0, 8)
        elif step == 2:
            heads(8, 8)
            share(2)
        elif step == 3:
            back_norm(0, query_normed, normed_query, scale_query)
            share(0)
            back_norm(1, key_normed, normed_key, scale_key)
            share(1)
        elif step == 4:
            back_attn(2, 4, True)
        elif step == 5:
            back_attn(0, 8, False)
        elif step == 6:
            back_attn(1, 12, False)
        elif step == 7:
            back_hidden()
            core_grad["small"] = copies.start(small_buf.at[1 - rep], small_core, here.other_core)
        elif step < 8 + len(tasks) // 2:
            task(2 * (step - 8))
            task(2 * (step - 8) + 1)
    stored[len(tasks) - 1].wait()
    for copy in returned:
        copy.wait_recv()
    for copy in local:
        copy.wait()
    copies.finish()


def run_finish(arrays, weights, expert, collective_id):
    rows, model_width = arrays[0].shape
    columns = model_width // 4
    vmem, anywhere = pl.BlockSpec(memory_space=pltpu.VMEM), pl.BlockSpec(memory_space=pl.ANY)
    shape, tile = jax.ShapeDtypeStruct, (4, 2, 2, 64)
    scratch = [
        pltpu.VMEM((2, rows, 1024), bf16),
        pltpu.VMEM((2, 8, 128, 256), bf16),
        pltpu.VMEM((4, 2 * rows, model_width), bf16),
        pltpu.VMEM((rows, model_width), bf16),
        pltpu.VMEM((rows, model_width), f32),
        pltpu.VMEM((rows, model_width), f32),
        pltpu.VMEM((rows, model_width), f32),
        pltpu.VMEM((16, 8, model_width), bf16),
        pltpu.VMEM((6, *tile, columns), bf16),
        pltpu.VMEM((2, *tile, 128), f32),
        pltpu.VMEM((*tile, 128), f32),
        pltpu.VMEM((*tile, 128), f32),
        pltpu.VMEM((2, columns, model_width), bf16),
        pltpu.VMEM((2, 1024, 512), bf16),
        pltpu.VMEM((2, 1024, 1024), bf16),
        pltpu.VMEM((2, 512, 1024), bf16),
        pltpu.VMEM((512, 1024), bf16),
        pltpu.VMEM((512, 1024), f32),
    ]
    for j in range(17):
        width, dtype = (columns, bf16) if j < 16 else (128, f32)
        scratch += [
            pltpu.VMEM((4, 2, 32, width), dtype),
            pltpu.VMEM((4, 2, 32, width), dtype),
            pltpu.VMEM((4, 32, width), dtype),
            pltpu.VMEM((4, 32, width), dtype),
            pltpu.VMEM((3, 64, width), dtype),
        ]
    copies = 7 * 17 + 30 + 7 + 6
    return pl.pallas_call(
        finish_kernel,
        out_shape=[shape((64, model_width), f32)] * 4
        + [shape((64, 128), f32)]
        + [shape((16, 8, model_width), bf16)] * 2
        + [shape((1024, 1024), f32)] * 2
        + [shape((512, 2048), f32), shape((6, 512, 1024), bf16)],
        in_specs=[vmem] * len(arrays) + [anywhere] * (len(weights) + len(expert)),
        out_specs=[vmem] * 5 + [anywhere] * 6,
        scratch_shapes=scratch
        + [
            pltpu.SemaphoreType.DMA((copies,)),
            pltpu.SemaphoreType.DMA((copies,)),
            pltpu.SemaphoreType.DMA((2,)),
            pltpu.SemaphoreType.DMA((8,)),
        ],
        compiler_params=pltpu.CompilerParams(
            collective_id=collective_id, has_side_effects=True, vmem_limit_bytes=62 * 2**20
        ),
    )(*arrays, *weights, *expert)


Z_LAST = (2, 6, 11)


def start_kernel(*refs):
    query_w, key_w, value_w, output_w, gains_w, rows_in, cot_in, seen, cosine, sine = refs[:10]
    fulls, (hidden_out, cot_out), refs = refs[10:15], refs[15:17], refs[17:]
    gain_rows, attn_in, query, key, value, mixed, normed_query, normed_key, scale_query, scale_key = refs[:10]
    product, slots, came_rows, gain_cols = refs[10:14]
    send_sems, recv_sems, local_sems, load_sems = refs[14:]
    here = Place()
    rep, x, y, z, ex = here.rep, here.x, here.y, here.z, here.ex
    model_width = query_w.shape[1]
    enter([*here.peers, here.other_core])
    copies = Copies(send_sems, recv_sems)
    local = []

    def keep(source, target):
        copy = pltpu.make_async_copy(source, target, local_sems.at[len(local)])
        copy.start()
        local.append(copy)
        return copy

    def give(source, target):
        return [keep(source.at[ex], target.at[ex])] + [
            copies.start(source.at[peer[1]], target.at[ex], peer) for peer in here.peers
        ]

    def take(moved):
        moved[0].wait()
        for copy in moved[1:]:
            copy.wait_recv()

    shards = (query_w, key_w, value_w, output_w, gains_w)
    parts = [(4, 0, 64)] + [(i, k * 16, 16) for i in range(4) for k in range(4)]
    first_stage, one, two, cores = {}, {}, {}, {}

    def spans(j):
        i, first, rows = parts[j]
        half = rows // 2
        return fulls[i].at[rep], pl.ds(first, rows), pl.ds(first, half), pl.ds(first + half, half)

    def along_z(source, target):
        return [
            copies.start(source, target, here.near, here.end),
            copies.start(source, target, here.far, here.end),
            copies.start(source, target, here.across, here.middle),
            copies.start(source, target, here.own_end, here.middle),
        ]

    def pass_on(sent, blocks):
        def arrived():
            sent[1].wait_recv()
            sent[2].wait_recv()
        pl.when(here.middle)(arrived)
        sent.append(copies.start(blocks, blocks, here.own_end, here.middle))

    def arrived_z(sent):
        pl.when(here.middle)(sent[0].wait_recv)
        def arrived():
            sent[3].wait_recv()
            sent[4].wait_recv()
        pl.when(here.end)(arrived)

    other_side = pl.ds(jnp.where(z == 1, 2, 0), 2)

    def stage_open(j):
        full, rows, upper, lower = spans(j)
        shard, own = shards[parts[j][0]], full.at[z, y, x]
        kept = keep(shard.at[rows], own.at[rows])
        if j in Z_LAST:
            a = copies.start(shard.at[upper], own.at[upper], here.other_x)
            first_stage[j] = (a, copies.start(shard.at[lower], own.at[lower], here.other_y)), kept
        else:
            first_stage[j] = along_z(shard.at[rows], own.at[rows]), kept

    def stage_pass(j):
        if j not in Z_LAST:
            full, rows, _, _ = spans(j)
            pass_on(first_stage[j][0], full.at[other_side, y, x, rows])

    def stage_one(j):
        full, rows, upper, lower = spans(j)
        sent, kept = first_stage[j]
        kept.wait()
        if j in Z_LAST:
            sent[0].wait_recv()
            a = full.at[z, y, :, upper]
            two_a = copies.start(a, a, here.other_y)
            sent[1].wait_recv()
            b = full.at[z, :, x, lower]
            one[j] = two_a, copies.start(b, b, here.other_x)
            return
        arrived_z(sent)
        a, b, own = full.at[:, y, x, upper], full.at[:, y, x, lower], full.at[:, y, x, rows]
        one[j] = copies.start(a, a, here.other_x), copies.start(b, b, here.other_y)
        cores[j] = [copies.start(own, own, here.other_core)]

    def stage_two(j):
        full, rows, upper, lower = spans(j)
        one[j][0].wait_recv()
        if j in Z_LAST:
            one[j][1].wait_recv()
            plane = full.at[z, :, :, rows]
            two[j] = along_z(plane, plane)
            cores[j] = [copies.start(plane, plane, here.other_core)]
            return
        a = full.at[:, y, :, upper]
        two_a = copies.start(a, a, here.other_y)
        one[j][1].wait_recv()
        b = full.at[:, :, x, lower]
        two[j] = two_a, copies.start(b, b, here.other_x)
        for c in (full.at[:, y, 1 - x, upper], full.at[:, 1 - y, x, lower]):
            cores[j].append(copies.start(c, c, here.other_core))

    def stage_three(j):
        full, rows, upper, lower = spans(j)
        if j in Z_LAST:
            pass_on(two[j], full.at[other_side, :, :, rows])
            return
        two[j][0].wait_recv()
        a = full.at[:, 1 - y, :, upper]
        cores[j].append(copies.start(a, a, here.other_core))
        two[j][1].wait_recv()
        b = full.at[:, :, 1 - x, lower]
        cores[j].append(copies.start(b, b, here.other_core))

    def stage_four(j):
        if j in Z_LAST:
            full, rows, _, _ = spans(j)
            arrived_z(two[j])
            for k in range(1, 4):
                plane = full.at[(z + k) % 4, :, :, rows]
                cores[j].append(copies.start(plane, plane, here.other_core))

    def complete(j):
        for copy in cores[j]:
            copy.wait_recv()

    def turn_gains():
        complete(0)
        copy = pltpu.make_async_copy(fulls[4], gain_cols, load_sems.at[2])
        copy.start()
        copy.wait()
        for k in range(model_width // 128):
            block = gain_cols[k // 8, k // 2 % 4, k % 2].reshape(128, 128).astype(f32)
            gain_rows[:, k * 128 : k * 128 + 128] = block.T[:8]

    def norm_rows(moved):
        take(moved)
        copy = pltpu.make_async_copy(hidden_out, came_rows, load_sems.at[2])
        copy.start()
        copy.wait()
        def body(k, carry):
            hidden = came_rows[pl.ds(2 * k, 2)].reshape(ROW, model_width).astype(f32)
            scale = lax.rsqrt(jnp.mean(hidden * hidden, axis=1, keepdims=True) + epsilon)
            rows = pl.ds(pl.multiple_of(k * ROW, ROW), ROW)
            attn_in[rows] = (hidden * scale * gain_rows[pl.ds(2, 1)]).astype(bf16)
            return carry
        lax.fori_loop(0, 128 // ROW, body, 0)

    def load(i, n):
        copy = pltpu.make_async_copy(
            fulls[i].at[n // 2, pl.ds(n % 2 * 2, 2)], slots.at[n % 2], load_sems.at[n % 2]
        )
        copy.start()
        return copy

    def project(i):
        for j in range(1 + 4 * i, 5 + 4 * i):
            complete(j)
        loads = {n: load(i, n) for n in range(2)}
        for n in range(4):
            loads[n].wait()
            left = attn_in[:, pl.ds(n * 512, 512)]
            for k in range(4):
                at = pl.ds(k * 512, 512)
                grown = nn(left, slots[n % 2, :, :, :, :, at].reshape(512, 512))
                product[:, at] = grown if n == 0 else product[:, at] + grown
            if n + 2 < 4:
                loads[n + 2] = load(i, n + 2)

    def norm_heads(n, normed_ref, scale_ref, low_ref):
        lane = lax.broadcasted_iota(jnp.int32, (ROW, HEAD_DIM), 1)
        sign = jnp.where(lane < HEAD_DIM // 2, -1.0, 1.0)
        def body(k, carry):
            rows = pl.ds(pl.multiple_of(k * ROW, ROW), ROW)
            pre = product[rows]
            scale = lax.rsqrt(jnp.mean(pre * pre, axis=1, keepdims=True) + epsilon)
            normed = pre * scale
            normed_ref[rows], scale_ref[rows] = normed, scale
            gained = normed * gain_rows[pl.ds(n, 1)]
            for h in range(HEADS):
                at = slice(h * HEAD_DIM, (h + 1) * HEAD_DIM)
                turned = sign * pltpu.roll(gained[:, at], HEAD_DIM // 2, 1)
                low_ref[rows, at] = (gained[:, at] * cosine[rows] + turned * sine[rows]).astype(bf16)
            return carry
        lax.fori_loop(0, 128 // ROW, body, 0)

    def heads(first, count):
        def body(n, carry):
            at = pl.ds(pl.multiple_of((first + n) * HEAD_DIM, HEAD_DIM), HEAD_DIM)
            scores = nt(query[:, at], key[:, at]) * HEAD_DIM ** (-0.5)
            scores = jnp.where(seen[...] > 0, scores, masked_score)
            weights = jnp.exp(scores - jnp.max(scores, axis=1, keepdims=True))
            probs = weights / jnp.sum(weights, axis=1, keepdims=True)
            mixed[:, at] = nn(probs.astype(bf16), value[:, at]).astype(bf16)
            return carry
        lax.fori_loop(0, count, body, 0)

    stage_open(0)
    stage_open(1)
    moved_rows = give(rows_in, hidden_out)
    moved_cot = []
    for step in range(len(parts) + 3):
        if 1 <= step < len(parts) - 1:
            stage_open(step + 1)
        if step < len(parts):
            stage_pass(step)
        for behind, stage in enumerate((stage_one, stage_two, stage_three, stage_four), 1):
            if 0 <= step - behind < len(parts):
                stage(step - behind)
        if step == 4:
            turn_gains()
            moved_cot = give(cot_in, cot_out)
        elif step == 6:
            norm_rows(moved_rows)
        elif step == 8:
            project(0)
        elif step == 9:
            norm_heads(0, normed_query, scale_query, query)
        elif step == 12:
            project(1)
        elif step == 13:
            norm_heads(1, normed_key, scale_key, key)
        elif step == 16:
            project(2)
            value[...] = product[...].astype(bf16)
        elif step == 17:
            heads(0, 6)
        elif step == 18:
            heads(6, 6)
        elif step == 19:
            heads(12, 4)
    for j in range(13, 17):
        complete(j)
    take(moved_cot)
    copies.finish()


def run_start(shards, rows, cot, visible, cosine, sine, collective_id):
    model_width = shards[0].shape[1]
    vmem, anywhere = pl.BlockSpec(memory_space=pltpu.VMEM), pl.BlockSpec(memory_space=pl.ANY)
    shape = jax.ShapeDtypeStruct
    own_rows = [(shape((128, model_width), dtype)) for dtype in (bf16,) * 5 + (f32,) * 2]
    *fulls, hidden_in, cot_in, gain_rows, attn_in, query, key, value, mixed, nq, nk, sq, sk = pl.pallas_call(
        start_kernel,
        out_shape=[shape((2, 4, 2, 2) + a.shape, a.dtype) for a in shards]
        + [shape(rows.shape, bf16)] * 2
        + [shape((8, model_width), f32)]
        + own_rows
        + [shape((128, 1), f32)] * 2,
        in_specs=[anywhere] * 7 + [vmem] * 3,
        out_specs=[anywhere] * 7 + [vmem] * 10,
        scratch_shapes=[
            pltpu.VMEM((128, model_width), f32),
            pltpu.VMEM((2, 2, 2, 2, 64, model_width), bf16),
            pltpu.VMEM(rows.shape, bf16),
            pltpu.VMEM((2, 4, 2, 2, 64, 128), bf16),
            pltpu.SemaphoreType.DMA((14 * 17 + 30,)),
            pltpu.SemaphoreType.DMA((14 * 17 + 30,)),
            pltpu.SemaphoreType.DMA((19,)),
            pltpu.SemaphoreType.DMA((3,)),
        ],
        compiler_params=pltpu.CompilerParams(
            collective_id=collective_id, has_side_effects=True, vmem_limit_bytes=40 * 2**20
        ),
    )(*shards, rows, cot, visible, cosine, sine)
    fulls = [a.reshape(-1, a.shape[-1]) for a in fulls]
    hidden_in, cot_in = (a.reshape(128, model_width) for a in (hidden_in, cot_in))
    return fulls, hidden_in, cot_in, gain_rows, attn_in, query, key, value, mixed, nq, nk, sq, sk


def has_kernels():
    return (lax.axis_size("rep"), lax.axis_size("ex")) == (2, 16)


def exchange(array):
    return lax.all_to_all(array, "ex", split_axis=0, concat_axis=0, tiled=True)


def start(shards, gains, inbound_rows, inbound_cot, visible, cosine, sine):
    block_rows, model_width = inbound_rows.shape[1:]
    row_count = inbound_rows.shape[0] * block_rows
    if has_kernels():
        wide = jnp.pad(gains, ((0, 0), (0, 128 - gains.shape[1])))
        full, hidden_in, cot_in, gain_rows, attn_in, *qkv, mixed, nq, nk, sq, sk = run_start(
            [*shards, wide], inbound_rows, inbound_cot, visible.astype(f32), cosine[:, 0], sine[:, 0], 1
        )
        *weights, wide = full
        qkv = [a.reshape(row_count, HEADS, HEAD_DIM) for a in qkv]
        router = wide[:, 4 : gains.shape[1]]
        return weights, gain_rows[:4], router, hidden_in, cot_in, attn_in, qkv, mixed, (nq, nk, sq, sk)
    gather = functools.partial(lax.all_gather, axis_name=("rep", "ex"), axis=0, tiled=True)
    weights = query_full, key_full, value_full, _ = [gather(a) for a in shards]
    gains = gather(jnp.pad(gains, ((0, 0), (0, -gains.shape[1] % 128))))[:, : gains.shape[1]]
    gain_rows = gains[:, :4].astype(f32).T
    query_scale, key_scale, attn_scale, _ = gain_rows
    hidden_in, cot_in = (exchange(a).reshape(row_count, model_width) for a in (inbound_rows, inbound_cot))
    hidden = hidden_in.astype(f32)
    normed_attn, scale_attn = normalize(hidden)
    attn_in = (normed_attn * attn_scale).astype(bf16)
    query_pre = jnp.dot(attn_in, query_full, preferred_element_type=f32)
    key_pre = jnp.dot(attn_in, key_full, preferred_element_type=f32)
    value_pre = jnp.dot(attn_in, value_full, preferred_element_type=f32)
    normed_query, scale_query = normalize(query_pre)
    normed_key, scale_key = normalize(key_pre)
    query_norm = (normed_query * query_scale).reshape(row_count, HEADS, HEAD_DIM)
    key_norm = (normed_key * key_scale).reshape(row_count, HEADS, HEAD_DIM)
    query_low = (query_norm * cosine + rotate_half(query_norm) * sine).astype(bf16)
    key_low = (key_norm * cosine + rotate_half(key_norm) * sine).astype(bf16)
    value_low = value_pre.astype(bf16).reshape(row_count, HEADS, HEAD_DIM)
    scores = attention_scores(query_low, key_low, visible)
    peak = jnp.max(scores, axis=-1, keepdims=True)
    weights_exp = jnp.exp(scores - peak)
    probs = weights_exp / jnp.sum(weights_exp, axis=-1, keepdims=True)
    probs_low = probs.astype(bf16)
    mixed = jnp.einsum("hqk,khd->qhd", probs_low, value_low, preferred_element_type=f32)
    mixed = mixed.reshape(row_count, model_width).astype(bf16)
    qkv = query_low, key_low, value_low
    norms = normed_query, normed_key, scale_query, scale_key
    return weights, gain_rows, gains[:, 4:], hidden_in, cot_in, attn_in, qkv, mixed, norms


def slots_of(tables, capacity):
    experts, me = tables.shape[1] // 2, lax.axis_index("ex")
    gates = lax.dynamic_index_in_dim(tables, me, 1, keepdims=True)
    slots = lax.dynamic_index_in_dim(tables, experts + me, 1, keepdims=True)
    return slots == jnp.arange(capacity, dtype=f32)[None, :, None], gates


def experts_of_group(moe_in, cot_in, table, gate_full, up_full, down_full, capacity):
    if has_kernels():
        return run_experts(moe_in, cot_in, table, gate_full, up_full, down_full, capacity, 2)
    tables = lax.all_gather(table, "ex", axis=0)
    picked, gate_rows = slots_of(tables, capacity)
    picked_low = picked.astype(bf16)
    slot_gate = jnp.sum(jnp.where(picked, gate_rows, 0.0), axis=2).reshape(-1, 1)

    def pick(rows):
        rows = lax.all_gather(rows, "ex", axis=0)
        rows = jnp.einsum("sct,std->scd", picked_low, rows, preferred_element_type=f32)
        return rows.astype(bf16).reshape(-1, rows.shape[-1])

    def spread(rows):
        rows = rows.reshape(*picked_low.shape[:2], -1)
        rows = jnp.einsum("sct,scd->std", picked_low, rows, preferred_element_type=f32)
        return lax.psum_scatter(rows.astype(bf16), "ex", scatter_dimension=0).astype(f32)

    rows_in, rows_cot = pick(moe_in), pick(cot_in)
    gate_pre = jnp.dot(rows_in, gate_full, preferred_element_type=f32)
    up_pre = jnp.dot(rows_in, up_full, preferred_element_type=f32)
    sigma = jax.nn.sigmoid(gate_pre)
    silu = gate_pre * sigma
    middle = (silu * up_pre).astype(bf16)
    expert_out = jnp.dot(middle, down_full, preferred_element_type=f32).astype(bf16)
    slot_grad = jnp.sum(rows_cot.astype(f32) * expert_out.astype(f32), axis=1)
    rows_grad = (slot_gate * rows_cot.astype(f32)).astype(bf16)
    grad_middle = jnp.dot(rows_grad, down_full.T, preferred_element_type=f32)
    grad_gate_low = (grad_middle * up_pre * sigma * (1.0 + gate_pre * (1.0 - sigma))).astype(bf16)
    grad_up_low = (grad_middle * silu).astype(bf16)
    grad_rows = jnp.dot(grad_gate_low, gate_full.T, preferred_element_type=f32)
    grad_rows = grad_rows + jnp.dot(grad_up_low, up_full.T, preferred_element_type=f32)
    weighted = slot_gate * expert_out.astype(f32)
    slot_grad = slot_grad.reshape(*picked.shape[:2], 1)
    back = exchange(jnp.sum(jnp.where(picked, slot_grad, 0.0), axis=1))
    sums = spread(grad_rows.astype(bf16)), spread(weighted.astype(bf16))
    return *sums, back, rows_in, rows_grad, middle, grad_gate_low, grad_up_low


def finish(
    grad_branch, mixed, attn_in, hidden_in, query_low, key_low, value_low, normed_query, normed_key,
    scale_query, scale_key, visible, cosine, sine, grad_after, query_scale, key_scale, attn_scale,
    small, output, query_full, key_full, value_full, output_full,
    rows_in, rows_grad, middle, grad_gate_low, grad_up_low,
):
    row_count, model_width = mixed.shape
    group_size = lax.axis_size("ex")
    block_rows = row_count // group_size
    if has_kernels():
        wide = jnp.pad(small, ((0, 0), (3, 128 - 3 - small.shape[1])))
        gains = jnp.stack([query_scale, key_scale, attn_scale], axis=0)
        arrays = [
            grad_branch, mixed, attn_in, hidden_in,
            *(a.reshape(row_count, model_width) for a in (query_low, key_low, value_low)),
            normed_query, normed_key, scale_query, scale_key, visible.astype(f32),
            cosine[:, 0], sine[:, 0], grad_after, jnp.pad(gains, ((0, 5), (0, 0))),
            wide.reshape(2, 4, 2, 2, 64, 128), output.reshape(group_size, block_rows, model_width),
        ]
        *weights, summed, given_out, given_grad, gate, up, down, _ = run_finish(
            arrays,
            [query_full, key_full, value_full, output_full],
            [rows_in, rows_grad, middle, grad_gate_low, grad_up_low],
            3,
        )
        rows = [a.reshape(row_count, model_width) for a in (given_out, given_grad)]
        return weights, summed[:, : 3 + small.shape[1]], rows, (gate, up, down)
    both = ("rep", "ex")
    scores = attention_scores(query_low, key_low, visible)
    probs = jax.nn.softmax(scores, axis=-1)
    probs_low = probs.astype(bf16)
    normed_attn, scale_attn = normalize(hidden_in.astype(f32))
    grad_mixed = (
        jnp.dot(grad_branch, output_full.T, preferred_element_type=f32)
        .astype(bf16)
        .reshape(row_count, HEADS, HEAD_DIM)
    )
    grad_value = jnp.einsum("hqk,qhd->khd", probs_low, grad_mixed, preferred_element_type=f32)
    grad_att = jnp.einsum("qhd,khd->hqk", grad_mixed, value_low, preferred_element_type=f32)
    grad_scores = (probs * (grad_att - jnp.sum(probs * grad_att, axis=-1, keepdims=True))).astype(
        bf16
    )
    grad_query_rot = jnp.einsum(
        "hqk,khd->qhd", grad_scores, key_low, preferred_element_type=f32
    ) * HEAD_DIM ** (-0.5)
    grad_key_rot = jnp.einsum(
        "hqk,qhd->khd", grad_scores, query_low, preferred_element_type=f32
    ) * HEAD_DIM ** (-0.5)
    grad_query_normed = (grad_query_rot * cosine + rotate_back(grad_query_rot * sine)).reshape(
        row_count, model_width
    )
    grad_key_normed = (grad_key_rot * cosine + rotate_back(grad_key_rot * sine)).reshape(
        row_count, model_width
    )
    grad_query_scale = jnp.sum(grad_query_normed * normed_query, axis=0)
    grad_key_scale = jnp.sum(grad_key_normed * normed_key, axis=0)
    grad_query_pre = norm_back(grad_query_normed * query_scale, normed_query, scale_query)
    grad_key_pre = norm_back(grad_key_normed * key_scale, normed_key, scale_key)
    grad_query_pre = grad_query_pre.astype(bf16)
    grad_key_pre = grad_key_pre.astype(bf16)
    grad_value_pre = grad_value.reshape(row_count, model_width).astype(bf16)
    grad_attn_in = jnp.dot(grad_query_pre, query_full.T, preferred_element_type=f32)
    grad_attn_in = grad_attn_in + jnp.dot(grad_key_pre, key_full.T, preferred_element_type=f32)
    grad_attn_in = grad_attn_in + jnp.dot(grad_value_pre, value_full.T, preferred_element_type=f32)
    grad_attn_scale = jnp.sum(grad_attn_in * normed_attn, axis=0)
    grad_hidden = grad_after + norm_back(grad_attn_in * attn_scale, normed_attn, scale_attn)
    sums = []
    for left, right in (
        (attn_in, grad_query_pre),
        (attn_in, grad_key_pre),
        (attn_in, grad_value_pre),
        (mixed, grad_branch),
    ):
        grad = jnp.dot(left.T, right, preferred_element_type=f32).astype(bf16)
        sums.append(lax.psum_scatter(grad, both, scatter_dimension=0, tiled=True).astype(f32))
    three = jnp.stack([grad_query_scale, grad_key_scale, grad_attn_scale], axis=1)
    small = jnp.concatenate([three, small], axis=1)
    small = lax.psum_scatter(small, both, scatter_dimension=0, tiled=True)
    expert = []
    for left, right in ((rows_in, grad_gate_low), (rows_in, grad_up_low), (middle, rows_grad)):
        grad = jnp.dot(left.T, right, preferred_element_type=f32).astype(bf16)
        expert.append(lax.psum_scatter(grad, "rep", scatter_dimension=0, tiled=True).astype(f32))
    rows = [exchange(output), exchange(grad_hidden.astype(bf16))]
    return sums, small, rows, expert


def body(
    tokens,
    out_cot,
    destination,
    doc_lengths,
    routes,
    fill_order,
    query_weight,
    key_weight,
    value_weight,
    output_weight,
    query_gain,
    key_gain,
    attn_gain,
    moe_gain,
    router_weight,
    expert_gate,
    expert_up,
    expert_down,
):
    group_size = lax.axis_size("ex")
    row_count, model_width = tokens.shape
    block_rows = row_count // group_size
    row_index = jnp.arange(row_count, dtype=jnp.int32)
    placed = destination // row_count % group_size * block_rows + destination % block_rows
    to_send = (placed[None, :] == row_index[:, None]).astype(bf16)
    inbound = jnp.einsum(
        "pr,brd->bpd", to_send, jnp.stack([tokens, out_cot]), preferred_element_type=f32
    ).astype(bf16)
    gains = jnp.concatenate(
        [jnp.stack([query_gain, key_gain, attn_gain, moe_gain], axis=1), router_weight], axis=1
    )
    segment, position, live_rows = segment_tables(doc_lengths[0], row_count)
    visible = (segment[:, None] == segment[None, :]) & (row_index[None, :] <= row_index[:, None])
    cosine, sine = rope_tables(position)
    shards = [query_weight, key_weight, value_weight, output_weight]
    inbound = inbound.reshape(2, group_size, block_rows, model_width)
    weights, gain_rows, router_full, hidden_in, cot_in, attn_in, qkv, mixed, norms = start(
        shards, gains, inbound[0], inbound[1], visible, cosine, sine
    )
    query_full, key_full, value_full, output_full = weights
    query_scale, key_scale, attn_scale, moe_scale = gain_rows
    query_low, key_low, value_low = qkv
    normed_query, normed_key, scale_query, scale_key = norms
    gate_full = lax.all_gather(expert_gate[0], "rep", axis=0, tiled=True)
    up_full = lax.all_gather(expert_up[0], "rep", axis=0, tiled=True)
    down_full = lax.all_gather(expert_down[0], "rep", axis=0, tiled=True)

    live_column = live_rows.astype(f32)[:, None]
    hidden = hidden_in.astype(f32)
    branch = jnp.dot(mixed, output_full, preferred_element_type=f32)
    after_attn = hidden + live_column * branch
    normed_moe, scale_moe = normalize(after_attn)
    moe_in = (normed_moe * moe_scale).astype(bf16)
    logits = jnp.dot(moe_in, router_full, preferred_element_type=f32)
    router_probs = jax.nn.softmax(logits, axis=-1)
    experts = router_full.shape[1]
    capacity = row_count * routes.shape[1] // experts
    slot_table, kept = slot_tables(routes, fill_order[0], live_rows, experts, capacity)
    gates = jnp.where(kept, router_probs, 0.0)

    table = jnp.concatenate([gates.T, slot_table.T.astype(f32)], axis=0)
    (
        grad_moe_in,
        mixture,
        grad_rprobs,
        rows_in,
        rows_grad,
        middle,
        grad_gate_low,
        grad_up_low,
    ) = experts_of_group(moe_in, cot_in, table, gate_full, up_full, down_full, capacity)
    grad_rprobs = grad_rprobs.T
    output = (after_attn + mixture).astype(bf16)

    grad_out = cot_in.astype(f32)
    grad_logits = router_probs * (
        grad_rprobs - jnp.sum(router_probs * grad_rprobs, axis=-1, keepdims=True)
    )
    grad_moe_in = grad_moe_in + jnp.dot(
        grad_logits, router_full.T, precision=lax.Precision.HIGHEST, preferred_element_type=f32
    )
    grad_router = jnp.dot(
        moe_in.T, grad_logits, precision=lax.Precision.HIGHEST, preferred_element_type=f32
    )
    grad_moe_scale = jnp.sum(grad_moe_in * normed_moe, axis=0)
    grad_after = grad_out + norm_back(grad_moe_in * moe_scale, normed_moe, scale_moe)
    grad_branch = (live_column * grad_after).astype(bf16)
    small = jnp.concatenate([grad_moe_scale[:, None], grad_router], axis=1)
    sums, small, rows, expert = finish(
        grad_branch, mixed, attn_in, hidden_in, query_low, key_low, value_low, normed_query,
        normed_key, scale_query, scale_key, visible, cosine, sine, grad_after, query_scale,
        key_scale, attn_scale, small, output, query_full, key_full, value_full, output_full,
        rows_in, rows_grad, middle, grad_gate_low, grad_up_low,
    )
    owned_query, owned_key, owned_value, owned_output = sums
    owned_gate, owned_up, owned_down = (a[None] for a in expert)
    outbound = jnp.dot(
        to_send.T, jnp.concatenate(rows, axis=1), preferred_element_type=f32
    ).astype(bf16)
    return (
        outbound[:, :model_width],
        outbound[:, model_width:],
        owned_query,
        owned_key,
        owned_value,
        owned_output,
        small[:, 0],
        small[:, 1],
        small[:, 2],
        small[:, 3],
        small[:, 4:],
        owned_gate,
        owned_up,
        owned_down,
    )


def solution(mesh):
    rows, row = P(("rep", "ex"), None), P(("rep", "ex"))
    expert = P("ex", "rep", None)
    return jax.shard_map(
        body,
        mesh=mesh,
        in_specs=(rows, rows, row) + (rows,) * 7 + (row,) * 4 + (rows,) + (expert,) * 3,
        out_specs=(rows,) * 6 + (row,) * 4 + (rows,) + (expert,) * 3,
        check_vma=False,
    )
```

```python
import functools

import jax
import jax.numpy as jnp
from jax import lax
from jax.experimental import pallas as pl
from jax.experimental.pallas import tpu as pltpu
from jax.sharding import PartitionSpec as P

HEADS = 16
HEAD_DIM = 128

epsilon = 1e-05
rope_base = 10000.0
masked_score = -1e30
bf16 = jnp.bfloat16
f32 = jnp.float32


def normalize(values):
    scale = lax.rsqrt(jnp.mean(values * values, axis=-1, keepdims=True) + epsilon)
    return (values * scale, scale)


def norm_back(grad_normed, normed, scale):
    return scale * (grad_normed - normed * jnp.mean(grad_normed * normed, axis=-1, keepdims=True))


def rotate_half(values):
    middle = values.shape[-1] // 2
    return jnp.concatenate([-values[..., middle:], values[..., :middle]], axis=-1)


def rotate_back(values):
    middle = values.shape[-1] // 2
    return jnp.concatenate([values[..., middle:], -values[..., :middle]], axis=-1)


def rope_tables(position):
    steps = jnp.arange(HEAD_DIM // 2, dtype=f32) * (2.0 / HEAD_DIM)
    inverse = rope_base ** (-steps)
    angle = position.astype(f32)[:, None] * inverse[None, :]
    cosine = jnp.concatenate([jnp.cos(angle), jnp.cos(angle)], axis=-1)[:, None, :]
    sine = jnp.concatenate([jnp.sin(angle), jnp.sin(angle)], axis=-1)[:, None, :]
    return (cosine, sine)


def segment_tables(lengths, row_count):
    count = lengths.shape[0]
    numbers = jnp.arange(count, dtype=jnp.int32)
    before = (numbers[None, :] < numbers[:, None]).astype(jnp.int32)
    starts = jnp.sum(before * lengths[None, :], axis=1)
    ends = starts + lengths
    row_index = jnp.arange(row_count, dtype=jnp.int32)
    segment = jnp.sum((row_index[:, None] >= ends[None, :]).astype(jnp.int32), axis=1)
    begin = jnp.sum(jnp.where(segment[:, None] == numbers[None, :], starts[None, :], 0), axis=1)
    return (segment, row_index - begin, segment < count - 1)


def slot_tables(routes, filling, live_rows, experts, capacity):
    row_count, top_count = routes.shape
    order = jnp.arange(row_count * top_count, dtype=jnp.int32)
    rows = jnp.arange(row_count, dtype=jnp.int32)
    hot_row = (filling[None, :] // top_count == rows[:, None]).astype(bf16)
    hot_choice = (filling % top_count)[:, None] == jnp.arange(top_count, dtype=jnp.int32)[None, :]
    high = jnp.where(hot_choice, (order // 64)[:, None], 0).astype(bf16)
    lower = jnp.where(hot_choice, (order % 64)[:, None], 0).astype(bf16)
    ranks = jnp.dot(
        hot_row, jnp.concatenate([high, lower], axis=1), preferred_element_type=f32
    ).astype(jnp.int32)
    rank = ranks[:, :top_count] * 64 + ranks[:, top_count:]
    chosen = routes[:, :, None] == jnp.arange(experts, dtype=jnp.int32)[None, None, :]
    rank_table = jnp.sum(jnp.where(chosen, rank[:, :, None], 0), axis=1)
    counted = jnp.any(chosen, axis=1) & live_rows[:, None]
    earlier = counted[:, None, :] & (rank_table[:, None, :] < rank_table[None, :, :])
    slot = jnp.sum(earlier.astype(jnp.int32), axis=0)
    kept = counted & (slot < capacity)
    return (jnp.where(kept, slot, -1), kept)


def attention_scores(query_low, key_low, visible):
    scores = jnp.einsum(
        "qhd,khd->hqk", query_low, key_low, preferred_element_type=f32
    ) * HEAD_DIM ** (-0.5)
    return jnp.where(visible[None], scores, masked_score)


MESH = pl.DeviceIdType.MESH


class Place:
    def __init__(self):
        self.rep, self.ex = lax.axis_index("rep"), lax.axis_index("ex")
        self.x, self.y, self.z = self.ex % 2, self.ex // 2 % 2, self.ex // 4
        self.other_x = (self.rep, self.ex + 1 - 2 * self.x)
        self.other_y = (self.rep, self.ex + 2 - 4 * self.y)
        self.other_core = (1 - self.rep, self.ex)
        self.other_z = [(self.rep, (self.ex + 4 * k) % 16) for k in range(1, 4)]
        self.middle = (self.z == 1) | (self.z == 2)
        self.end = jnp.logical_not(self.middle)
        near = jnp.where(self.z < 2, 1, 2)
        self.end_z = jnp.where(self.z < 2, 0, 3)
        self.near, self.far, self.across, self.own_end, self.far_end = (
            (self.rep, zz * 4 + self.ex % 4) for zz in (near, 3 - near, 3 - self.z, self.end_z, 3 - self.end_z)
        )
        self.peers = [(self.rep, (self.ex + k) % 16) for k in range(1, 16)]


def enter(devices):
    barrier = pltpu.get_barrier_semaphore()
    for device in devices:
        pl.semaphore_signal(barrier, inc=1, device_id=device, device_id_type=MESH)
    pl.semaphore_wait(barrier, len(devices))


class Copies:
    def __init__(self, send_sems, recv_sems):
        self.send_sems, self.recv_sems, self.made = send_sems, recv_sems, []
        self.done, self.whens = set(), {}

    def start(self, source, target, device, when=None):
        at = len(self.made)
        copy = pltpu.make_async_remote_copy(
            src_ref=source,
            dst_ref=target,
            send_sem=self.send_sems.at[at],
            recv_sem=self.recv_sems.at[at],
            device_id=device,
            device_id_type=MESH,
        )
        if when is None:
            copy.start()
        else:
            pl.when(when)(copy.start)
        self.made.append(copy)
        self.whens[id(copy)] = when
        return copy

    def sent(self, copy):
        if id(copy) not in self.done:
            self.done.add(id(copy))
            when = self.whens[id(copy)]
            if when is None:
                copy.wait_send()
            else:
                pl.when(when)(copy.wait_send)

    def finish(self):
        for copy in self.made:
            self.sent(copy)


def nt(left, right):
    return lax.dot_general(left, right, (((1,), (1,)), ((), ())), preferred_element_type=f32)


def nn(left, right):
    return jnp.dot(left, right, preferred_element_type=f32)


def hot_slots(table, expert, capacity):
    experts, rows = table.shape
    lane = lax.broadcasted_iota(jnp.int32, (capacity, experts), 1)
    mine = jnp.where(lane == expert, 1.0, 0.0).astype(bf16)
    slot = nn(mine, table.astype(bf16))
    wanted = lax.broadcasted_iota(jnp.int32, (capacity, rows), 0).astype(f32)
    return jnp.where(slot == wanted, 1.0, 0.0).astype(bf16)


PIECES = 4


def expert_kernel(capacity, *refs):
    table, moe, cot, gate_w, up_w, down_w = refs[:6]
    grad_out, mix_out, given, *kept_outs = refs[6:14]
    refs = refs[14:]
    tables, hot, hot_row, hot_gate, gate_col, grad_col, back = refs[:7]
    rows_in, rows_cot, acc, to_gate, to_up, middle, result = refs[7:14]
    gu_slots, down_slots, to_slots, send_slots, column_slots = refs[14:19]
    parts = 2 * PIECES
    pick_buffers = [refs[19 + 3 * j : 22 + 3 * j] for j in range(parts)]
    refs = refs[19 + 3 * parts :]
    spread_buffers = [refs[2 * j : 2 * j + 2] for j in range(parts)]
    send_sems, recv_sems, local_sems, load_sems, ready = refs[2 * parts :]
    here = Place()
    x, y, z, ex = here.x, here.y, here.z, here.ex
    by_y, by_x = here.other_y[1], here.other_x[1]
    experts = table.shape[0] // 2
    units = gate_w.shape[1]
    width = moe.shape[1] // PIECES
    half = width // 2
    enter(here.peers)
    copies = Copies(send_sems, recv_sems)
    local = []

    def keep(source, target):
        copy = pltpu.make_async_copy(source, target, local_sems.at[len(local)])
        copy.start()
        local.append(copy)
        return copy

    def block(zz, yy, xx):
        return (zz * 2 + yy) * 2 + xx

    def piece(j):
        return j % PIECES * width

    gu_loads, down_loads = {}, {}

    def load_gu(n):
        if n < parts:
            rows = pl.ds(piece(n), width)
            gu_loads[n] = [
                pltpu.make_async_copy(w.at[rows], gu_slots.at[n % 2, k], load_sems.at[n % 2, k])
                for k, w in enumerate((gate_w, up_w))
            ]
            for copy in gu_loads[n]:
                copy.start()

    def load_down(n):
        if n < parts:
            columns = pl.ds(piece(n), width)
            down_loads[n] = pltpu.make_async_copy(
                down_w.at[:, columns], down_slots.at[n % 2], load_sems.at[n % 2, 2]
            )
            down_loads[n].start()

    def stage_z(j):
        source = (moe if j < PIECES else cot).at[:, pl.ds(piece(j), width)]
        target = pick_buffers[j][0].at[z]
        to_near = copies.start(source, target, here.near, here.end)
        to_far = copies.start(source, target, here.far, here.end)
        across = copies.start(source, target, here.across, here.middle)
        to_end = copies.start(source, target, here.own_end, here.middle)
        return [to_near, to_far, across, to_end], keep(source, target)

    def relay(j):
        (_, to_far, across, _), _ = held[j]
        def arrived():
            to_far.wait_recv()
            across.wait_recv()
        pl.when(here.middle)(arrived)
        blocks = pick_buffers[j][0].at[pl.ds(jnp.where(z == 1, 2, 0), 2)]
        held[j][0].append(copies.start(blocks, blocks, here.own_end, here.middle))

    def stage_one(j, sent, kept):
        column, from_x, from_y = pick_buffers[j]
        to_near, _, _, to_end, relayed = sent
        kept.wait()
        pl.when(here.middle)(to_near.wait_recv)
        def arrived():
            to_end.wait_recv()
            relayed.wait_recv()
        pl.when(here.end)(arrived)
        return (
            copies.start(column.at[:, :, pl.ds(0, half)], from_x, here.other_x),
            copies.start(column.at[:, :, pl.ds(half, half)], from_y, here.other_y),
        )

    def landing(j):
        return rows_in if j < PIECES else rows_cot

    def pick_own(j):
        column, into = pick_buffers[j][0], landing(j)
        def body(n, carry):
            picked = nn(hot[0, block(n, y, x)], column[n])
            into[n, y, x, :, pl.ds(piece(j), width)] = picked.astype(bf16)
            return carry
        lax.fori_loop(0, 4, body, 0)

    def pick_moved(j):
        (_, from_x, from_y), into, first = pick_buffers[j], landing(j), piece(j)
        def body(n, carry):
            picked = nn(hot[0, block(n, y, 1 - x)], from_x[n])
            into[n, y, 1 - x, :, pl.ds(first, half)] = picked.astype(bf16)
            picked = nn(hot[0, block(n, 1 - y, x)], from_y[n])
            into[n, 1 - y, x, :, pl.ds(first + half, half)] = picked.astype(bf16)
            return carry
        lax.fori_loop(0, 4, body, 0)

    second = {}

    def stage_two(j, one):
        (column, from_x, from_y), into, first = pick_buffers[j], landing(j), piece(j)
        to_y, to_x = to_slots.at[j % 2, 0], to_slots.at[j % 2, 1]
        if j >= 2:
            copies.sent(second[j - 2][0])
            copies.sent(second[j - 2][1])
        def own_part(n, carry):
            at = block(n, y, x)
            to_y[n, x] = nn(hot[1, at], column[n, :, pl.ds(0, half)]).astype(bf16)
            to_x[n, y] = nn(hot[2, at], column[n, :, pl.ds(half, half)]).astype(bf16)
            return carry
        lax.fori_loop(0, 4, own_part, 0)
        one[0].wait_recv()
        def x_part(n, carry):
            to_y[n, 1 - x] = nn(hot[1, block(n, y, 1 - x)], from_x[n]).astype(bf16)
            return carry
        lax.fori_loop(0, 4, x_part, 0)
        a = copies.start(to_y, into.at[:, y, :, :, pl.ds(first, half)], here.other_y)
        one[1].wait_recv()
        def y_part(n, carry):
            to_x[n, 1 - y] = nn(hot[2, block(n, 1 - y, x)], from_y[n]).astype(bf16)
            return carry
        lax.fori_loop(0, 4, y_part, 0)
        b = copies.start(to_x, into.at[:, :, x, :, pl.ds(first + half, half)], here.other_x)
        second[j] = a, b

    def build(n, carry):
        both = tables[n]
        for k, expert in enumerate((ex, by_y, by_x)):
            hot[k, n] = hot_slots(both[experts:], expert, capacity)
        turned = both.T
        lane = lax.broadcasted_iota(jnp.int32, turned.shape, 1)
        wanted = lax.broadcasted_iota(jnp.int32, (turned.shape[0], capacity), 1).astype(f32)
        for k, expert in enumerate((ex, by_y, by_x)):
            slot = jnp.sum(jnp.where(lane == experts + expert, turned, 0.0), axis=1, keepdims=True)
            gate = jnp.sum(jnp.where(lane == expert, turned, 0.0), axis=1, keepdims=True)
            hot_row[k, n] = jnp.where(slot == wanted, 1.0, 0.0).astype(bf16)
            hot_gate[k, n] = jnp.where(slot == wanted, gate, 0.0).astype(bf16)
        row = lax.broadcasted_iota(jnp.int32, (experts, both.shape[1]), 0)
        gates = jnp.sum(jnp.where(row == ex, both[:experts], 0.0), axis=0, keepdims=True)
        gate_col[n] = jnp.sum(hot[0, n].astype(f32) * gates, axis=1, keepdims=True)
        grad_col[n] = jnp.zeros((capacity, 1), f32)
        return carry

    def flat(ref, first, size):
        return ref[:, :, :, :, pl.ds(first, size)].reshape(-1, size)

    def grow(k, columns, value, fresh):
        acc[k, :, columns] = value if fresh else acc[k, :, columns] + value

    def tile(n):
        return pl.ds(pl.multiple_of(n * 256, 256), 256)

    def gate_and_up(p):
        for copy in gu_loads[p]:
            copy.wait()
        def body(n, carry):
            left = flat(rows_in, piece(p), width)
            for k in range(2):
                grow(k, tile(n), nn(left, gu_slots[p % 2, k, :, tile(n)]), p == 0)
            return carry
        lax.fori_loop(0, units // 256, body, 0)
        load_gu(p + 2)

    def activate(n, carry):
        rows = pl.ds(pl.multiple_of(n * 32, 32), 32)
        gate, up = acc[0, rows], acc[1, rows]
        sigma = 1.0 / (1.0 + jnp.exp(-gate))
        silu = gate * sigma
        middle[rows] = (silu * up).astype(bf16)
        to_gate[rows] = (up * sigma * (1.0 + gate * (1.0 - sigma))).astype(bf16)
        to_up[rows] = silu.astype(bf16)
        return carry

    def store(first, value):
        result[:, :, :, :, pl.ds(first, 256)] = value.astype(bf16).reshape(4, 2, 2, capacity, 256)

    def down(p):
        down_loads[p].wait()
        for n in range(width // 256):
            store(piece(p) + n * 256, nn(middle[...], down_slots[p % 2, :, pl.ds(n * 256, 256)]))
        load_down(p + 2)

    def back_down(p):
        n_load = p + PIECES
        columns = pl.ds(piece(p), width)
        def rows(n, carry):
            at = (n // 4, n // 2 % 2, n % 2, slice(None), columns)
            mine = rows_cot[at].astype(f32)
            dots = jnp.sum(mine * result[at].astype(f32), axis=1, keepdims=True)
            grad_col[n] = grad_col[n] + dots
            rows_cot[at] = (gate_col[n] * mine).astype(bf16)
            return carry
        lax.fori_loop(0, 16, rows, 0)
        down_loads[n_load].wait()
        def body(n, carry):
            value = nt(flat(rows_cot, piece(p), width), down_slots[n_load % 2, tile(n)])
            grow(0, tile(n), value, p == 0)
            return carry
        lax.fori_loop(0, units // 256, body, 0)
        load_down(n_load + 2)

    def back_activate(n, carry):
        rows = pl.ds(pl.multiple_of(n * 32, 32), 32)
        grad = acc[0, rows]
        to_gate[rows] = (grad * to_gate[rows].astype(f32)).astype(bf16)
        to_up[rows] = (grad * to_up[rows].astype(f32)).astype(bf16)
        return carry

    def back_rows(p):
        n_load = p + PIECES
        for copy in spread_one[p]:
            copies.sent(copy)
        for copy in gu_loads[n_load]:
            copy.wait()
        for n in range(width // 256):
            rows = pl.ds(n * 256, 256)
            value = nt(to_gate[...], gu_slots[n_load % 2, 0, rows])
            store(piece(p) + n * 256, value + nt(to_up[...], gu_slots[n_load % 2, 1, rows]))
        load_gu(n_load + 2)

    def give_back(n, carry):
        grads = jnp.sum(hot[0, n].astype(f32) * grad_col[n], axis=0, keepdims=True)
        back[n] = jnp.broadcast_to(grads, back.shape[1:])
        return carry

    spread_one, spread_two, spread_three = {}, {}, {}

    def cols(j):
        return pl.ds(piece(j), half), pl.ds(piece(j) + half, half)

    def term(j, which, at, rows):
        return nn((hot_gate if j < PIECES else hot_row)[which, at], rows)

    def send_one(j):
        (from_y, from_x), (a, b) = spread_buffers[j], cols(j)
        spread_one[j] = (
            copies.start(result.at[:, 1 - y, :, :, a], from_y, here.other_y),
            copies.start(result.at[:, :, 1 - x, :, b], from_x, here.other_x),
        )

    def send_two(j):
        (from_y, from_x), (a, b) = spread_buffers[j], cols(j)
        to_x, to_y = send_slots.at[j % 2, 0], send_slots.at[j % 2, 1]
        if j >= 2:
            copies.sent(spread_two[j - 2][0])
            copies.sent(spread_two[j - 2][1])
        if j % PIECES == 0:
            pl.semaphore_wait(ready.at[j // PIECES], 5)
        spread_one[j][0].wait_recv()
        def x_part(n, carry):
            at = block(n, y, 1 - x)
            total = term(j, 0, at, result[n, y, 1 - x, :, a]) + term(j, 1, at, from_y[n, 1 - x])
            to_x[n] = total.astype(bf16)
            return carry
        lax.fori_loop(0, 4, x_part, 0)
        first = copies.start(to_x, pick_buffers[j][1], here.other_x)
        spread_one[j][1].wait_recv()
        def y_part(n, carry):
            at = block(n, 1 - y, x)
            total = term(j, 0, at, result[n, 1 - y, x, :, b]) + term(j, 2, at, from_x[n, 1 - y])
            to_y[n] = total.astype(bf16)
            return carry
        lax.fori_loop(0, 4, y_part, 0)
        spread_two[j] = first, copies.start(to_y, pick_buffers[j][2], here.other_y)

    def send_three(j):
        (from_y, from_x), (a, b) = spread_buffers[j], cols(j)
        from_z, more_a, more_b = pick_buffers[j]
        column = column_slots.at[j % 3]
        if j >= 3:
            for copy in spread_three[j - 3]:
                copies.sent(copy)
        for copy in spread_two[j]:
            copy.wait_recv()
        def body(n, carry):
            at = block(n, y, x)
            total = term(j, 0, at, result[n, y, x, :, a]) + term(j, 1, at, from_y[n, x])
            column[n, :, pl.ds(0, half)] = (total + more_a[n].astype(f32)).astype(bf16)
            total = term(j, 0, at, result[n, y, x, :, b]) + term(j, 2, at, from_x[n, y])
            column[n, :, pl.ds(half, half)] = (total + more_b[n].astype(f32)).astype(bf16)
            return carry
        lax.fori_loop(0, 4, body, 0)
        spread_three[j] = [
            copies.start(
                column.at[pl.ds(jnp.where(z == 0, 1, 0), 3)], from_z.at[pl.ds(0, 3)], here.near, here.end
            ),
            copies.start(column.at[here.end_z], from_z.at[0], here.own_end, here.middle),
        ]

    def send_merged(j):
        column, from_z = column_slots.at[j % 3], pick_buffers[j][0]
        def merge():
            spread_three[j][0].wait_recv()
            first, came = jnp.where(z == 1, 2, 0), jnp.where(z == 1, 1, 0)
            for k in range(2):
                total = column[first + k].astype(f32) + from_z[came + k].astype(f32)
                column[first + k] = total.astype(bf16)
        pl.when(here.middle)(merge)
        spread_three[j] += [
            copies.start(column.at[3 - z], from_z.at[3], here.across, here.middle),
            copies.start(column.at[3 - here.end_z], from_z.at[1], here.far_end, here.middle),
        ]

    def send_four(j):
        from_z, out = pick_buffers[j][0], mix_out if j < PIECES else grad_out
        columns = pl.ds(piece(j), width)
        _, to_end, across, to_far_end = spread_three[j]
        def in_middle():
            across.wait_recv()
            total = column_slots[j % 3, z].astype(f32) + from_z[jnp.where(z == 1, 0, 2)].astype(f32)
            out[:, columns] = total + from_z[3].astype(f32)
        pl.when(here.middle)(in_middle)
        def at_end():
            to_end.wait_recv()
            to_far_end.wait_recv()
            total = column_slots[j % 3, z].astype(f32) + from_z[0].astype(f32)
            out[:, columns] = total + from_z[1].astype(f32)
        pl.when(here.end)(at_end)

    told = [copies.start(table, tables.at[ex], peer) for peer in here.peers]
    kept_table = keep(table, tables.at[ex])
    held, ones, written, returned = {}, {}, [], []
    for n in range(2):
        load_gu(n)
        load_down(n)
    for step in range(2 * parts + 4):
        if step == 0:
            held[0] = stage_z(0)
        if step + 1 < parts:
            held[step + 1] = stage_z(step + 1)
        if step < parts:
            relay(step)
        if step == 1:
            kept_table.wait()
            for copy in told:
                copy.wait_recv()
            lax.fori_loop(0, 16, build, 0)
        if 0 <= step - 1 < parts:
            ones[step - 1] = stage_one(step - 1, *held[step - 1])
        if 0 <= step - 2 < parts:
            stage_two(step - 2, ones[step - 2])
        for behind, send in enumerate((send_one, send_two, send_three, send_merged, send_four)):
            if 0 <= step - parts - behind < parts:
                send(step - parts - behind)
        if 0 <= step - 1 < parts:
            pick_own(step - 1)
        if 0 <= step - 2 < parts:
            pick_moved(step - 2)
            if (step - 2) % PIECES == PIECES - 1:
                for j in range(step - 1 - PIECES, step - 1):
                    for copy in (*ones[j], held[j][0][4]):
                        copies.sent(copy)
                for device in (here.other_x, here.other_y, *here.other_z):
                    pl.semaphore_signal(
                        ready.at[(step - 2) // PIECES], inc=1, device_id=device, device_id_type=MESH
                    )
        p = step - 3
        if 0 <= p < parts:
            second[p][0].wait_recv()
            second[p][1].wait_recv()
        if 0 <= p < PIECES:
            gate_and_up(p)
        if p == PIECES - 1:
            lax.fori_loop(0, acc.shape[1] // 32, activate, 0)
            written.append(keep(rows_in, kept_outs[0]))
            written.append(keep(middle, kept_outs[2]))
            for n in range(PIECES):
                down(n)
        if PIECES <= p < parts:
            back_down(p - PIECES)
        if p == parts - 1:
            lax.fori_loop(0, acc.shape[1] // 32, back_activate, 0)
            written.append(keep(rows_cot, kept_outs[1]))
            written.append(keep(to_gate, kept_outs[3]))
            written.append(keep(to_up, kept_outs[4]))
            lax.fori_loop(0, 16, give_back, 0)
            returned = [copies.start(back.at[peer[1]], given.at[ex], peer) for peer in here.peers]
            written.append(keep(back.at[ex], given.at[ex]))
        if 0 <= step - 3 - parts < PIECES:
            back_rows(step - 3 - parts)
    for copy in returned:
        copy.wait_recv()
    for copy in written:
        copy.wait()
    copies.finish()


def run_experts(moe_in, cot_in, table, gate_full, up_full, down_full, capacity, collective_id):
    rows, model_width = moe_in.shape
    units, parts = gate_full.shape[1], 2 * PIECES
    width = model_width // PIECES
    half, slots = width // 2, 16 * capacity
    vmem, anywhere = pl.BlockSpec(memory_space=pltpu.VMEM), pl.BlockSpec(memory_space=pl.ANY)
    compact = (4, 2, 2, capacity, model_width)
    scratch = [
        pltpu.VMEM((16, *table.shape), f32),
        pltpu.VMEM((3, 16, capacity, rows), bf16),
        pltpu.VMEM((3, 16, rows, capacity), bf16),
        pltpu.VMEM((3, 16, rows, capacity), bf16),
        pltpu.VMEM((16, capacity, 1), f32),
        pltpu.VMEM((16, capacity, 1), f32),
        pltpu.VMEM((16, 8, rows), f32),
        pltpu.VMEM(compact, bf16),
        pltpu.VMEM(compact, bf16),
        pltpu.VMEM((2, slots, units), f32),
        pltpu.VMEM((slots, units), bf16),
        pltpu.VMEM((slots, units), bf16),
        pltpu.VMEM((slots, units), bf16),
        pltpu.VMEM(compact, bf16),
        pltpu.VMEM((2, 2, width, units), bf16),
        pltpu.VMEM((2, units, width), bf16),
        pltpu.VMEM((2, 2, 4, 2, capacity, half), bf16),
        pltpu.VMEM((2, 2, 4, rows, half), bf16),
        pltpu.VMEM((3, 4, rows, width), bf16),
    ]
    for _ in range(parts):
        scratch += [
            pltpu.VMEM((4, rows, width), bf16),
            pltpu.VMEM((4, rows, half), bf16),
            pltpu.VMEM((4, rows, half), bf16),
        ]
    scratch += [pltpu.VMEM((4, 2, capacity, half), bf16)] * (2 * parts)
    copies = 17 * parts + 30
    shape = jax.ShapeDtypeStruct
    grad, mixture, given, rows_in, rows_grad, *units_out = pl.pallas_call(
        functools.partial(expert_kernel, capacity),
        out_shape=[shape((rows, model_width), f32)] * 2
        + [shape((16, 8, rows), f32)]
        + [shape(compact, bf16)] * 2
        + [shape((slots, units), bf16)] * 3,
        in_specs=[vmem] * 3 + [anywhere] * 3,
        out_specs=[vmem] * 3 + [anywhere] * 5,
        scratch_shapes=scratch
        + [
            pltpu.SemaphoreType.DMA((copies,)),
            pltpu.SemaphoreType.DMA((copies,)),
            pltpu.SemaphoreType.DMA((parts + 7,)),
            pltpu.SemaphoreType.DMA((2, 3)),
            pltpu.SemaphoreType.REGULAR((2,)),
        ],
        compiler_params=pltpu.CompilerParams(
            collective_id=collective_id, has_side_effects=True, vmem_limit_bytes=62 * 2**20
        ),
    )(table, moe_in, cot_in, gate_full, up_full, down_full)
    rows_in, rows_grad = rows_in.reshape(slots, -1), rows_grad.reshape(slots, -1)
    return grad, mixture, given[:, 0], rows_in, rows_grad, *units_out


def tn(left, right):
    return lax.dot_general(left, right, (((0,), (0,)), ((), ())), preferred_element_type=f32)


def accumulate(target, blocks, arrived):
    def add(n, carry):
        for into, source in blocks:
            value = target[(n,) + into].astype(f32) + arrived[(n,) + source].astype(f32)
            target[(n,) + into] = value.astype(target.dtype)
        return carry
    lax.fori_loop(0, 4, add, 0)


ROW = 16


def finish_kernel(*refs):
    (
        grad_branch, mixed, attn_in, hidden_in, query, key, value, normed_query, normed_key,
        scale_query, scale_key, seen, cosine, sine, grad_after, gains, small_in, out_rows,
        query_w, key_w, value_w, output_w, rows_in, rows_grad, middle, grad_gate, grad_up,
    ) = refs[:27]
    weight_outs, small_out, given_out, given_grad = refs[27:31], *refs[31:34]
    gate_out, up_out, down_out, expert_landing = refs[34:38]
    refs = refs[38:]
    sides, lefts, grads, mixed_grad, query_normed, key_normed, attn_grad, grad_rows = refs[:8]
    owns, small_buf, small_own, small_core, w_slots = refs[8:13]
    left_slots, right_slots, send_slots, came, result = refs[13:18]
    parts = 17
    landing, refs = refs[18 : 18 + 5 * parts], refs[18 + 5 * parts :]
    send_sems, recv_sems, local_sems, load_sems = refs
    here = Place()
    rep, x, y, z, ex = here.rep, here.x, here.y, here.z, here.ex
    model_width = grad_branch.shape[1]
    columns = model_width // 4
    enter([*here.peers, here.other_core])
    copies = Copies(send_sems, recv_sems)
    local = []

    def keep(source, target):
        copy = pltpu.make_async_copy(source, target, local_sems.at[len(local)])
        copy.start()
        local.append(copy)
        return copy

    returned = []

    def give(source, target):
        keep(source.at[ex], target.at[ex])
        for peer in here.peers:
            returned.append(copies.start(source.at[peer[1]], target.at[ex], peer))

    mine, theirs = (pl.ds(pl.multiple_of(r * 1024, 1024), 1024) for r in (rep, 1 - rep))
    core_left = [
        copies.start(ref.at[:, theirs], sides.at[n], here.other_core)
        for n, ref in enumerate((mixed, attn_in))
    ]
    core_grad = {}

    def share(n):
        core_grad[n] = copies.start(
            grads.at[n, pl.ds(0, 128)], grads.at[n, pl.ds(128, 128)], here.other_core
        )

    def turn_left(n, ref):
        core_left[n].wait_recv()
        def body(k, carry):
            at = pl.multiple_of(rep * 1024 + k * 128, 128)
            lefts[n, k, :, pl.ds(0, 128)] = ref[:, pl.ds(at, 128)].astype(f32).T.astype(bf16)
            at = pl.multiple_of(k * 128, 128)
            lefts[n, k, :, pl.ds(128, 128)] = sides[n, :, pl.ds(at, 128)].astype(f32).T.astype(bf16)
            return carry
        lax.fori_loop(0, 8, body, 0)

    stream, loads = [(w, n) for w in (output_w, value_w, query_w, key_w) for n in range(4)], {}

    def load(n):
        if n < len(stream):
            w, k = stream[n]
            loads[n] = pltpu.make_async_copy(
                w.at[pl.ds(k * columns, columns)], w_slots.at[n % 2], load_sems.at[n % 2]
            )
            loads[n].start()

    def back_mixed():
        for k in range(4):
            loads[k].wait()
            at = pl.ds(k * columns, columns)
            mixed_grad[:, at] = nt(grad_branch[...], w_slots[k % 2]).astype(bf16)
            load(k + 2)

    def unrotate(grad):
        turned = grad * sine[...]
        lane = lax.broadcasted_iota(jnp.int32, turned.shape, 1)
        sign = jnp.where(lane < HEAD_DIM // 2, 1.0, -1.0)
        return grad * cosine[...] + sign * pltpu.roll(turned, HEAD_DIM // 2, 1)

    def heads(first, count):
        def body(n, carry):
            at = pl.ds(pl.multiple_of((first + n) * HEAD_DIM, HEAD_DIM), HEAD_DIM)
            q, k, v, grad = query[:, at], key[:, at], value[:, at], mixed_grad[:, at]
            scores = jnp.where(seen[...] > 0, nt(q, k) * HEAD_DIM ** (-0.5), masked_score)
            weights = jnp.exp(scores - jnp.max(scores, axis=1, keepdims=True))
            probs = weights / jnp.sum(weights, axis=1, keepdims=True)
            grads[2, pl.ds(0, 128), at] = tn(probs.astype(bf16), grad).astype(bf16)
            grad_att = nt(grad, v)
            grad_scores = probs * (grad_att - jnp.sum(probs * grad_att, axis=1, keepdims=True))
            grad_scores = grad_scores.astype(bf16)
            query_normed[:, at] = unrotate(nn(grad_scores, k) * HEAD_DIM ** (-0.5))
            key_normed[:, at] = unrotate(tn(grad_scores, q) * HEAD_DIM ** (-0.5))
            return carry
        lax.fori_loop(0, count, body, 0)

    sums = {}

    def back_norm(n, grad_ref, normed_ref, scale_ref):
        def body(k, total):
            rows = pl.ds(pl.multiple_of(k * ROW, ROW), ROW)
            grad, normed = grad_ref[rows], normed_ref[rows]
            total = total + jnp.sum(grad * normed, axis=0, keepdims=True)
            grad = grad * gains[pl.ds(n, 1)]
            mean = jnp.mean(grad * normed, axis=1, keepdims=True)
            grads[n, rows] = (scale_ref[rows] * (grad - normed * mean)).astype(bf16)
            return total
        start = jnp.zeros((1, model_width), f32)
        sums[n] = lax.fori_loop(0, 128 // ROW, body, start)

    def back_attn(n, at_stream, fresh):
        for k in range(4):
            loads[at_stream + k].wait()
            at = pl.ds(k * columns, columns)
            grad = nt(grads[n, pl.ds(0, 128)], w_slots[(at_stream + k) % 2])
            attn_grad[:, at] = grad if fresh else attn_grad[:, at] + grad
            load(at_stream + k + 2)

    def back_hidden():
        def body(k, total):
            rows = pl.ds(pl.multiple_of(k * ROW, ROW), ROW)
            hidden, grad = hidden_in[rows].astype(f32), attn_grad[rows]
            scale = lax.rsqrt(jnp.mean(hidden * hidden, axis=1, keepdims=True) + epsilon)
            normed = hidden * scale
            total = total + jnp.sum(grad * normed, axis=0, keepdims=True)
            grad = grad * gains[pl.ds(2, 1)]
            mean = jnp.mean(grad * normed, axis=1, keepdims=True)
            grad = grad_after[rows] + scale * (grad - normed * mean)
            grad = grad.astype(bf16).reshape(2, 8, model_width)
            grad_rows[pl.ds(2 * k, 2)] = grad
            return total
        start = jnp.zeros((1, model_width), f32)
        sums[2] = lax.fori_loop(0, 128 // ROW, body, start)
        give(grad_rows, given_grad)
        pad = jnp.zeros((124, 128), f32)
        for k in range(model_width // 128):
            at = slice(k * 128, k * 128 + 128)
            rows = [*(sums[n][:, at] for n in range(3)), gains[pl.ds(3, 1), at]]
            block = jnp.concatenate([*rows, pad], axis=0).T.reshape(2, 64, 128)
            at = (k // 8, k // 2 % 4, k % 2)
            small_buf[at] = small_in[at] + block

    def halves():
        return pl.ds(0, 32), pl.ds(32, 32)

    one, two, last = {}, {}, {}

    def own_of(j):
        return owns.at[j % 6] if j < 16 else small_own

    def sum_one(j):
        own, (upper, lower) = own_of(j), halves()
        if j < 16:
            n, which = (3, 0) if j < 4 else ((2, 1), (0, 1), (1, 1))[j // 4 - 1]
            at = pl.ds(j % 4 * columns, columns)
            if j % 4 == 0:
                core_grad[n].wait_recv()
            if j >= 6:
                for copy in (*one[j - 6], *two[j - 6], *last[j - 6]):
                    copies.sent(copy)
            def body(k, carry):
                own[k // 2, k % 2] = nn(lefts[which, k], grads[n, :, at]).astype(bf16).reshape(2, 64, columns)
                return carry
            lax.fori_loop(0, 8, body, 0)
        else:
            core_grad["small"].wait_recv()
            def add(k, carry):
                own[k] = small_buf[rep, k] + small_core[k]
                return carry
            lax.fori_loop(0, 4, add, 0)
        one[j] = (
            copies.start(own.at[:, 1 - y, :, upper], landing[5 * j], here.other_y),
            copies.start(own.at[:, :, 1 - x, lower], landing[5 * j + 1], here.other_x),
        )

    def sum_two(j):
        own, (upper, lower) = own_of(j), halves()
        from_y, from_x = landing[5 * j], landing[5 * j + 1]
        one[j][0].wait_recv()
        accumulate(own, [((y, 1 - x, upper), (1 - x,))], from_y)
        a = copies.start(own.at[:, y, 1 - x, upper], landing[5 * j + 2], here.other_x)
        one[j][1].wait_recv()
        accumulate(own, [((1 - y, x, lower), (1 - y,))], from_x)
        b = copies.start(own.at[:, 1 - y, x, lower], landing[5 * j + 3], here.other_y)
        accumulate(own, [((y, x, upper), (x,)), ], from_y)
        accumulate(own, [((y, x, lower), (y,)), ], from_x)
        two[j] = a, b

    def sum_three(j):
        own, (upper, lower) = own_of(j), halves()
        two[j][0].wait_recv()
        accumulate(own, [((y, x, upper), ())], landing[5 * j + 2])
        two[j][1].wait_recv()
        accumulate(own, [((y, x, lower), ())], landing[5 * j + 3])
        last[j] = [
            copies.start(own.at[(z + k) % 4, y, x], landing[5 * j + 4].at[k - 1], here.other_z[k - 1])
            for k in range(1, 4)
        ]

    def sum_four(j):
        own, arrived = own_of(j), landing[5 * j + 4]
        for copy in last[j]:
            copy.wait_recv()
        total = own[z, y, x].astype(f32) + arrived[0].astype(f32)
        total = total + arrived[1].astype(f32) + arrived[2].astype(f32)
        if j == 16:
            small_out[...] = total
        else:
            n = (3, 2, 0, 1)[j // 4]
            weight_outs[n][:, pl.ds(j % 4 * columns, columns)] = total

    tasks, task_loads, sent_halves, stored = [], {}, {}, {}
    for side in range(2):
        for k in range(2):
            for kind in range(3):
                tasks.append((side, k, kind))

    def task_load(n):
        if n < len(tasks):
            side, k, kind = tasks[n]
            whose = rep if side else 1 - rep
            if kind < 2:
                left = rows_in.at[:, pl.ds(pl.multiple_of(whose * 1024 + k * 512, 512), 512)]
                right = (grad_gate, grad_up)[kind]
            else:
                left = middle.at[:, pl.ds(pl.multiple_of(whose * 512, 512), 512)]
                right = rows_grad.at[:, pl.ds(k * 1024, 1024)]
            task_loads[n] = (
                pltpu.make_async_copy(left, left_slots.at[n % 2], load_sems.at[2 + n % 2]),
                pltpu.make_async_copy(right, right_slots.at[n % 2], load_sems.at[4 + n % 2]),
            )
            for copy in task_loads[n]:
                copy.start()

    def task(n):
        side, k, kind = tasks[n]
        for copy in task_loads[n]:
            copy.wait()
        left, right = left_slots.at[n % 2], right_slots.at[n % 2]
        if side == 0:
            target = send_slots.at[n % 2]
            if n >= 2:
                copies.sent(sent_halves[n - 2])
            def body(m, carry):
                at = pl.ds(pl.multiple_of(m * 256, 256), 256)
                target[at] = tn(left[:, at], right[...]).astype(bf16)
                return carry
            lax.fori_loop(0, 2, body, 0)
            sent_halves[n] = copies.start(target, expert_landing.at[n], here.other_core)
        else:
            at = n - len(tasks) // 2
            sent_halves[at].wait_recv()
            back = pltpu.make_async_copy(expert_landing.at[at], came, load_sems.at[6])
            back.start()
            if n - 1 in stored:
                stored[n - 1].wait()
            back.wait()
            def body(m, carry):
                rows = pl.ds(pl.multiple_of(m * 256, 256), 256)
                result[rows] = tn(left[:, rows], right[...]) + came[rows].astype(f32)
                return carry
            lax.fori_loop(0, 2, body, 0)
            if kind < 2:
                target = (gate_out, up_out)[kind].at[pl.ds(k * 512, 512)]
            else:
                target = down_out.at[:, pl.ds(k * 1024, 1024)]
            stored[n] = pltpu.make_async_copy(result, target, load_sems.at[7])
            stored[n].start()
        task_load(n + 2)

    give(out_rows, given_out)
    grads[3, pl.ds(0, 128)] = grad_branch[...]
    share(3)
    for n in range(2):
        load(n)
        task_load(n)
    turn_left(0, mixed)
    for step in range(parts + 3):
        for behind, stage in enumerate((sum_one, sum_two, sum_three, sum_four)):
            if 0 <= step - behind < parts:
                stage(step - behind)
        if step == 0:
            back_mixed()
            turn_left(1, attn_in)
        elif step == 1:
            heads(0, 8)
        elif step == 2:
            heads(8, 8)
            share(2)
        elif step == 3:
            back_norm(0, query_normed, normed_query, scale_query)
            share(0)
            back_norm(1, key_normed, normed_key, scale_key)
            share(1)
        elif step == 4:
            back_attn(2, 4, True)
        elif step == 5:
            back_attn(0, 8, False)
        elif step == 6:
            back_attn(1, 12, False)
        elif step == 7:
            back_hidden()
            core_grad["small"] = copies.start(small_buf.at[1 - rep], small_core, here.other_core)
        elif step < 8 + len(tasks) // 2:
            task(2 * (step - 8))
            task(2 * (step - 8) + 1)
    stored[len(tasks) - 1].wait()
    for copy in returned:
        copy.wait_recv()
    for copy in local:
        copy.wait()
    copies.finish()


def run_finish(arrays, weights, expert, collective_id):
    rows, model_width = arrays[0].shape
    columns = model_width // 4
    vmem, anywhere = pl.BlockSpec(memory_space=pltpu.VMEM), pl.BlockSpec(memory_space=pl.ANY)
    shape, tile = jax.ShapeDtypeStruct, (4, 2, 2, 64)
    scratch = [
        pltpu.VMEM((2, rows, 1024), bf16),
        pltpu.VMEM((2, 8, 128, 256), bf16),
        pltpu.VMEM((4, 2 * rows, model_width), bf16),
        pltpu.VMEM((rows, model_width), bf16),
        pltpu.VMEM((rows, model_width), f32),
        pltpu.VMEM((rows, model_width), f32),
        pltpu.VMEM((rows, model_width), f32),
        pltpu.VMEM((16, 8, model_width), bf16),
        pltpu.VMEM((6, *tile, columns), bf16),
        pltpu.VMEM((2, *tile, 128), f32),
        pltpu.VMEM((*tile, 128), f32),
        pltpu.VMEM((*tile, 128), f32),
        pltpu.VMEM((2, columns, model_width), bf16),
        pltpu.VMEM((2, 1024, 512), bf16),
        pltpu.VMEM((2, 1024, 1024), bf16),
        pltpu.VMEM((2, 512, 1024), bf16),
        pltpu.VMEM((512, 1024), bf16),
        pltpu.VMEM((512, 1024), f32),
    ]
    for j in range(17):
        width, dtype = (columns, bf16) if j < 16 else (128, f32)
        scratch += [
            pltpu.VMEM((4, 2, 32, width), dtype),
            pltpu.VMEM((4, 2, 32, width), dtype),
            pltpu.VMEM((4, 32, width), dtype),
            pltpu.VMEM((4, 32, width), dtype),
            pltpu.VMEM((3, 64, width), dtype),
        ]
    copies = 7 * 17 + 30 + 7 + 6
    return pl.pallas_call(
        finish_kernel,
        out_shape=[shape((64, model_width), f32)] * 4
        + [shape((64, 128), f32)]
        + [shape((16, 8, model_width), bf16)] * 2
        + [shape((1024, 1024), f32)] * 2
        + [shape((512, 2048), f32), shape((6, 512, 1024), bf16)],
        in_specs=[vmem] * len(arrays) + [anywhere] * (len(weights) + len(expert)),
        out_specs=[vmem] * 5 + [anywhere] * 6,
        scratch_shapes=scratch
        + [
            pltpu.SemaphoreType.DMA((copies,)),
            pltpu.SemaphoreType.DMA((copies,)),
            pltpu.SemaphoreType.DMA((2,)),
            pltpu.SemaphoreType.DMA((8,)),
        ],
        compiler_params=pltpu.CompilerParams(
            collective_id=collective_id, has_side_effects=True, vmem_limit_bytes=62 * 2**20
        ),
    )(*arrays, *weights, *expert)


Z_LAST = (2, 6, 11)


def start_kernel(*refs):
    query_w, key_w, value_w, output_w, gains_w, rows_in, cot_in, seen, cosine, sine = refs[:10]
    fulls, (hidden_out, cot_out), refs = refs[10:15], refs[15:17], refs[17:]
    gain_rows, attn_out, query_out, key_out, value_out, mixed, *norm_outs = refs[:10]
    product, slots, came_rows, gain_cols, attn_in, query, key, value = refs[10:18]
    normed_query, normed_key, scale_query, scale_key = refs[18:22]
    send_sems, recv_sems, local_sems, load_sems = refs[22:]
    here = Place()
    rep, x, y, z, ex = here.rep, here.x, here.y, here.z, here.ex
    model_width = query_w.shape[1]
    enter([*here.peers, here.other_core])
    copies = Copies(send_sems, recv_sems)
    local = []

    def keep(source, target):
        copy = pltpu.make_async_copy(source, target, local_sems.at[len(local)])
        copy.start()
        local.append(copy)
        return copy

    def give(source, target):
        return [keep(source.at[ex], target.at[ex])] + [
            copies.start(source.at[peer[1]], target.at[ex], peer) for peer in here.peers
        ]

    def take(moved):
        moved[0].wait()
        for copy in moved[1:]:
            copy.wait_recv()

    shards = (query_w, key_w, value_w, output_w, gains_w)
    parts = [(4, 0, 64)] + [(i, k * 16, 16) for i in range(4) for k in range(4)]
    first_stage, one, two, cores = {}, {}, {}, {}

    def spans(j):
        i, first, rows = parts[j]
        half = rows // 2
        return fulls[i].at[rep], pl.ds(first, rows), pl.ds(first, half), pl.ds(first + half, half)

    def along_z(source, target):
        return [
            copies.start(source, target, here.near, here.end),
            copies.start(source, target, here.far, here.end),
            copies.start(source, target, here.across, here.middle),
            copies.start(source, target, here.own_end, here.middle),
        ]

    def pass_on(sent, blocks):
        def arrived():
            sent[1].wait_recv()
            sent[2].wait_recv()
        pl.when(here.middle)(arrived)
        sent.append(copies.start(blocks, blocks, here.own_end, here.middle))

    def arrived_z(sent):
        pl.when(here.middle)(sent[0].wait_recv)
        def arrived():
            sent[3].wait_recv()
            sent[4].wait_recv()
        pl.when(here.end)(arrived)

    other_side = pl.ds(jnp.where(z == 1, 2, 0), 2)

    def stage_open(j):
        full, rows, upper, lower = spans(j)
        shard, own = shards[parts[j][0]], full.at[z, y, x]
        kept = keep(shard.at[rows], own.at[rows])
        if j in Z_LAST:
            a = copies.start(shard.at[upper], own.at[upper], here.other_x)
            first_stage[j] = (a, copies.start(shard.at[lower], own.at[lower], here.other_y)), kept
        else:
            first_stage[j] = along_z(shard.at[rows], own.at[rows]), kept

    def stage_pass(j):
        if j not in Z_LAST:
            full, rows, _, _ = spans(j)
            pass_on(first_stage[j][0], full.at[other_side, y, x, rows])

    def stage_one(j):
        full, rows, upper, lower = spans(j)
        sent, kept = first_stage[j]
        kept.wait()
        if j in Z_LAST:
            sent[0].wait_recv()
            a = full.at[z, y, :, upper]
            two_a = copies.start(a, a, here.other_y)
            sent[1].wait_recv()
            b = full.at[z, :, x, lower]
            one[j] = two_a, copies.start(b, b, here.other_x)
            return
        arrived_z(sent)
        a, b, own = full.at[:, y, x, upper], full.at[:, y, x, lower], full.at[:, y, x, rows]
        one[j] = copies.start(a, a, here.other_x), copies.start(b, b, here.other_y)
        cores[j] = [copies.start(own, own, here.other_core)]

    def stage_two(j):
        full, rows, upper, lower = spans(j)
        one[j][0].wait_recv()
        if j in Z_LAST:
            one[j][1].wait_recv()
            plane = full.at[z, :, :, rows]
            two[j] = along_z(plane, plane)
            cores[j] = [copies.start(plane, plane, here.other_core)]
            return
        a = full.at[:, y, :, upper]
        two_a = copies.start(a, a, here.other_y)
        one[j][1].wait_recv()
        b = full.at[:, :, x, lower]
        two[j] = two_a, copies.start(b, b, here.other_x)
        for c in (full.at[:, y, 1 - x, upper], full.at[:, 1 - y, x, lower]):
            cores[j].append(copies.start(c, c, here.other_core))

    def stage_three(j):
        full, rows, upper, lower = spans(j)
        if j in Z_LAST:
            pass_on(two[j], full.at[other_side, :, :, rows])
            return
        two[j][0].wait_recv()
        a = full.at[:, 1 - y, :, upper]
        cores[j].append(copies.start(a, a, here.other_core))
        two[j][1].wait_recv()
        b = full.at[:, :, 1 - x, lower]
        cores[j].append(copies.start(b, b, here.other_core))

    def stage_four(j):
        if j in Z_LAST:
            full, rows, _, _ = spans(j)
            arrived_z(two[j])
            for k in range(1, 4):
                plane = full.at[(z + k) % 4, :, :, rows]
                cores[j].append(copies.start(plane, plane, here.other_core))

    def complete(j):
        for copy in cores[j]:
            copy.wait_recv()

    def turn_gains():
        complete(0)
        copy = pltpu.make_async_copy(fulls[4], gain_cols, load_sems.at[2])
        copy.start()
        copy.wait()
        for k in range(model_width // 128):
            block = gain_cols[k // 8, k // 2 % 4, k % 2].reshape(128, 128).astype(f32)
            gain_rows[:, k * 128 : k * 128 + 128] = block.T[:8]

    def norm_rows(moved):
        take(moved)
        copy = pltpu.make_async_copy(hidden_out, came_rows, load_sems.at[2])
        copy.start()
        copy.wait()
        def body(k, carry):
            hidden = came_rows[pl.ds(2 * k, 2)].reshape(ROW, model_width).astype(f32)
            scale = lax.rsqrt(jnp.mean(hidden * hidden, axis=1, keepdims=True) + epsilon)
            rows = pl.ds(pl.multiple_of(k * ROW, ROW), ROW)
            attn_in[rows] = (hidden * scale * gain_rows[pl.ds(2, 1)]).astype(bf16)
            return carry
        lax.fori_loop(0, 128 // ROW, body, 0)

    def load(i, n):
        copy = pltpu.make_async_copy(
            fulls[i].at[n // 2, pl.ds(n % 2 * 2, 2)], slots.at[n % 2], load_sems.at[n % 2]
        )
        copy.start()
        return copy

    def project(i):
        for j in range(1 + 4 * i, 5 + 4 * i):
            complete(j)
        loads = {n: load(i, n) for n in range(2)}
        for n in range(4):
            loads[n].wait()
            left = attn_in[:, pl.ds(n * 512, 512)]
            for k in range(4):
                at = pl.ds(k * 512, 512)
                grown = nn(left, slots[n % 2, :, :, :, :, at].reshape(512, 512))
                product[:, at] = grown if n == 0 else product[:, at] + grown
            if n + 2 < 4:
                loads[n + 2] = load(i, n + 2)

    def norm_heads(n, normed_ref, scale_ref, low_ref):
        lane = lax.broadcasted_iota(jnp.int32, (ROW, HEAD_DIM), 1)
        sign = jnp.where(lane < HEAD_DIM // 2, -1.0, 1.0)
        def body(k, carry):
            rows = pl.ds(pl.multiple_of(k * ROW, ROW), ROW)
            pre = product[rows]
            scale = lax.rsqrt(jnp.mean(pre * pre, axis=1, keepdims=True) + epsilon)
            normed = pre * scale
            normed_ref[rows], scale_ref[rows] = normed, scale
            gained = normed * gain_rows[pl.ds(n, 1)]
            for h in range(HEADS):
                at = slice(h * HEAD_DIM, (h + 1) * HEAD_DIM)
                turned = sign * pltpu.roll(gained[:, at], HEAD_DIM // 2, 1)
                low_ref[rows, at] = (gained[:, at] * cosine[rows] + turned * sine[rows]).astype(bf16)
            return carry
        lax.fori_loop(0, 128 // ROW, body, 0)

    def heads(first, count):
        def body(n, carry):
            at = pl.ds(pl.multiple_of((first + n) * HEAD_DIM, HEAD_DIM), HEAD_DIM)
            scores = nt(query[:, at], key[:, at]) * HEAD_DIM ** (-0.5)
            scores = jnp.where(seen[...] > 0, scores, masked_score)
            weights = jnp.exp(scores - jnp.max(scores, axis=1, keepdims=True))
            probs = weights / jnp.sum(weights, axis=1, keepdims=True)
            mixed[:, at] = nn(probs.astype(bf16), value[:, at]).astype(bf16)
            return carry
        lax.fori_loop(0, count, body, 0)

    stage_open(0)
    stage_open(1)
    moved_rows = give(rows_in, hidden_out)
    moved_cot, written = [], []
    for step in range(len(parts) + 3):
        if 1 <= step < len(parts) - 1:
            stage_open(step + 1)
        if step < len(parts):
            stage_pass(step)
        for behind, stage in enumerate((stage_one, stage_two, stage_three, stage_four), 1):
            if 0 <= step - behind < len(parts):
                stage(step - behind)
        if step == 4:
            turn_gains()
        elif step == 6:
            norm_rows(moved_rows)
            written.append(keep(attn_in, attn_out))
        elif step == 8:
            project(0)
        elif step == 9:
            norm_heads(0, normed_query, scale_query, query)
            written.append(keep(query, query_out))
            written.append(keep(normed_query, norm_outs[0]))
            written.append(keep(scale_query, norm_outs[2]))
        elif step == 10:
            moved_cot = give(cot_in, cot_out)
        elif step == 12:
            project(1)
        elif step == 13:
            norm_heads(1, normed_key, scale_key, key)
            written.append(keep(key, key_out))
            written.append(keep(normed_key, norm_outs[1]))
            written.append(keep(scale_key, norm_outs[3]))
        elif step == 16:
            project(2)
            value[...] = product[...].astype(bf16)
            written.append(keep(value, value_out))
        elif step == 17:
            heads(0, 6)
        elif step == 18:
            heads(6, 6)
        elif step == 19:
            heads(12, 4)
    for j in range(13, 17):
        complete(j)
    take(moved_cot)
    for copy in written:
        copy.wait()
    copies.finish()


def run_start(shards, rows, cot, visible, cosine, sine, collective_id):
    model_width = shards[0].shape[1]
    vmem, anywhere = pl.BlockSpec(memory_space=pltpu.VMEM), pl.BlockSpec(memory_space=pl.ANY)
    shape = jax.ShapeDtypeStruct
    own_rows = [(shape((128, model_width), dtype)) for dtype in (bf16,) * 5 + (f32,) * 2]
    *fulls, hidden_in, cot_in, gain_rows, attn_in, query, key, value, mixed, nq, nk, sq, sk = pl.pallas_call(
        start_kernel,
        out_shape=[shape((2, 4, 2, 2) + a.shape, a.dtype) for a in shards]
        + [shape(rows.shape, bf16)] * 2
        + [shape((8, model_width), f32)]
        + own_rows
        + [shape((128, 1), f32)] * 2,
        in_specs=[anywhere] * 7 + [vmem] * 3,
        out_specs=[anywhere] * 7 + [vmem] + [anywhere] * 4 + [vmem] + [anywhere] * 4,
        scratch_shapes=[
            pltpu.VMEM((128, model_width), f32),
            pltpu.VMEM((2, 2, 2, 2, 64, model_width), bf16),
            pltpu.VMEM(rows.shape, bf16),
            pltpu.VMEM((2, 4, 2, 2, 64, 128), bf16),
            *[pltpu.VMEM((128, model_width), dtype) for dtype in (bf16,) * 4 + (f32,) * 2],
            *[pltpu.VMEM((128, 1), f32)] * 2,
            pltpu.SemaphoreType.DMA((14 * 17 + 30,)),
            pltpu.SemaphoreType.DMA((14 * 17 + 30,)),
            pltpu.SemaphoreType.DMA((27,)),
            pltpu.SemaphoreType.DMA((3,)),
        ],
        compiler_params=pltpu.CompilerParams(
            collective_id=collective_id, has_side_effects=True, vmem_limit_bytes=62 * 2**20
        ),
    )(*shards, rows, cot, visible, cosine, sine)
    fulls = [a.reshape(-1, a.shape[-1]) for a in fulls]
    hidden_in, cot_in = (a.reshape(128, model_width) for a in (hidden_in, cot_in))
    return fulls, hidden_in, cot_in, gain_rows, attn_in, query, key, value, mixed, nq, nk, sq, sk


def has_kernels():
    return (lax.axis_size("rep"), lax.axis_size("ex")) == (2, 16)


def exchange(array):
    return lax.all_to_all(array, "ex", split_axis=0, concat_axis=0, tiled=True)


def start(shards, gains, inbound_rows, inbound_cot, visible, cosine, sine):
    block_rows, model_width = inbound_rows.shape[1:]
    row_count = inbound_rows.shape[0] * block_rows
    if has_kernels():
        wide = jnp.pad(gains, ((0, 0), (0, 128 - gains.shape[1])))
        full, hidden_in, cot_in, gain_rows, attn_in, *qkv, mixed, nq, nk, sq, sk = run_start(
            [*shards, wide], inbound_rows, inbound_cot, visible.astype(f32), cosine[:, 0], sine[:, 0], 1
        )
        *weights, wide = full
        qkv = [a.reshape(row_count, HEADS, HEAD_DIM) for a in qkv]
        router = wide[:, 4 : gains.shape[1]]
        return weights, gain_rows[:4], router, hidden_in, cot_in, attn_in, qkv, mixed, (nq, nk, sq, sk)
    gather = functools.partial(lax.all_gather, axis_name=("rep", "ex"), axis=0, tiled=True)
    weights = query_full, key_full, value_full, _ = [gather(a) for a in shards]
    gains = gather(jnp.pad(gains, ((0, 0), (0, -gains.shape[1] % 128))))[:, : gains.shape[1]]
    gain_rows = gains[:, :4].astype(f32).T
    query_scale, key_scale, attn_scale, _ = gain_rows
    hidden_in, cot_in = (exchange(a).reshape(row_count, model_width) for a in (inbound_rows, inbound_cot))
    hidden = hidden_in.astype(f32)
    normed_attn, scale_attn = normalize(hidden)
    attn_in = (normed_attn * attn_scale).astype(bf16)
    query_pre = jnp.dot(attn_in, query_full, preferred_element_type=f32)
    key_pre = jnp.dot(attn_in, key_full, preferred_element_type=f32)
    value_pre = jnp.dot(attn_in, value_full, preferred_element_type=f32)
    normed_query, scale_query = normalize(query_pre)
    normed_key, scale_key = normalize(key_pre)
    query_norm = (normed_query * query_scale).reshape(row_count, HEADS, HEAD_DIM)
    key_norm = (normed_key * key_scale).reshape(row_count, HEADS, HEAD_DIM)
    query_low = (query_norm * cosine + rotate_half(query_norm) * sine).astype(bf16)
    key_low = (key_norm * cosine + rotate_half(key_norm) * sine).astype(bf16)
    value_low = value_pre.astype(bf16).reshape(row_count, HEADS, HEAD_DIM)
    scores = attention_scores(query_low, key_low, visible)
    peak = jnp.max(scores, axis=-1, keepdims=True)
    weights_exp = jnp.exp(scores - peak)
    probs = weights_exp / jnp.sum(weights_exp, axis=-1, keepdims=True)
    probs_low = probs.astype(bf16)
    mixed = jnp.einsum("hqk,khd->qhd", probs_low, value_low, preferred_element_type=f32)
    mixed = mixed.reshape(row_count, model_width).astype(bf16)
    qkv = query_low, key_low, value_low
    norms = normed_query, normed_key, scale_query, scale_key
    return weights, gain_rows, gains[:, 4:], hidden_in, cot_in, attn_in, qkv, mixed, norms


def slots_of(tables, capacity):
    experts, me = tables.shape[1] // 2, lax.axis_index("ex")
    gates = lax.dynamic_index_in_dim(tables, me, 1, keepdims=True)
    slots = lax.dynamic_index_in_dim(tables, experts + me, 1, keepdims=True)
    return slots == jnp.arange(capacity, dtype=f32)[None, :, None], gates


def experts_of_group(moe_in, cot_in, table, gate_full, up_full, down_full, capacity):
    if has_kernels():
        return run_experts(moe_in, cot_in, table, gate_full, up_full, down_full, capacity, 2)
    tables = lax.all_gather(table, "ex", axis=0)
    picked, gate_rows = slots_of(tables, capacity)
    picked_low = picked.astype(bf16)
    slot_gate = jnp.sum(jnp.where(picked, gate_rows, 0.0), axis=2).reshape(-1, 1)

    def pick(rows):
        rows = lax.all_gather(rows, "ex", axis=0)
        rows = jnp.einsum("sct,std->scd", picked_low, rows, preferred_element_type=f32)
        return rows.astype(bf16).reshape(-1, rows.shape[-1])

    def spread(rows):
        rows = rows.reshape(*picked_low.shape[:2], -1)
        rows = jnp.einsum("sct,scd->std", picked_low, rows, preferred_element_type=f32)
        return lax.psum_scatter(rows.astype(bf16), "ex", scatter_dimension=0).astype(f32)

    rows_in, rows_cot = pick(moe_in), pick(cot_in)
    gate_pre = jnp.dot(rows_in, gate_full, preferred_element_type=f32)
    up_pre = jnp.dot(rows_in, up_full, preferred_element_type=f32)
    sigma = jax.nn.sigmoid(gate_pre)
    silu = gate_pre * sigma
    middle = (silu * up_pre).astype(bf16)
    expert_out = jnp.dot(middle, down_full, preferred_element_type=f32).astype(bf16)
    slot_grad = jnp.sum(rows_cot.astype(f32) * expert_out.astype(f32), axis=1)
    rows_grad = (slot_gate * rows_cot.astype(f32)).astype(bf16)
    grad_middle = jnp.dot(rows_grad, down_full.T, preferred_element_type=f32)
    grad_gate_low = (grad_middle * up_pre * sigma * (1.0 + gate_pre * (1.0 - sigma))).astype(bf16)
    grad_up_low = (grad_middle * silu).astype(bf16)
    grad_rows = jnp.dot(grad_gate_low, gate_full.T, preferred_element_type=f32)
    grad_rows = grad_rows + jnp.dot(grad_up_low, up_full.T, preferred_element_type=f32)
    weighted = slot_gate * expert_out.astype(f32)
    slot_grad = slot_grad.reshape(*picked.shape[:2], 1)
    back = exchange(jnp.sum(jnp.where(picked, slot_grad, 0.0), axis=1))
    sums = spread(grad_rows.astype(bf16)), spread(weighted.astype(bf16))
    return *sums, back, rows_in, rows_grad, middle, grad_gate_low, grad_up_low


def exact_dot(left, right):
    return jnp.dot(left, right, precision=lax.Precision.HIGHEST, preferred_element_type=f32)


def finish(
    grad_branch, mixed, attn_in, hidden_in, query_low, key_low, value_low, normed_query, normed_key,
    scale_query, scale_key, visible, cosine, sine, grad_after, query_scale, key_scale, attn_scale,
    grad_moe_scale, moe_in, grad_logits, output, query_full, key_full, value_full, output_full,
    rows_in, rows_grad, middle, grad_gate_low, grad_up_low,
):
    row_count, model_width = mixed.shape
    group_size = lax.axis_size("ex")
    block_rows = row_count // group_size
    if has_kernels():
        experts = grad_logits.shape[1]
        wide = jnp.pad(grad_logits, ((0, 0), (4, 124 - experts)))
        wide = exact_dot(moe_in.T, wide)
        gains = jnp.stack([query_scale, key_scale, attn_scale, grad_moe_scale], axis=0)
        arrays = [
            grad_branch, mixed, attn_in, hidden_in,
            *(a.reshape(row_count, model_width) for a in (query_low, key_low, value_low)),
            normed_query, normed_key, scale_query, scale_key, visible.astype(f32),
            cosine[:, 0], sine[:, 0], grad_after, jnp.pad(gains, ((0, 4), (0, 0))),
            wide.reshape(2, 4, 2, 2, 64, 128), output.reshape(group_size, block_rows, model_width),
        ]
        *weights, summed, given_out, given_grad, gate, up, down, _ = run_finish(
            arrays,
            [query_full, key_full, value_full, output_full],
            [rows_in, rows_grad, middle, grad_gate_low, grad_up_low],
            3,
        )
        rows = [a.reshape(row_count, model_width) for a in (given_out, given_grad)]
        return weights, summed[:, : 4 + experts], rows, (gate, up, down)
    both = ("rep", "ex")
    scores = attention_scores(query_low, key_low, visible)
    probs = jax.nn.softmax(scores, axis=-1)
    probs_low = probs.astype(bf16)
    normed_attn, scale_attn = normalize(hidden_in.astype(f32))
    grad_mixed = (
        jnp.dot(grad_branch, output_full.T, preferred_element_type=f32)
        .astype(bf16)
        .reshape(row_count, HEADS, HEAD_DIM)
    )
    grad_value = jnp.einsum("hqk,qhd->khd", probs_low, grad_mixed, preferred_element_type=f32)
    grad_att = jnp.einsum("qhd,khd->hqk", grad_mixed, value_low, preferred_element_type=f32)
    grad_scores = (probs * (grad_att - jnp.sum(probs * grad_att, axis=-1, keepdims=True))).astype(
        bf16
    )
    grad_query_rot = jnp.einsum(
        "hqk,khd->qhd", grad_scores, key_low, preferred_element_type=f32
    ) * HEAD_DIM ** (-0.5)
    grad_key_rot = jnp.einsum(
        "hqk,qhd->khd", grad_scores, query_low, preferred_element_type=f32
    ) * HEAD_DIM ** (-0.5)
    grad_query_normed = (grad_query_rot * cosine + rotate_back(grad_query_rot * sine)).reshape(
        row_count, model_width
    )
    grad_key_normed = (grad_key_rot * cosine + rotate_back(grad_key_rot * sine)).reshape(
        row_count, model_width
    )
    grad_query_scale = jnp.sum(grad_query_normed * normed_query, axis=0)
    grad_key_scale = jnp.sum(grad_key_normed * normed_key, axis=0)
    grad_query_pre = norm_back(grad_query_normed * query_scale, normed_query, scale_query)
    grad_key_pre = norm_back(grad_key_normed * key_scale, normed_key, scale_key)
    grad_query_pre = grad_query_pre.astype(bf16)
    grad_key_pre = grad_key_pre.astype(bf16)
    grad_value_pre = grad_value.reshape(row_count, model_width).astype(bf16)
    grad_attn_in = jnp.dot(grad_query_pre, query_full.T, preferred_element_type=f32)
    grad_attn_in = grad_attn_in + jnp.dot(grad_key_pre, key_full.T, preferred_element_type=f32)
    grad_attn_in = grad_attn_in + jnp.dot(grad_value_pre, value_full.T, preferred_element_type=f32)
    grad_attn_scale = jnp.sum(grad_attn_in * normed_attn, axis=0)
    grad_hidden = grad_after + norm_back(grad_attn_in * attn_scale, normed_attn, scale_attn)
    sums = []
    for left, right in (
        (attn_in, grad_query_pre),
        (attn_in, grad_key_pre),
        (attn_in, grad_value_pre),
        (mixed, grad_branch),
    ):
        grad = jnp.dot(left.T, right, preferred_element_type=f32).astype(bf16)
        sums.append(lax.psum_scatter(grad, both, scatter_dimension=0, tiled=True).astype(f32))
    four = [grad_query_scale, grad_key_scale, grad_attn_scale, grad_moe_scale]
    grad_router = exact_dot(moe_in.T, grad_logits)
    small = jnp.concatenate([jnp.stack(four, axis=1), grad_router], axis=1)
    small = lax.psum_scatter(small, both, scatter_dimension=0, tiled=True)
    expert = []
    for left, right in ((rows_in, grad_gate_low), (rows_in, grad_up_low), (middle, rows_grad)):
        grad = jnp.dot(left.T, right, preferred_element_type=f32).astype(bf16)
        expert.append(lax.psum_scatter(grad, "rep", scatter_dimension=0, tiled=True).astype(f32))
    rows = [exchange(output), exchange(grad_hidden.astype(bf16))]
    return sums, small, rows, expert


def body(
    tokens,
    out_cot,
    destination,
    doc_lengths,
    routes,
    fill_order,
    query_weight,
    key_weight,
    value_weight,
    output_weight,
    query_gain,
    key_gain,
    attn_gain,
    moe_gain,
    router_weight,
    expert_gate,
    expert_up,
    expert_down,
):
    group_size = lax.axis_size("ex")
    row_count, model_width = tokens.shape
    block_rows = row_count // group_size
    row_index = jnp.arange(row_count, dtype=jnp.int32)
    placed = destination // row_count % group_size * block_rows + destination % block_rows
    to_send = (placed[None, :] == row_index[:, None]).astype(bf16)
    inbound = jnp.einsum(
        "pr,brd->bpd", to_send, jnp.stack([tokens, out_cot]), preferred_element_type=f32
    ).astype(bf16)
    gains = jnp.concatenate(
        [jnp.stack([query_gain, key_gain, attn_gain, moe_gain], axis=1), router_weight], axis=1
    )
    segment, position, live_rows = segment_tables(doc_lengths[0], row_count)
    visible = (segment[:, None] == segment[None, :]) & (row_index[None, :] <= row_index[:, None])
    cosine, sine = rope_tables(position)
    shards = [query_weight, key_weight, value_weight, output_weight]
    inbound = inbound.reshape(2, group_size, block_rows, model_width)
    weights, gain_rows, router_full, hidden_in, cot_in, attn_in, qkv, mixed, norms = start(
        shards, gains, inbound[0], inbound[1], visible, cosine, sine
    )
    query_full, key_full, value_full, output_full = weights
    query_scale, key_scale, attn_scale, moe_scale = gain_rows
    query_low, key_low, value_low = qkv
    normed_query, normed_key, scale_query, scale_key = norms
    gate_full = lax.all_gather(expert_gate[0], "rep", axis=0, tiled=True)
    up_full = lax.all_gather(expert_up[0], "rep", axis=0, tiled=True)
    down_full = lax.all_gather(expert_down[0], "rep", axis=0, tiled=True)

    live_column = live_rows.astype(f32)[:, None]
    hidden = hidden_in.astype(f32)
    branch = jnp.dot(mixed, output_full, preferred_element_type=f32)
    after_attn = hidden + live_column * branch
    normed_moe, scale_moe = normalize(after_attn)
    moe_in = (normed_moe * moe_scale).astype(bf16)
    logits = jnp.dot(moe_in, router_full, preferred_element_type=f32)
    router_probs = jax.nn.softmax(logits, axis=-1)
    experts = router_full.shape[1]
    capacity = row_count * routes.shape[1] // experts
    slot_table, kept = slot_tables(routes, fill_order[0], live_rows, experts, capacity)
    gates = jnp.where(kept, router_probs, 0.0)

    table = jnp.concatenate([gates.T, slot_table.T.astype(f32)], axis=0)
    (
        grad_moe_in,
        mixture,
        grad_rprobs,
        rows_in,
        rows_grad,
        middle,
        grad_gate_low,
        grad_up_low,
    ) = experts_of_group(moe_in, cot_in, table, gate_full, up_full, down_full, capacity)
    grad_rprobs = grad_rprobs.T
    output = (after_attn + mixture).astype(bf16)

    grad_out = cot_in.astype(f32)
    grad_logits = router_probs * (
        grad_rprobs - jnp.sum(router_probs * grad_rprobs, axis=-1, keepdims=True)
    )
    grad_moe_in = grad_moe_in + jnp.dot(
        grad_logits, router_full.T, precision=lax.Precision.HIGHEST, preferred_element_type=f32
    )
    grad_moe_scale = jnp.sum(grad_moe_in * normed_moe, axis=0)
    grad_after = grad_out + norm_back(grad_moe_in * moe_scale, normed_moe, scale_moe)
    grad_branch = (live_column * grad_after).astype(bf16)
    sums, small, rows, expert = finish(
        grad_branch, mixed, attn_in, hidden_in, query_low, key_low, value_low, normed_query,
        normed_key, scale_query, scale_key, visible, cosine, sine, grad_after, query_scale,
        key_scale, attn_scale, grad_moe_scale, moe_in, grad_logits, output, query_full, key_full, value_full, output_full,
        rows_in, rows_grad, middle, grad_gate_low, grad_up_low,
    )
    owned_query, owned_key, owned_value, owned_output = sums
    owned_gate, owned_up, owned_down = (a[None] for a in expert)
    outbound = jnp.dot(
        to_send.T, jnp.concatenate(rows, axis=1), preferred_element_type=f32
    ).astype(bf16)
    return (
        outbound[:, :model_width],
        outbound[:, model_width:],
        owned_query,
        owned_key,
        owned_value,
        owned_output,
        small[:, 0],
        small[:, 1],
        small[:, 2],
        small[:, 3],
        small[:, 4:],
        owned_gate,
        owned_up,
        owned_down,
    )


def solution(mesh):
    rows, row = P(("rep", "ex"), None), P(("rep", "ex"))
    expert = P("ex", "rep", None)
    return jax.shard_map(
        body,
        mesh=mesh,
        in_specs=(rows, rows, row) + (rows,) * 7 + (row,) * 4 + (rows,) + (expert,) * 3,
        out_specs=(rows,) * 6 + (row,) * 4 + (rows,) + (expert,) * 3,
        check_vma=False,
    )
```

```python
import functools

import jax
import jax.numpy as jnp
from jax import lax
from jax.experimental import pallas as pl
from jax.experimental.pallas import tpu as pltpu
from jax.sharding import PartitionSpec as P

HEADS = 16
HEAD_DIM = 128

epsilon = 1e-05
rope_base = 10000.0
masked_score = -1e30
bf16 = jnp.bfloat16
f32 = jnp.float32


def normalize(values):
    scale = lax.rsqrt(jnp.mean(values * values, axis=-1, keepdims=True) + epsilon)
    return (values * scale, scale)


def norm_back(grad_normed, normed, scale):
    return scale * (grad_normed - normed * jnp.mean(grad_normed * normed, axis=-1, keepdims=True))


def rotate_half(values):
    middle = values.shape[-1] // 2
    return jnp.concatenate([-values[..., middle:], values[..., :middle]], axis=-1)


def rotate_back(values):
    middle = values.shape[-1] // 2
    return jnp.concatenate([values[..., middle:], -values[..., :middle]], axis=-1)


def rope_tables(position):
    steps = jnp.arange(HEAD_DIM // 2, dtype=f32) * (2.0 / HEAD_DIM)
    inverse = rope_base ** (-steps)
    angle = position.astype(f32)[:, None] * inverse[None, :]
    cosine = jnp.concatenate([jnp.cos(angle), jnp.cos(angle)], axis=-1)[:, None, :]
    sine = jnp.concatenate([jnp.sin(angle), jnp.sin(angle)], axis=-1)[:, None, :]
    return (cosine, sine)


def segment_tables(lengths, row_count):
    count = lengths.shape[0]
    numbers = jnp.arange(count, dtype=jnp.int32)
    before = (numbers[None, :] < numbers[:, None]).astype(jnp.int32)
    starts = jnp.sum(before * lengths[None, :], axis=1)
    ends = starts + lengths
    row_index = jnp.arange(row_count, dtype=jnp.int32)
    segment = jnp.sum((row_index[:, None] >= ends[None, :]).astype(jnp.int32), axis=1)
    begin = jnp.sum(jnp.where(segment[:, None] == numbers[None, :], starts[None, :], 0), axis=1)
    return (segment, row_index - begin, segment < count - 1)


def slot_tables(routes, filling, live_rows, experts, capacity):
    row_count, top_count = routes.shape
    order = jnp.arange(row_count * top_count, dtype=jnp.int32)
    rows = jnp.arange(row_count, dtype=jnp.int32)
    hot_row = (filling[None, :] // top_count == rows[:, None]).astype(bf16)
    hot_choice = (filling % top_count)[:, None] == jnp.arange(top_count, dtype=jnp.int32)[None, :]
    high = jnp.where(hot_choice, (order // 64)[:, None], 0).astype(bf16)
    lower = jnp.where(hot_choice, (order % 64)[:, None], 0).astype(bf16)
    ranks = jnp.dot(
        hot_row, jnp.concatenate([high, lower], axis=1), preferred_element_type=f32
    ).astype(jnp.int32)
    rank = ranks[:, :top_count] * 64 + ranks[:, top_count:]
    chosen = routes[:, :, None] == jnp.arange(experts, dtype=jnp.int32)[None, None, :]
    rank_table = jnp.sum(jnp.where(chosen, rank[:, :, None], 0), axis=1)
    counted = jnp.any(chosen, axis=1) & live_rows[:, None]
    earlier = counted[:, None, :] & (rank_table[:, None, :] < rank_table[None, :, :])
    slot = jnp.sum(earlier.astype(jnp.int32), axis=0)
    kept = counted & (slot < capacity)
    return (jnp.where(kept, slot, -1), kept)


def attention_scores(query_low, key_low, visible):
    scores = jnp.einsum(
        "qhd,khd->hqk", query_low, key_low, preferred_element_type=f32
    ) * HEAD_DIM ** (-0.5)
    return jnp.where(visible[None], scores, masked_score)


MESH = pl.DeviceIdType.MESH


class Place:
    def __init__(self):
        self.rep, self.ex = lax.axis_index("rep"), lax.axis_index("ex")
        self.x, self.y, self.z = self.ex % 2, self.ex // 2 % 2, self.ex // 4
        self.other_x = (self.rep, self.ex + 1 - 2 * self.x)
        self.other_y = (self.rep, self.ex + 2 - 4 * self.y)
        self.other_core = (1 - self.rep, self.ex)
        self.other_z = [(self.rep, (self.ex + 4 * k) % 16) for k in range(1, 4)]
        self.middle = (self.z == 1) | (self.z == 2)
        self.end = jnp.logical_not(self.middle)
        near = jnp.where(self.z < 2, 1, 2)
        self.end_z = jnp.where(self.z < 2, 0, 3)
        self.near, self.far, self.across, self.own_end, self.far_end = (
            (self.rep, zz * 4 + self.ex % 4) for zz in (near, 3 - near, 3 - self.z, self.end_z, 3 - self.end_z)
        )
        self.peers = [(self.rep, (self.ex + k) % 16) for k in range(1, 16)]


def enter(devices):
    barrier = pltpu.get_barrier_semaphore()
    for device in devices:
        pl.semaphore_signal(barrier, inc=1, device_id=device, device_id_type=MESH)
    pl.semaphore_wait(barrier, len(devices))


class Copies:
    def __init__(self, send_sems, recv_sems):
        self.send_sems, self.recv_sems, self.made = send_sems, recv_sems, []
        self.done, self.whens = set(), {}

    def start(self, source, target, device, when=None):
        at = len(self.made)
        copy = pltpu.make_async_remote_copy(
            src_ref=source,
            dst_ref=target,
            send_sem=self.send_sems.at[at],
            recv_sem=self.recv_sems.at[at],
            device_id=device,
            device_id_type=MESH,
        )
        if when is None:
            copy.start()
        else:
            pl.when(when)(copy.start)
        self.made.append(copy)
        self.whens[id(copy)] = when
        return copy

    def sent(self, copy):
        if id(copy) not in self.done:
            self.done.add(id(copy))
            when = self.whens[id(copy)]
            if when is None:
                copy.wait_send()
            else:
                pl.when(when)(copy.wait_send)

    def finish(self):
        for copy in self.made:
            self.sent(copy)


def nt(left, right):
    return lax.dot_general(left, right, (((1,), (1,)), ((), ())), preferred_element_type=f32)


def nn(left, right):
    return jnp.dot(left, right, preferred_element_type=f32)


def hot_slots(table, expert, capacity):
    experts, rows = table.shape
    lane = lax.broadcasted_iota(jnp.int32, (capacity, experts), 1)
    mine = jnp.where(lane == expert, 1.0, 0.0).astype(bf16)
    slot = nn(mine, table.astype(bf16))
    wanted = lax.broadcasted_iota(jnp.int32, (capacity, rows), 0).astype(f32)
    return jnp.where(slot == wanted, 1.0, 0.0).astype(bf16)


PIECES = 4


def expert_kernel(capacity, *refs):
    table, moe, cot, gate_w, up_w, down_w = refs[:6]
    grad_out, mix_out, given, *kept_outs = refs[6:14]
    refs = refs[14:]
    tables, hot, hot_row, hot_gate, gate_col, grad_col, back = refs[:7]
    rows_in, rows_cot, acc, to_gate, to_up, middle, result = refs[7:14]
    gu_slots, down_slots, to_slots, send_slots, column_slots = refs[14:19]
    parts = 2 * PIECES
    pick_buffers = [refs[19 + 3 * j : 22 + 3 * j] for j in range(parts)]
    refs = refs[19 + 3 * parts :]
    spread_buffers = [refs[2 * j : 2 * j + 2] for j in range(parts)]
    send_sems, recv_sems, local_sems, load_sems, ready = refs[2 * parts :]
    here = Place()
    x, y, z, ex = here.x, here.y, here.z, here.ex
    by_y, by_x = here.other_y[1], here.other_x[1]
    experts = table.shape[0] // 2
    units = gate_w.shape[1]
    width = moe.shape[1] // PIECES
    half = width // 2
    enter(here.peers)
    copies = Copies(send_sems, recv_sems)
    local = []

    def keep(source, target):
        copy = pltpu.make_async_copy(source, target, local_sems.at[len(local)])
        copy.start()
        local.append(copy)
        return copy

    def block(zz, yy, xx):
        return (zz * 2 + yy) * 2 + xx

    def piece(j):
        return j % PIECES * width

    gu_loads, down_loads = {}, {}

    def load_gu(n):
        if n < parts:
            rows = pl.ds(piece(n), width)
            gu_loads[n] = [
                pltpu.make_async_copy(w.at[rows], gu_slots.at[n % 2, k], load_sems.at[n % 2, k])
                for k, w in enumerate((gate_w, up_w))
            ]
            for copy in gu_loads[n]:
                copy.start()

    def load_down(n):
        if n < parts:
            columns = pl.ds(piece(n), width)
            down_loads[n] = pltpu.make_async_copy(
                down_w.at[:, columns], down_slots.at[n % 2], load_sems.at[n % 2, 2]
            )
            down_loads[n].start()

    def stage_z(j):
        source = (moe if j < PIECES else cot).at[:, pl.ds(piece(j), width)]
        target = pick_buffers[j][0].at[z]
        to_near = copies.start(source, target, here.near, here.end)
        to_far = copies.start(source, target, here.far, here.end)
        across = copies.start(source, target, here.across, here.middle)
        to_end = copies.start(source, target, here.own_end, here.middle)
        return [to_near, to_far, across, to_end], keep(source, target)

    def relay(j):
        (_, to_far, across, _), _ = held[j]
        def arrived():
            to_far.wait_recv()
            across.wait_recv()
        pl.when(here.middle)(arrived)
        blocks = pick_buffers[j][0].at[pl.ds(jnp.where(z == 1, 2, 0), 2)]
        held[j][0].append(copies.start(blocks, blocks, here.own_end, here.middle))

    def stage_one(j, sent, kept):
        column, from_x, from_y = pick_buffers[j]
        to_near, _, _, to_end, relayed = sent
        kept.wait()
        pl.when(here.middle)(to_near.wait_recv)
        def arrived():
            to_end.wait_recv()
            relayed.wait_recv()
        pl.when(here.end)(arrived)
        return (
            copies.start(column.at[:, :, pl.ds(0, half)], from_x, here.other_x),
            copies.start(column.at[:, :, pl.ds(half, half)], from_y, here.other_y),
        )

    def landing(j):
        return rows_in if j < PIECES else rows_cot

    def pick_own(j):
        column, into = pick_buffers[j][0], landing(j)
        def body(n, carry):
            picked = nn(hot[0, block(n, y, x)], column[n])
            into[n, y, x, :, pl.ds(piece(j), width)] = picked.astype(bf16)
            return carry
        lax.fori_loop(0, 4, body, 0)

    def pick_moved(j):
        (_, from_x, from_y), into, first = pick_buffers[j], landing(j), piece(j)
        def body(n, carry):
            picked = nn(hot[0, block(n, y, 1 - x)], from_x[n])
            into[n, y, 1 - x, :, pl.ds(first, half)] = picked.astype(bf16)
            picked = nn(hot[0, block(n, 1 - y, x)], from_y[n])
            into[n, 1 - y, x, :, pl.ds(first + half, half)] = picked.astype(bf16)
            return carry
        lax.fori_loop(0, 4, body, 0)

    second = {}

    def stage_two(j, one):
        (column, from_x, from_y), into, first = pick_buffers[j], landing(j), piece(j)
        to_y, to_x = to_slots.at[j % 2, 0], to_slots.at[j % 2, 1]
        if j >= 2:
            copies.sent(second[j - 2][0])
            copies.sent(second[j - 2][1])
        def own_part(n, carry):
            at = block(n, y, x)
            to_y[n, x] = nn(hot[1, at], column[n, :, pl.ds(0, half)]).astype(bf16)
            to_x[n, y] = nn(hot[2, at], column[n, :, pl.ds(half, half)]).astype(bf16)
            return carry
        lax.fori_loop(0, 4, own_part, 0)
        one[0].wait_recv()
        def x_part(n, carry):
            to_y[n, 1 - x] = nn(hot[1, block(n, y, 1 - x)], from_x[n]).astype(bf16)
            return carry
        lax.fori_loop(0, 4, x_part, 0)
        a = copies.start(to_y, into.at[:, y, :, :, pl.ds(first, half)], here.other_y)
        one[1].wait_recv()
        def y_part(n, carry):
            to_x[n, 1 - y] = nn(hot[2, block(n, 1 - y, x)], from_y[n]).astype(bf16)
            return carry
        lax.fori_loop(0, 4, y_part, 0)
        b = copies.start(to_x, into.at[:, :, x, :, pl.ds(first + half, half)], here.other_x)
        second[j] = a, b

    def build(n, carry):
        both = tables[n]
        for k, expert in enumerate((ex, by_y, by_x)):
            hot[k, n] = hot_slots(both[experts:], expert, capacity)
        turned = both.T
        lane = lax.broadcasted_iota(jnp.int32, turned.shape, 1)
        wanted = lax.broadcasted_iota(jnp.int32, (turned.shape[0], capacity), 1).astype(f32)
        for k, expert in enumerate((ex, by_y, by_x)):
            slot = jnp.sum(jnp.where(lane == experts + expert, turned, 0.0), axis=1, keepdims=True)
            gate = jnp.sum(jnp.where(lane == expert, turned, 0.0), axis=1, keepdims=True)
            hot_row[k, n] = jnp.where(slot == wanted, 1.0, 0.0).astype(bf16)
            hot_gate[k, n] = jnp.where(slot == wanted, gate, 0.0).astype(bf16)
        row = lax.broadcasted_iota(jnp.int32, (experts, both.shape[1]), 0)
        gates = jnp.sum(jnp.where(row == ex, both[:experts], 0.0), axis=0, keepdims=True)
        gate_col[n] = jnp.sum(hot[0, n].astype(f32) * gates, axis=1, keepdims=True)
        grad_col[n] = jnp.zeros((capacity, 1), f32)
        return carry

    def flat(ref, first, size):
        return ref[:, :, :, :, pl.ds(first, size)].reshape(-1, size)

    def grow(k, columns, value, fresh):
        acc[k, :, columns] = value if fresh else acc[k, :, columns] + value

    def tile(n):
        return pl.ds(pl.multiple_of(n * 256, 256), 256)

    def gate_and_up(p):
        for copy in gu_loads[p]:
            copy.wait()
        def body(n, carry):
            left = flat(rows_in, piece(p), width)
            for k in range(2):
                grow(k, tile(n), nn(left, gu_slots[p % 2, k, :, tile(n)]), p == 0)
            return carry
        lax.fori_loop(0, units // 256, body, 0)
        load_gu(p + 2)

    def activate(n, carry):
        rows = pl.ds(pl.multiple_of(n * 32, 32), 32)
        gate, up = acc[0, rows], acc[1, rows]
        sigma = 1.0 / (1.0 + jnp.exp(-gate))
        silu = gate * sigma
        middle[rows] = (silu * up).astype(bf16)
        to_gate[rows] = (up * sigma * (1.0 + gate * (1.0 - sigma))).astype(bf16)
        to_up[rows] = silu.astype(bf16)
        return carry

    def store(first, value):
        result[:, :, :, :, pl.ds(first, 256)] = value.astype(bf16).reshape(4, 2, 2, capacity, 256)

    def down(p):
        down_loads[p].wait()
        for n in range(width // 256):
            store(piece(p) + n * 256, nn(middle[...], down_slots[p % 2, :, pl.ds(n * 256, 256)]))
        load_down(p + 2)

    def back_down(p):
        n_load = p + PIECES
        columns = pl.ds(piece(p), width)
        def rows(n, carry):
            at = (n // 4, n // 2 % 2, n % 2, slice(None), columns)
            mine = rows_cot[at].astype(f32)
            dots = jnp.sum(mine * result[at].astype(f32), axis=1, keepdims=True)
            grad_col[n] = grad_col[n] + dots
            rows_cot[at] = (gate_col[n] * mine).astype(bf16)
            return carry
        lax.fori_loop(0, 16, rows, 0)
        down_loads[n_load].wait()
        def body(n, carry):
            value = nt(flat(rows_cot, piece(p), width), down_slots[n_load % 2, tile(n)])
            grow(0, tile(n), value, p == 0)
            return carry
        lax.fori_loop(0, units // 256, body, 0)
        load_down(n_load + 2)

    def back_activate(n, carry):
        rows = pl.ds(pl.multiple_of(n * 32, 32), 32)
        grad = acc[0, rows]
        to_gate[rows] = (grad * to_gate[rows].astype(f32)).astype(bf16)
        to_up[rows] = (grad * to_up[rows].astype(f32)).astype(bf16)
        return carry

    def back_rows(p):
        n_load = p + PIECES
        for copy in spread_one[p]:
            copies.sent(copy)
        for copy in gu_loads[n_load]:
            copy.wait()
        for n in range(width // 256):
            rows = pl.ds(n * 256, 256)
            value = nt(to_gate[...], gu_slots[n_load % 2, 0, rows])
            store(piece(p) + n * 256, value + nt(to_up[...], gu_slots[n_load % 2, 1, rows]))
        load_gu(n_load + 2)

    def give_back(n, carry):
        grads = jnp.sum(hot[0, n].astype(f32) * grad_col[n], axis=0, keepdims=True)
        back[n] = jnp.broadcast_to(grads, back.shape[1:])
        return carry

    spread_one, spread_two, spread_three = {}, {}, {}

    def cols(j):
        return pl.ds(piece(j), half), pl.ds(piece(j) + half, half)

    def term(j, which, at, rows):
        return nn((hot_gate if j < PIECES else hot_row)[which, at], rows)

    def send_one(j):
        (from_y, from_x), (a, b) = spread_buffers[j], cols(j)
        spread_one[j] = (
            copies.start(result.at[:, 1 - y, :, :, a], from_y, here.other_y),
            copies.start(result.at[:, :, 1 - x, :, b], from_x, here.other_x),
        )

    def send_two(j):
        (from_y, from_x), (a, b) = spread_buffers[j], cols(j)
        to_x, to_y = send_slots.at[j % 2, 0], send_slots.at[j % 2, 1]
        if j >= 2:
            copies.sent(spread_two[j - 2][0])
            copies.sent(spread_two[j - 2][1])
        if j % PIECES == 0:
            pl.semaphore_wait(ready.at[j // PIECES], 5)
        spread_one[j][0].wait_recv()
        def x_part(n, carry):
            at = block(n, y, 1 - x)
            total = term(j, 0, at, result[n, y, 1 - x, :, a]) + term(j, 1, at, from_y[n, 1 - x])
            to_x[n] = total.astype(bf16)
            return carry
        lax.fori_loop(0, 4, x_part, 0)
        first = copies.start(to_x, pick_buffers[j][1], here.other_x)
        spread_one[j][1].wait_recv()
        def y_part(n, carry):
            at = block(n, 1 - y, x)
            total = term(j, 0, at, result[n, 1 - y, x, :, b]) + term(j, 2, at, from_x[n, 1 - y])
            to_y[n] = total.astype(bf16)
            return carry
        lax.fori_loop(0, 4, y_part, 0)
        spread_two[j] = first, copies.start(to_y, pick_buffers[j][2], here.other_y)

    def send_three(j):
        (from_y, from_x), (a, b) = spread_buffers[j], cols(j)
        from_z, more_a, more_b = pick_buffers[j]
        column = column_slots.at[j % 3]
        if j >= 3:
            for copy in spread_three[j - 3]:
                copies.sent(copy)
        for copy in spread_two[j]:
            copy.wait_recv()
        def body(n, carry):
            at = block(n, y, x)
            total = term(j, 0, at, result[n, y, x, :, a]) + term(j, 1, at, from_y[n, x])
            column[n, :, pl.ds(0, half)] = (total + more_a[n].astype(f32)).astype(bf16)
            total = term(j, 0, at, result[n, y, x, :, b]) + term(j, 2, at, from_x[n, y])
            column[n, :, pl.ds(half, half)] = (total + more_b[n].astype(f32)).astype(bf16)
            return carry
        lax.fori_loop(0, 4, body, 0)
        spread_three[j] = [
            copies.start(
                column.at[pl.ds(jnp.where(z == 0, 1, 0), 3)], from_z.at[pl.ds(0, 3)], here.near, here.end
            ),
            copies.start(column.at[here.end_z], from_z.at[0], here.own_end, here.middle),
        ]

    def send_merged(j):
        column, from_z = column_slots.at[j % 3], pick_buffers[j][0]
        def merge():
            spread_three[j][0].wait_recv()
            first, came = jnp.where(z == 1, 2, 0), jnp.where(z == 1, 1, 0)
            for k in range(2):
                total = column[first + k].astype(f32) + from_z[came + k].astype(f32)
                column[first + k] = total.astype(bf16)
        pl.when(here.middle)(merge)
        spread_three[j] += [
            copies.start(column.at[3 - z], from_z.at[3], here.across, here.middle),
            copies.start(column.at[3 - here.end_z], from_z.at[1], here.far_end, here.middle),
        ]

    def send_four(j):
        from_z, out = pick_buffers[j][0], mix_out if j < PIECES else grad_out
        columns = pl.ds(piece(j), width)
        _, to_end, across, to_far_end = spread_three[j]
        def in_middle():
            across.wait_recv()
            total = column_slots[j % 3, z].astype(f32) + from_z[jnp.where(z == 1, 0, 2)].astype(f32)
            out[:, columns] = total + from_z[3].astype(f32)
        pl.when(here.middle)(in_middle)
        def at_end():
            to_end.wait_recv()
            to_far_end.wait_recv()
            total = column_slots[j % 3, z].astype(f32) + from_z[0].astype(f32)
            out[:, columns] = total + from_z[1].astype(f32)
        pl.when(here.end)(at_end)

    told = [copies.start(table, tables.at[ex], peer) for peer in here.peers]
    kept_table = keep(table, tables.at[ex])
    held, ones, written, returned = {}, {}, [], []
    for n in range(2):
        load_gu(n)
        load_down(n)
    for step in range(2 * parts + 4):
        if step == 0:
            held[0] = stage_z(0)
        if step + 1 < parts:
            held[step + 1] = stage_z(step + 1)
        if step < parts:
            relay(step)
        if step == 1:
            kept_table.wait()
            for copy in told:
                copy.wait_recv()
            lax.fori_loop(0, 16, build, 0)
        if 0 <= step - 1 < parts:
            ones[step - 1] = stage_one(step - 1, *held[step - 1])
        if 0 <= step - 2 < parts:
            stage_two(step - 2, ones[step - 2])
        for behind, send in enumerate((send_one, send_two, send_three, send_merged, send_four)):
            if 0 <= step - parts - behind < parts:
                send(step - parts - behind)
        if 0 <= step - 1 < parts:
            pick_own(step - 1)
        if 0 <= step - 2 < parts:
            pick_moved(step - 2)
            if (step - 2) % PIECES == PIECES - 1:
                for j in range(step - 1 - PIECES, step - 1):
                    for copy in (*ones[j], held[j][0][4]):
                        copies.sent(copy)
                for device in (here.other_x, here.other_y, *here.other_z):
                    pl.semaphore_signal(
                        ready.at[(step - 2) // PIECES], inc=1, device_id=device, device_id_type=MESH
                    )
        p = step - 3
        if 0 <= p < parts:
            second[p][0].wait_recv()
            second[p][1].wait_recv()
        if 0 <= p < PIECES:
            gate_and_up(p)
        if p == PIECES - 1:
            lax.fori_loop(0, acc.shape[1] // 32, activate, 0)
            written.append(keep(rows_in, kept_outs[0]))
            written.append(keep(middle, kept_outs[2]))
            for n in range(PIECES):
                down(n)
        if PIECES <= p < parts:
            back_down(p - PIECES)
        if p == parts - 1:
            lax.fori_loop(0, acc.shape[1] // 32, back_activate, 0)
            written.append(keep(rows_cot, kept_outs[1]))
            written.append(keep(to_gate, kept_outs[3]))
            written.append(keep(to_up, kept_outs[4]))
            lax.fori_loop(0, 16, give_back, 0)
            returned = [copies.start(back.at[peer[1]], given.at[ex], peer) for peer in here.peers]
            written.append(keep(back.at[ex], given.at[ex]))
        if 0 <= step - 3 - parts < PIECES:
            back_rows(step - 3 - parts)
    for copy in returned:
        copy.wait_recv()
    for copy in written:
        copy.wait()
    copies.finish()


def run_experts(moe_in, cot_in, table, gate_full, up_full, down_full, capacity, collective_id):
    rows, model_width = moe_in.shape
    units, parts = gate_full.shape[1], 2 * PIECES
    width = model_width // PIECES
    half, slots = width // 2, 16 * capacity
    vmem, anywhere = pl.BlockSpec(memory_space=pltpu.VMEM), pl.BlockSpec(memory_space=pl.ANY)
    compact = (4, 2, 2, capacity, model_width)
    scratch = [
        pltpu.VMEM((16, *table.shape), f32),
        pltpu.VMEM((3, 16, capacity, rows), bf16),
        pltpu.VMEM((3, 16, rows, capacity), bf16),
        pltpu.VMEM((3, 16, rows, capacity), bf16),
        pltpu.VMEM((16, capacity, 1), f32),
        pltpu.VMEM((16, capacity, 1), f32),
        pltpu.VMEM((16, 8, rows), f32),
        pltpu.VMEM(compact, bf16),
        pltpu.VMEM(compact, bf16),
        pltpu.VMEM((2, slots, units), f32),
        pltpu.VMEM((slots, units), bf16),
        pltpu.VMEM((slots, units), bf16),
        pltpu.VMEM((slots, units), bf16),
        pltpu.VMEM(compact, bf16),
        pltpu.VMEM((2, 2, width, units), bf16),
        pltpu.VMEM((2, units, width), bf16),
        pltpu.VMEM((2, 2, 4, 2, capacity, half), bf16),
        pltpu.VMEM((2, 2, 4, rows, half), bf16),
        pltpu.VMEM((3, 4, rows, width), bf16),
    ]
    for _ in range(parts):
        scratch += [
            pltpu.VMEM((4, rows, width), bf16),
            pltpu.VMEM((4, rows, half), bf16),
            pltpu.VMEM((4, rows, half), bf16),
        ]
    scratch += [pltpu.VMEM((4, 2, capacity, half), bf16)] * (2 * parts)
    copies = 17 * parts + 30
    shape = jax.ShapeDtypeStruct
    grad, mixture, given, rows_in, rows_grad, *units_out = pl.pallas_call(
        functools.partial(expert_kernel, capacity),
        out_shape=[shape((rows, model_width), f32)] * 2
        + [shape((16, 8, rows), f32)]
        + [shape(compact, bf16)] * 2
        + [shape((slots, units), bf16)] * 3,
        in_specs=[vmem] * 3 + [anywhere] * 3,
        out_specs=[vmem] * 3 + [anywhere] * 5,
        scratch_shapes=scratch
        + [
            pltpu.SemaphoreType.DMA((copies,)),
            pltpu.SemaphoreType.DMA((copies,)),
            pltpu.SemaphoreType.DMA((parts + 7,)),
            pltpu.SemaphoreType.DMA((2, 3)),
            pltpu.SemaphoreType.REGULAR((2,)),
        ],
        compiler_params=pltpu.CompilerParams(
            collective_id=collective_id, has_side_effects=True, vmem_limit_bytes=62 * 2**20
        ),
    )(table, moe_in, cot_in, gate_full, up_full, down_full)
    rows_in, rows_grad = rows_in.reshape(slots, -1), rows_grad.reshape(slots, -1)
    return grad, mixture, given[:, 0], rows_in, rows_grad, *units_out


def tn(left, right):
    return lax.dot_general(left, right, (((0,), (0,)), ((), ())), preferred_element_type=f32)


def accumulate(target, blocks, arrived):
    def add(n, carry):
        for into, source in blocks:
            value = target[(n,) + into].astype(f32) + arrived[(n,) + source].astype(f32)
            target[(n,) + into] = value.astype(target.dtype)
        return carry
    lax.fori_loop(0, 4, add, 0)


ROW = 16
RATE = 3


def finish_kernel(*refs):
    (
        grad_branch, mixed, attn_in, hidden_in, query, key, value, normed_query, normed_key,
        scale_query, scale_key, seen, cosine, sine, grad_after, gains, small_in, out_rows,
        query_w, key_w, value_w, output_w, rows_in, rows_grad, middle, grad_gate, grad_up,
    ) = refs[:27]
    weight_outs, small_out, given_out, given_grad = refs[27:31], *refs[31:34]
    gate_out, up_out, down_out, expert_landing = refs[34:38]
    refs = refs[38:]
    sides, lefts, grads, mixed_grad, query_normed, key_normed, attn_grad, grad_rows = refs[:8]
    owns, small_buf, small_own, small_core, w_slots = refs[8:13]
    left_slots, right_slots, send_slots, came, result = refs[13:18]
    parts = 17
    landing, refs = refs[18 : 18 + 5 * parts], refs[18 + 5 * parts :]
    send_sems, recv_sems, local_sems, load_sems = refs
    here = Place()
    rep, x, y, z, ex = here.rep, here.x, here.y, here.z, here.ex
    model_width = grad_branch.shape[1]
    columns = model_width // 4
    enter([*here.peers, here.other_core])
    copies = Copies(send_sems, recv_sems)
    local = []

    def keep(source, target):
        copy = pltpu.make_async_copy(source, target, local_sems.at[len(local)])
        copy.start()
        local.append(copy)
        return copy

    returned, waiting = [], []

    def give(source, target):
        keep(source.at[ex], target.at[ex])
        waiting.extend((source.at[peer[1]], target.at[ex], peer) for peer in here.peers)

    def send_some(count):
        for _ in range(min(count, len(waiting))):
            returned.append(copies.start(*waiting.pop(0)))

    mine, theirs = (pl.ds(pl.multiple_of(r * 1024, 1024), 1024) for r in (rep, 1 - rep))
    core_left = [
        copies.start(ref.at[:, theirs], sides.at[n], here.other_core)
        for n, ref in enumerate((mixed, attn_in))
    ]
    core_grad = {}

    def share(n):
        core_grad[n] = copies.start(
            grads.at[n, pl.ds(0, 128)], grads.at[n, pl.ds(128, 128)], here.other_core
        )

    def turn_left(n, ref):
        core_left[n].wait_recv()
        def body(k, carry):
            at = pl.multiple_of(rep * 1024 + k * 128, 128)
            lefts[n, k, :, pl.ds(0, 128)] = ref[:, pl.ds(at, 128)].astype(f32).T.astype(bf16)
            at = pl.multiple_of(k * 128, 128)
            lefts[n, k, :, pl.ds(128, 128)] = sides[n, :, pl.ds(at, 128)].astype(f32).T.astype(bf16)
            return carry
        lax.fori_loop(0, 8, body, 0)

    stream, loads = [(w, n) for w in (output_w, value_w, query_w, key_w) for n in range(4)], {}

    def load(n):
        if n < len(stream):
            w, k = stream[n]
            loads[n] = pltpu.make_async_copy(
                w.at[pl.ds(k * columns, columns)], w_slots.at[n % 2], load_sems.at[n % 2]
            )
            loads[n].start()

    def back_mixed():
        for k in range(4):
            loads[k].wait()
            at = pl.ds(k * columns, columns)
            mixed_grad[:, at] = nt(grad_branch[...], w_slots[k % 2]).astype(bf16)
            load(k + 2)

    def unrotate(grad):
        turned = grad * sine[...]
        lane = lax.broadcasted_iota(jnp.int32, turned.shape, 1)
        sign = jnp.where(lane < HEAD_DIM // 2, 1.0, -1.0)
        return grad * cosine[...] + sign * pltpu.roll(turned, HEAD_DIM // 2, 1)

    def heads(first, count):
        def body(n, carry):
            at = pl.ds(pl.multiple_of((first + n) * HEAD_DIM, HEAD_DIM), HEAD_DIM)
            q, k, v, grad = query[:, at], key[:, at], value[:, at], mixed_grad[:, at]
            scores = jnp.where(seen[...] > 0, nt(q, k) * HEAD_DIM ** (-0.5), masked_score)
            weights = jnp.exp(scores - jnp.max(scores, axis=1, keepdims=True))
            probs = weights / jnp.sum(weights, axis=1, keepdims=True)
            grads[2, pl.ds(0, 128), at] = tn(probs.astype(bf16), grad).astype(bf16)
            grad_att = nt(grad, v)
            grad_scores = probs * (grad_att - jnp.sum(probs * grad_att, axis=1, keepdims=True))
            grad_scores = grad_scores.astype(bf16)
            query_normed[:, at] = unrotate(nn(grad_scores, k) * HEAD_DIM ** (-0.5))
            key_normed[:, at] = unrotate(tn(grad_scores, q) * HEAD_DIM ** (-0.5))
            return carry
        lax.fori_loop(0, count, body, 0)

    sums = {}

    def back_norm(n, grad_ref, normed_ref, scale_ref):
        def body(k, total):
            rows = pl.ds(pl.multiple_of(k * ROW, ROW), ROW)
            grad, normed = grad_ref[rows], normed_ref[rows]
            total = total + jnp.sum(grad * normed, axis=0, keepdims=True)
            grad = grad * gains[pl.ds(n, 1)]
            mean = jnp.mean(grad * normed, axis=1, keepdims=True)
            grads[n, rows] = (scale_ref[rows] * (grad - normed * mean)).astype(bf16)
            return total
        start = jnp.zeros((1, model_width), f32)
        sums[n] = lax.fori_loop(0, 128 // ROW, body, start)

    def back_attn(n, at_stream, fresh):
        for k in range(4):
            loads[at_stream + k].wait()
            at = pl.ds(k * columns, columns)
            grad = nt(grads[n, pl.ds(0, 128)], w_slots[(at_stream + k) % 2])
            attn_grad[:, at] = grad if fresh else attn_grad[:, at] + grad
            load(at_stream + k + 2)

    def back_hidden():
        def body(k, total):
            rows = pl.ds(pl.multiple_of(k * ROW, ROW), ROW)
            hidden, grad = hidden_in[rows].astype(f32), attn_grad[rows]
            scale = lax.rsqrt(jnp.mean(hidden * hidden, axis=1, keepdims=True) + epsilon)
            normed = hidden * scale
            total = total + jnp.sum(grad * normed, axis=0, keepdims=True)
            grad = grad * gains[pl.ds(2, 1)]
            mean = jnp.mean(grad * normed, axis=1, keepdims=True)
            grad = grad_after[rows] + scale * (grad - normed * mean)
            grad = grad.astype(bf16).reshape(2, 8, model_width)
            grad_rows[pl.ds(2 * k, 2)] = grad
            return total
        start = jnp.zeros((1, model_width), f32)
        sums[2] = lax.fori_loop(0, 128 // ROW, body, start)
        give(grad_rows, given_grad)
        pad = jnp.zeros((124, 128), f32)
        for k in range(model_width // 128):
            at = slice(k * 128, k * 128 + 128)
            rows = [*(sums[n][:, at] for n in range(3)), gains[pl.ds(3, 1), at]]
            block = jnp.concatenate([*rows, pad], axis=0).T.reshape(2, 64, 128)
            at = (k // 8, k // 2 % 4, k % 2)
            small_buf[at] = small_in[at] + block

    def halves():
        return pl.ds(0, 32), pl.ds(32, 32)

    one, two, last = {}, {}, {}

    def own_of(j):
        return owns.at[j % 6] if j < 16 else small_own

    def sum_one(j):
        own, (upper, lower) = own_of(j), halves()
        if j < 16:
            n, which = (3, 0) if j < 4 else ((2, 1), (0, 1), (1, 1))[j // 4 - 1]
            at = pl.ds(j % 4 * columns, columns)
            if j % 4 == 0:
                core_grad[n].wait_recv()
            if j >= 6:
                for copy in (*one[j - 6], *two[j - 6], *last[j - 6]):
                    copies.sent(copy)
            def body(k, carry):
                own[k // 2, k % 2] = nn(lefts[which, k], grads[n, :, at]).astype(bf16).reshape(2, 64, columns)
                return carry
            lax.fori_loop(0, 8, body, 0)
        else:
            core_grad["small"].wait_recv()
            def add(k, carry):
                own[k] = small_buf[rep, k] + small_core[k]
                return carry
            lax.fori_loop(0, 4, add, 0)
        one[j] = (
            copies.start(own.at[:, 1 - y, :, upper], landing[5 * j], here.other_y),
            copies.start(own.at[:, :, 1 - x, lower], landing[5 * j + 1], here.other_x),
        )

    def sum_two(j):
        own, (upper, lower) = own_of(j), halves()
        from_y, from_x = landing[5 * j], landing[5 * j + 1]
        one[j][0].wait_recv()
        accumulate(own, [((y, 1 - x, upper), (1 - x,))], from_y)
        a = copies.start(own.at[:, y, 1 - x, upper], landing[5 * j + 2], here.other_x)
        one[j][1].wait_recv()
        accumulate(own, [((1 - y, x, lower), (1 - y,))], from_x)
        b = copies.start(own.at[:, 1 - y, x, lower], landing[5 * j + 3], here.other_y)
        accumulate(own, [((y, x, upper), (x,)), ], from_y)
        accumulate(own, [((y, x, lower), (y,)), ], from_x)
        two[j] = a, b

    def sum_three(j):
        own, (upper, lower) = own_of(j), halves()
        two[j][0].wait_recv()
        accumulate(own, [((y, x, upper), ())], landing[5 * j + 2])
        two[j][1].wait_recv()
        accumulate(own, [((y, x, lower), ())], landing[5 * j + 3])
        last[j] = [
            copies.start(own.at[(z + k) % 4, y, x], landing[5 * j + 4].at[k - 1], here.other_z[k - 1])
            for k in range(1, 4)
        ]

    def sum_four(j):
        own, arrived = own_of(j), landing[5 * j + 4]
        for copy in last[j]:
            copy.wait_recv()
        total = own[z, y, x].astype(f32) + arrived[0].astype(f32)
        total = total + arrived[1].astype(f32) + arrived[2].astype(f32)
        if j == 16:
            small_out[...] = total
        else:
            n = (3, 2, 0, 1)[j // 4]
            weight_outs[n][:, pl.ds(j % 4 * columns, columns)] = total

    tasks, task_loads, sent_halves, stored = [], {}, {}, {}
    for side in range(2):
        for k in range(2):
            for kind in range(3):
                tasks.append((side, k, kind))

    def task_load(n):
        if n < len(tasks):
            side, k, kind = tasks[n]
            whose = rep if side else 1 - rep
            if kind < 2:
                left = rows_in.at[:, pl.ds(pl.multiple_of(whose * 1024 + k * 512, 512), 512)]
                right = (grad_gate, grad_up)[kind]
            else:
                left = middle.at[:, pl.ds(pl.multiple_of(whose * 512, 512), 512)]
                right = rows_grad.at[:, pl.ds(k * 1024, 1024)]
            task_loads[n] = (
                pltpu.make_async_copy(left, left_slots.at[n % 2], load_sems.at[2 + n % 2]),
                pltpu.make_async_copy(right, right_slots.at[n % 2], load_sems.at[4 + n % 2]),
            )
            for copy in task_loads[n]:
                copy.start()

    def task(n):
        side, k, kind = tasks[n]
        for copy in task_loads[n]:
            copy.wait()
        left, right = left_slots.at[n % 2], right_slots.at[n % 2]
        if side == 0:
            target = send_slots.at[n % 2]
            if n >= 2:
                copies.sent(sent_halves[n - 2])
            def body(m, carry):
                at = pl.ds(pl.multiple_of(m * 256, 256), 256)
                target[at] = tn(left[:, at], right[...]).astype(bf16)
                return carry
            lax.fori_loop(0, 2, body, 0)
            sent_halves[n] = copies.start(target, expert_landing.at[n], here.other_core)
        else:
            at = n - len(tasks) // 2
            sent_halves[at].wait_recv()
            back = pltpu.make_async_copy(expert_landing.at[at], came, load_sems.at[6])
            back.start()
            if n - 1 in stored:
                stored[n - 1].wait()
            back.wait()
            def body(m, carry):
                rows = pl.ds(pl.multiple_of(m * 256, 256), 256)
                result[rows] = tn(left[:, rows], right[...]) + came[rows].astype(f32)
                return carry
            lax.fori_loop(0, 2, body, 0)
            if kind < 2:
                target = (gate_out, up_out)[kind].at[pl.ds(k * 512, 512)]
            else:
                target = down_out.at[:, pl.ds(k * 1024, 1024)]
            stored[n] = pltpu.make_async_copy(result, target, load_sems.at[7])
            stored[n].start()
        task_load(n + 2)

    give(out_rows, given_out)
    grads[3, pl.ds(0, 128)] = grad_branch[...]
    share(3)
    for n in range(2):
        load(n)
        task_load(n)
    turn_left(0, mixed)
    for step in range(parts + 3):
        for behind, stage in enumerate((sum_one, sum_two, sum_three, sum_four)):
            if 0 <= step - behind < parts:
                stage(step - behind)
        send_some(RATE)
        if step == 0:
            back_mixed()
            turn_left(1, attn_in)
        elif step == 1:
            heads(0, 8)
        elif step == 2:
            heads(8, 8)
            share(2)
        elif step == 3:
            back_norm(0, query_normed, normed_query, scale_query)
            share(0)
            back_norm(1, key_normed, normed_key, scale_key)
            share(1)
        elif step == 4:
            back_attn(2, 4, True)
        elif step == 5:
            back_attn(0, 8, False)
        elif step == 6:
            back_attn(1, 12, False)
        elif step == 7:
            back_hidden()
            core_grad["small"] = copies.start(small_buf.at[1 - rep], small_core, here.other_core)
        elif step < 8 + len(tasks) // 2:
            task(2 * (step - 8))
            task(2 * (step - 8) + 1)
    send_some(len(waiting))
    stored[len(tasks) - 1].wait()
    for copy in returned:
        copy.wait_recv()
    for copy in local:
        copy.wait()
    copies.finish()


def run_finish(arrays, weights, expert, collective_id):
    rows, model_width = arrays[0].shape
    columns = model_width // 4
    vmem, anywhere = pl.BlockSpec(memory_space=pltpu.VMEM), pl.BlockSpec(memory_space=pl.ANY)
    shape, tile = jax.ShapeDtypeStruct, (4, 2, 2, 64)
    scratch = [
        pltpu.VMEM((2, rows, 1024), bf16),
        pltpu.VMEM((2, 8, 128, 256), bf16),
        pltpu.VMEM((4, 2 * rows, model_width), bf16),
        pltpu.VMEM((rows, model_width), bf16),
        pltpu.VMEM((rows, model_width), f32),
        pltpu.VMEM((rows, model_width), f32),
        pltpu.VMEM((rows, model_width), f32),
        pltpu.VMEM((16, 8, model_width), bf16),
        pltpu.VMEM((6, *tile, columns), bf16),
        pltpu.VMEM((2, *tile, 128), f32),
        pltpu.VMEM((*tile, 128), f32),
        pltpu.VMEM((*tile, 128), f32),
        pltpu.VMEM((2, columns, model_width), bf16),
        pltpu.VMEM((2, 1024, 512), bf16),
        pltpu.VMEM((2, 1024, 1024), bf16),
        pltpu.VMEM((2, 512, 1024), bf16),
        pltpu.VMEM((512, 1024), bf16),
        pltpu.VMEM((512, 1024), f32),
    ]
    for j in range(17):
        width, dtype = (columns, bf16) if j < 16 else (128, f32)
        scratch += [
            pltpu.VMEM((4, 2, 32, width), dtype),
            pltpu.VMEM((4, 2, 32, width), dtype),
            pltpu.VMEM((4, 32, width), dtype),
            pltpu.VMEM((4, 32, width), dtype),
            pltpu.VMEM((3, 64, width), dtype),
        ]
    copies = 7 * 17 + 30 + 7 + 6
    return pl.pallas_call(
        finish_kernel,
        out_shape=[shape((64, model_width), f32)] * 4
        + [shape((64, 128), f32)]
        + [shape((16, 8, model_width), bf16)] * 2
        + [shape((1024, 1024), f32)] * 2
        + [shape((512, 2048), f32), shape((6, 512, 1024), bf16)],
        in_specs=[vmem] * len(arrays) + [anywhere] * (len(weights) + len(expert)),
        out_specs=[vmem] * 5 + [anywhere] * 6,
        scratch_shapes=scratch
        + [
            pltpu.SemaphoreType.DMA((copies,)),
            pltpu.SemaphoreType.DMA((copies,)),
            pltpu.SemaphoreType.DMA((2,)),
            pltpu.SemaphoreType.DMA((8,)),
        ],
        compiler_params=pltpu.CompilerParams(
            collective_id=collective_id, has_side_effects=True, vmem_limit_bytes=62 * 2**20
        ),
    )(*arrays, *weights, *expert)


Z_LAST = (2, 6, 11)


def start_kernel(*refs):
    query_w, key_w, value_w, output_w, gains_w, rows_in, cot_in, seen, cosine, sine = refs[:10]
    fulls, (hidden_out, cot_out), refs = refs[10:15], refs[15:17], refs[17:]
    gain_rows, attn_out, query_out, key_out, value_out, mixed, *norm_outs = refs[:10]
    product, slots, came_rows, gain_cols, attn_in, query, key, value = refs[10:18]
    normed_query, normed_key, scale_query, scale_key = refs[18:22]
    send_sems, recv_sems, local_sems, load_sems = refs[22:]
    here = Place()
    rep, x, y, z, ex = here.rep, here.x, here.y, here.z, here.ex
    model_width = query_w.shape[1]
    enter([*here.peers, here.other_core])
    copies = Copies(send_sems, recv_sems)
    local = []

    def keep(source, target):
        copy = pltpu.make_async_copy(source, target, local_sems.at[len(local)])
        copy.start()
        local.append(copy)
        return copy

    def give(source, target):
        return [keep(source.at[ex], target.at[ex])] + [
            copies.start(source.at[peer[1]], target.at[ex], peer) for peer in here.peers
        ]

    def take(moved):
        moved[0].wait()
        for copy in moved[1:]:
            copy.wait_recv()

    shards = (query_w, key_w, value_w, output_w, gains_w)
    parts = [(4, 0, 64)] + [(i, k * 16, 16) for i in range(4) for k in range(4)]
    first_stage, one, two, cores = {}, {}, {}, {}

    def spans(j):
        i, first, rows = parts[j]
        half = rows // 2
        return fulls[i].at[rep], pl.ds(first, rows), pl.ds(first, half), pl.ds(first + half, half)

    def along_z(source, target):
        return [
            copies.start(source, target, here.near, here.end),
            copies.start(source, target, here.far, here.end),
            copies.start(source, target, here.across, here.middle),
            copies.start(source, target, here.own_end, here.middle),
        ]

    def pass_on(sent, blocks):
        def arrived():
            sent[1].wait_recv()
            sent[2].wait_recv()
        pl.when(here.middle)(arrived)
        sent.append(copies.start(blocks, blocks, here.own_end, here.middle))

    def arrived_z(sent):
        pl.when(here.middle)(sent[0].wait_recv)
        def arrived():
            sent[3].wait_recv()
            sent[4].wait_recv()
        pl.when(here.end)(arrived)

    other_side = pl.ds(jnp.where(z == 1, 2, 0), 2)

    def stage_open(j):
        full, rows, upper, lower = spans(j)
        shard, own = shards[parts[j][0]], full.at[z, y, x]
        kept = keep(shard.at[rows], own.at[rows])
        if j in Z_LAST:
            a = copies.start(shard.at[upper], own.at[upper], here.other_x)
            first_stage[j] = (a, copies.start(shard.at[lower], own.at[lower], here.other_y)), kept
        else:
            first_stage[j] = along_z(shard.at[rows], own.at[rows]), kept

    def stage_pass(j):
        if j not in Z_LAST:
            full, rows, _, _ = spans(j)
            pass_on(first_stage[j][0], full.at[other_side, y, x, rows])

    def stage_one(j):
        full, rows, upper, lower = spans(j)
        sent, kept = first_stage[j]
        kept.wait()
        if j in Z_LAST:
            sent[0].wait_recv()
            a = full.at[z, y, :, upper]
            two_a = copies.start(a, a, here.other_y)
            sent[1].wait_recv()
            b = full.at[z, :, x, lower]
            one[j] = two_a, copies.start(b, b, here.other_x)
            return
        arrived_z(sent)
        a, b, own = full.at[:, y, x, upper], full.at[:, y, x, lower], full.at[:, y, x, rows]
        one[j] = copies.start(a, a, here.other_x), copies.start(b, b, here.other_y)
        cores[j] = [copies.start(own, own, here.other_core)]

    def stage_two(j):
        full, rows, upper, lower = spans(j)
        one[j][0].wait_recv()
        if j in Z_LAST:
            one[j][1].wait_recv()
            plane = full.at[z, :, :, rows]
            two[j] = along_z(plane, plane)
            cores[j] = [copies.start(plane, plane, here.other_core)]
            return
        a = full.at[:, y, :, upper]
        two_a = copies.start(a, a, here.other_y)
        one[j][1].wait_recv()
        b = full.at[:, :, x, lower]
        two[j] = two_a, copies.start(b, b, here.other_x)
        for c in (full.at[:, y, 1 - x, upper], full.at[:, 1 - y, x, lower]):
            cores[j].append(copies.start(c, c, here.other_core))

    def stage_three(j):
        full, rows, upper, lower = spans(j)
        if j in Z_LAST:
            pass_on(two[j], full.at[other_side, :, :, rows])
            return
        two[j][0].wait_recv()
        a = full.at[:, 1 - y, :, upper]
        cores[j].append(copies.start(a, a, here.other_core))
        two[j][1].wait_recv()
        b = full.at[:, :, 1 - x, lower]
        cores[j].append(copies.start(b, b, here.other_core))

    def stage_four(j):
        if j in Z_LAST:
            full, rows, _, _ = spans(j)
            arrived_z(two[j])
            for k in range(1, 4):
                plane = full.at[(z + k) % 4, :, :, rows]
                cores[j].append(copies.start(plane, plane, here.other_core))

    def complete(j):
        for copy in cores[j]:
            copy.wait_recv()

    def turn_gains():
        complete(0)
        copy = pltpu.make_async_copy(fulls[4], gain_cols, load_sems.at[2])
        copy.start()
        copy.wait()
        for k in range(model_width // 128):
            block = gain_cols[k // 8, k // 2 % 4, k % 2].reshape(128, 128).astype(f32)
            gain_rows[:, k * 128 : k * 128 + 128] = block.T[:8]

    def norm_rows(moved):
        take(moved)
        copy = pltpu.make_async_copy(hidden_out, came_rows, load_sems.at[2])
        copy.start()
        copy.wait()
        def body(k, carry):
            hidden = came_rows[pl.ds(2 * k, 2)].reshape(ROW, model_width).astype(f32)
            scale = lax.rsqrt(jnp.mean(hidden * hidden, axis=1, keepdims=True) + epsilon)
            rows = pl.ds(pl.multiple_of(k * ROW, ROW), ROW)
            attn_in[rows] = (hidden * scale * gain_rows[pl.ds(2, 1)]).astype(bf16)
            return carry
        lax.fori_loop(0, 128 // ROW, body, 0)

    def load(i, n):
        copy = pltpu.make_async_copy(
            fulls[i].at[n // 2, pl.ds(n % 2 * 2, 2)], slots.at[n % 2], load_sems.at[n % 2]
        )
        copy.start()
        return copy

    def project(i):
        for j in range(1 + 4 * i, 5 + 4 * i):
            complete(j)
        loads = {n: load(i, n) for n in range(2)}
        for n in range(4):
            loads[n].wait()
            left = attn_in[:, pl.ds(n * 512, 512)]
            for k in range(4):
                at = pl.ds(k * 512, 512)
                grown = nn(left, slots[n % 2, :, :, :, :, at].reshape(512, 512))
                product[:, at] = grown if n == 0 else product[:, at] + grown
            if n + 2 < 4:
                loads[n + 2] = load(i, n + 2)

    def norm_heads(n, normed_ref, scale_ref, low_ref):
        lane = lax.broadcasted_iota(jnp.int32, (ROW, HEAD_DIM), 1)
        sign = jnp.where(lane < HEAD_DIM // 2, -1.0, 1.0)
        def body(k, carry):
            rows = pl.ds(pl.multiple_of(k * ROW, ROW), ROW)
            pre = product[rows]
            scale = lax.rsqrt(jnp.mean(pre * pre, axis=1, keepdims=True) + epsilon)
            normed = pre * scale
            normed_ref[rows], scale_ref[rows] = normed, scale
            gained = normed * gain_rows[pl.ds(n, 1)]
            for h in range(HEADS):
                at = slice(h * HEAD_DIM, (h + 1) * HEAD_DIM)
                turned = sign * pltpu.roll(gained[:, at], HEAD_DIM // 2, 1)
                low_ref[rows, at] = (gained[:, at] * cosine[rows] + turned * sine[rows]).astype(bf16)
            return carry
        lax.fori_loop(0, 128 // ROW, body, 0)

    def heads(first, count):
        def body(n, carry):
            at = pl.ds(pl.multiple_of((first + n) * HEAD_DIM, HEAD_DIM), HEAD_DIM)
            scores = nt(query[:, at], key[:, at]) * HEAD_DIM ** (-0.5)
            scores = jnp.where(seen[...] > 0, scores, masked_score)
            weights = jnp.exp(scores - jnp.max(scores, axis=1, keepdims=True))
            probs = weights / jnp.sum(weights, axis=1, keepdims=True)
            mixed[:, at] = nn(probs.astype(bf16), value[:, at]).astype(bf16)
            return carry
        lax.fori_loop(0, count, body, 0)

    stage_open(0)
    stage_open(1)
    moved_rows = give(rows_in, hidden_out)
    moved_cot, written = [], []
    for step in range(len(parts) + 3):
        if 1 <= step < len(parts) - 1:
            stage_open(step + 1)
        if step < len(parts):
            stage_pass(step)
        for behind, stage in enumerate((stage_one, stage_two, stage_three, stage_four), 1):
            if 0 <= step - behind < len(parts):
                stage(step - behind)
        if step == 4:
            turn_gains()
        elif step == 6:
            norm_rows(moved_rows)
            written.append(keep(attn_in, attn_out))
        elif step == 8:
            project(0)
        elif step == 9:
            norm_heads(0, normed_query, scale_query, query)
            written.append(keep(query, query_out))
            written.append(keep(normed_query, norm_outs[0]))
            written.append(keep(scale_query, norm_outs[2]))
        elif step == 10:
            moved_cot = give(cot_in, cot_out)
        elif step == 12:
            project(1)
        elif step == 13:
            norm_heads(1, normed_key, scale_key, key)
            written.append(keep(key, key_out))
            written.append(keep(normed_key, norm_outs[1]))
            written.append(keep(scale_key, norm_outs[3]))
        elif step == 16:
            project(2)
            value[...] = product[...].astype(bf16)
            written.append(keep(value, value_out))
        elif step == 17:
            heads(0, 6)
        elif step == 18:
            heads(6, 6)
        elif step == 19:
            heads(12, 4)
    for j in range(13, 17):
        complete(j)
    take(moved_cot)
    for copy in written:
        copy.wait()
    copies.finish()


def run_start(shards, rows, cot, visible, cosine, sine, collective_id):
    model_width = shards[0].shape[1]
    vmem, anywhere = pl.BlockSpec(memory_space=pltpu.VMEM), pl.BlockSpec(memory_space=pl.ANY)
    shape = jax.ShapeDtypeStruct
    own_rows = [(shape((128, model_width), dtype)) for dtype in (bf16,) * 5 + (f32,) * 2]
    *fulls, hidden_in, cot_in, gain_rows, attn_in, query, key, value, mixed, nq, nk, sq, sk = pl.pallas_call(
        start_kernel,
        out_shape=[shape((2, 4, 2, 2) + a.shape, a.dtype) for a in shards]
        + [shape(rows.shape, bf16)] * 2
        + [shape((8, model_width), f32)]
        + own_rows
        + [shape((128, 1), f32)] * 2,
        in_specs=[anywhere] * 7 + [vmem] * 3,
        out_specs=[anywhere] * 7 + [vmem] + [anywhere] * 4 + [vmem] + [anywhere] * 4,
        scratch_shapes=[
            pltpu.VMEM((128, model_width), f32),
            pltpu.VMEM((2, 2, 2, 2, 64, model_width), bf16),
            pltpu.VMEM(rows.shape, bf16),
            pltpu.VMEM((2, 4, 2, 2, 64, 128), bf16),
            *[pltpu.VMEM((128, model_width), dtype) for dtype in (bf16,) * 4 + (f32,) * 2],
            *[pltpu.VMEM((128, 1), f32)] * 2,
            pltpu.SemaphoreType.DMA((14 * 17 + 30,)),
            pltpu.SemaphoreType.DMA((14 * 17 + 30,)),
            pltpu.SemaphoreType.DMA((27,)),
            pltpu.SemaphoreType.DMA((3,)),
        ],
        compiler_params=pltpu.CompilerParams(
            collective_id=collective_id, has_side_effects=True, vmem_limit_bytes=62 * 2**20
        ),
    )(*shards, rows, cot, visible, cosine, sine)
    fulls = [a.reshape(-1, a.shape[-1]) for a in fulls]
    hidden_in, cot_in = (a.reshape(128, model_width) for a in (hidden_in, cot_in))
    return fulls, hidden_in, cot_in, gain_rows, attn_in, query, key, value, mixed, nq, nk, sq, sk


def has_kernels():
    return (lax.axis_size("rep"), lax.axis_size("ex")) == (2, 16)


def exchange(array):
    return lax.all_to_all(array, "ex", split_axis=0, concat_axis=0, tiled=True)


def start(shards, gains, inbound_rows, inbound_cot, visible, cosine, sine):
    block_rows, model_width = inbound_rows.shape[1:]
    row_count = inbound_rows.shape[0] * block_rows
    if has_kernels():
        wide = jnp.pad(gains, ((0, 0), (0, 128 - gains.shape[1])))
        full, hidden_in, cot_in, gain_rows, attn_in, *qkv, mixed, nq, nk, sq, sk = run_start(
            [*shards, wide], inbound_rows, inbound_cot, visible.astype(f32), cosine[:, 0], sine[:, 0], 1
        )
        *weights, wide = full
        qkv = [a.reshape(row_count, HEADS, HEAD_DIM) for a in qkv]
        router = wide[:, 4 : gains.shape[1]]
        return weights, gain_rows[:4], router, hidden_in, cot_in, attn_in, qkv, mixed, (nq, nk, sq, sk)
    gather = functools.partial(lax.all_gather, axis_name=("rep", "ex"), axis=0, tiled=True)
    weights = query_full, key_full, value_full, _ = [gather(a) for a in shards]
    gains = gather(jnp.pad(gains, ((0, 0), (0, -gains.shape[1] % 128))))[:, : gains.shape[1]]
    gain_rows = gains[:, :4].astype(f32).T
    query_scale, key_scale, attn_scale, _ = gain_rows
    hidden_in, cot_in = (exchange(a).reshape(row_count, model_width) for a in (inbound_rows, inbound_cot))
    hidden = hidden_in.astype(f32)
    normed_attn, scale_attn = normalize(hidden)
    attn_in = (normed_attn * attn_scale).astype(bf16)
    query_pre = jnp.dot(attn_in, query_full, preferred_element_type=f32)
    key_pre = jnp.dot(attn_in, key_full, preferred_element_type=f32)
    value_pre = jnp.dot(attn_in, value_full, preferred_element_type=f32)
    normed_query, scale_query = normalize(query_pre)
    normed_key, scale_key = normalize(key_pre)
    query_norm = (normed_query * query_scale).reshape(row_count, HEADS, HEAD_DIM)
    key_norm = (normed_key * key_scale).reshape(row_count, HEADS, HEAD_DIM)
    query_low = (query_norm * cosine + rotate_half(query_norm) * sine).astype(bf16)
    key_low = (key_norm * cosine + rotate_half(key_norm) * sine).astype(bf16)
    value_low = value_pre.astype(bf16).reshape(row_count, HEADS, HEAD_DIM)
    scores = attention_scores(query_low, key_low, visible)
    peak = jnp.max(scores, axis=-1, keepdims=True)
    weights_exp = jnp.exp(scores - peak)
    probs = weights_exp / jnp.sum(weights_exp, axis=-1, keepdims=True)
    probs_low = probs.astype(bf16)
    mixed = jnp.einsum("hqk,khd->qhd", probs_low, value_low, preferred_element_type=f32)
    mixed = mixed.reshape(row_count, model_width).astype(bf16)
    qkv = query_low, key_low, value_low
    norms = normed_query, normed_key, scale_query, scale_key
    return weights, gain_rows, gains[:, 4:], hidden_in, cot_in, attn_in, qkv, mixed, norms


def slots_of(tables, capacity):
    experts, me = tables.shape[1] // 2, lax.axis_index("ex")
    gates = lax.dynamic_index_in_dim(tables, me, 1, keepdims=True)
    slots = lax.dynamic_index_in_dim(tables, experts + me, 1, keepdims=True)
    return slots == jnp.arange(capacity, dtype=f32)[None, :, None], gates


def experts_of_group(moe_in, cot_in, table, gate_full, up_full, down_full, capacity):
    if has_kernels():
        return run_experts(moe_in, cot_in, table, gate_full, up_full, down_full, capacity, 2)
    tables = lax.all_gather(table, "ex", axis=0)
    picked, gate_rows = slots_of(tables, capacity)
    picked_low = picked.astype(bf16)
    slot_gate = jnp.sum(jnp.where(picked, gate_rows, 0.0), axis=2).reshape(-1, 1)

    def pick(rows):
        rows = lax.all_gather(rows, "ex", axis=0)
        rows = jnp.einsum("sct,std->scd", picked_low, rows, preferred_element_type=f32)
        return rows.astype(bf16).reshape(-1, rows.shape[-1])

    def spread(rows):
        rows = rows.reshape(*picked_low.shape[:2], -1)
        rows = jnp.einsum("sct,scd->std", picked_low, rows, preferred_element_type=f32)
        return lax.psum_scatter(rows.astype(bf16), "ex", scatter_dimension=0).astype(f32)

    rows_in, rows_cot = pick(moe_in), pick(cot_in)
    gate_pre = jnp.dot(rows_in, gate_full, preferred_element_type=f32)
    up_pre = jnp.dot(rows_in, up_full, preferred_element_type=f32)
    sigma = jax.nn.sigmoid(gate_pre)
    silu = gate_pre * sigma
    middle = (silu * up_pre).astype(bf16)
    expert_out = jnp.dot(middle, down_full, preferred_element_type=f32).astype(bf16)
    slot_grad = jnp.sum(rows_cot.astype(f32) * expert_out.astype(f32), axis=1)
    rows_grad = (slot_gate * rows_cot.astype(f32)).astype(bf16)
    grad_middle = jnp.dot(rows_grad, down_full.T, preferred_element_type=f32)
    grad_gate_low = (grad_middle * up_pre * sigma * (1.0 + gate_pre * (1.0 - sigma))).astype(bf16)
    grad_up_low = (grad_middle * silu).astype(bf16)
    grad_rows = jnp.dot(grad_gate_low, gate_full.T, preferred_element_type=f32)
    grad_rows = grad_rows + jnp.dot(grad_up_low, up_full.T, preferred_element_type=f32)
    weighted = slot_gate * expert_out.astype(f32)
    slot_grad = slot_grad.reshape(*picked.shape[:2], 1)
    back = exchange(jnp.sum(jnp.where(picked, slot_grad, 0.0), axis=1))
    sums = spread(grad_rows.astype(bf16)), spread(weighted.astype(bf16))
    return *sums, back, rows_in, rows_grad, middle, grad_gate_low, grad_up_low


def exact_dot(left, right):
    return jnp.dot(left, right, precision=lax.Precision.HIGHEST, preferred_element_type=f32)


def finish(
    grad_branch, mixed, attn_in, hidden_in, query_low, key_low, value_low, normed_query, normed_key,
    scale_query, scale_key, visible, cosine, sine, grad_after, query_scale, key_scale, attn_scale,
    grad_moe_scale, moe_in, grad_logits, output, query_full, key_full, value_full, output_full,
    rows_in, rows_grad, middle, grad_gate_low, grad_up_low,
):
    row_count, model_width = mixed.shape
    group_size = lax.axis_size("ex")
    block_rows = row_count // group_size
    if has_kernels():
        experts = grad_logits.shape[1]
        wide = jnp.pad(grad_logits, ((0, 0), (4, 124 - experts)))
        wide = exact_dot(moe_in.T, wide)
        gains = jnp.stack([query_scale, key_scale, attn_scale, grad_moe_scale], axis=0)
        arrays = [
            grad_branch, mixed, attn_in, hidden_in,
            *(a.reshape(row_count, model_width) for a in (query_low, key_low, value_low)),
            normed_query, normed_key, scale_query, scale_key, visible.astype(f32),
            cosine[:, 0], sine[:, 0], grad_after, jnp.pad(gains, ((0, 4), (0, 0))),
            wide.reshape(2, 4, 2, 2, 64, 128), output.reshape(group_size, block_rows, model_width),
        ]
        *weights, summed, given_out, given_grad, gate, up, down, _ = run_finish(
            arrays,
            [query_full, key_full, value_full, output_full],
            [rows_in, rows_grad, middle, grad_gate_low, grad_up_low],
            3,
        )
        rows = [a.reshape(row_count, model_width) for a in (given_out, given_grad)]
        return weights, summed[:, : 4 + experts], rows, (gate, up, down)
    both = ("rep", "ex")
    scores = attention_scores(query_low, key_low, visible)
    probs = jax.nn.softmax(scores, axis=-1)
    probs_low = probs.astype(bf16)
    normed_attn, scale_attn = normalize(hidden_in.astype(f32))
    grad_mixed = (
        jnp.dot(grad_branch, output_full.T, preferred_element_type=f32)
        .astype(bf16)
        .reshape(row_count, HEADS, HEAD_DIM)
    )
    grad_value = jnp.einsum("hqk,qhd->khd", probs_low, grad_mixed, preferred_element_type=f32)
    grad_att = jnp.einsum("qhd,khd->hqk", grad_mixed, value_low, preferred_element_type=f32)
    grad_scores = (probs * (grad_att - jnp.sum(probs * grad_att, axis=-1, keepdims=True))).astype(
        bf16
    )
    grad_query_rot = jnp.einsum(
        "hqk,khd->qhd", grad_scores, key_low, preferred_element_type=f32
    ) * HEAD_DIM ** (-0.5)
    grad_key_rot = jnp.einsum(
        "hqk,qhd->khd", grad_scores, query_low, preferred_element_type=f32
    ) * HEAD_DIM ** (-0.5)
    grad_query_normed = (grad_query_rot * cosine + rotate_back(grad_query_rot * sine)).reshape(
        row_count, model_width
    )
    grad_key_normed = (grad_key_rot * cosine + rotate_back(grad_key_rot * sine)).reshape(
        row_count, model_width
    )
    grad_query_scale = jnp.sum(grad_query_normed * normed_query, axis=0)
    grad_key_scale = jnp.sum(grad_key_normed * normed_key, axis=0)
    grad_query_pre = norm_back(grad_query_normed * query_scale, normed_query, scale_query)
    grad_key_pre = norm_back(grad_key_normed * key_scale, normed_key, scale_key)
    grad_query_pre = grad_query_pre.astype(bf16)
    grad_key_pre = grad_key_pre.astype(bf16)
    grad_value_pre = grad_value.reshape(row_count, model_width).astype(bf16)
    grad_attn_in = jnp.dot(grad_query_pre, query_full.T, preferred_element_type=f32)
    grad_attn_in = grad_attn_in + jnp.dot(grad_key_pre, key_full.T, preferred_element_type=f32)
    grad_attn_in = grad_attn_in + jnp.dot(grad_value_pre, value_full.T, preferred_element_type=f32)
    grad_attn_scale = jnp.sum(grad_attn_in * normed_attn, axis=0)
    grad_hidden = grad_after + norm_back(grad_attn_in * attn_scale, normed_attn, scale_attn)
    sums = []
    for left, right in (
        (attn_in, grad_query_pre),
        (attn_in, grad_key_pre),
        (attn_in, grad_value_pre),
        (mixed, grad_branch),
    ):
        grad = jnp.dot(left.T, right, preferred_element_type=f32).astype(bf16)
        sums.append(lax.psum_scatter(grad, both, scatter_dimension=0, tiled=True).astype(f32))
    four = [grad_query_scale, grad_key_scale, grad_attn_scale, grad_moe_scale]
    grad_router = exact_dot(moe_in.T, grad_logits)
    small = jnp.concatenate([jnp.stack(four, axis=1), grad_router], axis=1)
    small = lax.psum_scatter(small, both, scatter_dimension=0, tiled=True)
    expert = []
    for left, right in ((rows_in, grad_gate_low), (rows_in, grad_up_low), (middle, rows_grad)):
        grad = jnp.dot(left.T, right, preferred_element_type=f32).astype(bf16)
        expert.append(lax.psum_scatter(grad, "rep", scatter_dimension=0, tiled=True).astype(f32))
    rows = [exchange(output), exchange(grad_hidden.astype(bf16))]
    return sums, small, rows, expert


def body(
    tokens,
    out_cot,
    destination,
    doc_lengths,
    routes,
    fill_order,
    query_weight,
    key_weight,
    value_weight,
    output_weight,
    query_gain,
    key_gain,
    attn_gain,
    moe_gain,
    router_weight,
    expert_gate,
    expert_up,
    expert_down,
):
    group_size = lax.axis_size("ex")
    row_count, model_width = tokens.shape
    block_rows = row_count // group_size
    row_index = jnp.arange(row_count, dtype=jnp.int32)
    placed = destination // row_count % group_size * block_rows + destination % block_rows
    to_send = (placed[None, :] == row_index[:, None]).astype(bf16)
    inbound = jnp.einsum(
        "pr,brd->bpd", to_send, jnp.stack([tokens, out_cot]), preferred_element_type=f32
    ).astype(bf16)
    gains = jnp.concatenate(
        [jnp.stack([query_gain, key_gain, attn_gain, moe_gain], axis=1), router_weight], axis=1
    )
    segment, position, live_rows = segment_tables(doc_lengths[0], row_count)
    visible = (segment[:, None] == segment[None, :]) & (row_index[None, :] <= row_index[:, None])
    cosine, sine = rope_tables(position)
    shards = [query_weight, key_weight, value_weight, output_weight]
    inbound = inbound.reshape(2, group_size, block_rows, model_width)
    weights, gain_rows, router_full, hidden_in, cot_in, attn_in, qkv, mixed, norms = start(
        shards, gains, inbound[0], inbound[1], visible, cosine, sine
    )
    query_full, key_full, value_full, output_full = weights
    query_scale, key_scale, attn_scale, moe_scale = gain_rows
    query_low, key_low, value_low = qkv
    normed_query, normed_key, scale_query, scale_key = norms
    gate_full = lax.all_gather(expert_gate[0], "rep", axis=0, tiled=True)
    up_full = lax.all_gather(expert_up[0], "rep", axis=0, tiled=True)
    down_full = lax.all_gather(expert_down[0], "rep", axis=0, tiled=True)

    live_column = live_rows.astype(f32)[:, None]
    hidden = hidden_in.astype(f32)
    branch = jnp.dot(mixed, output_full, preferred_element_type=f32)
    after_attn = hidden + live_column * branch
    normed_moe, scale_moe = normalize(after_attn)
    moe_in = (normed_moe * moe_scale).astype(bf16)
    logits = jnp.dot(moe_in, router_full, preferred_element_type=f32)
    router_probs = jax.nn.softmax(logits, axis=-1)
    experts = router_full.shape[1]
    capacity = row_count * routes.shape[1] // experts
    slot_table, kept = slot_tables(routes, fill_order[0], live_rows, experts, capacity)
    gates = jnp.where(kept, router_probs, 0.0)

    table = jnp.concatenate([gates.T, slot_table.T.astype(f32)], axis=0)
    (
        grad_moe_in,
        mixture,
        grad_rprobs,
        rows_in,
        rows_grad,
        middle,
        grad_gate_low,
        grad_up_low,
    ) = experts_of_group(moe_in, cot_in, table, gate_full, up_full, down_full, capacity)
    grad_rprobs = grad_rprobs.T
    output = (after_attn + mixture).astype(bf16)

    grad_out = cot_in.astype(f32)
    grad_logits = router_probs * (
        grad_rprobs - jnp.sum(router_probs * grad_rprobs, axis=-1, keepdims=True)
    )
    grad_moe_in = grad_moe_in + jnp.dot(
        grad_logits, router_full.T, precision=lax.Precision.HIGHEST, preferred_element_type=f32
    )
    grad_moe_scale = jnp.sum(grad_moe_in * normed_moe, axis=0)
    grad_after = grad_out + norm_back(grad_moe_in * moe_scale, normed_moe, scale_moe)
    grad_branch = (live_column * grad_after).astype(bf16)
    sums, small, rows, expert = finish(
        grad_branch, mixed, attn_in, hidden_in, query_low, key_low, value_low, normed_query,
        normed_key, scale_query, scale_key, visible, cosine, sine, grad_after, query_scale,
        key_scale, attn_scale, grad_moe_scale, moe_in, grad_logits, output, query_full, key_full, value_full, output_full,
        rows_in, rows_grad, middle, grad_gate_low, grad_up_low,
    )
    owned_query, owned_key, owned_value, owned_output = sums
    owned_gate, owned_up, owned_down = (a[None] for a in expert)
    outbound = jnp.dot(
        to_send.T, jnp.concatenate(rows, axis=1), preferred_element_type=f32
    ).astype(bf16)
    return (
        outbound[:, :model_width],
        outbound[:, model_width:],
        owned_query,
        owned_key,
        owned_value,
        owned_output,
        small[:, 0],
        small[:, 1],
        small[:, 2],
        small[:, 3],
        small[:, 4:],
        owned_gate,
        owned_up,
        owned_down,
    )


def solution(mesh):
    rows, row = P(("rep", "ex"), None), P(("rep", "ex"))
    expert = P("ex", "rep", None)
    return jax.shard_map(
        body,
        mesh=mesh,
        in_specs=(rows, rows, row) + (rows,) * 7 + (row,) * 4 + (rows,) + (expert,) * 3,
        out_specs=(rows,) * 6 + (row,) * 4 + (rows,) + (expert,) * 3,
        check_vma=False,
    )
```
